32 devices in a mesh: tower: 2 (over x), dp: 16 (over z, y, core).
Axes of the slice: x: 2, y: 2, z: 4, core: 2. Of those that a mesh axis runs over, the one named last changes fastest.
Arguments:
- tokens: bfloat16 [2, 128, 77, 768], P('tower', 'dp'), as said below
- lengths: int32 [128], P('dp'), may hold values from 5 to 77, as said below
- ln1_gain: bfloat16 [2, 768], P('tower', 'dp'), as said below
- ln1_bias: bfloat16 [2, 768], P('tower', 'dp'), as said below
- qkv_weight: bfloat16 [2, 768, 3, 768], P('tower', 'dp'), as said below
- qv_bias: bfloat16 [2, 2, 768], P('tower', None, 'dp'), as said below
- out_weight: bfloat16 [2, 768, 768], P('tower', 'dp'), as said below
- out_bias: bfloat16 [2, 768], P('tower', 'dp'), as said below
- ln2_gain: bfloat16 [2, 768], P('tower', 'dp'), as said below
- ln2_bias: bfloat16 [2, 768], P('tower', 'dp'), as said below
- fc_weight: bfloat16 [2, 768, 3072], P('tower', 'dp'), as said below
- fc_bias: bfloat16 [2, 3072], P('tower', 'dp'), as said below
- down_weight: bfloat16 [2, 3072, 768], P('tower', 'dp'), as said below
- down_bias: bfloat16 [2, 768], P('tower', 'dp'), as said below
- final_gain: bfloat16 [2, 768], P('tower', 'dp'), as said below
- final_bias: bfloat16 [2, 768], P('tower', 'dp'), as said below
- embed_weight: bfloat16 [2, 768, 512], P('tower', 'dp'), as said below
- logit_scale: float32 [1], replicated, may hold values from 3.4 to 4.1
Outputs:
- block_out: bfloat16 [2, 128, 77, 768], P('tower', 'dp')
- tokens_grad: float32 [2, 128, 77, 768], P('tower', 'dp')
- loss: float32 [1], replicated
- ln1_gain_grad: float32 [2, 768], P('tower', 'dp')
- ln1_bias_grad: float32 [2, 768], P('tower', 'dp')
- qkv_weight_grad: float32 [2, 768, 3, 768], P('tower', 'dp')
- qv_bias_grad: float32 [2, 2, 768], P('tower', None, 'dp')
- out_weight_grad: float32 [2, 768, 768], P('tower', 'dp')
- out_bias_grad: float32 [2, 768], P('tower', 'dp')
- ln2_gain_grad: float32 [2, 768], P('tower', 'dp')
- ln2_bias_grad: float32 [2, 768], P('tower', 'dp')
- fc_weight_grad: float32 [2, 768, 3072], P('tower', 'dp')
- fc_bias_grad: float32 [2, 3072], P('tower', 'dp')
- down_weight_grad: float32 [2, 3072, 768], P('tower', 'dp')
- down_bias_grad: float32 [2, 768], P('tower', 'dp')
- final_gain_grad: float32 [2, 768], P('tower', 'dp')
- final_bias_grad: float32 [2, 768], P('tower', 'dp')
- embed_weight_grad: float32 [2, 768, 512], P('tower', 'dp')
- logit_scale_grad: float32 [1], replicated
The draws below stay inside these ranges and needn't reach their ends.
Inputs may be any that keep to these rules, and one draw needn't show every extreme that they name: `tokens`: image slot zero from row 50 on; text slot zero from feature 512 on. `lengths`: device 0 of dp holds a caption of 77 slots and one of 5. `ln1_gain`: text slot zero from feature 512 on. `ln1_bias`: text slot zero from feature 512 on. `qkv_weight`: text slot zero outside its first 512 rows and first 512 columns of each third. `qv_bias`: text slot zero from feature 512 on. `out_weight`: text slot zero outside its leading 512 x 512 block. `out_bias`: text slot zero from feature 512 on. `ln2_gain`: text slot zero from feature 512 on. `ln2_bias`: text slot zero from feature 512 on. `fc_weight`: text slot zero outside its leading 512 x 2048 block. `fc_bias`: text slot zero from unit 2048 on. `down_weight`: text slot zero outside its leading 2048 x 512 block. `down_bias`: text slot zero from feature 512 on. `final_gain`: text slot zero from feature 512 on. `final_bias`: text slot zero from feature 512 on. `embed_weight`: text slot zero from row 512 on.
All inputs are finite; a program needn't handle non-finite values.
Results may differ from the reference program's by a relative error of at most 0.02.
The reference program's roundings to bfloat16 on the way count: a program that leaves them out, or rounds other values in their place, can miss the bound.
Values may be sent and summed in bfloat16 or wider, within the bound.
No kernel may reach another device: no remote copies, remote signals or barrier semaphores. Data moves between devices by JAX's collectives and lax.ppermute only.
A program may use at most 192 MiB of HBM per device.

```python
import jax
import jax.numpy as jnp
from jax import lax

DI = 768
DT = 512
HD = 64
FI = 3072
FT = 2048
EMB = 512
ROWS = 77
IMG_ROWS = 50
MIN_LEN = 5
SAMP_DEV = 8
SAMPLES = 128


def region(full_shape, limits):
    inside = jnp.ones(full_shape, jnp.float32)
    for axis_pos, limit_val in enumerate(limits):
        index_grid = lax.broadcasted_iota(jnp.int32, full_shape, axis_pos)
        inside = inside * (index_grid < limit_val).astype(jnp.float32)
    return inside


def tower_pair(key, tag, part_shape, img_limits, txt_limits, sampler):
    base_key = jax.random.fold_in(key, tag)
    img_key, txt_key = jax.random.split(base_key)
    img_part = sampler(img_key, part_shape, 0) * region(part_shape, img_limits)
    txt_part = sampler(txt_key, part_shape, 1) * region(part_shape, txt_limits)
    return jnp.stack([img_part, txt_part])


def normal_clip(sub_key, part_shape, spread):
    return spread * jnp.clip(jax.random.normal(sub_key, part_shape, jnp.float32), -4.0, 4.0)


def weight_sampler(img_fan, txt_fan, boost_gain):

    def sampler(sub_key, part_shape, tower_slot):
        fan_size = img_fan if tower_slot == 0 else txt_fan
        return normal_clip(sub_key, part_shape, boost_gain * fan_size ** (-0.5))
    return sampler


def gain_sampler(sub_key, part_shape, tower_slot):
    return 1.0 + 0.3 * jax.random.uniform(sub_key, part_shape, jnp.float32, -1.0, 1.0)


def bias_sampler(sub_key, part_shape, tower_slot):
    return normal_clip(sub_key, part_shape, 0.2)


def token_sampler(sub_key, part_shape, tower_slot):
    return normal_clip(sub_key, part_shape, 1.0)


def draw_tokens(key, part):
    return tower_pair(key, 11, (SAMPLES, ROWS, DI), (SAMPLES, IMG_ROWS, DI), (SAMPLES, ROWS, DT), token_sampler).astype(jnp.bfloat16)


def draw_lengths(key, part):
    length_draw = jax.random.randint(jax.random.fold_in(key, 12), (SAMPLES,), MIN_LEN, ROWS + 1)
    slot_index = jnp.arange(SAMPLES)
    length_draw = jnp.where(slot_index == 0, ROWS, length_draw)
    return jnp.where(slot_index == 1, MIN_LEN, length_draw).astype(jnp.int32)


def width_vector(key, tag, sampler):
    return tower_pair(key, tag, (DI,), (DI,), (DT,), sampler).astype(jnp.bfloat16)


def draw_ln1_gain(key, part):
    return width_vector(key, 13, gain_sampler)


def draw_ln1_bias(key, part):
    return width_vector(key, 14, bias_sampler)


def draw_qkv_weight(key, part):
    return tower_pair(key, 15, (DI, 3, DI), (DI, 3, DI), (DT, 3, DT), weight_sampler(DI, DT, 1.0)).astype(jnp.bfloat16)


def draw_qv_bias(key, part):
    return tower_pair(key, 16, (2, DI), (2, DI), (2, DT), bias_sampler).astype(jnp.bfloat16)


def draw_out_weight(key, part):
    return tower_pair(key, 17, (DI, DI), (DI, DI), (DT, DT), weight_sampler(DI, DT, 4.0)).astype(jnp.bfloat16)


def draw_out_bias(key, part):
    return width_vector(key, 18, bias_sampler)


def draw_ln2_gain(key, part):
    return width_vector(key, 19, gain_sampler)


def draw_ln2_bias(key, part):
    return width_vector(key, 20, bias_sampler)


def draw_fc_weight(key, part):
    return tower_pair(key, 21, (DI, FI), (DI, FI), (DT, FT), weight_sampler(DI, DT, 1.0)).astype(jnp.bfloat16)


def draw_fc_bias(key, part):
    return tower_pair(key, 22, (FI,), (FI,), (FT,), bias_sampler).astype(jnp.bfloat16)


def draw_down_weight(key, part):
    return tower_pair(key, 23, (FI, DI), (FI, DI), (FT, DT), weight_sampler(FI, FT, 1.0)).astype(jnp.bfloat16)


def draw_down_bias(key, part):
    return width_vector(key, 24, bias_sampler)


def draw_final_gain(key, part):
    return width_vector(key, 25, gain_sampler)


def draw_final_bias(key, part):
    return width_vector(key, 26, bias_sampler)


def draw_embed_weight(key, part):
    return tower_pair(key, 27, (DI, EMB), (DI, EMB), (DT, EMB), weight_sampler(DI, DT, 1.0)).astype(jnp.bfloat16)


def setup_inputs(seed: int = 0) -> dict:
    seeds = jax.random.split(jax.random.key(seed), 19)
    return {
        "tokens": draw_tokens(jax.random.fold_in(seeds[18], 71), 0),
        "lengths": draw_lengths(jax.random.fold_in(seeds[18], 71), 0),
        "ln1_gain": draw_ln1_gain(jax.random.fold_in(seeds[18], 71), 0),
        "ln1_bias": draw_ln1_bias(jax.random.fold_in(seeds[18], 71), 0),
        "qkv_weight": draw_qkv_weight(jax.random.fold_in(seeds[18], 71), 0),
        "qv_bias": draw_qv_bias(jax.random.fold_in(seeds[18], 71), 0),
        "out_weight": draw_out_weight(jax.random.fold_in(seeds[18], 71), 0),
        "out_bias": draw_out_bias(jax.random.fold_in(seeds[18], 71), 0),
        "ln2_gain": draw_ln2_gain(jax.random.fold_in(seeds[18], 71), 0),
        "ln2_bias": draw_ln2_bias(jax.random.fold_in(seeds[18], 71), 0),
        "fc_weight": draw_fc_weight(jax.random.fold_in(seeds[18], 71), 0),
        "fc_bias": draw_fc_bias(jax.random.fold_in(seeds[18], 71), 0),
        "down_weight": draw_down_weight(jax.random.fold_in(seeds[18], 71), 0),
        "down_bias": draw_down_bias(jax.random.fold_in(seeds[18], 71), 0),
        "final_gain": draw_final_gain(jax.random.fold_in(seeds[18], 71), 0),
        "final_bias": draw_final_bias(jax.random.fold_in(seeds[18], 71), 0),
        "embed_weight": draw_embed_weight(jax.random.fold_in(seeds[18], 71), 0),
        "logit_scale": jnp.clip(jax.random.uniform(seeds[17], (1,), jnp.float32, 3.4, 4.1), 3.4, 4.1),
    }


EPS = 1e-05
NORM_EPS = 1e-06
GELU_K = 1.702
NEG_FILL = -1e+30
HIGH = lax.Precision.HIGHEST

@jax.custom_vjp
def low(v):
    return lax.optimization_barrier(v.astype(jnp.bfloat16)).astype(jnp.float32)

@jax.custom_vjp
def low_back(v):
    return v

def low_keep(v):
    return (low(v), None)

def low_pass(kept, grad):
    return (grad,)

def back_keep(v):
    return (v, None)

def back_low(kept, grad):
    return (low(grad),)
low.defvjp(low_keep, low_pass)
low_back.defvjp(back_keep, back_low)

def layer_norm(values, norm_gain, norm_bias):
    centre = lax.optimization_barrier(jnp.mean(values, axis=-1, keepdims=True))
    shifted = values - centre
    spread = lax.optimization_barrier(jnp.mean(shifted * shifted, axis=-1, keepdims=True))
    return shifted * lax.rsqrt(spread + EPS) * norm_gain + norm_bias

def block_group(stream, allowed, row_keep, params):
    gain_one, bias_one, w_qkv, b_qv, w_out, b_out, gain_two, bias_two, w_fc, b_fc, w_down, b_down = params
    samples, seq_len, width_real = stream.shape
    head_count = width_real // HD
    normed_one = low(layer_norm(stream, gain_one, bias_one))
    qkv_bias = jnp.stack([b_qv[0], jnp.zeros_like(b_qv[0]), b_qv[1]])
    qkv_all = low(low_back(jnp.einsum('srd,dcn->srcn', normed_one, w_qkv, precision=HIGH) + qkv_bias))
    qkv_all = qkv_all.reshape(samples, seq_len, 3, head_count, HD)
    scores = low_back(jnp.einsum('sqhd,skhd->shqk', qkv_all[:, :, 0], qkv_all[:, :, 1], precision=HIGH) * HD ** (-0.5))
    scores = jnp.where(allowed[:, None], scores, NEG_FILL)
    attn_probs = low(jax.nn.softmax(scores, axis=-1))
    head_mix = low(low_back(jnp.einsum('shqk,skhd->sqhd', attn_probs, qkv_all[:, :, 2], precision=HIGH)))
    head_mix = head_mix.reshape(samples, seq_len, width_real)
    attn_out = low_back(jnp.einsum('srd,de->sre', head_mix, w_out, precision=HIGH) + b_out)
    middle = stream + attn_out
    normed_two = low(layer_norm(middle, gain_two, bias_two))
    hidden_pre = low_back(jnp.einsum('srd,df->srf', normed_two, w_fc, precision=HIGH) + b_fc)
    hidden_act = low(hidden_pre * jax.nn.sigmoid(GELU_K * hidden_pre))
    branch = low_back(jnp.einsum('srf,fd->srd', hidden_act, w_down, precision=HIGH) + b_down)
    return row_keep[:, :, None] * (middle + branch)

def run_tower(stream, seq_lens, params, causal):
    sample_count, seq_len, width_real = stream.shape
    query_pos = lax.broadcasted_iota(jnp.int32, (seq_len, seq_len), 0)
    key_pos = lax.broadcasted_iota(jnp.int32, (seq_len, seq_len), 1)
    allowed = key_pos[None] < seq_lens[:, None, None]
    if causal:
        allowed = allowed & (key_pos <= query_pos)[None]
    row_pos = lax.broadcasted_iota(jnp.int32, (sample_count, seq_len), 1)
    row_keep = (row_pos < seq_lens[:, None]).astype(jnp.float32)
    group_count = sample_count // SAMP_DEV

    def one_group(pieces):
        return block_group(pieces[0], pieces[1], pieces[2], params)
    outputs = lax.map(jax.checkpoint(one_group), (stream.reshape(group_count, SAMP_DEV, seq_len, width_real), allowed.reshape(group_count, SAMP_DEV, seq_len, seq_len), row_keep.reshape(group_count, SAMP_DEV, seq_len)))
    return outputs.reshape(sample_count, seq_len, width_real)

def embed_head(pooled, norm_gain, norm_bias, w_embed):
    normed = low(layer_norm(pooled, norm_gain, norm_bias))
    projected = low_back(jnp.dot(normed, w_embed, precision=HIGH))
    return low(projected * lax.rsqrt(lax.optimization_barrier(jnp.sum(projected * projected, axis=-1, keepdims=True)) + NORM_EPS))

def direction_loss(own_rows, other_rows, logit_mult):
    similar = low_back(jnp.dot(own_rows, other_rows.T, precision=HIGH))
    logits = logit_mult * similar
    log_total = jax.nn.logsumexp(logits, axis=-1)
    return jnp.sum(log_total - jnp.diagonal(logits))

def forward(lengths, tokens_f, ln1_gain, ln1_bias, qkv_weight, qv_bias, out_weight, out_bias, ln2_gain, ln2_bias, fc_weight, fc_bias, down_weight, down_bias, final_gain, final_bias, embed_weight, logit_scale):

    def tower_params(slot_index, width_real, hidden_real):
        return (ln1_gain[slot_index, :width_real], ln1_bias[slot_index, :width_real], qkv_weight[slot_index, :width_real, :, :width_real], qv_bias[slot_index, :, :width_real], out_weight[slot_index, :width_real, :width_real], out_bias[slot_index, :width_real], ln2_gain[slot_index, :width_real], ln2_bias[slot_index, :width_real], fc_weight[slot_index, :width_real, :hidden_real], fc_bias[slot_index, :hidden_real], down_weight[slot_index, :hidden_real, :width_real], down_bias[slot_index, :width_real])
    img_stream = tokens_f[0, :, :IMG_ROWS, :DI]
    txt_stream = tokens_f[1, :, :, :DT]
    img_lens = jnp.full((SAMPLES,), IMG_ROWS, jnp.int32)
    img_out = run_tower(img_stream, img_lens, tower_params(0, DI, FI), False)
    txt_out = run_tower(txt_stream, lengths, tower_params(1, DT, FT), True)
    img_pooled = img_out[:, 0]
    pool_index = (lengths - 1).astype(jnp.int32)
    txt_pooled = jnp.take_along_axis(txt_out, pool_index[:, None, None], axis=1)[:, 0]
    img_embed = embed_head(img_pooled, final_gain[0, :DI], final_bias[0, :DI], embed_weight[0, :DI])
    txt_embed = embed_head(txt_pooled, final_gain[1, :DT], final_bias[1, :DT], embed_weight[1, :DT])
    logit_mult = jnp.exp(logit_scale[0])
    summed = 0.5 * (direction_loss(img_embed, txt_embed, logit_mult) + direction_loss(txt_embed, img_embed, logit_mult))
    block_img = jnp.pad(img_out, ((0, 0), (0, ROWS - IMG_ROWS), (0, 0)))
    block_txt = jnp.pad(txt_out, ((0, 0), (0, 0), (0, DI - DT)))
    return (summed, jnp.stack([block_img, block_txt]))

def reference(tokens, lengths, ln1_gain, ln1_bias, qkv_weight, qv_bias, out_weight, out_bias, ln2_gain, ln2_bias, fc_weight, fc_bias, down_weight, down_bias, final_gain, final_bias, embed_weight, logit_scale):
    floats = [tokens, ln1_gain, ln1_bias, qkv_weight, qv_bias, out_weight, out_bias, ln2_gain, ln2_bias, fc_weight, fc_bias, down_weight, down_bias, final_gain, final_bias, embed_weight]
    floats = [item.astype(jnp.float32) for item in floats] + [logit_scale.astype(jnp.float32)]

    def objective(*values):
        return forward(lengths, *values)
    summed, back_fn, block_all = jax.vjp(objective, *floats, has_aux=True)
    gradients = back_fn(jnp.ones_like(summed))
    loss = (summed / SAMPLES).reshape(1)
    return (block_all.astype(jnp.bfloat16), gradients[0], loss, gradients[1], gradients[2], gradients[3], gradients[4], gradients[5], gradients[6], gradients[7], gradients[8], gradients[9], gradients[10], gradients[11], gradients[12], gradients[13], gradients[14], gradients[15], gradients[16])
```

```python
import jax
import jax.numpy as jnp
from jax import lax
from jax.experimental import pallas as pl
from jax.experimental.pallas import tpu as pltpu
from jax.sharding import PartitionSpec as P

DI = 768
DT = 512
HD = 64
IMG_ROWS = 50
EMB = 512


EPS = 1e-05
NORM_EPS = 1e-06
GELU_K = 1.702
NEG_FILL = -1e30


def swapped(block, axis, stride):
    count = lax.axis_size(axis)
    route = []
    for low in range(count):
        high = low | 1 << stride
        if high != low and high < count:
            route += [(low, high), (high, low)]
    return lax.ppermute(block, axis, route)


def masked_norm(values, norm_gain, norm_bias, col_keep, width_real):
    row_mean = jnp.sum(values * col_keep, axis=-1, keepdims=True) / width_real
    centred = (values - row_mean) * col_keep
    row_var = jnp.sum(centred * centred, axis=-1, keepdims=True) / width_real
    inv_std = lax.rsqrt(row_var + EPS)
    normed = centred * inv_std
    return (normed * norm_gain + norm_bias, normed, inv_std)


def masked_norm_back(grad_out, norm_gain, normed, inv_std, col_keep, width_real):
    grad_normed = grad_out * norm_gain
    mean_grad = jnp.sum(grad_normed, axis=-1, keepdims=True) / width_real
    mean_cross = jnp.sum(grad_normed * normed, axis=-1, keepdims=True) / width_real
    grad_in = col_keep * inv_std * (grad_normed - mean_grad - normed * mean_cross)
    return (grad_in, jnp.sum(grad_out * normed, axis=0), jnp.sum(grad_out, axis=0))


def contract_rows(left_op, right_op):
    return lax.dot_general(
        left_op, right_op, (((0,), (0,)), ((), ())), preferred_element_type=jnp.float32
    )


def contract_cols(left_op, right_op):
    return lax.dot_general(
        left_op, right_op, (((1,), (1,)), ((), ())), preferred_element_type=jnp.float32
    )


def column_sum(values):
    return jnp.sum(values, axis=0, dtype=jnp.float32)


def body(
    tokens,
    lengths,
    ln1_gain,
    ln1_bias,
    qkv_weight,
    qv_bias,
    out_weight,
    out_bias,
    ln2_gain,
    ln2_bias,
    fc_weight,
    fc_bias,
    down_weight,
    down_bias,
    final_gain,
    final_bias,
    embed_weight,
    logit_scale,
):
    f32 = jnp.float32
    bf16 = jnp.bfloat16
    tower_index = lax.axis_index("tower")
    dp_index = lax.axis_index("dp")
    dp_count = lax.axis_size("dp")
    samples, seq_rows, width_all = (tokens.shape[1], tokens.shape[2], tokens.shape[3])
    head_count = width_all // HD
    sample_total = samples * dp_count
    flat_rows = samples * seq_rows
    is_text = tower_index == 1
    width_int = jnp.where(is_text, DT, DI)
    width_real = width_int.astype(f32)
    col_keep = (lax.broadcasted_iota(jnp.int32, (width_all,), 0) < width_int).astype(f32)
    seq_lens = jnp.where(is_text, lengths, IMG_ROWS)
    positions = lax.broadcasted_iota(jnp.int32, (samples, seq_rows), 1)
    row_keep = (positions < seq_lens[:, None]).astype(f32).reshape(flat_rows, 1)
    query_pos = lax.broadcasted_iota(jnp.int32, (seq_rows, seq_rows), 0)
    key_pos = lax.broadcasted_iota(jnp.int32, (seq_rows, seq_rows), 1)
    allowed = (key_pos[None] < seq_lens[:, None, None]) & (
        jnp.logical_not(is_text) | (key_pos <= query_pos)
    )[None]
    pool_pos = jnp.where(is_text, lengths - 1, 0)
    pool_hot = (positions == pool_pos[:, None]).astype(f32)
    score_mult = float(HD) ** (-0.5)
    gathered = (
        lax.all_gather(ln1_gain[0], "dp", axis=0, tiled=True),
        lax.all_gather(ln1_bias[0], "dp", axis=0, tiled=True),
        lax.all_gather(qkv_weight[0], "dp", axis=0, tiled=True),
        lax.all_gather(qv_bias[0], "dp", axis=1, tiled=True),
        lax.all_gather(out_weight[0], "dp", axis=0, tiled=True),
        lax.all_gather(out_bias[0], "dp", axis=0, tiled=True),
        lax.all_gather(ln2_gain[0], "dp", axis=0, tiled=True),
        lax.all_gather(ln2_bias[0], "dp", axis=0, tiled=True),
        lax.all_gather(fc_weight[0], "dp", axis=0, tiled=True),
        lax.all_gather(fc_bias[0], "dp", axis=0, tiled=True),
        lax.all_gather(down_weight[0], "dp", axis=0, tiled=True),
        lax.all_gather(down_bias[0], "dp", axis=0, tiled=True),
        lax.all_gather(final_gain[0], "dp", axis=0, tiled=True),
        lax.all_gather(final_bias[0], "dp", axis=0, tiled=True),
        lax.all_gather(embed_weight[0], "dp", axis=0, tiled=True),
    )
    (
        gain_one,
        bias_one,
        w_qkv,
        b_qv,
        w_out,
        b_out,
        gain_two,
        bias_two,
        w_fc,
        b_fc,
        w_down,
        b_down,
        gain_final,
        bias_final,
        w_embed,
    ) = gathered
    stream = tokens[0].astype(f32).reshape(flat_rows, width_all)
    normed_h1, norm_one, inv_one = masked_norm(
        stream, gain_one.astype(f32), bias_one.astype(f32), col_keep, width_real
    )
    normed_one = normed_h1.astype(bf16)
    qkv_bias = jnp.concatenate(
        [b_qv[0].astype(f32), jnp.zeros((width_all,), f32), b_qv[1].astype(f32)]
    )
    qkv_flat = (
        jnp.dot(normed_one, w_qkv.reshape(width_all, 3 * width_all), preferred_element_type=f32)
        + qkv_bias
    )
    qkv_low = qkv_flat.astype(bf16).reshape(samples, seq_rows, 3, head_count, HD)
    query_all = qkv_low[:, :, 0]
    key_all = qkv_low[:, :, 1]
    value_all = qkv_low[:, :, 2]

    def masked_scores():
        raw = (
            jnp.einsum("sqhd,skhd->shqk", query_all, key_all, preferred_element_type=f32)
            * score_mult
        )
        return jnp.where(allowed[:, None], raw, NEG_FILL)

    scores = masked_scores()
    row_top = jnp.max(scores, axis=-1, keepdims=True)
    exp_terms = jnp.exp(scores - row_top)
    exp_sum = jnp.sum(exp_terms, axis=-1, keepdims=True)
    log_total = row_top + jnp.log(exp_sum)
    attn_probs = (exp_terms / exp_sum).astype(bf16)
    head_mix = jnp.einsum("shqk,skhd->sqhd", attn_probs, value_all, preferred_element_type=f32)
    head_mix_low = head_mix.astype(bf16).reshape(flat_rows, width_all)
    attn_out = jnp.dot(head_mix_low, w_out, preferred_element_type=f32) + b_out.astype(f32)
    middle = stream + attn_out
    normed_h2, norm_two, inv_two = masked_norm(
        middle, gain_two.astype(f32), bias_two.astype(f32), col_keep, width_real
    )
    normed_two = normed_h2.astype(bf16)
    hidden_pre = jnp.dot(normed_two, w_fc, preferred_element_type=f32) + b_fc.astype(f32)
    gate_sig = jax.nn.sigmoid(GELU_K * hidden_pre)
    act_low = (hidden_pre * gate_sig).astype(bf16)
    branch = jnp.dot(act_low, w_down, preferred_element_type=f32) + b_down.astype(f32)
    block_rows = row_keep * (middle + branch)
    block_out = block_rows.astype(bf16).reshape(1, samples, seq_rows, width_all)
    block_three = block_rows.reshape(samples, seq_rows, width_all)
    pooled = jnp.take_along_axis(block_three, pool_pos[:, None, None], axis=1)[:, 0]
    normed_hf, norm_final, inv_final = masked_norm(
        pooled, gain_final.astype(f32), bias_final.astype(f32), col_keep, width_real
    )
    head_low = normed_hf.astype(bf16)
    projected = jnp.dot(head_low, w_embed, preferred_element_type=f32)
    inv_norm = lax.rsqrt(jnp.sum(projected * projected, axis=-1, keepdims=True) + NORM_EPS)
    embed_low = (projected * inv_norm).astype(bf16)
    own_all = lax.all_gather(embed_low, "dp", axis=0, tiled=True)
    others = swapped(own_all, "tower", 0)
    logit_mult = jnp.exp(logit_scale[0])
    similar = contract_cols(embed_low, others)
    logits = logit_mult * similar
    logit_top = jnp.max(logits, axis=-1, keepdims=True)
    logit_total = logit_top + jnp.log(jnp.sum(jnp.exp(logits - logit_top), axis=-1, keepdims=True))
    label_col = dp_index * samples + lax.broadcasted_iota(jnp.int32, (samples, 1), 0)
    label_hot = (lax.broadcasted_iota(jnp.int32, (samples, sample_total), 1) == label_col).astype(
        f32
    )
    diag_logit = jnp.sum(label_hot * logits, axis=-1, keepdims=True)
    loss_part = jnp.sum(logit_total - diag_logit) / (2.0 * sample_total)
    grad_logits = (jnp.exp(logits - logit_total) - label_hot) * 0.5
    scale_part = logit_mult * jnp.sum(grad_logits * similar)
    grad_sims = (logit_mult * grad_logits).astype(bf16)
    grad_own = jnp.dot(grad_sims, others, preferred_element_type=f32)
    grad_others = contract_rows(grad_sims, embed_low)
    sent_back = swapped(grad_others, "tower", 0)
    returned = lax.psum_scatter(sent_back, "dp", scatter_dimension=0, tiled=True)
    totals = lax.psum((loss_part, scale_part), ("tower", "dp"))
    grad_embed = grad_own + returned
    again = (
        lax.all_gather(ln1_gain[0], "dp", axis=0, tiled=True),
        lax.all_gather(qkv_weight[0], "dp", axis=0, tiled=True),
        lax.all_gather(out_weight[0], "dp", axis=0, tiled=True),
        lax.all_gather(ln2_gain[0], "dp", axis=0, tiled=True),
        lax.all_gather(fc_weight[0], "dp", axis=0, tiled=True),
        lax.all_gather(down_weight[0], "dp", axis=0, tiled=True),
        lax.all_gather(final_gain[0], "dp", axis=0, tiled=True),
        lax.all_gather(embed_weight[0], "dp", axis=0, tiled=True),
    )
    (
        back_gain_one,
        back_qkv,
        back_out,
        back_gain_two,
        back_fc,
        back_down,
        back_gain_final,
        back_embed,
    ) = again
    cross_term = jnp.sum(grad_embed * projected, axis=-1, keepdims=True)
    grad_proj = inv_norm * grad_embed - projected * inv_norm * inv_norm * inv_norm * cross_term
    grad_proj_low = grad_proj.astype(bf16)
    grad_head = contract_cols(grad_proj_low, back_embed)
    grad_pooled, d_gain_final, d_bias_final = masked_norm_back(
        grad_head, back_gain_final.astype(f32), norm_final, inv_final, col_keep, width_real
    )
    grad_rows = (pool_hot[:, :, None] * grad_pooled[:, None, :]).reshape(flat_rows, width_all)
    grad_branch_low = grad_rows.astype(bf16)
    d_down_b = column_sum(grad_branch_low)
    grad_act = contract_cols(grad_branch_low, back_down)
    grad_pre_low = (
        grad_act * (gate_sig + GELU_K * hidden_pre * gate_sig * (1.0 - gate_sig))
    ).astype(bf16)
    d_fc_b = column_sum(grad_pre_low)
    grad_norm_two = contract_cols(grad_pre_low, back_fc)
    grad_mid_norm, d_gain_two, d_bias_two = masked_norm_back(
        grad_norm_two, back_gain_two.astype(f32), norm_two, inv_two, col_keep, width_real
    )
    grad_middle = grad_rows + grad_mid_norm
    grad_attn_low = grad_middle.astype(bf16)
    d_out_b = column_sum(grad_attn_low)
    grad_mix_low = (
        contract_cols(grad_attn_low, back_out)
        .astype(bf16)
        .reshape(samples, seq_rows, head_count, HD)
    )
    probs_again = jnp.exp(masked_scores() - log_total)
    probs_low = probs_again.astype(bf16)
    grad_value = jnp.einsum("shqk,sqhd->skhd", probs_low, grad_mix_low, preferred_element_type=f32)
    grad_probs = jnp.einsum("sqhd,skhd->shqk", grad_mix_low, value_all, preferred_element_type=f32)
    grad_scores = probs_again * (
        grad_probs - jnp.sum(probs_again * grad_probs, axis=-1, keepdims=True)
    )
    grad_scores_low = grad_scores.astype(bf16)
    grad_query = (
        jnp.einsum("shqk,skhd->sqhd", grad_scores_low, key_all, preferred_element_type=f32)
        * score_mult
    )
    grad_key = (
        jnp.einsum("shqk,sqhd->skhd", grad_scores_low, query_all, preferred_element_type=f32)
        * score_mult
    )
    grad_qkv_low = (
        jnp.stack([grad_query, grad_key, grad_value], axis=2)
        .astype(bf16)
        .reshape(flat_rows, 3 * width_all)
    )
    d_qkv_w = contract_rows(normed_one, grad_qkv_low).reshape(width_all, 3, width_all)
    qkv_sums = column_sum(grad_qkv_low).reshape(3, width_all)
    d_qv_b = jnp.stack([qkv_sums[0], qkv_sums[2]])
    grad_norm_one = contract_cols(grad_qkv_low, back_qkv.reshape(width_all, 3 * width_all))
    grad_in_norm, d_gain_one, d_bias_one = masked_norm_back(
        grad_norm_one, back_gain_one.astype(f32), norm_one, inv_one, col_keep, width_real
    )
    tokens_grad = (grad_middle + grad_in_norm).reshape(1, samples, seq_rows, width_all)
    d_embed_w = contract_rows(head_low, grad_proj_low)
    d_down_w = contract_rows(act_low, grad_branch_low)
    d_fc_w = contract_rows(normed_two, grad_pre_low)
    d_out_w = contract_rows(head_mix_low, grad_attn_low)
    shares = (
        lax.psum_scatter(d_gain_one, "dp", scatter_dimension=0, tiled=True),
        lax.psum_scatter(d_bias_one, "dp", scatter_dimension=0, tiled=True),
        lax.psum_scatter(d_qkv_w, "dp", scatter_dimension=0, tiled=True),
        lax.psum_scatter(d_qv_b, "dp", scatter_dimension=1, tiled=True),
        lax.psum_scatter(d_out_w, "dp", scatter_dimension=0, tiled=True),
        lax.psum_scatter(d_out_b, "dp", scatter_dimension=0, tiled=True),
        lax.psum_scatter(d_gain_two, "dp", scatter_dimension=0, tiled=True),
        lax.psum_scatter(d_bias_two, "dp", scatter_dimension=0, tiled=True),
        lax.psum_scatter(d_fc_w, "dp", scatter_dimension=0, tiled=True),
        lax.psum_scatter(d_fc_b, "dp", scatter_dimension=0, tiled=True),
        lax.psum_scatter(d_down_w, "dp", scatter_dimension=0, tiled=True),
        lax.psum_scatter(d_down_b, "dp", scatter_dimension=0, tiled=True),
        lax.psum_scatter(d_gain_final, "dp", scatter_dimension=0, tiled=True),
        lax.psum_scatter(d_bias_final, "dp", scatter_dimension=0, tiled=True),
        lax.psum_scatter(d_embed_w, "dp", scatter_dimension=0, tiled=True),
    )
    results = list(shares)
    outputs = [item[None] for item in results]
    loss = totals[0].reshape(1)
    logit_scale_grad = totals[1].reshape(1)
    return (
        block_out,
        tokens_grad,
        loss,
        outputs[0],
        outputs[1],
        outputs[2],
        outputs[3],
        outputs[4],
        outputs[5],
        outputs[6],
        outputs[7],
        outputs[8],
        outputs[9],
        outputs[10],
        outputs[11],
        outputs[12],
        outputs[13],
        outputs[14],
        logit_scale_grad,
    )


RING_Z = (0, 1, 2, 3, 3, 2, 1, 0)
RING_Y = (0, 0, 0, 0, 1, 1, 1, 1)
ITEMS = 16
PAD_ROWS = 80
F32 = jnp.float32
BF16 = jnp.bfloat16
ANY = pl.BlockSpec(memory_space=pl.ANY)
VMEM = pl.BlockSpec(memory_space=pltpu.VMEM)
SMEM = pl.BlockSpec(memory_space=pltpu.SMEM)
META_LEN, META_POOL, META_TEXT, META_Z = 16, 24, 32, 36


def call(kernel, name, ins, outs, scratch, flops=0, touched=0):
    specs = [spec for spec, _ in ins]
    return pl.pallas_call(
        kernel,
        name=name,
        out_shape=[jax.ShapeDtypeStruct(shape, dtype) for shape, dtype in outs],
        in_specs=specs,
        out_specs=[VMEM for _ in outs],
        scratch_shapes=scratch,
        compiler_params=pltpu.CompilerParams(vmem_limit_bytes=60 * 1024 * 1024),
        cost_estimate=pl.CostEstimate(flops=flops, bytes_accessed=touched, transcendentals=0),
    )(*[item for _, item in ins])


def dot(left, right, left_dim=1, right_dim=0):
    return lax.dot_general(
        left, right, (((left_dim,), (right_dim,)), ((), ())), preferred_element_type=F32
    )


def slots(refs):
    own, other, h1, s1, h2, s2, h3, s3, h4, s4 = refs
    views = [own, other]
    for pair in (h1, s1, h2, s2, h3, s3):
        views += [pair.at[0], pair.at[1]]
    return views + [h4, s4]


def fetch(meta, refs, row, rows, lane, lanes, dst, dst_lane, sem, per_owner=None):
    step = rows if per_owner is None else per_owner
    for slot, view in enumerate(slots(refs)):
        at = pl.multiple_of(meta[slot] * step, 16)
        pltpu.make_async_copy(
            view.at[pl.ds(row, rows), pl.ds(lane, lanes)],
            dst.at[pl.ds(at, rows), pl.ds(dst_lane, lanes)],
            sem,
        ).start()


def drain(dst, sem):
    pltpu.make_async_copy(dst, dst, sem).wait()


def lane_keep(meta, width):
    real = jnp.where(meta[META_TEXT] == 1, DT, DI)
    lanes = lax.broadcasted_iota(jnp.int32, (1, width), 1)
    return (lanes < real).astype(F32)


def width_inv(meta):
    return jnp.where(meta[META_TEXT] == 1, 1.0 / DT, 1.0 / DI).astype(F32)


def normalize(values, keep, winv):
    mean = jnp.sum(values, axis=-1, keepdims=True) * winv
    centred = (values - mean) * keep
    var = jnp.sum(centred * centred, axis=-1, keepdims=True) * winv
    inv = lax.rsqrt(var + EPS)
    return centred * inv, inv


def normalize_back(grad_out, gain, normed, inv, keep, winv):
    grad_normed = grad_out * gain
    mean_grad = jnp.sum(grad_normed, axis=-1, keepdims=True) * winv
    mean_cross = jnp.sum(grad_normed * normed, axis=-1, keepdims=True) * winv
    return keep * inv * (grad_normed - mean_grad - normed * mean_cross)


def row_sum(values):
    return jnp.sum(values, axis=0, keepdims=True)


def head_rows(rows):
    heads = lax.broadcasted_iota(jnp.int32, rows.shape, 1) // HD
    parts = [jnp.where(heads == head, rows, 0.0) for head in range(16)]
    return jnp.concatenate(parts, axis=0).astype(BF16)


def attend_kernel(meta, tok, *rest):
    refs, (mixed, keys, values, norm_low, small_out, pooled), scratch = rest[:10], rest[10:16], rest[16:]
    weights, small, normed, queries, pool_acc, wsem, ssem = scratch
    for slot, view in enumerate(slots(refs)):
        pltpu.make_async_copy(view.at[pl.ds(160, 16), :], small.at[slot], ssem).start()
    for third in range(3):
        fetch(meta, refs, third * 48, 48, 0, DI, weights, third * DI, wsem)
    keep, winv = lane_keep(meta, DI), width_inv(meta)
    drain(small, ssem)
    vectors = jnp.sum(small[...].astype(F32), axis=0)
    small_out[...] = vectors
    samples, seq = tok.shape[0], tok.shape[1]

    @pl.loop(0, samples)
    def _(s):
        norm, _ = normalize(tok[s].astype(F32), keep, winv)
        norm_low[s, 64:80, :] = jnp.zeros((16, DI), BF16)
        normed[s, 64:80, :] = jnp.zeros((16, DI), BF16)
        norm_low[s, 0:seq, :] = norm.astype(BF16)
        normed[s, 0:seq, :] = (norm * small_out[0:1, :] + small_out[1:2, :]).astype(BF16)

    drain(weights, wsem)
    rows = samples * PAD_ROWS

    for third, dst, bias in ((0, queries, 2), (1, keys, None), (2, values, 3)):

        @pl.loop(0, DI // 256)
        def _(j, third=third, dst=dst, bias=bias):
            lanes = pl.ds(pl.multiple_of(j * 256, 256), 256)
            wide = pl.ds(pl.multiple_of(third * DI + j * 256, 256), 256)
            prod = dot(normed[...].reshape(rows, DI), weights[:, wide])
            if bias is not None:
                prod = prod + small_out[bias : bias + 1, lanes]
            dst[:, lanes] = prod.astype(BF16)

    text = meta[META_TEXT] == 1
    query_pos = lax.broadcasted_iota(jnp.int32, (PAD_ROWS, PAD_ROWS), 0)
    key_pos = lax.broadcasted_iota(jnp.int32, (PAD_ROWS, PAD_ROWS), 1)
    head_of = lax.broadcasted_iota(jnp.int32, (PAD_ROWS, 256), 1) // HD
    head_masks = [(head_of == i).astype(F32) for i in range(4)]
    low_masks = [m.astype(BF16) for m in head_masks]
    row_pos = lax.broadcasted_iota(jnp.int32, (PAD_ROWS, 256), 0)
    reach = jnp.where(text, query_pos, PAD_ROWS)

    @pl.loop(0, samples)
    def _(s):
        at = pl.ds(pl.multiple_of(s * PAD_ROWS, 16), PAD_ROWS)
        length, pool = meta[META_LEN + s], meta[META_POOL + s]
        allowed = (key_pos < length) & (key_pos <= reach)
        for group in range(3):
            lanes = pl.ds(group * 256, 256)
            query, key, value = queries[at, lanes], keys[at, lanes], values[at, lanes]
            spread = jnp.concatenate([query * m for m in low_masks], axis=0)
            raw = dot(spread, key, 1, 1) * (float(HD) ** -0.5)
            raw = jnp.where(allowed[None], raw.reshape(4, PAD_ROWS, PAD_ROWS), NEG_FILL)
            terms = jnp.exp(raw - jnp.max(raw, axis=-1, keepdims=True))
            probs = terms / jnp.sum(terms, axis=-1, keepdims=True)
            out = dot(probs.astype(BF16).reshape(4 * PAD_ROWS, PAD_ROWS), value)
            total = out[0:PAD_ROWS] * head_masks[0]
            for i in range(1, 4):
                total = total + out[i * PAD_ROWS : (i + 1) * PAD_ROWS] * head_masks[i]
            low = total.astype(BF16)
            mixed[s, :, lanes] = low
            pool_acc[pl.ds(s, 1), lanes] = row_sum(jnp.where(row_pos == pool, low.astype(F32), 0.0))

    pooled[...] = pool_acc[...].astype(BF16)


def attend(meta, tok, refs):
    samples = tok.shape[0]
    rows = samples * PAD_ROWS
    return call(
        attend_kernel,
        "attend",
        [(SMEM, meta), (VMEM, tok)] + [(ANY, r) for r in refs],
        [
            ((samples, PAD_ROWS, DI), BF16),
            ((rows, DI), BF16),
            ((rows, DI), BF16),
            ((samples, PAD_ROWS, DI), BF16),
            ((16, DI), F32),
            ((samples, DI), BF16),
        ],
        [
            pltpu.VMEM((DI, 3 * DI), BF16),
            pltpu.VMEM((ITEMS, 16, DI), BF16),
            pltpu.VMEM((samples, PAD_ROWS, DI), BF16),
            pltpu.VMEM((rows, DI), BF16),
            pltpu.VMEM((samples, DI), F32),
            pltpu.SemaphoreType.DMA,
            pltpu.SemaphoreType.DMA,
        ],
        flops=2 * rows * DI * 3 * DI,
        touched=10_000_000,
    )


def hidden_kernel(meta, tok, mixed, vec, *rest):
    refs, (middle, act), (w_out, w_fc, normed, osem, fsem) = rest[:10], rest[10:12], rest[12:]
    fetch(meta, refs, 0, 48, 0, DI, w_out, 0, osem)
    for block in range(4):
        fetch(meta, refs, 48 + 48 * block, 48, 0, DI, w_fc, block * DI, fsem)
    keep, winv = lane_keep(meta, DI), width_inv(meta)
    samples, seq = tok.shape[0], tok.shape[1]
    rows = samples * PAD_ROWS
    drain(w_out, osem)

    @pl.loop(0, DI // 256)
    def _(j):
        lanes = pl.ds(pl.multiple_of(j * 256, 256), 256)
        prod = dot(mixed[...].reshape(rows, DI), w_out[:, lanes]) + vec[4:5, lanes]
        middle[:, :, lanes] = prod.reshape(samples, PAD_ROWS, 256)

    @pl.loop(0, samples)
    def _(s):
        total = middle[s, 0:seq, :] + tok[s].astype(F32)
        middle[s, 0:seq, :] = total
        norm, _ = normalize(total, keep, winv)
        normed[s, 64:80, :] = jnp.zeros((16, DI), BF16)
        normed[s, 0:seq, :] = (norm * vec[5:6, :] + vec[6:7, :]).astype(BF16)

    drain(w_fc, fsem)
    for block in range(4):

        @pl.loop(0, DI // 256)
        def _(j, block=block):
            lanes = pl.ds(pl.multiple_of(j * 256, 256), 256)
            wide = pl.ds(pl.multiple_of(block * DI + j * 256, 256), 256)
            pre = dot(normed[...].reshape(rows, DI), w_fc[:, wide])
            pre = pre + vec[10 + block : 11 + block, lanes]
            act[:, wide] = (pre * jax.nn.sigmoid(GELU_K * pre)).astype(BF16)


def hidden(meta, tok, mixed, vec, refs):
    samples = tok.shape[0]
    rows = samples * PAD_ROWS
    return call(
        hidden_kernel,
        "hidden",
        [(SMEM, meta), (VMEM, tok), (VMEM, mixed), (VMEM, vec)] + [(ANY, r) for r in refs],
        [((samples, PAD_ROWS, DI), F32), ((rows, 4 * DI), BF16)],
        [
            pltpu.VMEM((DI, DI), BF16),
            pltpu.VMEM((DI, 4 * DI), BF16),
            pltpu.VMEM((samples, PAD_ROWS, DI), BF16),
            pltpu.SemaphoreType.DMA,
            pltpu.SemaphoreType.DMA,
        ],
        flops=2 * rows * DI * 5 * DI,
        touched=14_000_000,
    )


def finish_kernel(meta, middle, act, vec, *rest):
    refs, (block_out,), (w_down, acc, sem) = rest[:10], rest[10:11], rest[11:]
    fetch(meta, refs, 0, 192, 0, DI, w_down, 0, sem)
    samples, seq = block_out.shape[0], block_out.shape[1]
    drain(w_down, sem)

    @pl.loop(0, DI // 256)
    def _(j):
        lanes = pl.ds(pl.multiple_of(j * 256, 256), 256)
        prod = dot(act[...], w_down[:, lanes]) + vec[7:8, lanes]
        acc[:, :, lanes] = prod.reshape(samples, PAD_ROWS, 256)

    row_pos = lax.broadcasted_iota(jnp.int32, (seq, DI), 0)

    @pl.loop(0, samples)
    def _(s):
        total = acc[s, 0:seq, :] + middle[s, 0:seq, :]
        block_out[s] = jnp.where(row_pos < meta[META_LEN + s], total, 0.0).astype(BF16)


def finish(meta, middle, act, vec, refs, seq):
    samples = middle.shape[0]
    rows = samples * PAD_ROWS
    return call(
        finish_kernel,
        "finish",
        [(SMEM, meta), (VMEM, middle), (VMEM, act), (VMEM, vec)] + [(ANY, r) for r in refs],
        [((samples, seq, DI), BF16)],
        [
            pltpu.VMEM((4 * DI, DI), BF16),
            pltpu.VMEM((samples, PAD_ROWS, DI), F32),
            pltpu.SemaphoreType.DMA,
        ],
        flops=2 * rows * DI * 4 * DI,
        touched=13_000_000,
    )[0]


def fetch_embed(meta, refs, dst, sem):
    for slot, view in enumerate(slots(refs)):
        at = pl.multiple_of(meta[slot] * 48, 16)
        for row, rows, lane, lanes, to_row, to_lane in (
            (192, 32, 0, EMB, 0, 0),
            (192, 16, EMB, 256, 32, 0),
            (208, 16, EMB, 256, 32, 256),
        ):
            pltpu.make_async_copy(
                view.at[pl.ds(row, rows), pl.ds(lane, lanes)],
                dst.at[pl.ds(pl.multiple_of(at + to_row, 16), rows), pl.ds(to_lane, lanes)],
                sem,
            ).start()


def pooled_kernel(meta, vec, *rest):
    first, second, third, mixes = rest[:10], rest[10:20], rest[20:30], rest[30:34]
    outs, scratch = rest[34:47], rest[47:]
    (e_out, proj_out, head_out, normf_out, invf_out, n2_out, norm2_out, inv2_out, pre_out,
     act_out, q_out, norm1_out, mix_out) = outs
    w_q, w_out, w_fc, w_down, w_emb, xs, mix, sems = scratch
    for slot, view in enumerate(slots(first)):
        pltpu.make_async_copy(view.at[pl.ds(144, 16), :], xs.at[meta[slot]], sems.at[0]).start()
    for i, ref in enumerate(mixes):
        pltpu.make_async_copy(ref, mix.at[meta[META_Z + i]], sems.at[1]).start()
    fetch(meta, second, 0, 48, 0, DI, w_out, 0, sems.at[2])
    for block in range(4):
        fetch(meta, second, 48 + 48 * block, 48, 0, DI, w_fc, block * DI, sems.at[3])
    fetch(meta, third, 0, 192, 0, DI, w_down, 0, sems.at[4])
    fetch_embed(meta, third, w_emb, sems.at[5])
    fetch(meta, first, 0, 48, 0, DI, w_q, 0, sems.at[6])
    keep, winv = lane_keep(meta, DI), width_inv(meta)
    drain(xs, sems.at[0])
    stream = xs[...].astype(F32)[:, :8, :].reshape(ITEMS * 8, DI)
    drain(mix, sems.at[1])
    mixed = mix[...].reshape(ITEMS * 8, DI)
    mix_out[...] = mixed
    drain(w_out, sems.at[2])
    middle = stream + dot(mixed, w_out[...]) + vec[4:5, :]
    norm2, inv2 = normalize(middle, keep, winv)
    n2 = (norm2 * vec[5:6, :] + vec[6:7, :]).astype(BF16)
    n2_out[...] = n2
    norm2_out[...] = norm2
    inv2_out[...] = jnp.broadcast_to(inv2, (ITEMS * 8, 128))
    drain(w_fc, sems.at[3])
    for block in range(4):

        @pl.loop(0, DI // 256)
        def _(j, block=block):
            lanes = pl.ds(pl.multiple_of(j * 256, 256), 256)
            wide = pl.ds(pl.multiple_of(block * DI + j * 256, 256), 256)
            pre = dot(n2_out[...], w_fc[:, wide]) + vec[10 + block : 11 + block, lanes]
            pre_out[:, wide] = pre
            act_out[:, wide] = (pre * jax.nn.sigmoid(GELU_K * pre)).astype(BF16)

    drain(w_down, sems.at[4])
    last = middle + dot(act_out[...], w_down[...]) + vec[7:8, :]
    normf, invf = normalize(last, keep, winv)
    normf_out[...] = normf
    invf_out[...] = jnp.broadcast_to(invf, (ITEMS * 8, 128))
    head = (normf * vec[8:9, :] + vec[9:10, :]).astype(BF16)
    head_out[...] = head
    drain(w_emb, sems.at[5])
    proj = dot(head, w_emb[...])
    proj_out[...] = proj
    scale = lax.rsqrt(jnp.sum(proj * proj, axis=-1, keepdims=True) + NORM_EPS)
    e_out[...] = (proj * scale).astype(BF16)
    norm1, _ = normalize(stream, keep, winv)
    norm1_out[...] = norm1.astype(BF16)
    drain(w_q, sems.at[6])
    n1 = (norm1 * vec[0:1, :] + vec[1:2, :]).astype(BF16)
    q_out[...] = (dot(n1, w_q[...]) + vec[2:3, :]).astype(BF16)


def pooled_forward(meta, vec, first, second, third, mixes):
    n = ITEMS * 8
    return call(
        pooled_kernel,
        "pooled_forward",
        [(SMEM, meta), (VMEM, vec)] + [(ANY, r) for r in (*first, *second, *third, *mixes)],
        [
            ((n, EMB), BF16),
            ((n, EMB), F32),
            ((n, DI), BF16),
            ((n, DI), F32),
            ((n, 128), F32),
            ((n, DI), BF16),
            ((n, DI), F32),
            ((n, 128), F32),
            ((n, 4 * DI), F32),
            ((n, 4 * DI), BF16),
            ((n, DI), BF16),
            ((n, DI), BF16),
            ((n, DI), BF16),
        ],
        [
            pltpu.VMEM((DI, DI), BF16),
            pltpu.VMEM((DI, DI), BF16),
            pltpu.VMEM((DI, 4 * DI), BF16),
            pltpu.VMEM((4 * DI, DI), BF16),
            pltpu.VMEM((DI, EMB), BF16),
            pltpu.VMEM((ITEMS, 16, DI), BF16),
            pltpu.VMEM((4, 32, DI), BF16),
            pltpu.SemaphoreType.DMA((7,)),
        ],
        flops=2 * n * DI * 11 * DI,
        touched=16_000_000,
    )


def one_direction(left, right, mult):
    sims = dot(left, right, 1, 1)
    logits = mult * sims
    top = jnp.max(logits, axis=-1, keepdims=True)
    total = top + jnp.log(jnp.sum(jnp.exp(logits - top), axis=-1, keepdims=True))
    count = sims.shape[0]
    eye = lax.broadcasted_iota(jnp.int32, (count, count), 0) == lax.broadcasted_iota(
        jnp.int32, (count, count), 1
    )
    hot = eye.astype(F32)
    lost = jnp.sum(total - jnp.sum(hot * logits, axis=-1, keepdims=True), axis=0, keepdims=True)
    grad = (jnp.exp(logits - total) - hot) * 0.5
    scale = jnp.sum(jnp.sum(grad * sims, axis=-1, keepdims=True), axis=0, keepdims=True)
    return lost, scale, mult * grad


def chain_kernel(meta, mult_ref, e_own_ref, e_oth_ref, vec, proj_ref, normf_ref, invf_ref, norm2_ref,
                 inv2_ref, pre_ref, head_sl, act_sl, n2_sl, mix_sl, *rest):
    second, third = rest[:10], rest[10:20]
    outs, scratch = rest[20:30], rest[30:]
    (loss_out, d_emb, d_down, d_fc, d_out, vec_grads, fcb_grads, mid_out, gm_out, unused) = outs
    w_out, w_fc, w_down, w_emb, gpre, sems = scratch
    fetch_embed(meta, third, w_emb, sems.at[0])
    fetch(meta, third, 0, 192, 0, DI, w_down, 0, sems.at[1])
    for block in range(4):
        fetch(meta, second, 48 + 48 * block, 48, 0, DI, w_fc, block * DI, sems.at[2])
    fetch(meta, second, 0, 48, 0, DI, w_out, 0, sems.at[3])
    keep, winv = lane_keep(meta, DI), width_inv(meta)
    text = meta[META_TEXT].astype(F32)
    mult = mult_ref[0]
    own, oth = e_own_ref[...].astype(F32), e_oth_ref[...].astype(F32)
    e_img = (own * (1.0 - text) + oth * text).astype(BF16)
    e_txt = (oth * (1.0 - text) + own * text).astype(BF16)
    lost_img, scale_img, grad_img = one_direction(e_img, e_txt, mult)
    lost_txt, scale_txt, grad_txt = one_direction(e_txt, e_img, mult)
    count = own.shape[0]
    loss = (lost_img + lost_txt) / (2.0 * count)
    scale = mult * (scale_img + scale_txt)
    row_id = lax.broadcasted_iota(jnp.int32, (8, 128), 0)
    loss_out[...] = jnp.where(
        row_id == 0, jnp.broadcast_to(loss, (8, 128)), jnp.broadcast_to(scale, (8, 128))
    )
    grad_own = (grad_img * (1.0 - text) + grad_txt * text).astype(BF16)
    grad_oth = (grad_txt * (1.0 - text) + grad_img * text).astype(BF16)
    oth_low = e_oth_ref[...]
    grad_e = dot(grad_own, oth_low) + dot(grad_oth, oth_low, 0, 0)
    proj = proj_ref[...]
    r = lax.rsqrt(jnp.sum(proj * proj, axis=-1, keepdims=True) + NORM_EPS)
    cross = jnp.sum(grad_e * proj, axis=-1, keepdims=True)
    grad_proj = (r * grad_e - proj * (r * r * r) * cross).astype(BF16)
    d_emb[...] = dot(head_sl[...], grad_proj, 0, 0)
    drain(w_emb, sems.at[0])
    grad_head = dot(grad_proj, w_emb[...], 1, 1)
    normf = normf_ref[...]
    grad_y = normalize_back(grad_head, vec[8:9, :], normf, invf_ref[:, 0:1], keep, winv)
    vec_grads[0:1, :] = row_sum(grad_head * normf)
    vec_grads[1:2, :] = row_sum(grad_head)
    branch = grad_y.astype(BF16)
    vec_grads[2:3, :] = row_sum(branch.astype(F32))
    d_down[...] = dot(act_sl[...], branch, 0, 0)
    drain(w_down, sems.at[1])

    for block in range(6):
        lanes = pl.ds(block * 512, 512)
        grad_act = dot(branch, w_down[lanes, :], 1, 1)
        pre = pre_ref[:, lanes]
        gate = jax.nn.sigmoid(GELU_K * pre)
        low = (grad_act * (gate + GELU_K * pre * gate * (1.0 - gate))).astype(BF16)
        gpre[:, lanes] = low
        fcb_grads[:, lanes] = jnp.broadcast_to(row_sum(low.astype(F32)), (8, 512))

    drain(w_fc, sems.at[2])
    grad_n2 = dot(gpre[...], w_fc[...], 1, 1)

    @pl.loop(0, 6)
    def _(j):
        lanes = pl.ds(pl.multiple_of(j * 512, 512), 512)
        d_fc[:, lanes] = dot(n2_sl[...], gpre[:, lanes], 0, 0)

    norm2 = norm2_ref[...]
    vec_grads[3:4, :] = row_sum(grad_n2 * norm2)
    vec_grads[4:5, :] = row_sum(grad_n2)
    grad_mid = grad_y + normalize_back(grad_n2, vec[5:6, :], norm2, inv2_ref[:, 0:1], keep, winv)
    mid_out[...] = grad_mid
    attn = grad_mid.astype(BF16)
    vec_grads[5:6, :] = row_sum(attn.astype(F32))
    d_out[...] = dot(mix_sl[...], attn, 0, 0)
    drain(w_out, sems.at[3])
    gm_out[...] = dot(attn, w_out[...], 1, 1).astype(BF16)
    vec_grads[6:8, :] = jnp.zeros((2, DI), F32)
    unused[...] = jnp.zeros((8, 128), F32)


def chain(meta, mult, e_own, e_oth, vec, saved, slices, second, third):
    n = ITEMS * 8
    plain = [e_own, e_oth, vec, *saved, *slices]
    return call(
        chain_kernel,
        "chain",
        [(SMEM, meta), (SMEM, mult)]
        + [(VMEM, item) for item in plain]
        + [(ANY, r) for r in (*second, *third)],
        [
            ((8, 128), F32),
            ((48, EMB), F32),
            ((192, DI), F32),
            ((48, 4 * DI), F32),
            ((48, DI), F32),
            ((8, DI), F32),
            ((8, 4 * DI), F32),
            ((n, DI), F32),
            ((n, DI), BF16),
            ((8, 128), F32),
        ],
        [
            pltpu.VMEM((DI, DI), BF16),
            pltpu.VMEM((DI, 4 * DI), BF16),
            pltpu.VMEM((4 * DI, DI), BF16),
            pltpu.VMEM((DI, EMB), BF16),
            pltpu.VMEM((n, 4 * DI), BF16),
            pltpu.SemaphoreType.DMA((4,)),
        ],
        flops=2 * n * DI * 10 * DI,
        touched=16_000_000,
    )


PAYLOAD = 160


def scores_kernel(meta, keys, values, norm_low, q_own, gm_own, payload, gk_out, gv_out, gq_out):
    rows = keys.shape[0]
    samples = rows // PAD_ROWS
    q_rows = head_rows(q_own[...].astype(F32))
    m_rows = head_rows(gm_own[...].astype(F32))
    raw = dot(keys[...], q_rows, 1, 1) * (float(HD) ** -0.5)
    shape = (samples, PAD_ROWS, 128)
    row_sample = lax.broadcasted_iota(jnp.int32, shape, 0)
    row_key = lax.broadcasted_iota(jnp.int32, shape, 1)
    lane = lax.broadcasted_iota(jnp.int32, shape, 2)
    limit = jnp.zeros((samples, 1, 128), jnp.int32)
    sample_id = lax.broadcasted_iota(jnp.int32, (samples, 1, 128), 0)
    for s in range(samples):
        limit = jnp.where(sample_id == s, meta[META_LEN + s], limit)
    valid = (lane % 8 == row_sample) & (row_key < limit) & (lane < 96)
    raw = jnp.where(valid, raw.reshape(shape), NEG_FILL)
    top = jnp.max(jnp.max(raw, axis=0, keepdims=True), axis=1, keepdims=True)
    terms = jnp.where(valid, jnp.exp(raw - top), 0.0)
    total = jnp.sum(jnp.sum(terms, axis=0, keepdims=True), axis=1, keepdims=True)
    probs = terms / jnp.maximum(total, 1e-30)
    grad_probs = dot(values[...], m_rows, 1, 1).reshape(shape)
    cross = jnp.sum(jnp.sum(probs * grad_probs, axis=0, keepdims=True), axis=1, keepdims=True)
    gk = (probs * (grad_probs - cross)).reshape(rows, 128).astype(BF16)
    gv = probs.reshape(rows, 128).astype(BF16)
    gk_out[...] = gk
    gv_out[...] = gv
    back = dot(gk, keys[...], 0, 0) * (float(HD) ** -0.5)
    heads = lax.broadcasted_iota(jnp.int32, (8, DI), 1) // HD
    grad_q = jnp.zeros((8, DI), F32)
    for head in range(DI // HD):
        grad_q = grad_q + jnp.where(heads == head, back[head * 8 : head * 8 + 8], 0.0)
    gq_low = grad_q.astype(BF16)
    gq_out[...] = gq_low
    norm = norm_low[...].reshape(rows, DI)
    z_key = dot(norm, gk, 0, 0).astype(BF16)
    z_value = dot(norm, gv, 0, 0).astype(BF16)
    sum_key = row_sum(gk.astype(F32))
    sum_value = row_sum(gv.astype(F32))
    key_high = sum_key.astype(BF16).astype(F32)
    value_high = sum_value.astype(BF16).astype(F32)
    row_id = lax.broadcasted_iota(jnp.int32, (16, 128), 0)
    sums = jnp.zeros((16, 128), F32)
    for at, value in enumerate((key_high, sum_key - key_high, value_high, sum_value - value_high)):
        sums = jnp.where(row_id == at, jnp.broadcast_to(value, (16, 128)), sums)
    sums = sums.astype(BF16)
    gq_wide = gq_low.astype(F32)
    gq_tall = jnp.concatenate(
        [gq_wide[:, i * 128 : (i + 1) * 128] for i in range(DI // 128)], axis=0
    ).astype(BF16)
    for owner in range(ITEMS):
        base = owner * PAYLOAD
        payload[base : base + 48, :] = z_key[owner * 48 : owner * 48 + 48]
        payload[base + 48 : base + 64, :] = sums
        payload[base + 64 : base + 112, :] = z_value[owner * 48 : owner * 48 + 48]
        payload[base + 112 : base + 160, :] = gq_tall


def scores(meta, keys, values, norm_low, q_own, gm_own):
    rows = keys.shape[0]
    return call(
        scores_kernel,
        "scores",
        [(SMEM, meta)] + [(VMEM, item) for item in (keys, values, norm_low, q_own, gm_own)],
        [
            ((ITEMS * PAYLOAD, 128), BF16),
            ((rows, 128), BF16),
            ((rows, 128), BF16),
            ((8, DI), BF16),
        ],
        [],
        flops=2 * rows * DI * 700,
        touched=5_000_000,
    )


def shard_kernel(got, q_all, gm_all, norm_sl, w_own, gain, bias, d_qkv, sums_out, gains_out, big, left):
    scale = float(HD) ** -0.5

    def build(source):
        @pl.loop(0, ITEMS)
        def _(j):
            rows = source[pl.ds(pl.multiple_of(j * 8, 8), 8), :]
            big[pl.ds(pl.multiple_of(j * 128, 128), 128), :] = head_rows(rows)

    def spread(start):
        for j in range(ITEMS):
            left[:, j * 128 : (j + 1) * 128] = got[j, start : start + 64, :]

    build(q_all)
    spread(0)
    by_key = dot(left[...], big[...]) * scale
    m_key, s_key = by_key[0:48], by_key[48:49] + by_key[49:50]
    build(gm_all)
    spread(48)
    by_value = dot(left[...], big[...])
    m_value, s_value = by_value[16:64], by_value[2:3] + by_value[3:4]
    tall = got[:, 112:160, :].astype(F32)
    grad_q = jnp.concatenate(
        [tall[:, i * 8 : i * 8 + 8, :].reshape(ITEMS * 8, 128) for i in range(DI // 128)], axis=1
    )
    s_query = row_sum(grad_q)
    m_query = dot(norm_sl[...], grad_q.astype(BF16), 0, 0)
    gain_col, bias_col = gain[:, 0:1], bias[:, 0:1]
    d_gain = jnp.zeros((48, 1), F32)
    d_bias = jnp.zeros((48, 1), F32)
    for third, (moment, total) in enumerate(((m_query, s_query), (m_key, s_key), (m_value, s_value))):
        d_qkv[third] = gain_col * moment + bias_col * total
        weight = w_own[third].astype(F32)
        d_gain = d_gain + jnp.sum(weight * moment, axis=-1, keepdims=True)
        d_bias = d_bias + jnp.sum(weight * total, axis=-1, keepdims=True)
    lane = lax.broadcasted_iota(jnp.int32, (48, 128), 1)
    gains_out[...] = jnp.where(
        lane == 0, jnp.broadcast_to(d_gain, (48, 128)), jnp.broadcast_to(d_bias, (48, 128))
    )
    row_id = lax.broadcasted_iota(jnp.int32, (8, DI), 0)
    sums_out[...] = jnp.where(
        row_id == 0, jnp.broadcast_to(s_query, (8, DI)), jnp.broadcast_to(s_value, (8, DI))
    )


def shard_grads(got, q_all, gm_all, norm_sl, w_own, gain, bias):
    return call(
        shard_kernel,
        "shard_grads",
        [(VMEM, item) for item in (got, q_all, gm_all, norm_sl, w_own, gain, bias)],
        [((3, 48, DI), F32), ((8, DI), F32), ((48, 128), F32)],
        [pltpu.VMEM((ITEMS * 128, DI), BF16), pltpu.VMEM((64, ITEMS * 128), BF16)],
        flops=2 * 64 * 2048 * DI * 2,
        touched=2_000_000,
    )


def stream_kernel(meta, tok, gk, gv, q_own, gm_own, gq, mid_own, vec, *rest):
    refs, (out,), (weights, acc, sem) = rest[:10], rest[10:11], rest[11:]
    for third in range(3):
        fetch(meta, refs, third * 48, 48, 0, DI, weights, third * DI, sem)
    keep, winv = lane_keep(meta, DI), width_inv(meta)
    samples, seq = tok.shape[0], tok.shape[1]
    q_rows = head_rows(q_own[...].astype(F32))
    m_rows = head_rows(gm_own[...].astype(F32))
    drain(weights, sem)
    u_key = (dot(q_rows, weights[:, DI : 2 * DI], 1, 1) * (float(HD) ** -0.5)).astype(BF16)
    u_value = dot(m_rows, weights[:, 2 * DI :], 1, 1).astype(BF16)
    u_query = dot(gq[...], weights[:, :DI], 1, 1)
    grad = dot(gk[...], u_key) + dot(gv[...], u_value)
    acc[...] = grad.reshape(samples, PAD_ROWS, DI)
    row_pos = lax.broadcasted_iota(jnp.int32, (seq, DI), 0)
    for s in range(samples):
        hit = row_pos == meta[META_POOL + s]
        norm, inv = normalize(tok[s].astype(F32), keep, winv)
        total = acc[s, 0:seq, :] + jnp.where(hit, u_query[s : s + 1, :], 0.0)
        back = normalize_back(total, vec[0:1, :], norm, inv, keep, winv)
        out[s] = back + jnp.where(hit, mid_own[s : s + 1, :], 0.0)


def stream_grads(meta, tok, gk, gv, q_own, gm_own, gq, mid_own, vec, refs):
    samples, seq = tok.shape[0], tok.shape[1]
    rows = samples * PAD_ROWS
    return call(
        stream_kernel,
        "stream_grads",
        [(SMEM, meta)]
        + [(VMEM, item) for item in (tok, gk, gv, q_own, gm_own, gq, mid_own, vec)]
        + [(ANY, r) for r in refs],
        [((samples, seq, DI), F32)],
        [
            pltpu.VMEM((DI, 3 * DI), BF16),
            pltpu.VMEM((samples, PAD_ROWS, DI), F32),
            pltpu.SemaphoreType.DMA,
        ],
        flops=2 * rows * DI * 600,
        touched=7_000_000,
    )[0]


BOTH = ("tower", "dp")


def device(tower, place, core):
    return tower * 16 + (RING_Z[place] * 2 + RING_Y[place]) * 2 + core


def routes(towers):
    swap, turn = [], []
    for tower in range(towers):
        for place in range(8):
            for core, step in ((0, 1), (1, -1)):
                here = device(tower, place, core)
                swap.append((here, device(tower, place, 1 - core)))
                turn.append((here, device(tower, (place + step) % 8, core)))
    return swap, turn


def ring_gather(shard, swap, turn):
    other = lax.ppermute(shard, BOTH, swap)
    held = jnp.stack([shard, other])
    items = [shard, other]
    for _ in range(3):
        held = lax.ppermute(held, BOTH, turn)
        items += [held, lax.ppermute(held, BOTH, swap)]
    held = lax.ppermute(held[0], BOTH, turn)
    return items + [held, lax.ppermute(held, BOTH, swap)]


def owner_table(dp_index):
    core = dp_index % 2
    row = dp_index // 2 % 2
    depth = dp_index // 4
    place = jnp.where(row == 0, depth, 7 - depth)

    def owner(where, which):
        where = where % 8
        z = jnp.where(where < 4, where, 7 - where)
        y = (where >= 4).astype(jnp.int32)
        return (z * 2 + y) * 2 + which

    sign = jnp.where(core == 0, -1, 1)
    found = [owner(place, core), owner(place, 1 - core)]
    for hop in range(1, 4):
        ahead, behind = place + sign * hop, place - sign * hop
        found += [owner(ahead, core), owner(ahead, 1 - core)]
        found += [owner(behind, 1 - core), owner(behind, core)]
    return found + [owner(place + 4, core), owner(place + 4, 1 - core)]


def gather_rows(rows, dp_index, towers):
    def pairs(move):
        return [
            (tower * 16 + (z * 2 + y) * 2 + c, tower * 16 + move(z, y, c))
            for tower in range(towers)
            for z in range(4)
            for y in range(2)
            for c in range(2)
        ]

    other = lax.ppermute(rows, BOTH, pairs(lambda z, y, c: (z * 2 + y) * 2 + 1 - c))
    first = dp_index % 2 == 0
    rows = jnp.concatenate([jnp.where(first, rows, other), jnp.where(first, other, rows)])
    other = lax.ppermute(rows, BOTH, pairs(lambda z, y, c: (z * 2 + 1 - y) * 2 + c))
    first = dp_index // 2 % 2 == 0
    rows = jnp.concatenate([jnp.where(first, rows, other), jnp.where(first, other, rows)])
    blocks = [rows]
    for hop in range(1, 4):
        blocks.append(
            lax.ppermute(rows, BOTH, pairs(lambda z, y, c, hop=hop: ((z + hop) % 4 * 2 + y) * 2 + c))
        )
    return blocks


def ring_body(
    tokens,
    lengths,
    ln1_gain,
    ln1_bias,
    qkv_weight,
    qv_bias,
    out_weight,
    out_bias,
    ln2_gain,
    ln2_bias,
    fc_weight,
    fc_bias,
    down_weight,
    down_bias,
    final_gain,
    final_bias,
    embed_weight,
    logit_scale,
):
    towers = lax.axis_size("tower")
    tower_index = lax.axis_index("tower")
    dp_index = lax.axis_index("dp")
    swap, turn = routes(towers)
    is_text = tower_index == 1
    tok = tokens[0]
    seq = tok.shape[1]
    seq_lens = jnp.where(is_text, lengths, IMG_ROWS)
    pool_pos = jnp.where(is_text, lengths - 1, 0)
    depth = dp_index // 4
    meta = jnp.stack(
        owner_table(dp_index)
        + [seq_lens[i] for i in range(8)]
        + [pool_pos[i] for i in range(8)]
        + [is_text.astype(jnp.int32), dp_index, dp_index * 0, dp_index * 0]
        + [(depth - hop) % 4 for hop in range(4)]
    ).astype(jnp.int32)

    w_own = qkv_weight[0].transpose(1, 0, 2)
    vectors = jnp.concatenate(
        [ln1_gain, ln1_bias, qv_bias[0], out_bias, ln2_gain, ln2_bias, down_bias, final_gain, final_bias]
    )
    lane = lax.broadcasted_iota(jnp.int32, (1, DI), 1)
    spread = jnp.where(lane // 48 == dp_index, jnp.tile(vectors, (1, ITEMS)), 0)
    wide = lax.broadcasted_iota(jnp.int32, (1, 4 * DI), 1)
    fc_spread = jnp.where(wide // 192 == dp_index, jnp.tile(fc_bias, (1, ITEMS)), 0).reshape(4, DI)
    x_pooled = jnp.take_along_axis(tok, pool_pos[:, None, None], axis=1)[:, 0]
    first_own = jnp.concatenate(
        [
            w_own.reshape(144, DI),
            x_pooled,
            jnp.zeros((8, DI), BF16),
            spread,
            fc_spread,
            jnp.zeros((2, DI), BF16),
        ]
    )
    second_own = jnp.concatenate(
        [out_weight[0], fc_weight[0].reshape(48, 4, DI).transpose(1, 0, 2).reshape(192, DI)]
    )
    emb = embed_weight[0]
    tail = emb[32:48]
    emb_rows = jnp.concatenate(
        [emb[:32], jnp.concatenate([tail[:, :256], tail[:, 256:]], axis=0)], axis=1
    )
    third_own = jnp.concatenate([down_weight[0], emb_rows])

    first = ring_gather(first_own, swap, turn)
    second = ring_gather(second_own, swap, turn)
    third = ring_gather(third_own, swap, turn)

    mixed, keys, values, norm_low, vec, mixed_pooled = attend(meta, tok, first)
    mixes = gather_rows(mixed_pooled, dp_index, towers)
    middle, act = hidden(meta, tok, mixed, vec, second)
    (e_own, proj, head, normf, invf, n2, norm2, inv2, pre, act_p, q_all, norm1, mix_all) = pooled_forward(
        meta, vec, first, second, third, mixes
    )
    across = [(t * 16 + d, (1 - t) * 16 + d) for t in range(2) for d in range(16)]
    e_oth = lax.ppermute(e_own, BOTH, across)

    def columns(array, size):
        return lax.dynamic_slice_in_dim(array, dp_index * size, size, axis=1)

    slices = (columns(head, 48), columns(act_p, 192), columns(n2, 48), columns(mix_all, 48))
    norm_sl = columns(norm1, 48)
    block_out = finish(meta, middle, act, vec, third, seq)
    mult = jnp.exp(logit_scale)
    loss_rows, d_emb, d_down, d_fc, d_out, vec_grads, fcb_grads, mid_all, gm_all, _ = chain(
        meta, mult, e_own, e_oth, vec, (proj, normf, invf, norm2, inv2, pre), slices, second, third
    )

    def own_rows(array):
        return lax.dynamic_slice_in_dim(array, dp_index * 8, 8, axis=0)

    q_own, gm_own, mid_own = own_rows(q_all), own_rows(gm_all), own_rows(mid_all)
    payload, gk, gv, gq = scores(meta, keys, values, norm_low, q_own, gm_own)
    got = lax.all_to_all(payload, "dp", 0, 0, tiled=True).reshape(ITEMS, PAYLOAD, 128)
    tokens_grad = stream_grads(meta, tok, gk, gv, q_own, gm_own, gq, mid_own, vec, first)
    gain = jnp.broadcast_to(ln1_gain[0].astype(F32)[:, None], (48, 128))
    bias = jnp.broadcast_to(ln1_bias[0].astype(F32)[:, None], (48, 128))
    d_qkv, sums, gains = shard_grads(
        got, q_all.astype(F32), gm_all.astype(F32), norm_sl, w_own, gain, bias
    )
    own_vec = columns(vec_grads, 48)
    own_sums = columns(sums, 48)
    d_fcb = columns(fcb_grads, 192)[0:1]
    return (
        block_out[None],
        tokens_grad[None],
        loss_rows[0, 0:1],
        gains[:, 0][None],
        gains[:, 1][None],
        d_qkv.transpose(1, 0, 2)[None],
        own_sums[0:2][None],
        d_out[None],
        own_vec[5:6],
        own_vec[3:4],
        own_vec[4:5],
        d_fc[None],
        d_fcb,
        d_down[None],
        own_vec[2:3],
        own_vec[0:1],
        own_vec[1:2],
        d_emb[None],
        loss_rows[1, 0:1],
    )


def solution(mesh):
    aligned = mesh.shape["dp"] == ITEMS and mesh.shape["tower"] == 2
    return jax.shard_map(
        ring_body if aligned else body,
        mesh=mesh,
        in_specs=(
            P("tower", "dp", None, None),
            P("dp"),
            P("tower", "dp"),
            P("tower", "dp"),
            P("tower", "dp", None, None),
            P("tower", None, "dp"),
            P("tower", "dp", None),
            P("tower", "dp"),
            P("tower", "dp"),
            P("tower", "dp"),
            P("tower", "dp", None),
            P("tower", "dp"),
            P("tower", "dp", None),
            P("tower", "dp"),
            P("tower", "dp"),
            P("tower", "dp"),
            P("tower", "dp", None),
            P(),
        ),
        out_specs=(
            P("tower", "dp", None, None),
            P("tower", "dp", None, None),
            P(),
            P("tower", "dp"),
            P("tower", "dp"),
            P("tower", "dp", None, None),
            P("tower", None, "dp"),
            P("tower", "dp", None),
            P("tower", "dp"),
            P("tower", "dp"),
            P("tower", "dp"),
            P("tower", "dp", None),
            P("tower", "dp"),
            P("tower", "dp", None),
            P("tower", "dp"),
            P("tower", "dp"),
            P("tower", "dp"),
            P("tower", "dp", None),
            P(),
        ),
        check_vma=False,
    )
```

```python
import jax
import jax.numpy as jnp
from jax import lax
from jax.experimental import pallas as pl
from jax.experimental.pallas import tpu as pltpu
from jax.sharding import PartitionSpec as P

DI = 768
DT = 512
HD = 64
IMG_ROWS = 50
EMB = 512


EPS = 1e-05
NORM_EPS = 1e-06
GELU_K = 1.702
NEG_FILL = -1e30


def swapped(block, axis, stride):
    count = lax.axis_size(axis)
    route = []
    for low in range(count):
        high = low | 1 << stride
        if high != low and high < count:
            route += [(low, high), (high, low)]
    return lax.ppermute(block, axis, route)


def masked_norm(values, norm_gain, norm_bias, col_keep, width_real):
    row_mean = jnp.sum(values * col_keep, axis=-1, keepdims=True) / width_real
    centred = (values - row_mean) * col_keep
    row_var = jnp.sum(centred * centred, axis=-1, keepdims=True) / width_real
    inv_std = lax.rsqrt(row_var + EPS)
    normed = centred * inv_std
    return (normed * norm_gain + norm_bias, normed, inv_std)


def masked_norm_back(grad_out, norm_gain, normed, inv_std, col_keep, width_real):
    grad_normed = grad_out * norm_gain
    mean_grad = jnp.sum(grad_normed, axis=-1, keepdims=True) / width_real
    mean_cross = jnp.sum(grad_normed * normed, axis=-1, keepdims=True) / width_real
    grad_in = col_keep * inv_std * (grad_normed - mean_grad - normed * mean_cross)
    return (grad_in, jnp.sum(grad_out * normed, axis=0), jnp.sum(grad_out, axis=0))


def contract_rows(left_op, right_op):
    return lax.dot_general(
        left_op, right_op, (((0,), (0,)), ((), ())), preferred_element_type=jnp.float32
    )


def contract_cols(left_op, right_op):
    return lax.dot_general(
        left_op, right_op, (((1,), (1,)), ((), ())), preferred_element_type=jnp.float32
    )


def column_sum(values):
    return jnp.sum(values, axis=0, dtype=jnp.float32)


def body(
    tokens,
    lengths,
    ln1_gain,
    ln1_bias,
    qkv_weight,
    qv_bias,
    out_weight,
    out_bias,
    ln2_gain,
    ln2_bias,
    fc_weight,
    fc_bias,
    down_weight,
    down_bias,
    final_gain,
    final_bias,
    embed_weight,
    logit_scale,
):
    f32 = jnp.float32
    bf16 = jnp.bfloat16
    tower_index = lax.axis_index("tower")
    dp_index = lax.axis_index("dp")
    dp_count = lax.axis_size("dp")
    samples, seq_rows, width_all = (tokens.shape[1], tokens.shape[2], tokens.shape[3])
    head_count = width_all // HD
    sample_total = samples * dp_count
    flat_rows = samples * seq_rows
    is_text = tower_index == 1
    width_int = jnp.where(is_text, DT, DI)
    width_real = width_int.astype(f32)
    col_keep = (lax.broadcasted_iota(jnp.int32, (width_all,), 0) < width_int).astype(f32)
    seq_lens = jnp.where(is_text, lengths, IMG_ROWS)
    positions = lax.broadcasted_iota(jnp.int32, (samples, seq_rows), 1)
    row_keep = (positions < seq_lens[:, None]).astype(f32).reshape(flat_rows, 1)
    query_pos = lax.broadcasted_iota(jnp.int32, (seq_rows, seq_rows), 0)
    key_pos = lax.broadcasted_iota(jnp.int32, (seq_rows, seq_rows), 1)
    allowed = (key_pos[None] < seq_lens[:, None, None]) & (
        jnp.logical_not(is_text) | (key_pos <= query_pos)
    )[None]
    pool_pos = jnp.where(is_text, lengths - 1, 0)
    pool_hot = (positions == pool_pos[:, None]).astype(f32)
    score_mult = float(HD) ** (-0.5)
    gathered = (
        lax.all_gather(ln1_gain[0], "dp", axis=0, tiled=True),
        lax.all_gather(ln1_bias[0], "dp", axis=0, tiled=True),
        lax.all_gather(qkv_weight[0], "dp", axis=0, tiled=True),
        lax.all_gather(qv_bias[0], "dp", axis=1, tiled=True),
        lax.all_gather(out_weight[0], "dp", axis=0, tiled=True),
        lax.all_gather(out_bias[0], "dp", axis=0, tiled=True),
        lax.all_gather(ln2_gain[0], "dp", axis=0, tiled=True),
        lax.all_gather(ln2_bias[0], "dp", axis=0, tiled=True),
        lax.all_gather(fc_weight[0], "dp", axis=0, tiled=True),
        lax.all_gather(fc_bias[0], "dp", axis=0, tiled=True),
        lax.all_gather(down_weight[0], "dp", axis=0, tiled=True),
        lax.all_gather(down_bias[0], "dp", axis=0, tiled=True),
        lax.all_gather(final_gain[0], "dp", axis=0, tiled=True),
        lax.all_gather(final_bias[0], "dp", axis=0, tiled=True),
        lax.all_gather(embed_weight[0], "dp", axis=0, tiled=True),
    )
    (
        gain_one,
        bias_one,
        w_qkv,
        b_qv,
        w_out,
        b_out,
        gain_two,
        bias_two,
        w_fc,
        b_fc,
        w_down,
        b_down,
        gain_final,
        bias_final,
        w_embed,
    ) = gathered
    stream = tokens[0].astype(f32).reshape(flat_rows, width_all)
    normed_h1, norm_one, inv_one = masked_norm(
        stream, gain_one.astype(f32), bias_one.astype(f32), col_keep, width_real
    )
    normed_one = normed_h1.astype(bf16)
    qkv_bias = jnp.concatenate(
        [b_qv[0].astype(f32), jnp.zeros((width_all,), f32), b_qv[1].astype(f32)]
    )
    qkv_flat = (
        jnp.dot(normed_one, w_qkv.reshape(width_all, 3 * width_all), preferred_element_type=f32)
        + qkv_bias
    )
    qkv_low = qkv_flat.astype(bf16).reshape(samples, seq_rows, 3, head_count, HD)
    query_all = qkv_low[:, :, 0]
    key_all = qkv_low[:, :, 1]
    value_all = qkv_low[:, :, 2]

    def masked_scores():
        raw = (
            jnp.einsum("sqhd,skhd->shqk", query_all, key_all, preferred_element_type=f32)
            * score_mult
        )
        return jnp.where(allowed[:, None], raw, NEG_FILL)

    scores = masked_scores()
    row_top = jnp.max(scores, axis=-1, keepdims=True)
    exp_terms = jnp.exp(scores - row_top)
    exp_sum = jnp.sum(exp_terms, axis=-1, keepdims=True)
    log_total = row_top + jnp.log(exp_sum)
    attn_probs = (exp_terms / exp_sum).astype(bf16)
    head_mix = jnp.einsum("shqk,skhd->sqhd", attn_probs, value_all, preferred_element_type=f32)
    head_mix_low = head_mix.astype(bf16).reshape(flat_rows, width_all)
    attn_out = jnp.dot(head_mix_low, w_out, preferred_element_type=f32) + b_out.astype(f32)
    middle = stream + attn_out
    normed_h2, norm_two, inv_two = masked_norm(
        middle, gain_two.astype(f32), bias_two.astype(f32), col_keep, width_real
    )
    normed_two = normed_h2.astype(bf16)
    hidden_pre = jnp.dot(normed_two, w_fc, preferred_element_type=f32) + b_fc.astype(f32)
    gate_sig = jax.nn.sigmoid(GELU_K * hidden_pre)
    act_low = (hidden_pre * gate_sig).astype(bf16)
    branch = jnp.dot(act_low, w_down, preferred_element_type=f32) + b_down.astype(f32)
    block_rows = row_keep * (middle + branch)
    block_out = block_rows.astype(bf16).reshape(1, samples, seq_rows, width_all)
    block_three = block_rows.reshape(samples, seq_rows, width_all)
    pooled = jnp.take_along_axis(block_three, pool_pos[:, None, None], axis=1)[:, 0]
    normed_hf, norm_final, inv_final = masked_norm(
        pooled, gain_final.astype(f32), bias_final.astype(f32), col_keep, width_real
    )
    head_low = normed_hf.astype(bf16)
    projected = jnp.dot(head_low, w_embed, preferred_element_type=f32)
    inv_norm = lax.rsqrt(jnp.sum(projected * projected, axis=-1, keepdims=True) + NORM_EPS)
    embed_low = (projected * inv_norm).astype(bf16)
    own_all = lax.all_gather(embed_low, "dp", axis=0, tiled=True)
    others = swapped(own_all, "tower", 0)
    logit_mult = jnp.exp(logit_scale[0])
    similar = contract_cols(embed_low, others)
    logits = logit_mult * similar
    logit_top = jnp.max(logits, axis=-1, keepdims=True)
    logit_total = logit_top + jnp.log(jnp.sum(jnp.exp(logits - logit_top), axis=-1, keepdims=True))
    label_col = dp_index * samples + lax.broadcasted_iota(jnp.int32, (samples, 1), 0)
    label_hot = (lax.broadcasted_iota(jnp.int32, (samples, sample_total), 1) == label_col).astype(
        f32
    )
    diag_logit = jnp.sum(label_hot * logits, axis=-1, keepdims=True)
    loss_part = jnp.sum(logit_total - diag_logit) / (2.0 * sample_total)
    grad_logits = (jnp.exp(logits - logit_total) - label_hot) * 0.5
    scale_part = logit_mult * jnp.sum(grad_logits * similar)
    grad_sims = (logit_mult * grad_logits).astype(bf16)
    grad_own = jnp.dot(grad_sims, others, preferred_element_type=f32)
    grad_others = contract_rows(grad_sims, embed_low)
    sent_back = swapped(grad_others, "tower", 0)
    returned = lax.psum_scatter(sent_back, "dp", scatter_dimension=0, tiled=True)
    totals = lax.psum((loss_part, scale_part), ("tower", "dp"))
    grad_embed = grad_own + returned
    again = (
        lax.all_gather(ln1_gain[0], "dp", axis=0, tiled=True),
        lax.all_gather(qkv_weight[0], "dp", axis=0, tiled=True),
        lax.all_gather(out_weight[0], "dp", axis=0, tiled=True),
        lax.all_gather(ln2_gain[0], "dp", axis=0, tiled=True),
        lax.all_gather(fc_weight[0], "dp", axis=0, tiled=True),
        lax.all_gather(down_weight[0], "dp", axis=0, tiled=True),
        lax.all_gather(final_gain[0], "dp", axis=0, tiled=True),
        lax.all_gather(embed_weight[0], "dp", axis=0, tiled=True),
    )
    (
        back_gain_one,
        back_qkv,
        back_out,
        back_gain_two,
        back_fc,
        back_down,
        back_gain_final,
        back_embed,
    ) = again
    cross_term = jnp.sum(grad_embed * projected, axis=-1, keepdims=True)
    grad_proj = inv_norm * grad_embed - projected * inv_norm * inv_norm * inv_norm * cross_term
    grad_proj_low = grad_proj.astype(bf16)
    grad_head = contract_cols(grad_proj_low, back_embed)
    grad_pooled, d_gain_final, d_bias_final = masked_norm_back(
        grad_head, back_gain_final.astype(f32), norm_final, inv_final, col_keep, width_real
    )
    grad_rows = (pool_hot[:, :, None] * grad_pooled[:, None, :]).reshape(flat_rows, width_all)
    grad_branch_low = grad_rows.astype(bf16)
    d_down_b = column_sum(grad_branch_low)
    grad_act = contract_cols(grad_branch_low, back_down)
    grad_pre_low = (
        grad_act * (gate_sig + GELU_K * hidden_pre * gate_sig * (1.0 - gate_sig))
    ).astype(bf16)
    d_fc_b = column_sum(grad_pre_low)
    grad_norm_two = contract_cols(grad_pre_low, back_fc)
    grad_mid_norm, d_gain_two, d_bias_two = masked_norm_back(
        grad_norm_two, back_gain_two.astype(f32), norm_two, inv_two, col_keep, width_real
    )
    grad_middle = grad_rows + grad_mid_norm
    grad_attn_low = grad_middle.astype(bf16)
    d_out_b = column_sum(grad_attn_low)
    grad_mix_low = (
        contract_cols(grad_attn_low, back_out)
        .astype(bf16)
        .reshape(samples, seq_rows, head_count, HD)
    )
    probs_again = jnp.exp(masked_scores() - log_total)
    probs_low = probs_again.astype(bf16)
    grad_value = jnp.einsum("shqk,sqhd->skhd", probs_low, grad_mix_low, preferred_element_type=f32)
    grad_probs = jnp.einsum("sqhd,skhd->shqk", grad_mix_low, value_all, preferred_element_type=f32)
    grad_scores = probs_again * (
        grad_probs - jnp.sum(probs_again * grad_probs, axis=-1, keepdims=True)
    )
    grad_scores_low = grad_scores.astype(bf16)
    grad_query = (
        jnp.einsum("shqk,skhd->sqhd", grad_scores_low, key_all, preferred_element_type=f32)
        * score_mult
    )
    grad_key = (
        jnp.einsum("shqk,sqhd->skhd", grad_scores_low, query_all, preferred_element_type=f32)
        * score_mult
    )
    grad_qkv_low = (
        jnp.stack([grad_query, grad_key, grad_value], axis=2)
        .astype(bf16)
        .reshape(flat_rows, 3 * width_all)
    )
    d_qkv_w = contract_rows(normed_one, grad_qkv_low).reshape(width_all, 3, width_all)
    qkv_sums = column_sum(grad_qkv_low).reshape(3, width_all)
    d_qv_b = jnp.stack([qkv_sums[0], qkv_sums[2]])
    grad_norm_one = contract_cols(grad_qkv_low, back_qkv.reshape(width_all, 3 * width_all))
    grad_in_norm, d_gain_one, d_bias_one = masked_norm_back(
        grad_norm_one, back_gain_one.astype(f32), norm_one, inv_one, col_keep, width_real
    )
    tokens_grad = (grad_middle + grad_in_norm).reshape(1, samples, seq_rows, width_all)
    d_embed_w = contract_rows(head_low, grad_proj_low)
    d_down_w = contract_rows(act_low, grad_branch_low)
    d_fc_w = contract_rows(normed_two, grad_pre_low)
    d_out_w = contract_rows(head_mix_low, grad_attn_low)
    shares = (
        lax.psum_scatter(d_gain_one, "dp", scatter_dimension=0, tiled=True),
        lax.psum_scatter(d_bias_one, "dp", scatter_dimension=0, tiled=True),
        lax.psum_scatter(d_qkv_w, "dp", scatter_dimension=0, tiled=True),
        lax.psum_scatter(d_qv_b, "dp", scatter_dimension=1, tiled=True),
        lax.psum_scatter(d_out_w, "dp", scatter_dimension=0, tiled=True),
        lax.psum_scatter(d_out_b, "dp", scatter_dimension=0, tiled=True),
        lax.psum_scatter(d_gain_two, "dp", scatter_dimension=0, tiled=True),
        lax.psum_scatter(d_bias_two, "dp", scatter_dimension=0, tiled=True),
        lax.psum_scatter(d_fc_w, "dp", scatter_dimension=0, tiled=True),
        lax.psum_scatter(d_fc_b, "dp", scatter_dimension=0, tiled=True),
        lax.psum_scatter(d_down_w, "dp", scatter_dimension=0, tiled=True),
        lax.psum_scatter(d_down_b, "dp", scatter_dimension=0, tiled=True),
        lax.psum_scatter(d_gain_final, "dp", scatter_dimension=0, tiled=True),
        lax.psum_scatter(d_bias_final, "dp", scatter_dimension=0, tiled=True),
        lax.psum_scatter(d_embed_w, "dp", scatter_dimension=0, tiled=True),
    )
    results = list(shares)
    outputs = [item[None] for item in results]
    loss = totals[0].reshape(1)
    logit_scale_grad = totals[1].reshape(1)
    return (
        block_out,
        tokens_grad,
        loss,
        outputs[0],
        outputs[1],
        outputs[2],
        outputs[3],
        outputs[4],
        outputs[5],
        outputs[6],
        outputs[7],
        outputs[8],
        outputs[9],
        outputs[10],
        outputs[11],
        outputs[12],
        outputs[13],
        outputs[14],
        logit_scale_grad,
    )


RING_Z = (0, 1, 2, 3, 3, 2, 1, 0)
RING_Y = (0, 0, 0, 0, 1, 1, 1, 1)
ITEMS = 16
N = ITEMS * 8
F32 = jnp.float32
BF16 = jnp.bfloat16
ANY = pl.BlockSpec(memory_space=pl.ANY)
VMEM = pl.BlockSpec(memory_space=pltpu.VMEM)
SMEM = pl.BlockSpec(memory_space=pltpu.SMEM)
SCALE = float(HD) ** -0.5
PAYLOAD = 160


def call(kernel, name, ins, outs, scratch, flops=0, touched=0):
    return pl.pallas_call(
        kernel,
        name=name,
        out_shape=[jax.ShapeDtypeStruct(shape, dtype) for _, shape, dtype in outs],
        in_specs=[spec for spec, _ in ins],
        out_specs=[spec for spec, _, _ in outs],
        scratch_shapes=scratch,
        compiler_params=pltpu.CompilerParams(vmem_limit_bytes=60 * 1024 * 1024),
        cost_estimate=pl.CostEstimate(flops=flops, bytes_accessed=touched, transcendentals=0),
    )(*[item for _, item in ins])


def dot(left, right, left_dim=1, right_dim=0):
    return lax.dot_general(
        left, right, (((left_dim,), (right_dim,)), ((), ())), preferred_element_type=F32
    )


def aligned(index, size):
    return pl.multiple_of(index, size)


def owner_table(dp_index):
    core = dp_index % 2
    row = dp_index // 2 % 2
    depth = dp_index // 4
    place = jnp.where(row == 0, depth, 7 - depth)

    def chip(where):
        where = (where + 8) % 8
        z = jnp.where(where < 4, where, 7 - where)
        y = jnp.where(where < 4, 0, 1)
        return (z * 2 + y) * 2

    sign = jnp.where(core == 0, -1, 1)
    found = [chip(place)]
    for hop in range(1, 4):
        found += [chip(place + sign * hop), chip(place - sign * hop)]
    return found + [chip(place + 4) + core, chip(place + 4) + 1 - core]


class Place:
    def __init__(self, lengths):
        self.dp = lax.axis_index("dp")
        self.text = lax.axis_index("tower") == 1
        self.lengths = lengths
        self.keep = (
            lax.broadcasted_iota(jnp.int32, (1, DI), 1) < jnp.where(self.text, DT, DI)
        ).astype(F32)
        self.winv = jnp.where(self.text, 1.0 / DT, 1.0 / DI).astype(F32)

    def length(self, s):
        return jnp.where(self.text, self.lengths[s], IMG_ROWS)

    def pool(self, s):
        return jnp.where(self.text, self.lengths[s] - 1, 0)

    def column(self, pick):
        ids = lax.broadcasted_iota(jnp.int32, (1, 8, 1), 1)
        column = jnp.zeros((1, 8, 1), jnp.int32)
        for s in range(8):
            column = jnp.where(ids == s, pick(s), column)
        return column

    def either(self, path, image):
        @pl.when(self.text)
        def _():
            path(DT, 77)

        @pl.when(jnp.logical_not(self.text))
        def _():
            path(DI, image)

    def mine(self, visit):
        for owner in range(ITEMS):

            @pl.when(self.dp == owner)
            def _(owner=owner):
                visit(owner)


def copy(src, dst, sem):
    found = pltpu.make_async_copy(src, dst, sem)
    found.start()
    return found


def drain(dst, sem):
    pltpu.make_async_copy(dst, dst, sem).wait()


def fetch(owners, refs, row, rows, dst, sem):
    for owner, ref in zip(owners, refs):
        if len(ref.shape) == 3:
            copy(ref.at[:, pl.ds(row, rows), :], dst.at[pl.ds(owner, 2)], sem)
        else:
            copy(ref.at[pl.ds(row, rows), :], dst.at[owner], sem)


def embed_matrix(packed):
    tail = jnp.concatenate([packed[:, 0:16, EMB:DI], packed[:, 16:32, EMB:DI]], axis=2)
    return jnp.concatenate([packed[:, :, 0:EMB], tail], axis=1).reshape(DI, EMB)


def normalize(values, keep, winv):
    mean = jnp.sum(values, axis=-1, keepdims=True) * winv
    centred = (values - mean) * keep
    var = jnp.sum(centred * centred, axis=-1, keepdims=True) * winv
    inv = lax.rsqrt(var + EPS)
    return centred * inv, inv


def normalize_back(grad_out, gain, normed, inv, keep, winv):
    grad_normed = grad_out * gain
    mean_grad = jnp.sum(grad_normed, axis=-1, keepdims=True) * winv
    mean_cross = jnp.sum(grad_normed * normed, axis=-1, keepdims=True) * winv
    return keep * inv * (grad_normed - mean_grad - normed * mean_cross)


def row_sum(values):
    return jnp.sum(values, axis=0, keepdims=True)


def head_rows(rows):
    heads = lax.broadcasted_iota(jnp.int32, rows.shape, 1) // HD
    parts = [jnp.where(heads == head, rows, 0.0) for head in range(16)]
    return jnp.concatenate(parts, axis=0).astype(BF16)


def chunks(count, visit):
    @pl.loop(0, count // 14)
    def _(i):
        visit(i * 14, aligned(i * 112, 16), 14)

    if count % 14:
        at = count - count % 14
        visit(at, at * 8, count % 14)


def pack_first_kernel(lengths, qkv, tok, *rest):
    here = Place(lengths)
    vectors, (qv_bias, fc_bias, out) = rest[:8], rest[8:]
    out[0:144, :] = qkv[...]
    sub = lax.broadcasted_iota(jnp.int32, (8, DI), 0)
    pooled = jnp.zeros((8, DI), F32)
    for s in range(8):
        pooled = jnp.where(sub == s, tok[here.pool(s)].astype(F32), pooled)
    out[144:160, :] = jnp.concatenate([pooled, jnp.zeros((8, DI), F32)], axis=0).astype(BF16)
    lane = lax.broadcasted_iota(jnp.int32, (1, DI), 1) // 48 == here.dp
    short = [v[...].astype(F32) for v in vectors]
    pair = qv_bias[...].astype(F32)
    short[2:2] = [pair[0:1], pair[1:2]]
    rows = [jnp.where(lane, jnp.concatenate([v] * ITEMS, axis=1), 0.0) for v in short]
    wide = lax.broadcasted_iota(jnp.int32, (1, 4 * DI), 1) // 192 == here.dp
    fc = jnp.where(wide, jnp.concatenate([fc_bias[...].astype(F32)] * ITEMS, axis=1), 0.0)
    rows += [fc[:, i * DI : (i + 1) * DI] for i in range(4)]
    row_id = lax.broadcasted_iota(jnp.int32, (16, DI), 0)
    small = jnp.zeros((16, DI), F32)
    for at, row in enumerate(rows):
        small = jnp.where(row_id == at, jnp.broadcast_to(row, (16, DI)), small)
    out[160:176, :] = small.astype(BF16)


def pack_first(lengths, qkv, tok, vectors, qv_bias, fc_bias):
    return call(
        pack_first_kernel,
        "pack_first",
        [(SMEM, lengths)] + [(VMEM, item) for item in (qkv, tok, *vectors, qv_bias, fc_bias)],
        [(VMEM, (176, DI), BF16)],
        [],
        touched=1_500_000,
    )[0]


def pack_rest_kernel(w_out, w_fc, w_emb, out):
    out[0:48, :] = w_out[...]
    out[48:80, 0:EMB] = w_emb[0:32, :]
    out[48:64, EMB:DI] = w_emb[32:48, 0:256]
    out[64:80, EMB:DI] = w_emb[32:48, 256:EMB]
    for block in range(4):
        out[80 + 48 * block : 128 + 48 * block, :] = w_fc[:, block * DI : (block + 1) * DI]


def pack_rest(w_out, w_fc, w_emb):
    return call(
        pack_rest_kernel,
        "pack_rest",
        [(VMEM, item) for item in (w_out, w_fc, w_emb)],
        [(VMEM, (272, DI), BF16)],
        [],
        touched=1_500_000,
    )[0]


def attend_kernel(lengths, tok, *rest):
    first, (keys_hbm, values_hbm, norm_hbm, mixed, vec, pooled), scratch = rest[:9], rest[9:15], rest[15:]
    weights, small, normed, keys, values, norm_low, qf, kf, vf, mf, sems, outs = scratch
    here = Place(lengths)
    owners = owner_table(here.dp)
    fetch(owners, first, 160, 16, small, sems.at[0])
    fetch(owners, first, 0, 144, weights, sems.at[1])
    keep, winv = here.keep, here.winv
    drain(small, sems.at[0])
    vec[...] = jnp.sum(small[...].astype(F32), axis=0)

    def norm_chunk(position, row, count):
        x = tok[pl.ds(position, count)].astype(F32).reshape(count * 8, DI)
        norm, _ = normalize(x, keep, winv)
        norm_low[pl.ds(row, count * 8), :] = norm.astype(BF16)
        normed[pl.ds(row, count * 8), :] = (norm * vec[0:1, :] + vec[1:2, :]).astype(BF16)

    def path(width, count):
        rows = count * 8
        span = 80 if count == 77 else count
        chunks(count, norm_chunk)
        if span > count:
            for dst in (qf, kf, vf):
                dst[:, rows : span * 8, :] = jnp.zeros((6, span * 8 - rows, 128), F32)
        drain(weights, sems.at[1])
        for third, dst, low, bias in ((0, qf, None, 2), (1, kf, keys, None), (2, vf, values, 3)):

            @pl.loop(0, width // 256)
            def _(j, third=third, dst=dst, low=low, bias=bias):
                lanes = pl.ds(aligned(j * 256, 256), 256)
                weight = weights[:, third * 48 : third * 48 + 48, lanes].reshape(DI, 256)
                prod = dot(normed[0:rows, 0:width], weight[0:width])
                if bias is not None:
                    prod = prod + vec[bias : bias + 1, lanes]
                if third == 0:
                    prod = prod.astype(BF16).astype(F32) * SCALE
                dst[2 * j, 0:rows, :] = prod[:, 0:128]
                dst[2 * j + 1, 0:rows, :] = prod[:, 128:256]
                if low is not None:
                    low[0:rows, lanes] = prod.astype(BF16)

        saved = [
            copy(keys, keys_hbm, outs.at[0]),
            copy(values, values_hbm, outs.at[1]),
            copy(norm_low, norm_hbm, outs.at[2]),
        ]
        key_pos = lax.broadcasted_iota(jnp.int32, (span, 2 * span), 0)
        query_pos = lax.broadcasted_iota(jnp.int32, (span, 2 * span), 1) % span
        low_half = lax.broadcasted_iota(jnp.int32, (span, 128), 1) < HD

        @pl.loop(0, 8)
        def _(s):
            at = pl.ds(s, span, stride=8)
            allowed = key_pos < here.length(s)
            if width == DT:
                allowed = allowed & (key_pos <= query_pos)
            pairs = range(width // 128)
            raws = []
            for pair in pairs:
                query, key = qf.at[pair][at, :], kf.at[pair][at, :].astype(BF16)
                spread = [jnp.where(low_half, query, 0.0), jnp.where(low_half, 0.0, query)]
                spread = jnp.concatenate(spread, axis=0).astype(BF16)
                raws.append(dot(key, spread, 1, 1))
            probs = []
            for raw in raws:
                raw = jnp.where(allowed, raw, NEG_FILL)
                terms = jnp.exp(raw - jnp.max(raw, axis=0, keepdims=True))
                probs.append((terms / jnp.sum(terms, axis=0, keepdims=True)).astype(BF16))
            for pair in pairs:
                out = dot(probs[pair], vf.at[pair][at, :].astype(BF16), 0, 0)
                mf.at[pair][at, :] = jnp.where(low_half, out[0:span], out[span : 2 * span])

        for i in range(width // 128):
            mixed[0:rows, 128 * i : 128 * i + 128] = mf[i, 0:rows, :].astype(BF16)
        for item in saved:
            item.wait()

    here.either(path, 56)
    row_id = lax.broadcasted_iota(jnp.int32, (8, DI), 0)
    picked = jnp.zeros((8, DI), F32)
    for s in range(8):
        at = pl.ds(aligned(here.pool(s) * 8, 8), 8)
        block = jnp.concatenate([mf[i, at, :] for i in range(6)], axis=1)
        picked = jnp.where(row_id == s, block, picked)
    tall = jnp.concatenate([jnp.where(keep > 0.0, picked, 0.0), jnp.zeros((8, DI), F32)], axis=0)
    for owner in range(ITEMS):
        pooled[owner] = tall.astype(BF16)


def attend(lengths, tok, first):
    rows = tok.shape[0] * tok.shape[1]
    high = (tok.shape[0] + 3) * tok.shape[1]
    return call(
        attend_kernel,
        "attend",
        [(SMEM, lengths), (VMEM, tok)] + [(ANY, r) for r in first],
        [
            (ANY, (rows, DI), BF16),
            (ANY, (rows, DI), BF16),
            (ANY, (rows, DI), BF16),
            (VMEM, (rows, DI), BF16),
            (VMEM, (16, DI), F32),
            (VMEM, (ITEMS, 16, DI), BF16),
        ],
        [
            pltpu.VMEM((ITEMS, 144, DI), BF16),
            pltpu.VMEM((ITEMS, 16, DI), BF16),
            pltpu.VMEM((rows, DI), BF16),
            pltpu.VMEM((rows, DI), BF16),
            pltpu.VMEM((rows, DI), BF16),
            pltpu.VMEM((rows, DI), BF16),
            pltpu.VMEM((6, high, 128), F32),
            pltpu.VMEM((6, high, 128), F32),
            pltpu.VMEM((6, high, 128), F32),
            pltpu.VMEM((6, high, 128), F32),
            pltpu.SemaphoreType.DMA((2,)),
            pltpu.SemaphoreType.DMA((3,)),
        ],
        flops=12_000_000_000,
        touched=14_000_000,
    )


def widen_kernel(lengths, tok, vec, mixed_hbm, *rest):
    first, second, mixes = rest[:9], rest[9:18], rest[18]
    outs, scratch = rest[19:31], rest[31:]
    (act_hbm, middle_hbm, mid_out, norm2_out, inv2_out, slope_out, act_p, q_out, q_own, n2_sl, mix_sl,
     norm_sl) = outs
    w_q, w_out, w_fc, xs, ms, mix, n2_all, norm1_all, middle, act, sems = scratch
    here = Place(lengths)
    owners = owner_table(here.dp)
    rows_all = mixed_hbm.shape[0]
    fetch(owners, second, 0, 48, w_out, sems.at[2])
    pooled_in = copy(mixes, ms, sems.at[1])
    full = copy(mixed_hbm, mix.at[pl.ds(N, rows_all), :], sems.at[5])
    fetch(owners, first, 144, 16, xs, sems.at[0])
    fetch(owners, second, 80, 192, w_fc, sems.at[3])
    fetch(owners, first, 0, 48, w_q, sems.at[4])
    keep, winv = here.keep, here.winv
    drain(w_out, sems.at[2])
    pooled_in.wait()
    mix[0:N, :] = ms[...].astype(F32)[:, :8, :].reshape(N, DI).astype(BF16)
    full.wait()

    def norm_chunk(position, row, count):
        at = pl.ds(N + row, count * 8)
        total = middle[at, :] + tok[pl.ds(position, count)].astype(F32).reshape(count * 8, DI)
        middle[at, :] = total
        norm, _ = normalize(total, keep, winv)
        n2_all[at, :] = (norm * vec[5:6, :] + vec[6:7, :]).astype(BF16)

    def path(width, count):
        rows = N + count * 8
        norm_rows = N + (count if width == DT else 56) * 8

        @pl.loop(0, width // 256)
        def _(j):
            lanes = pl.ds(aligned(j * 256, 256), 256)
            weight = w_out[:, :, lanes].reshape(DI, 256)[0:width]
            middle[0:norm_rows, lanes] = dot(mix[0:norm_rows, 0:width], weight) + vec[4:5, lanes]

        if width < DI:
            middle[0:norm_rows, width:DI] = jnp.zeros((norm_rows, DI - width), F32)
        chunks(count if width == DT else 56, norm_chunk)
        saved = copy(middle.at[pl.ds(N, rows_all), :], middle_hbm, sems.at[7])
        drain(xs, sems.at[0])
        stream = xs[...].astype(F32)[:, :8, :].reshape(N, DI)
        pooled = stream + middle[0:N, :]
        mid_out[...] = pooled
        norm2, inv2 = normalize(pooled, keep, winv)
        n2_all[0:N, :] = (norm2 * vec[5:6, :] + vec[6:7, :]).astype(BF16)
        norm2_out[...] = norm2
        inv2_out[...] = jnp.broadcast_to(inv2, (N, 128))
        norm1, _ = normalize(stream, keep, winv)
        norm1_all[...] = norm1.astype(BF16)
        drain(w_fc, sems.at[3])
        for block in range(4):

            @pl.loop(0, 3 if width == DI else (3, 3, 2, 0)[block])
            def _(j, block=block):
                lanes = pl.ds(aligned(j * 256, 256), 256)
                wide = pl.ds(aligned(block * DI + j * 256, 256), 256)
                weight = w_fc[:, block * 48 : block * 48 + 48, lanes].reshape(DI, 256)[0:width]
                pre = dot(n2_all[0:rows, 0:width], weight) + vec[10 + block : 11 + block, lanes]
                gate = jax.nn.sigmoid(GELU_K * pre)
                low = (pre * gate).astype(BF16)
                act_p[:, wide] = low[0:N]
                act[0 : rows - N, wide] = low[N:rows]
                pre, gate = pre[0:N], gate[0:N]
                slope_out[:, wide] = gate + GELU_K * pre * gate * (1.0 - gate)
                copy(act.at[pl.ds(0, rows - N), wide], act_hbm.at[pl.ds(0, rows - N), wide], sems.at[6])

        if width < DI:
            act_p[:, 4 * width : 4 * DI] = jnp.zeros((N, 4 * DI - 4 * width), BF16)
            slope_out[:, 4 * width : 4 * DI] = jnp.zeros((N, 4 * DI - 4 * width), F32)
        drain(w_q, sems.at[4])
        n1 = (norm1 * vec[0:1, :] + vec[1:2, :]).astype(BF16)
        q_out[...] = (dot(n1, w_q[...].reshape(DI, DI)) + vec[2:3, :]).astype(BF16).astype(F32)
        q_own[...] = q_out[pl.ds(aligned(here.dp * 8, 8), 8), :]
        drain(act.at[pl.ds(0, rows - N), pl.ds(0, 4 * width)], sems.at[6])
        saved.wait()

    here.either(path, 50)

    def mine(owner):
        lanes = slice(owner * 48, owner * 48 + 48)
        n2_sl[...] = n2_all[0:N, lanes]
        mix_sl[...] = mix[0:N, lanes]
        norm_sl[...] = norm1_all[:, lanes]

    here.mine(mine)


def widen(lengths, tok, vec, mixed, first, second, mixes):
    rows = mixed.shape[0]
    return call(
        widen_kernel,
        "widen",
        [(SMEM, lengths), (VMEM, tok), (VMEM, vec), (ANY, mixed)]
        + [(ANY, r) for r in (*first, *second, mixes)],
        [
            (ANY, (rows, 4 * DI), BF16),
            (ANY, (rows, DI), F32),
            (VMEM, (N, DI), F32),
            (VMEM, (N, DI), F32),
            (VMEM, (N, 128), F32),
            (VMEM, (N, 4 * DI), F32),
            (VMEM, (N, 4 * DI), BF16),
            (VMEM, (N, DI), F32),
            (VMEM, (8, DI), F32),
            (VMEM, (N, 48), BF16),
            (VMEM, (N, 48), BF16),
            (VMEM, (N, 48), BF16),
        ],
        [
            pltpu.VMEM((ITEMS, 48, DI), BF16),
            pltpu.VMEM((ITEMS, 48, DI), BF16),
            pltpu.VMEM((ITEMS, 192, DI), BF16),
            pltpu.VMEM((ITEMS, 16, DI), BF16),
            pltpu.VMEM((ITEMS, 16, DI), BF16),
            pltpu.VMEM((N + rows, DI), BF16),
            pltpu.VMEM((N + rows, DI), BF16),
            pltpu.VMEM((N, DI), BF16),
            pltpu.VMEM((N + rows, DI), F32),
            pltpu.VMEM((rows, 4 * DI), BF16),
            pltpu.SemaphoreType.DMA((8,)),
        ],
        flops=13_000_000_000,
        touched=14_000_000,
    )


def head_kernel(lengths, vec, middle_hbm, act_hbm, *rest):
    second, down, outs, scratch = rest[:9], rest[9:18], rest[18:24], rest[24:]
    e_out, proj_out, normf_out, invf_out, head_sl, act_sl = outs
    w_down, w_emb, head_all, middle, act, sems = scratch
    here = Place(lengths)
    owners = owner_table(here.dp)
    early = [copy(act_hbm, act, sems.at[5]), copy(middle_hbm, middle, sems.at[6])]
    for owner, ref in zip(owners, down):
        dst = w_down.at[pl.ds(owner, 2)] if len(ref.shape) == 3 else w_down.at[owner]
        copy(ref, dst, sems.at[owner // 4])
    fetch(owners, second, 48, 32, w_emb, sems.at[4])
    keep, winv = here.keep, here.winv
    for item in early:
        item.wait()
    last = middle[...] + vec[7:8, :]
    for part in range(4):
        drain(w_down.at[pl.ds(part * 4, 4)], sems.at[part])
        last = last + dot(act[:, part * DI : part * DI + DI], w_down[part * 4 : part * 4 + 4].reshape(DI, DI))
    normf, invf = normalize(last, keep, winv)
    normf_out[...] = normf
    invf_out[...] = jnp.broadcast_to(invf, (N, 128))
    head_all[...] = (normf * vec[8:9, :] + vec[9:10, :]).astype(BF16)
    drain(w_emb, sems.at[4])
    proj = dot(head_all[...], embed_matrix(w_emb[...]))
    proj_out[...] = proj
    scale = lax.rsqrt(jnp.sum(proj * proj, axis=-1, keepdims=True) + NORM_EPS)
    e_out[...] = (proj * scale).astype(BF16)

    def mine(owner):
        head_sl[...] = head_all[:, owner * 48 : owner * 48 + 48]
        act_sl[...] = act[:, owner * 192 : owner * 192 + 192]

    here.mine(mine)


def pooled_head(lengths, vec, middle, act, second, down):
    return call(
        head_kernel,
        "pooled_head",
        [(SMEM, lengths), (VMEM, vec), (ANY, middle), (ANY, act)] + [(ANY, r) for r in (*second, *down)],
        [
            (VMEM, (N, EMB), BF16),
            (VMEM, (N, EMB), F32),
            (VMEM, (N, DI), F32),
            (VMEM, (N, 128), F32),
            (VMEM, (N, 48), BF16),
            (VMEM, (N, 192), BF16),
        ],
        [
            pltpu.VMEM((ITEMS, 192, DI), BF16),
            pltpu.VMEM((ITEMS, 32, DI), BF16),
            pltpu.VMEM((N, DI), BF16),
            pltpu.VMEM((N, DI), F32),
            pltpu.VMEM((N, 4 * DI), BF16),
            pltpu.SemaphoreType.DMA((7,)),
        ],
        flops=6_000_000_000,
        touched=8_000_000,
    )


def one_direction(left, right, mult):
    sims = dot(left, right, 1, 1)
    logits = mult * sims
    top = jnp.max(logits, axis=-1, keepdims=True)
    total = top + jnp.log(jnp.sum(jnp.exp(logits - top), axis=-1, keepdims=True))
    count = sims.shape[0]
    eye = lax.broadcasted_iota(jnp.int32, (count, count), 0) == lax.broadcasted_iota(
        jnp.int32, (count, count), 1
    )
    hot = eye.astype(F32)
    lost = jnp.sum(total - jnp.sum(hot * logits, axis=-1, keepdims=True), axis=0, keepdims=True)
    grad = (jnp.exp(logits - total) - hot) * 0.5
    scale = jnp.sum(jnp.sum(grad * sims, axis=-1, keepdims=True), axis=0, keepdims=True)
    return lost, scale, mult * grad


def chain_kernel(lengths, log_mult, e_own_ref, e_oth_ref, vec, q_own, head_sl, act_sl, n2_sl, mix_sl, *rest):
    (proj_hbm, normf_hbm, invf_hbm, norm2_hbm, inv2_hbm, slope_hbm, keys_hbm, values_hbm, norm_hbm), rest = (
        rest[:9], rest[9:]
    )
    second, down = rest[:9], rest[9:18]
    outs, scratch = rest[18:38], rest[38:]
    (loss_out, scale_out, d_emb_hbm, d_down_hbm, d_fc_hbm, d_out_hbm, g_final, b_final, b_down, g_two, b_two, b_out, b_fc,
     mid_own, gm_out, gm_own, payload, gk_out, gv_out, gq_out) = outs
    (w_out, w_fc, w_down, w_emb, gpre, mid_all, proj_v, normf_v, invf_v, norm2_v, inv2_v, slope, keys,
     values, norm_low, vec_grads, fcb_grads, d_emb, d_down, d_fc, d_out, sems, ins, ends) = scratch
    here = Place(lengths)
    owners = owner_table(here.dp)
    early = [
        copy(src, dst, ins.at[i])
        for i, (src, dst) in enumerate(
            ((proj_hbm, proj_v), (normf_hbm, normf_v), (invf_hbm, invf_v))
        )
    ]
    fetch(owners, second, 48, 32, w_emb, sems.at[0])
    fetch(owners, down, 0, 192, w_down, sems.at[1])
    slope_in = copy(slope_hbm, slope, ins.at[3])
    fetch(owners, second, 80, 192, w_fc, sems.at[2])
    later = [copy(norm2_hbm, norm2_v, ins.at[4]), copy(inv2_hbm, inv2_v, ins.at[5])]
    fetch(owners, second, 0, 48, w_out, sems.at[3])
    last = [
        copy(src, dst, ins.at[6 + i])
        for i, (src, dst) in enumerate(((keys_hbm, keys), (values_hbm, values), (norm_hbm, norm_low)))
    ]
    keep, winv = here.keep, here.winv
    text = here.text.astype(F32)
    mult = jnp.exp(jnp.full((1, 128), log_mult[0], F32))[:, 0:1]
    own, oth = e_own_ref[...].astype(F32), e_oth_ref[...].astype(F32)
    e_img = (own * (1.0 - text) + oth * text).astype(BF16)
    e_txt = (oth * (1.0 - text) + own * text).astype(BF16)
    lost_img, scale_img, grad_img = one_direction(e_img, e_txt, mult)
    lost_txt, scale_txt, grad_txt = one_direction(e_txt, e_img, mult)
    loss_out[...] = (lost_img + lost_txt) / (2.0 * N)
    scale_out[...] = mult * (scale_img + scale_txt)
    grad_own = (grad_img * (1.0 - text) + grad_txt * text).astype(BF16)
    grad_oth = (grad_txt * (1.0 - text) + grad_img * text).astype(BF16)
    oth_low = e_oth_ref[...]
    grad_e = dot(grad_own, oth_low) + dot(grad_oth, oth_low, 0, 0)
    for item in early:
        item.wait()
    proj = proj_v[...]
    r = lax.rsqrt(jnp.sum(proj * proj, axis=-1, keepdims=True) + NORM_EPS)
    cross = jnp.sum(grad_e * proj, axis=-1, keepdims=True)
    grad_proj = (r * grad_e - proj * (r * r * r) * cross).astype(BF16)
    drain(w_emb, sems.at[0])
    grad_head = dot(grad_proj, embed_matrix(w_emb[...]), 1, 1)
    normf = normf_v[...]
    grad_y = normalize_back(grad_head, vec[8:9, :], normf, invf_v[:, 0:1], keep, winv)
    branch = grad_y.astype(BF16)
    d_emb[...] = dot(head_sl[...], grad_proj, 0, 0)
    stored = [copy(d_emb, d_emb_hbm, ends.at[0])]
    vec_grads[0:1, :] = row_sum(grad_head * normf)
    vec_grads[1:2, :] = row_sum(grad_head)
    vec_grads[2:3, :] = row_sum(branch.astype(F32))
    d_down[...] = dot(act_sl[...], branch, 0, 0)
    stored.append(copy(d_down, d_down_hbm, ends.at[1]))
    drain(w_down, sems.at[1])
    slope_in.wait()
    for block in range(4):
        lanes = pl.ds(block * DI, DI)
        back = dot(branch, w_down[block * 4 : block * 4 + 4].reshape(DI, DI), 1, 1)
        low = (back * slope[:, lanes]).astype(BF16)
        gpre[:, lanes] = low
        fcb_grads[:, lanes] = jnp.broadcast_to(row_sum(low.astype(F32)), (8, DI))

    drain(w_fc, sems.at[2])
    grad_n2 = jnp.zeros((N, DI), F32)
    for block in range(4):
        weight = w_fc[:, block * 48 : block * 48 + 48, :].reshape(DI, DI)
        grad_n2 = grad_n2 + dot(gpre[:, block * DI : block * DI + DI], weight, 1, 1)
    for item in later:
        item.wait()
    norm2 = norm2_v[...]
    vec_grads[3:4, :] = row_sum(grad_n2 * norm2)
    vec_grads[4:5, :] = row_sum(grad_n2)
    grad_mid = grad_y + normalize_back(grad_n2, vec[5:6, :], norm2, inv2_v[:, 0:1], keep, winv)
    mid_all[...] = grad_mid
    own_rows = pl.ds(aligned(here.dp * 8, 8), 8)
    mid_own[...] = mid_all[own_rows, :]
    attn = grad_mid.astype(BF16)
    vec_grads[5:6, :] = row_sum(attn.astype(F32))
    drain(w_out, sems.at[3])
    gm_out[...] = dot(attn, w_out[...].reshape(DI, DI), 1, 1).astype(BF16).astype(F32)
    gm_own[...] = gm_out[own_rows, :]

    @pl.loop(0, 6)
    def _(j):
        lanes = pl.ds(aligned(j * 512, 512), 512)
        d_fc[:, lanes] = dot(n2_sl[...], gpre[:, lanes], 0, 0)

    d_out[...] = dot(mix_sl[...], attn, 0, 0)
    stored += [copy(d_fc, d_fc_hbm, ends.at[2]), copy(d_out, d_out_hbm, ends.at[3])]

    def mine(owner):
        lanes = slice(owner * 48, owner * 48 + 48)
        for at, dst in enumerate((g_final, b_final, b_down, g_two, b_two, b_out)):
            dst[...] = vec_grads[at : at + 1, lanes]
        b_fc[...] = fcb_grads[0:1, owner * 192 : owner * 192 + 192]

    here.mine(mine)
    for item in last:
        item.wait()
    q_rows = head_rows(q_own[...])
    m_rows = head_rows(gm_own[...])
    lane_sample = lax.broadcasted_iota(jnp.int32, (1, 128), 1) % 8
    limit = jnp.zeros((1, 128), jnp.int32)
    for s in range(8):
        limit = jnp.where(lane_sample == s, here.length(s), limit)

    def path(width, count):
        rows = count * 8
        raw = dot(keys[0:rows, 0:width], q_rows[:, 0:width], 1, 1) * SCALE
        row = lax.broadcasted_iota(jnp.int32, (rows, 128), 0)
        lane = lax.broadcasted_iota(jnp.int32, (rows, 128), 1)
        valid = (lane % 8 == row % 8) & (row // 8 < limit) & (lane < width // 8)
        raw = jnp.where(valid, raw, NEG_FILL)
        top = jnp.max(raw, axis=0, keepdims=True)
        terms = jnp.where(valid, jnp.exp(raw - top), 0.0)
        probs = terms / jnp.maximum(row_sum(terms), 1e-30)
        grad_probs = dot(values[0:rows, 0:width], m_rows[:, 0:width], 1, 1)
        crossed = row_sum(probs * grad_probs)
        gk = (probs * (grad_probs - crossed)).astype(BF16)
        gv = probs.astype(BF16)
        gk_out[0:rows, :] = gk
        gv_out[0:rows, :] = gv
        back = dot(gk, keys[0:rows, 0:width], 0, 0) * SCALE
        heads = lax.broadcasted_iota(jnp.int32, (8, width), 1) // HD
        grad_q = jnp.zeros((8, width), F32)
        for head in range(width // HD):
            grad_q = grad_q + jnp.where(heads == head, back[head * 8 : head * 8 + 8], 0.0)
        if width < DI:
            grad_q = jnp.concatenate([grad_q, jnp.zeros((8, DI - width), F32)], axis=1)
        gq_low = grad_q.astype(BF16)
        gq_out[...] = gq_low
        norm = norm_low[0:rows, :]
        z_key = dot(norm, gk, 0, 0).astype(BF16)
        z_value = dot(norm, gv, 0, 0).astype(BF16)
        sum_key = row_sum(gk.astype(F32))
        sum_value = row_sum(gv.astype(F32))
        key_high = sum_key.astype(BF16).astype(F32)
        value_high = sum_value.astype(BF16).astype(F32)
        row_id = lax.broadcasted_iota(jnp.int32, (16, 128), 0)
        sums = jnp.zeros((16, 128), F32)
        for at, value in enumerate((key_high, sum_key - key_high, value_high, sum_value - value_high)):
            sums = jnp.where(row_id == at, jnp.broadcast_to(value, (16, 128)), sums)
        sums = sums.astype(BF16)
        gq_wide = gq_low.astype(F32)
        gq_tall = jnp.concatenate(
            [gq_wide[:, i * 128 : (i + 1) * 128] for i in range(DI // 128)], axis=0
        ).astype(BF16)
        for owner in range(ITEMS):
            base = owner * PAYLOAD
            payload[base : base + 48, :] = z_key[owner * 48 : owner * 48 + 48]
            payload[base + 48 : base + 64, :] = sums
            payload[base + 64 : base + 112, :] = z_value[owner * 48 : owner * 48 + 48]
            payload[base + 112 : base + 160, :] = gq_tall

    here.either(path, 56)
    for item in stored:
        item.wait()


def chain(lengths, log_mult, e_own, e_oth, vec, q_own, slices, saved, second, down):
    rows = saved[-1].shape[0]
    return call(
        chain_kernel,
        "chain",
        [(SMEM, lengths), (SMEM, log_mult)]
        + [(VMEM, item) for item in (e_own, e_oth, vec, q_own, *slices)]
        + [(ANY, r) for r in (*saved, *second, *down)],
        [
            (VMEM, (1, 1), F32),
            (VMEM, (1, 1), F32),
            (ANY, (48, EMB), F32),
            (ANY, (192, DI), F32),
            (ANY, (48, 4 * DI), F32),
            (ANY, (48, DI), F32),
        ]
        + [(VMEM, (1, 48), F32)] * 6
        + [
            (VMEM, (1, 192), F32),
            (VMEM, (8, DI), F32),
            (VMEM, (N, DI), F32),
            (VMEM, (8, DI), F32),
            (VMEM, (ITEMS * PAYLOAD, 128), BF16),
            (VMEM, (rows, 128), BF16),
            (VMEM, (rows, 128), BF16),
            (VMEM, (8, DI), BF16),
        ],
        [
            pltpu.VMEM((ITEMS, 48, DI), BF16),
            pltpu.VMEM((ITEMS, 192, DI), BF16),
            pltpu.VMEM((ITEMS, 192, DI), BF16),
            pltpu.VMEM((ITEMS, 32, DI), BF16),
            pltpu.VMEM((N, 4 * DI), BF16),
            pltpu.VMEM((N, DI), F32),
            pltpu.VMEM((N, EMB), F32),
            pltpu.VMEM((N, DI), F32),
            pltpu.VMEM((N, 128), F32),
            pltpu.VMEM((N, DI), F32),
            pltpu.VMEM((N, 128), F32),
            pltpu.VMEM((N, 4 * DI), F32),
            pltpu.VMEM((rows, DI), BF16),
            pltpu.VMEM((rows, DI), BF16),
            pltpu.VMEM((rows, DI), BF16),
            pltpu.VMEM((8, DI), F32),
            pltpu.VMEM((8, 4 * DI), F32),
            pltpu.VMEM((48, EMB), F32),
            pltpu.VMEM((192, DI), F32),
            pltpu.VMEM((48, 4 * DI), F32),
            pltpu.VMEM((48, DI), F32),
            pltpu.SemaphoreType.DMA((4,)),
            pltpu.SemaphoreType.DMA((9,)),
            pltpu.SemaphoreType.DMA((4,)),
        ],
        flops=15_000_000_000,
        touched=20_000_000,
    )


def close_kernel(lengths, tok, vec, gk, gv, q_own, gm_own, gq, mid_own, act_hbm, middle_hbm, *rest):
    first, down, (block_out, out), scratch = rest[:9], rest[9:18], rest[18:20], rest[20:]
    weights, w_down, act, middle, acc, sems = scratch
    here = Place(lengths)
    owners = owner_table(here.dp)
    fetch(owners, first, 0, 144, weights, sems.at[0])
    early = [copy(act_hbm, act, sems.at[1]), copy(middle_hbm, middle, sems.at[2])]
    fetch(owners, down, 0, 192, w_down, sems.at[3])
    keep, winv = here.keep, here.winv
    q_rows = head_rows(q_own[...])
    m_rows = head_rows(gm_own[...])
    pool = here.column(here.pool)
    length = here.column(here.length)
    all_rows = out.shape[0]
    drain(weights, sems.at[0])
    u_key = (dot(q_rows, weights[:, 48:96, :].reshape(DI, DI), 1, 1) * SCALE).astype(BF16)
    u_value = dot(m_rows, weights[:, 96:144, :].reshape(DI, DI), 1, 1).astype(BF16)
    u_query = dot(gq[...], weights[:, 0:48, :].reshape(DI, DI), 1, 1)

    def path(width, count):
        rows = count * 8
        acc[0:rows, :] = dot(gk[0:rows, :], u_key) + dot(gv[0:rows, :], u_value)

        def back_chunk(position, row, count):
            at = pl.ds(row, count * 8)
            hit = lax.broadcasted_iota(jnp.int32, (count, 8, DI), 0) + position == pool
            norm, inv = normalize(tok[pl.ds(position, count)].astype(F32).reshape(count * 8, DI), keep, winv)
            total = acc[at, :] + jnp.where(hit, u_query[None], 0.0).reshape(count * 8, DI)
            back = normalize_back(total, vec[0:1, :], norm, inv, keep, winv)
            out[at, :] = back + jnp.where(hit, mid_own[...][None], 0.0).reshape(count * 8, DI)

        chunks(count, back_chunk)
        if rows < all_rows:
            out[rows:all_rows, :] = jnp.zeros((all_rows - rows, DI), F32)
        for item in early:
            item.wait()
        drain(w_down, sems.at[3])
        short = count if width == DT else IMG_ROWS
        rows = short * 8

        @pl.loop(0, width // 256)
        def _(j):
            lanes = pl.ds(aligned(j * 256, 256), 256)
            weight = w_down[:, :, lanes].reshape(4 * DI, 256)[0 : 4 * width]
            total = dot(act[0:rows, 0 : 4 * width], weight)
            total = (total + vec[7:8, lanes] + middle[0:rows, lanes]).reshape(short, 8, 256)
            where = lax.broadcasted_iota(jnp.int32, (short, 8, 256), 0)
            block_out[0:rows, lanes] = jnp.where(where < length, total, 0.0).reshape(rows, 256).astype(BF16)

        if width < DI:
            block_out[:, width:DI] = jnp.zeros((all_rows, DI - width), BF16)
        if rows < all_rows:
            block_out[rows:all_rows, :] = jnp.zeros((all_rows - rows, DI), BF16)

    here.either(path, 56)


def close(lengths, tok, vec, gk, gv, q_own, gm_own, gq, mid_own, act, middle, first, down):
    rows = tok.shape[0] * tok.shape[1]
    return call(
        close_kernel,
        "close",
        [(SMEM, lengths)]
        + [(VMEM, item) for item in (tok, vec, gk, gv, q_own, gm_own, gq, mid_own)]
        + [(ANY, r) for r in (act, middle, *first, *down)],
        [(VMEM, (rows, DI), BF16), (VMEM, (rows, DI), F32)],
        [
            pltpu.VMEM((ITEMS, 144, DI), BF16),
            pltpu.VMEM((ITEMS, 192, DI), BF16),
            pltpu.VMEM((rows, 4 * DI), BF16),
            pltpu.VMEM((rows, DI), F32),
            pltpu.VMEM((rows, DI), F32),
            pltpu.SemaphoreType.DMA((4,)),
        ],
        flops=10_000_000_000,
        touched=18_000_000,
    )


def shard_kernel(got, q_all, gm_all, norm_sl, w_own, gain, bias, d_qkv, g_one, b_one, qv_out, big, left):
    dp = lax.axis_index("dp")

    def build(source):
        @pl.loop(0, ITEMS)
        def _(j):
            rows = source[pl.ds(aligned(j * 8, 8), 8), :]
            big[pl.ds(aligned(j * 128, 128), 128), :] = head_rows(rows)

    def spread(start):
        for j in range(ITEMS):
            left[:, j * 128 : (j + 1) * 128] = got[j, start : start + 64, :]

    def column(row):
        square = (48, 48)
        same = lax.broadcasted_iota(jnp.int32, square, 0) == lax.broadcasted_iota(jnp.int32, square, 1)
        return jnp.sum(jnp.where(same, row[...].astype(F32), 0.0), axis=1, keepdims=True)

    build(q_all)
    spread(0)
    by_key = dot(left[...], big[...]) * SCALE
    m_key, s_key = by_key[0:48], by_key[48:49] + by_key[49:50]
    build(gm_all)
    spread(48)
    by_value = dot(left[...], big[...])
    m_value, s_value = by_value[16:64], by_value[2:3] + by_value[3:4]
    tall = got[:, 112:160, :].astype(F32)
    grad_q = jnp.concatenate(
        [tall[:, i * 8 : i * 8 + 8, :].reshape(N, 128) for i in range(DI // 128)], axis=1
    )
    s_query = row_sum(grad_q)
    m_query = dot(norm_sl[...], grad_q.astype(BF16), 0, 0)
    gain_col, bias_col = column(gain), column(bias)
    by_gain = jnp.zeros((48, DI), F32)
    by_bias = jnp.zeros((48, DI), F32)
    for third, (moment, total) in enumerate(((m_query, s_query), (m_key, s_key), (m_value, s_value))):
        d_qkv[third] = gain_col * moment + bias_col * total
        weight = w_own[third].astype(F32)
        by_gain = by_gain + weight * moment
        by_bias = by_bias + weight * total
    ones = jnp.ones((8, DI), F32)
    line = (((1,), (1,)), ((), ()))
    for dst, item in ((g_one, by_gain), (b_one, by_bias)):
        dst[...] = lax.dot_general(
            ones, item, line, precision=lax.Precision.HIGHEST, preferred_element_type=F32
        )[0:1]
    for owner in range(ITEMS):

        @pl.when(dp == owner)
        def _(owner=owner):
            lanes = slice(owner * 48, owner * 48 + 48)
            qv_out[0:1, :] = s_query[:, lanes]
            qv_out[1:2, :] = s_value[:, lanes]


def shard_grads(got, q_all, gm_all, norm_sl, w_own, gain, bias):
    plain = (got, q_all, gm_all, norm_sl, w_own, gain, bias)
    return call(
        shard_kernel,
        "shard_grads",
        [(VMEM, item) for item in plain],
        [
            (VMEM, (3, 48, DI), F32),
            (VMEM, (1, 48), F32),
            (VMEM, (1, 48), F32),
            (VMEM, (2, 48), F32),
        ],
        [pltpu.VMEM((ITEMS * 128, DI), BF16), pltpu.VMEM((64, ITEMS * 128), BF16)],
        flops=5_000_000_000,
        touched=2_000_000,
    )


BOTH = ("tower", "dp")


def device(tower, place, core):
    return tower * 16 + (RING_Z[place] * 2 + RING_Y[place]) * 2 + core


def routes(towers):
    swap, turn = [], []
    for tower in range(towers):
        for place in range(8):
            for core, step in ((0, 1), (1, -1)):
                here = device(tower, place, core)
                swap.append((here, device(tower, place, 1 - core)))
                turn.append((here, device(tower, (place + step) % 8, core)))
    return swap, turn


def after(item, *earlier):
    return lax.optimization_barrier((item, *earlier))[0] if earlier else item


class Ring:
    def __init__(self, shard, swap, turn, first_core):
        other = lax.ppermute(shard, BOTH, swap)
        self.swap, self.turn, self.first_core = swap, turn, first_core
        held = jnp.stack([jnp.where(first_core, shard, other), jnp.where(first_core, other, shard)])
        self.items = [held]
        self.last = held
        self.hops = 0

    def step(self, *earlier, swap_after=()):
        held = self.last
        if self.hops == 3:
            held = jnp.where(self.first_core, held[0], held[1])
        held = lax.ppermute(after(held, *earlier), BOTH, self.turn)
        self.items += [held, lax.ppermute(after(held, *swap_after), BOTH, self.swap)]
        self.last = held
        self.hops += 1
        return held


def ring_body(
    tokens,
    lengths,
    ln1_gain,
    ln1_bias,
    qkv_weight,
    qv_bias,
    out_weight,
    out_bias,
    ln2_gain,
    ln2_bias,
    fc_weight,
    fc_bias,
    down_weight,
    down_bias,
    final_gain,
    final_bias,
    embed_weight,
    logit_scale,
):
    towers = lax.axis_size("tower")
    dp_index = lax.axis_index("dp")
    swap, turn = routes(towers)
    tok = tokens[0].transpose(1, 0, 2)
    w_own = qkv_weight[0].transpose(1, 0, 2)
    vectors = (ln1_gain, ln1_bias, out_bias, ln2_gain, ln2_bias, down_bias, final_gain, final_bias)
    first_own = pack_first(lengths, w_own.reshape(144, DI), tok, vectors, qv_bias[0], fc_bias)
    second_own = pack_rest(out_weight[0], fc_weight[0], embed_weight[0])
    first_core = dp_index % 2 == 0

    qkv_ring = Ring(first_own, swap, turn, first_core)
    wide_ring = Ring(second_own, swap, turn, first_core)
    down_ring = Ring(down_weight[0], swap, turn, first_core)
    q1 = qkv_ring.step()
    wide_ring.step(q1)
    qkv_ring.step()
    q3 = qkv_ring.step()
    qkv_ring.step()
    first = qkv_ring.items
    keys, values, norm_low, mixed, vec, pooled = attend(lengths, tok, first)
    w2 = wide_ring.step(q3, swap_after=(vec,))
    d1 = down_ring.step(q3, swap_after=(vec,))
    mixes = lax.all_to_all(after(pooled, w2, d1), "dp", 0, 0, tiled=True)
    w3 = wide_ring.step(vec)
    d2 = down_ring.step(vec)
    wide_ring.step()
    d3 = down_ring.step(w3, swap_after=(mixes,))
    second = wide_ring.items
    mixed = after(mixed, d3)
    act, middle, mid_p, norm2, inv2, slope, act_p, q_all, q_own, n2_sl, mix_sl, norm_sl = widen(
        lengths, tok, vec, mixed, first, second, mixes
    )
    down_ring.step(mixes, swap_after=(q_own,))
    down = down_ring.items
    e_own, proj, normf, invf, head_sl, act_sl = pooled_head(lengths, vec, mid_p, act_p, second, down)
    across = [(t * 16 + d, (1 - t) * 16 + d) for t in range(2) for d in range(16)]
    e_oth = lax.ppermute(e_own, BOTH, across)
    (loss, scale, d_emb, d_down, d_fc, d_out, g_final, b_final, b_down, g_two, b_two, b_out, b_fc,
     mid_own, gm_all, gm_own, payload, gk, gv, gq) = chain(
        lengths, logit_scale, e_own, e_oth, vec, q_own, (head_sl, act_sl, n2_sl, mix_sl),
        (proj, normf, invf, norm2, inv2, slope, keys, values, norm_low), second, down,
    )
    got = lax.all_to_all(payload, "dp", 0, 0, tiled=True).reshape(ITEMS, PAYLOAD, 128)
    block_out, tokens_grad = close(
        lengths, tok, vec, gk, gv, q_own, gm_own, gq, mid_own, act, middle, first, down
    )
    d_qkv, g_one, b_one, qv_sums = shard_grads(got, q_all, gm_all, norm_sl, w_own, ln1_gain, ln1_bias)
    seq = tok.shape[0]
    return (
        block_out.reshape(seq, 8, DI).transpose(1, 0, 2)[None],
        tokens_grad.reshape(seq, 8, DI).transpose(1, 0, 2)[None],
        loss.reshape(1),
        g_one,
        b_one,
        d_qkv.transpose(1, 0, 2)[None],
        qv_sums[None],
        d_out[None],
        b_out,
        g_two,
        b_two,
        d_fc[None],
        b_fc,
        d_down[None],
        b_down,
        g_final,
        b_final,
        d_emb[None],
        scale.reshape(1),
    )


def solution(mesh):
    fits = mesh.shape["dp"] == ITEMS and mesh.shape["tower"] == 2
    return jax.shard_map(
        ring_body if fits else body,
        mesh=mesh,
        in_specs=(
            P("tower", "dp", None, None),
            P("dp"),
            P("tower", "dp"),
            P("tower", "dp"),
            P("tower", "dp", None, None),
            P("tower", None, "dp"),
            P("tower", "dp", None),
            P("tower", "dp"),
            P("tower", "dp"),
            P("tower", "dp"),
            P("tower", "dp", None),
            P("tower", "dp"),
            P("tower", "dp", None),
            P("tower", "dp"),
            P("tower", "dp"),
            P("tower", "dp"),
            P("tower", "dp", None),
            P(),
        ),
        out_specs=(
            P("tower", "dp", None, None),
            P("tower", "dp", None, None),
            P(),
            P("tower", "dp"),
            P("tower", "dp"),
            P("tower", "dp", None, None),
            P("tower", None, "dp"),
            P("tower", "dp", None),
            P("tower", "dp"),
            P("tower", "dp"),
            P("tower", "dp"),
            P("tower", "dp", None),
            P("tower", "dp"),
            P("tower", "dp", None),
            P("tower", "dp"),
            P("tower", "dp"),
            P("tower", "dp"),
            P("tower", "dp", None),
            P(),
        ),
        check_vma=False,
    )
```

```python
import jax
import jax.numpy as jnp
from jax import lax
from jax.experimental import pallas as pl
from jax.experimental.pallas import tpu as pltpu
from jax.sharding import PartitionSpec as P

DI = 768
DT = 512
HD = 64
IMG_ROWS = 50
EMB = 512


EPS = 1e-05
NORM_EPS = 1e-06
GELU_K = 1.702
NEG_FILL = -1e30


def swapped(block, axis, stride):
    count = lax.axis_size(axis)
    route = []
    for low in range(count):
        high = low | 1 << stride
        if high != low and high < count:
            route += [(low, high), (high, low)]
    return lax.ppermute(block, axis, route)


def masked_norm(values, norm_gain, norm_bias, col_keep, width_real):
    row_mean = jnp.sum(values * col_keep, axis=-1, keepdims=True) / width_real
    centred = (values - row_mean) * col_keep
    row_var = jnp.sum(centred * centred, axis=-1, keepdims=True) / width_real
    inv_std = lax.rsqrt(row_var + EPS)
    normed = centred * inv_std
    return (normed * norm_gain + norm_bias, normed, inv_std)


def masked_norm_back(grad_out, norm_gain, normed, inv_std, col_keep, width_real):
    grad_normed = grad_out * norm_gain
    mean_grad = jnp.sum(grad_normed, axis=-1, keepdims=True) / width_real
    mean_cross = jnp.sum(grad_normed * normed, axis=-1, keepdims=True) / width_real
    grad_in = col_keep * inv_std * (grad_normed - mean_grad - normed * mean_cross)
    return (grad_in, jnp.sum(grad_out * normed, axis=0), jnp.sum(grad_out, axis=0))


def contract_rows(left_op, right_op):
    return lax.dot_general(
        left_op, right_op, (((0,), (0,)), ((), ())), preferred_element_type=jnp.float32
    )


def contract_cols(left_op, right_op):
    return lax.dot_general(
        left_op, right_op, (((1,), (1,)), ((), ())), preferred_element_type=jnp.float32
    )


def column_sum(values):
    return jnp.sum(values, axis=0, dtype=jnp.float32)


def body(
    tokens,
    lengths,
    ln1_gain,
    ln1_bias,
    qkv_weight,
    qv_bias,
    out_weight,
    out_bias,
    ln2_gain,
    ln2_bias,
    fc_weight,
    fc_bias,
    down_weight,
    down_bias,
    final_gain,
    final_bias,
    embed_weight,
    logit_scale,
):
    f32 = jnp.float32
    bf16 = jnp.bfloat16
    tower_index = lax.axis_index("tower")
    dp_index = lax.axis_index("dp")
    dp_count = lax.axis_size("dp")
    samples, seq_rows, width_all = (tokens.shape[1], tokens.shape[2], tokens.shape[3])
    head_count = width_all // HD
    sample_total = samples * dp_count
    flat_rows = samples * seq_rows
    is_text = tower_index == 1
    width_int = jnp.where(is_text, DT, DI)
    width_real = width_int.astype(f32)
    col_keep = (lax.broadcasted_iota(jnp.int32, (width_all,), 0) < width_int).astype(f32)
    seq_lens = jnp.where(is_text, lengths, IMG_ROWS)
    positions = lax.broadcasted_iota(jnp.int32, (samples, seq_rows), 1)
    row_keep = (positions < seq_lens[:, None]).astype(f32).reshape(flat_rows, 1)
    query_pos = lax.broadcasted_iota(jnp.int32, (seq_rows, seq_rows), 0)
    key_pos = lax.broadcasted_iota(jnp.int32, (seq_rows, seq_rows), 1)
    allowed = (key_pos[None] < seq_lens[:, None, None]) & (
        jnp.logical_not(is_text) | (key_pos <= query_pos)
    )[None]
    pool_pos = jnp.where(is_text, lengths - 1, 0)
    pool_hot = (positions == pool_pos[:, None]).astype(f32)
    score_mult = float(HD) ** (-0.5)
    gathered = (
        lax.all_gather(ln1_gain[0], "dp", axis=0, tiled=True),
        lax.all_gather(ln1_bias[0], "dp", axis=0, tiled=True),
        lax.all_gather(qkv_weight[0], "dp", axis=0, tiled=True),
        lax.all_gather(qv_bias[0], "dp", axis=1, tiled=True),
        lax.all_gather(out_weight[0], "dp", axis=0, tiled=True),
        lax.all_gather(out_bias[0], "dp", axis=0, tiled=True),
        lax.all_gather(ln2_gain[0], "dp", axis=0, tiled=True),
        lax.all_gather(ln2_bias[0], "dp", axis=0, tiled=True),
        lax.all_gather(fc_weight[0], "dp", axis=0, tiled=True),
        lax.all_gather(fc_bias[0], "dp", axis=0, tiled=True),
        lax.all_gather(down_weight[0], "dp", axis=0, tiled=True),
        lax.all_gather(down_bias[0], "dp", axis=0, tiled=True),
        lax.all_gather(final_gain[0], "dp", axis=0, tiled=True),
        lax.all_gather(final_bias[0], "dp", axis=0, tiled=True),
        lax.all_gather(embed_weight[0], "dp", axis=0, tiled=True),
    )
    (
        gain_one,
        bias_one,
        w_qkv,
        b_qv,
        w_out,
        b_out,
        gain_two,
        bias_two,
        w_fc,
        b_fc,
        w_down,
        b_down,
        gain_final,
        bias_final,
        w_embed,
    ) = gathered
    stream = tokens[0].astype(f32).reshape(flat_rows, width_all)
    normed_h1, norm_one, inv_one = masked_norm(
        stream, gain_one.astype(f32), bias_one.astype(f32), col_keep, width_real
    )
    normed_one = normed_h1.astype(bf16)
    qkv_bias = jnp.concatenate(
        [b_qv[0].astype(f32), jnp.zeros((width_all,), f32), b_qv[1].astype(f32)]
    )
    qkv_flat = (
        jnp.dot(normed_one, w_qkv.reshape(width_all, 3 * width_all), preferred_element_type=f32)
        + qkv_bias
    )
    qkv_low = qkv_flat.astype(bf16).reshape(samples, seq_rows, 3, head_count, HD)
    query_all = qkv_low[:, :, 0]
    key_all = qkv_low[:, :, 1]
    value_all = qkv_low[:, :, 2]

    def masked_scores():
        raw = (
            jnp.einsum("sqhd,skhd->shqk", query_all, key_all, preferred_element_type=f32)
            * score_mult
        )
        return jnp.where(allowed[:, None], raw, NEG_FILL)

    scores = masked_scores()
    row_top = jnp.max(scores, axis=-1, keepdims=True)
    exp_terms = jnp.exp(scores - row_top)
    exp_sum = jnp.sum(exp_terms, axis=-1, keepdims=True)
    log_total = row_top + jnp.log(exp_sum)
    attn_probs = (exp_terms / exp_sum).astype(bf16)
    head_mix = jnp.einsum("shqk,skhd->sqhd", attn_probs, value_all, preferred_element_type=f32)
    head_mix_low = head_mix.astype(bf16).reshape(flat_rows, width_all)
    attn_out = jnp.dot(head_mix_low, w_out, preferred_element_type=f32) + b_out.astype(f32)
    middle = stream + attn_out
    normed_h2, norm_two, inv_two = masked_norm(
        middle, gain_two.astype(f32), bias_two.astype(f32), col_keep, width_real
    )
    normed_two = normed_h2.astype(bf16)
    hidden_pre = jnp.dot(normed_two, w_fc, preferred_element_type=f32) + b_fc.astype(f32)
    gate_sig = jax.nn.sigmoid(GELU_K * hidden_pre)
    act_low = (hidden_pre * gate_sig).astype(bf16)
    branch = jnp.dot(act_low, w_down, preferred_element_type=f32) + b_down.astype(f32)
    block_rows = row_keep * (middle + branch)
    block_out = block_rows.astype(bf16).reshape(1, samples, seq_rows, width_all)
    block_three = block_rows.reshape(samples, seq_rows, width_all)
    pooled = jnp.take_along_axis(block_three, pool_pos[:, None, None], axis=1)[:, 0]
    normed_hf, norm_final, inv_final = masked_norm(
        pooled, gain_final.astype(f32), bias_final.astype(f32), col_keep, width_real
    )
    head_low = normed_hf.astype(bf16)
    projected = jnp.dot(head_low, w_embed, preferred_element_type=f32)
    inv_norm = lax.rsqrt(jnp.sum(projected * projected, axis=-1, keepdims=True) + NORM_EPS)
    embed_low = (projected * inv_norm).astype(bf16)
    own_all = lax.all_gather(embed_low, "dp", axis=0, tiled=True)
    others = swapped(own_all, "tower", 0)
    logit_mult = jnp.exp(logit_scale[0])
    similar = contract_cols(embed_low, others)
    logits = logit_mult * similar
    logit_top = jnp.max(logits, axis=-1, keepdims=True)
    logit_total = logit_top + jnp.log(jnp.sum(jnp.exp(logits - logit_top), axis=-1, keepdims=True))
    label_col = dp_index * samples + lax.broadcasted_iota(jnp.int32, (samples, 1), 0)
    label_hot = (lax.broadcasted_iota(jnp.int32, (samples, sample_total), 1) == label_col).astype(
        f32
    )
    diag_logit = jnp.sum(label_hot * logits, axis=-1, keepdims=True)
    loss_part = jnp.sum(logit_total - diag_logit) / (2.0 * sample_total)
    grad_logits = (jnp.exp(logits - logit_total) - label_hot) * 0.5
    scale_part = logit_mult * jnp.sum(grad_logits * similar)
    grad_sims = (logit_mult * grad_logits).astype(bf16)
    grad_own = jnp.dot(grad_sims, others, preferred_element_type=f32)
    grad_others = contract_rows(grad_sims, embed_low)
    sent_back = swapped(grad_others, "tower", 0)
    returned = lax.psum_scatter(sent_back, "dp", scatter_dimension=0, tiled=True)
    totals = lax.psum((loss_part, scale_part), ("tower", "dp"))
    grad_embed = grad_own + returned
    again = (
        lax.all_gather(ln1_gain[0], "dp", axis=0, tiled=True),
        lax.all_gather(qkv_weight[0], "dp", axis=0, tiled=True),
        lax.all_gather(out_weight[0], "dp", axis=0, tiled=True),
        lax.all_gather(ln2_gain[0], "dp", axis=0, tiled=True),
        lax.all_gather(fc_weight[0], "dp", axis=0, tiled=True),
        lax.all_gather(down_weight[0], "dp", axis=0, tiled=True),
        lax.all_gather(final_gain[0], "dp", axis=0, tiled=True),
        lax.all_gather(embed_weight[0], "dp", axis=0, tiled=True),
    )
    (
        back_gain_one,
        back_qkv,
        back_out,
        back_gain_two,
        back_fc,
        back_down,
        back_gain_final,
        back_embed,
    ) = again
    cross_term = jnp.sum(grad_embed * projected, axis=-1, keepdims=True)
    grad_proj = inv_norm * grad_embed - projected * inv_norm * inv_norm * inv_norm * cross_term
    grad_proj_low = grad_proj.astype(bf16)
    grad_head = contract_cols(grad_proj_low, back_embed)
    grad_pooled, d_gain_final, d_bias_final = masked_norm_back(
        grad_head, back_gain_final.astype(f32), norm_final, inv_final, col_keep, width_real
    )
    grad_rows = (pool_hot[:, :, None] * grad_pooled[:, None, :]).reshape(flat_rows, width_all)
    grad_branch_low = grad_rows.astype(bf16)
    d_down_b = column_sum(grad_branch_low)
    grad_act = contract_cols(grad_branch_low, back_down)
    grad_pre_low = (
        grad_act * (gate_sig + GELU_K * hidden_pre * gate_sig * (1.0 - gate_sig))
    ).astype(bf16)
    d_fc_b = column_sum(grad_pre_low)
    grad_norm_two = contract_cols(grad_pre_low, back_fc)
    grad_mid_norm, d_gain_two, d_bias_two = masked_norm_back(
        grad_norm_two, back_gain_two.astype(f32), norm_two, inv_two, col_keep, width_real
    )
    grad_middle = grad_rows + grad_mid_norm
    grad_attn_low = grad_middle.astype(bf16)
    d_out_b = column_sum(grad_attn_low)
    grad_mix_low = (
        contract_cols(grad_attn_low, back_out)
        .astype(bf16)
        .reshape(samples, seq_rows, head_count, HD)
    )
    probs_again = jnp.exp(masked_scores() - log_total)
    probs_low = probs_again.astype(bf16)
    grad_value = jnp.einsum("shqk,sqhd->skhd", probs_low, grad_mix_low, preferred_element_type=f32)
    grad_probs = jnp.einsum("sqhd,skhd->shqk", grad_mix_low, value_all, preferred_element_type=f32)
    grad_scores = probs_again * (
        grad_probs - jnp.sum(probs_again * grad_probs, axis=-1, keepdims=True)
    )
    grad_scores_low = grad_scores.astype(bf16)
    grad_query = (
        jnp.einsum("shqk,skhd->sqhd", grad_scores_low, key_all, preferred_element_type=f32)
        * score_mult
    )
    grad_key = (
        jnp.einsum("shqk,sqhd->skhd", grad_scores_low, query_all, preferred_element_type=f32)
        * score_mult
    )
    grad_qkv_low = (
        jnp.stack([grad_query, grad_key, grad_value], axis=2)
        .astype(bf16)
        .reshape(flat_rows, 3 * width_all)
    )
    d_qkv_w = contract_rows(normed_one, grad_qkv_low).reshape(width_all, 3, width_all)
    qkv_sums = column_sum(grad_qkv_low).reshape(3, width_all)
    d_qv_b = jnp.stack([qkv_sums[0], qkv_sums[2]])
    grad_norm_one = contract_cols(grad_qkv_low, back_qkv.reshape(width_all, 3 * width_all))
    grad_in_norm, d_gain_one, d_bias_one = masked_norm_back(
        grad_norm_one, back_gain_one.astype(f32), norm_one, inv_one, col_keep, width_real
    )
    tokens_grad = (grad_middle + grad_in_norm).reshape(1, samples, seq_rows, width_all)
    d_embed_w = contract_rows(head_low, grad_proj_low)
    d_down_w = contract_rows(act_low, grad_branch_low)
    d_fc_w = contract_rows(normed_two, grad_pre_low)
    d_out_w = contract_rows(head_mix_low, grad_attn_low)
    shares = (
        lax.psum_scatter(d_gain_one, "dp", scatter_dimension=0, tiled=True),
        lax.psum_scatter(d_bias_one, "dp", scatter_dimension=0, tiled=True),
        lax.psum_scatter(d_qkv_w, "dp", scatter_dimension=0, tiled=True),
        lax.psum_scatter(d_qv_b, "dp", scatter_dimension=1, tiled=True),
        lax.psum_scatter(d_out_w, "dp", scatter_dimension=0, tiled=True),
        lax.psum_scatter(d_out_b, "dp", scatter_dimension=0, tiled=True),
        lax.psum_scatter(d_gain_two, "dp", scatter_dimension=0, tiled=True),
        lax.psum_scatter(d_bias_two, "dp", scatter_dimension=0, tiled=True),
        lax.psum_scatter(d_fc_w, "dp", scatter_dimension=0, tiled=True),
        lax.psum_scatter(d_fc_b, "dp", scatter_dimension=0, tiled=True),
        lax.psum_scatter(d_down_w, "dp", scatter_dimension=0, tiled=True),
        lax.psum_scatter(d_down_b, "dp", scatter_dimension=0, tiled=True),
        lax.psum_scatter(d_gain_final, "dp", scatter_dimension=0, tiled=True),
        lax.psum_scatter(d_bias_final, "dp", scatter_dimension=0, tiled=True),
        lax.psum_scatter(d_embed_w, "dp", scatter_dimension=0, tiled=True),
    )
    results = list(shares)
    outputs = [item[None] for item in results]
    loss = totals[0].reshape(1)
    logit_scale_grad = totals[1].reshape(1)
    return (
        block_out,
        tokens_grad,
        loss,
        outputs[0],
        outputs[1],
        outputs[2],
        outputs[3],
        outputs[4],
        outputs[5],
        outputs[6],
        outputs[7],
        outputs[8],
        outputs[9],
        outputs[10],
        outputs[11],
        outputs[12],
        outputs[13],
        outputs[14],
        logit_scale_grad,
    )


RING_Z = (0, 1, 2, 3, 3, 2, 1, 0)
RING_Y = (0, 0, 0, 0, 1, 1, 1, 1)
ITEMS = 16
N = ITEMS * 8
F32 = jnp.float32
BF16 = jnp.bfloat16
ANY = pl.BlockSpec(memory_space=pl.ANY)
VMEM = pl.BlockSpec(memory_space=pltpu.VMEM)
SMEM = pl.BlockSpec(memory_space=pltpu.SMEM)
SCALE = float(HD) ** -0.5
PAYLOAD = 160


def call(kernel, name, ins, outs, scratch, flops=0, touched=0):
    return pl.pallas_call(
        kernel,
        name=name,
        out_shape=[jax.ShapeDtypeStruct(shape, dtype) for _, shape, dtype in outs],
        in_specs=[spec for spec, _ in ins],
        out_specs=[spec for spec, _, _ in outs],
        scratch_shapes=scratch,
        compiler_params=pltpu.CompilerParams(vmem_limit_bytes=67043328),
        cost_estimate=pl.CostEstimate(flops=flops, bytes_accessed=touched, transcendentals=0),
    )(*[item for _, item in ins])


def dot(left, right, left_dim=1, right_dim=0):
    return lax.dot_general(
        left, right, (((left_dim,), (right_dim,)), ((), ())), preferred_element_type=F32
    )


def aligned(index, size):
    return pl.multiple_of(index, size)


def owner_table(dp_index):
    core = dp_index % 2
    row = dp_index // 2 % 2
    depth = dp_index // 4
    place = jnp.where(row == 0, depth, 7 - depth)

    def chip(where):
        where = (where + 8) % 8
        z = jnp.where(where < 4, where, 7 - where)
        y = jnp.where(where < 4, 0, 1)
        return (z * 2 + y) * 2

    sign = jnp.where(core == 0, -1, 1)
    found = [chip(place)]
    for hop in range(1, 4):
        found += [chip(place + sign * hop), chip(place - sign * hop)]
    return found + [chip(place + 4) + core, chip(place + 4) + 1 - core]


class Place:
    def __init__(self, lengths):
        self.dp = lax.axis_index("dp")
        self.text = lax.axis_index("tower") == 1
        self.lengths = lengths
        self.keep = (
            lax.broadcasted_iota(jnp.int32, (1, DI), 1) < jnp.where(self.text, DT, DI)
        ).astype(F32)
        self.winv = jnp.where(self.text, 1.0 / DT, 1.0 / DI).astype(F32)

    def length(self, s):
        return jnp.where(self.text, self.lengths[s], IMG_ROWS)

    def pool(self, s):
        return jnp.where(self.text, self.lengths[s] - 1, 0)

    def column(self, pick):
        ids = lax.broadcasted_iota(jnp.int32, (1, 8, 1), 1)
        column = jnp.zeros((1, 8, 1), jnp.int32)
        for s in range(8):
            column = jnp.where(ids == s, pick(s), column)
        return column

    def either(self, path, image):
        @pl.when(self.text)
        def _():
            path(DT, 77)

        @pl.when(jnp.logical_not(self.text))
        def _():
            path(DI, image)

    def mine(self, visit):
        for owner in range(ITEMS):

            @pl.when(self.dp == owner)
            def _(owner=owner):
                visit(owner)


def copy(src, dst, sem):
    found = pltpu.make_async_copy(src, dst, sem)
    found.start()
    return found


def drain(dst, sem):
    pltpu.make_async_copy(dst, dst, sem).wait()


def fetch(owners, refs, row, rows, dst, sem):
    for owner, ref in zip(owners, refs):
        if len(ref.shape) == 3:
            copy(ref.at[:, pl.ds(row, rows), :], dst.at[pl.ds(owner, 2)], sem)
        else:
            copy(ref.at[pl.ds(row, rows), :], dst.at[owner], sem)


def embed_matrix(packed):
    tail = jnp.concatenate([packed[:, 0:16, EMB:DI], packed[:, 16:32, EMB:DI]], axis=2)
    return jnp.concatenate([packed[:, :, 0:EMB], tail], axis=1).reshape(DI, EMB)


def normalize(values, keep, winv):
    mean = jnp.sum(values, axis=-1, keepdims=True) * winv
    centred = (values - mean) * keep
    var = jnp.sum(centred * centred, axis=-1, keepdims=True) * winv
    inv = lax.rsqrt(var + EPS)
    return centred * inv, inv


def normalize_back(grad_out, gain, normed, inv, keep, winv):
    grad_normed = grad_out * gain
    mean_grad = jnp.sum(grad_normed, axis=-1, keepdims=True) * winv
    mean_cross = jnp.sum(grad_normed * normed, axis=-1, keepdims=True) * winv
    return keep * inv * (grad_normed - mean_grad - normed * mean_cross)


def row_sum(values):
    return jnp.sum(values, axis=0, keepdims=True)


def head_rows(rows):
    heads = lax.broadcasted_iota(jnp.int32, rows.shape, 1) // HD
    parts = [jnp.where(heads == head, rows, 0.0) for head in range(16)]
    return jnp.concatenate(parts, axis=0).astype(BF16)


def chunks(count, visit):
    @pl.loop(0, count // 14)
    def _(i):
        visit(i * 14, aligned(i * 112, 16), 14)

    if count % 14:
        at = count - count % 14
        visit(at, at * 8, count % 14)


def pack_first_kernel(lengths, qkv, tok, *rest):
    here = Place(lengths)
    vectors, (qv_bias, fc_bias, out) = rest[:8], rest[8:]
    out[0:144, :] = qkv[...]
    sub = lax.broadcasted_iota(jnp.int32, (8, DI), 0)
    pooled = jnp.zeros((8, DI), F32)
    for s in range(8):
        pooled = jnp.where(sub == s, tok[here.pool(s)].astype(F32), pooled)
    out[144:160, :] = jnp.concatenate([pooled, jnp.zeros((8, DI), F32)], axis=0).astype(BF16)
    lane = lax.broadcasted_iota(jnp.int32, (1, DI), 1) // 48 == here.dp
    short = [v[...].astype(F32) for v in vectors]
    pair = qv_bias[...].astype(F32)
    short[2:2] = [pair[0:1], pair[1:2]]
    rows = [jnp.where(lane, jnp.concatenate([v] * ITEMS, axis=1), 0.0) for v in short]
    wide = lax.broadcasted_iota(jnp.int32, (1, 4 * DI), 1) // 192 == here.dp
    fc = jnp.where(wide, jnp.concatenate([fc_bias[...].astype(F32)] * ITEMS, axis=1), 0.0)
    rows += [fc[:, i * DI : (i + 1) * DI] for i in range(4)]
    row_id = lax.broadcasted_iota(jnp.int32, (16, DI), 0)
    small = jnp.zeros((16, DI), F32)
    for at, row in enumerate(rows):
        small = jnp.where(row_id == at, jnp.broadcast_to(row, (16, DI)), small)
    out[160:176, :] = small.astype(BF16)


def pack_first(lengths, qkv, tok, vectors, qv_bias, fc_bias):
    return call(
        pack_first_kernel,
        "pack_first",
        [(SMEM, lengths)] + [(VMEM, item) for item in (qkv, tok, *vectors, qv_bias, fc_bias)],
        [(VMEM, (176, DI), BF16)],
        [],
        touched=1_500_000,
    )[0]


def pack_rest_kernel(w_out, w_fc, w_emb, out):
    out[0:48, :] = w_out[...]
    out[48:80, 0:EMB] = w_emb[0:32, :]
    out[48:64, EMB:DI] = w_emb[32:48, 0:256]
    out[64:80, EMB:DI] = w_emb[32:48, 256:EMB]
    for block in range(4):
        out[80 + 48 * block : 128 + 48 * block, :] = w_fc[:, block * DI : (block + 1) * DI]


def pack_rest(w_out, w_fc, w_emb):
    return call(
        pack_rest_kernel,
        "pack_rest",
        [(VMEM, item) for item in (w_out, w_fc, w_emb)],
        [(VMEM, (272, DI), BF16)],
        [],
        touched=1_500_000,
    )[0]


def sample_limits(here):
    lane_sample = lax.broadcasted_iota(jnp.int32, (1, 128), 1) % 8
    limit = jnp.zeros((1, 128), jnp.int32)
    for s in range(8):
        limit = jnp.where(lane_sample == s, here.length(s), limit)
    return limit


def own_heads(tall, width):
    heads = lax.broadcasted_iota(jnp.int32, (8, width), 1) // HD
    total = jnp.zeros((8, width), F32)
    for head in range(width // HD):
        total = total + jnp.where(heads == head, tall[head * 8 : head * 8 + 8], 0.0)
    if width < DI:
        total = jnp.concatenate([total, jnp.zeros((8, DI - width), F32)], axis=1)
    return total


def tall_rows(rows):
    return jnp.concatenate([rows[:, i * 128 : (i + 1) * 128] for i in range(DI // 128)], axis=0)


def wide_rows(tall):
    tall = tall.astype(F32)
    return jnp.concatenate(
        [tall[:, i * 8 : i * 8 + 8, :].reshape(N, 128) for i in range(DI // 128)], axis=1
    )


def pooled_kernel(lengths, tok, *rest):
    first, outs, scratch = rest[:9], rest[9:18], rest[18:]
    keys_hbm, values_hbm, norm_hbm, normed_hbm, vec, pooled, q_own, probs_out, gv_out = outs
    weights, small, normed, keys, values, norm_low, sems, ends = scratch
    here = Place(lengths)
    owners = owner_table(here.dp)
    fetch(owners, first, 160, 16, small, sems.at[0])
    fetch(owners, first, 0, 144, weights, sems.at[1])
    keep, winv = here.keep, here.winv
    drain(small, sems.at[0])
    vec[...] = jnp.sum(small[...].astype(F32), axis=0)
    limit = sample_limits(here)
    sub = lax.broadcasted_iota(jnp.int32, (8, DI), 0)
    picked = jnp.zeros((8, DI), F32)
    for s in range(8):
        picked = jnp.where(sub == s, tok[here.pool(s)].astype(F32), picked)
    pooled_norm, _ = normalize(picked, keep, winv)
    pooled_normed = (pooled_norm * vec[0:1, :] + vec[1:2, :]).astype(BF16)

    def norm_chunk(position, row, count):
        x = tok[pl.ds(position, count)].astype(F32).reshape(count * 8, DI)
        norm, _ = normalize(x, keep, winv)
        norm_low[pl.ds(row, count * 8), :] = norm.astype(BF16)
        normed[pl.ds(row, count * 8), :] = (norm * vec[0:1, :] + vec[1:2, :]).astype(BF16)

    def path(width, count):
        rows = count * 8
        chunks(count, norm_chunk)
        saved = [copy(norm_low, norm_hbm, ends.at[0]), copy(normed, normed_hbm, ends.at[1])]
        drain(weights, sems.at[1])
        for third, low, bias in ((1, keys, None), (2, values, 3)):

            @pl.loop(0, width // 256)
            def _(j, third=third, low=low, bias=bias):
                lanes = pl.ds(aligned(j * 256, 256), 256)
                weight = weights[:, third * 48 : third * 48 + 48, lanes].reshape(DI, 256)
                prod = dot(normed[0:rows, 0:width], weight[0:width])
                if bias is not None:
                    prod = prod + vec[bias : bias + 1, lanes]
                low[0:rows, lanes] = prod.astype(BF16)

        saved += [copy(keys, keys_hbm, ends.at[2]), copy(values, values_hbm, ends.at[3])]
        query = dot(pooled_normed, weights[:, 0:48, :].reshape(DI, DI)) + vec[2:3, :]
        query = query.astype(BF16).astype(F32)
        q_own[...] = query
        q_rows = head_rows(query)
        raw = dot(keys[0:rows, 0:width], q_rows[:, 0:width], 1, 1) * SCALE
        row = lax.broadcasted_iota(jnp.int32, (rows, 128), 0)
        lane = lax.broadcasted_iota(jnp.int32, (rows, 128), 1)
        valid = (lane % 8 == row % 8) & (row // 8 < limit) & (lane < width // 8)
        raw = jnp.where(valid, raw, NEG_FILL)
        terms = jnp.where(valid, jnp.exp(raw - jnp.max(raw, axis=0, keepdims=True)), 0.0)
        probs = terms / jnp.maximum(row_sum(terms), 1e-30)
        low_probs = probs.astype(BF16)
        probs_out[0:rows, :] = probs
        gv_out[0:rows, :] = low_probs
        mixed = own_heads(dot(low_probs, values[0:rows, 0:width], 0, 0), width)
        tall = tall_rows(mixed).astype(BF16)
        for owner in range(ITEMS):
            pooled[owner] = tall
        for item in saved:
            item.wait()

    here.either(path, 56)


def attend_pooled(lengths, tok, first):
    rows = tok.shape[0] * tok.shape[1]
    return call(
        pooled_kernel,
        "attend_pooled",
        [(SMEM, lengths), (VMEM, tok)] + [(ANY, r) for r in first],
        [(ANY, (rows, DI), BF16)] * 4
        + [
            (VMEM, (16, DI), F32),
            (VMEM, (ITEMS, 48, 128), BF16),
            (VMEM, (8, DI), F32),
            (VMEM, (rows, 128), F32),
            (VMEM, (rows, 128), BF16),
        ],
        [
            pltpu.VMEM((ITEMS, 144, DI), BF16),
            pltpu.VMEM((ITEMS, 16, DI), BF16),
            pltpu.VMEM((rows, DI), BF16),
            pltpu.VMEM((rows, DI), BF16),
            pltpu.VMEM((rows, DI), BF16),
            pltpu.VMEM((rows, DI), BF16),
            pltpu.SemaphoreType.DMA((2,)),
            pltpu.SemaphoreType.DMA((4,)),
        ],
        flops=7_000_000_000,
        touched=10_000_000,
    )


def attend_kernel(lengths, vec, gv, normed_hbm, keys_hbm, values_hbm, norm_hbm, *rest):
    first, (mixed, z_value), scratch = rest[:9], rest[9:11], rest[11:]
    weights, normed, keys, values, norm_low, qf, kf, vf, mf, sems = scratch
    here = Place(lengths)
    owners = owner_table(here.dp)
    fetch(owners, first, 0, 48, weights, sems.at[0])
    early = [
        copy(src, dst, sems.at[1 + i])
        for i, (src, dst) in enumerate(
            ((normed_hbm, normed), (keys_hbm, keys), (values_hbm, values), (norm_hbm, norm_low))
        )
    ]
    drain(weights, sems.at[0])
    for item in early:
        item.wait()

    def path(width, count):
        rows = count * 8
        span = 80 if count == 77 else count
        if span > count:
            for dst in (qf, kf, vf):
                dst[:, rows : span * 8, :] = jnp.zeros((6, span * 8 - rows, 128), F32)

        @pl.loop(0, width // 256)
        def _(j):
            lanes = pl.ds(aligned(j * 256, 256), 256)
            weight = weights[:, :, lanes].reshape(DI, 256)
            prod = dot(normed[0:rows, 0:width], weight[0:width]) + vec[2:3, lanes]
            prod = prod.astype(BF16).astype(F32) * SCALE
            for dst, item in ((qf, prod), (kf, keys[0:rows, lanes].astype(F32)), (vf, values[0:rows, lanes].astype(F32))):
                dst[2 * j, 0:rows, :] = item[:, 0:128]
                dst[2 * j + 1, 0:rows, :] = item[:, 128:256]

        key_pos = lax.broadcasted_iota(jnp.int32, (span, 2 * span), 0)
        query_pos = lax.broadcasted_iota(jnp.int32, (span, 2 * span), 1) % span
        low_half = lax.broadcasted_iota(jnp.int32, (span, 128), 1) < HD

        @pl.loop(0, 8)
        def _(s):
            at = pl.ds(s, span, stride=8)
            allowed = key_pos < here.length(s)
            if width == DT:
                allowed = allowed & (key_pos <= query_pos)
            pairs = range(width // 128)
            raws = []
            for pair in pairs:
                query, key = qf.at[pair][at, :], kf.at[pair][at, :].astype(BF16)
                spread = [jnp.where(low_half, query, 0.0), jnp.where(low_half, 0.0, query)]
                spread = jnp.concatenate(spread, axis=0).astype(BF16)
                raws.append(dot(key, spread, 1, 1))
            probs = []
            for raw in raws:
                raw = jnp.where(allowed, raw, NEG_FILL)
                terms = jnp.exp(raw - jnp.max(raw, axis=0, keepdims=True))
                probs.append((terms / jnp.sum(terms, axis=0, keepdims=True)).astype(BF16))
            for pair in pairs:
                out = dot(probs[pair], vf.at[pair][at, :].astype(BF16), 0, 0)
                mf.at[pair][at, :] = jnp.where(low_half, out[0:span], out[span : 2 * span])

        for i in range(width // 128):
            mixed[0:rows, 128 * i : 128 * i + 128] = mf[i, 0:rows, :].astype(BF16)
        z_value[...] = dot(norm_low[0:rows, :], gv[0:rows, :], 0, 0).astype(BF16)

    here.either(path, 56)


def attend(lengths, vec, gv, normed, keys, values, norm_low, first):
    rows = keys.shape[0]
    high = rows + 24
    return call(
        attend_kernel,
        "attend",
        [(SMEM, lengths), (VMEM, vec), (VMEM, gv)]
        + [(ANY, r) for r in (normed, keys, values, norm_low, *first)],
        [(VMEM, (rows, DI), BF16), (VMEM, (DI, 128), BF16)],
        [
            pltpu.VMEM((ITEMS, 48, DI), BF16),
            pltpu.VMEM((rows, DI), BF16),
            pltpu.VMEM((rows, DI), BF16),
            pltpu.VMEM((rows, DI), BF16),
            pltpu.VMEM((rows, DI), BF16),
            pltpu.VMEM((6, high, 128), F32),
            pltpu.VMEM((6, high, 128), F32),
            pltpu.VMEM((6, high, 128), F32),
            pltpu.VMEM((6, high, 128), F32),
            pltpu.SemaphoreType.DMA((5,)),
        ],
        flops=9_000_000_000,
        touched=10_000_000,
    )


def forward_kernel(lengths, vec, mixes, *rest):
    first, second, down = rest[:9], rest[9:18], rest[18:27]
    outs, scratch = rest[27:38], rest[38:]
    (e_out, proj_out, normf_out, invf_out, norm2_out, inv2_out, slope_out, n2_sl, mix_sl, head_sl,
     act_sl) = outs
    w_out, w_fc, w_down, w_emb, xs, mix, n2, act, head_all, sems = scratch
    here = Place(lengths)
    owners = owner_table(here.dp)
    fetch(owners, second, 0, 48, w_out, sems.at[1])
    fetch(owners, first, 144, 16, xs, sems.at[0])
    fetch(owners, second, 80, 192, w_fc, sems.at[2])
    keep, winv = here.keep, here.winv
    mix[...] = wide_rows(mixes[...]).astype(BF16)
    drain(w_out, sems.at[1])
    drain(xs, sems.at[0])
    fetch(owners, down, 0, 192, w_down, sems.at[3])
    fetch(owners, second, 48, 32, w_emb, sems.at[4])
    stream = xs[...].astype(F32)[:, :8, :].reshape(N, DI)
    middle = stream + dot(mix[...], w_out[...].reshape(DI, DI)) + vec[4:5, :]
    norm2, inv2 = normalize(middle, keep, winv)
    n2[...] = (norm2 * vec[5:6, :] + vec[6:7, :]).astype(BF16)
    norm2_out[...] = norm2
    inv2_out[...] = jnp.broadcast_to(inv2, (N, 128))
    drain(w_fc, sems.at[2])
    for block in range(4):
        lanes = pl.ds(block * DI, DI)
        weight = w_fc[:, block * 48 : block * 48 + 48, :].reshape(DI, DI)
        pre = dot(n2[...], weight) + vec[10 + block : 11 + block, :]
        gate = jax.nn.sigmoid(GELU_K * pre)
        act[:, lanes] = (pre * gate).astype(BF16)
        slope_out[:, lanes] = gate + GELU_K * pre * gate * (1.0 - gate)

    drain(w_down, sems.at[3])
    last = middle + dot(act[...], w_down[...].reshape(4 * DI, DI)) + vec[7:8, :]
    normf, invf = normalize(last, keep, winv)
    normf_out[...] = normf
    invf_out[...] = jnp.broadcast_to(invf, (N, 128))
    head_all[...] = (normf * vec[8:9, :] + vec[9:10, :]).astype(BF16)
    drain(w_emb, sems.at[4])
    proj = dot(head_all[...], embed_matrix(w_emb[...]))
    proj_out[...] = proj
    scale = lax.rsqrt(jnp.sum(proj * proj, axis=-1, keepdims=True) + NORM_EPS)
    e_out[...] = (proj * scale).astype(BF16)

    def mine(owner):
        lanes = slice(owner * 48, owner * 48 + 48)
        n2_sl[...] = n2[:, lanes]
        mix_sl[...] = mix[:, lanes]
        head_sl[...] = head_all[:, lanes]
        act_sl[...] = act[:, owner * 192 : owner * 192 + 192]

    here.mine(mine)


def pooled_forward(lengths, vec, mixes, first, second, down):
    return call(
        forward_kernel,
        "pooled_forward",
        [(SMEM, lengths), (VMEM, vec), (VMEM, mixes)] + [(ANY, r) for r in (*first, *second, *down)],
        [
            (VMEM, (N, EMB), BF16),
            (VMEM, (N, EMB), F32),
            (VMEM, (N, DI), F32),
            (VMEM, (N, 128), F32),
            (VMEM, (N, DI), F32),
            (VMEM, (N, 128), F32),
            (VMEM, (N, 4 * DI), F32),
            (VMEM, (N, 48), BF16),
            (VMEM, (N, 48), BF16),
            (VMEM, (N, 48), BF16),
            (VMEM, (N, 192), BF16),
        ],
        [
            pltpu.VMEM((ITEMS, 48, DI), BF16),
            pltpu.VMEM((ITEMS, 192, DI), BF16),
            pltpu.VMEM((ITEMS, 192, DI), BF16),
            pltpu.VMEM((ITEMS, 32, DI), BF16),
            pltpu.VMEM((ITEMS, 16, DI), BF16),
            pltpu.VMEM((N, DI), BF16),
            pltpu.VMEM((N, DI), BF16),
            pltpu.VMEM((N, 4 * DI), BF16),
            pltpu.VMEM((N, DI), BF16),
            pltpu.SemaphoreType.DMA((5,)),
        ],
        flops=11_000_000_000,
        touched=16_000_000,
    )


def middle_kernel(lengths, tok_hbm, vec, mixed_hbm, *rest):
    second = rest[:9]
    (n2_hbm, middle_hbm), scratch = rest[9:11], rest[11:]
    w_out, middle, tok, mixed, n2, sems = scratch
    here = Place(lengths)
    owners = owner_table(here.dp)
    rows_in = copy(mixed_hbm, mixed, sems.at[1])
    fetch(owners, second, 0, 48, w_out, sems.at[0])
    tok_in = copy(tok_hbm, tok, sems.at[2])
    keep, winv = here.keep, here.winv
    rows_in.wait()
    drain(w_out, sems.at[0])

    def norm_chunk(position, row, count):
        at = pl.ds(row, count * 8)
        total = middle[at, :] + tok[pl.ds(position, count)].astype(F32).reshape(count * 8, DI)
        middle[at, :] = total
        norm, _ = normalize(total, keep, winv)
        n2[at, :] = (norm * vec[5:6, :] + vec[6:7, :]).astype(BF16)
        copy(middle.at[at, :], middle_hbm.at[at, :], sems.at[3])
        copy(n2.at[at, :], n2_hbm.at[at, :], sems.at[4])

    def path(width, count):
        rows = count * 8

        @pl.loop(0, width // 256)
        def _(j):
            lanes = pl.ds(aligned(j * 256, 256), 256)
            weight = w_out[:, :, lanes].reshape(DI, 256)[0:width]
            middle[0:rows, lanes] = dot(mixed[0:rows, 0:width], weight) + vec[4:5, lanes]

        if width < DI:
            middle[0:rows, width:DI] = jnp.zeros((rows, DI - width), F32)
        tok_in.wait()
        chunks(count, norm_chunk)
        drain(middle.at[pl.ds(0, rows), :], sems.at[3])
        drain(n2.at[pl.ds(0, rows), :], sems.at[4])

    here.either(path, 56)


def middle_part(lengths, tok, vec, mixed, second):
    rows = mixed.shape[0]
    return call(
        middle_kernel,
        "middle_part",
        [(SMEM, lengths), (ANY, tok), (VMEM, vec), (ANY, mixed)] + [(ANY, r) for r in second],
        [(ANY, (rows, DI), BF16), (ANY, (rows, DI), F32)],
        [
            pltpu.VMEM((ITEMS, 48, DI), BF16),
            pltpu.VMEM((rows, DI), F32),
            pltpu.VMEM(tok.shape, BF16),
            pltpu.VMEM((rows, DI), BF16),
            pltpu.VMEM((rows, DI), BF16),
            pltpu.SemaphoreType.DMA((5,)),
        ],
        flops=5_000_000_000,
        touched=8_000_000,
    )


def one_direction(left, right, mult):
    sims = dot(left, right, 1, 1)
    logits = mult * sims
    top = jnp.max(logits, axis=-1, keepdims=True)
    total = top + jnp.log(jnp.sum(jnp.exp(logits - top), axis=-1, keepdims=True))
    count = sims.shape[0]
    eye = lax.broadcasted_iota(jnp.int32, (count, count), 0) == lax.broadcasted_iota(
        jnp.int32, (count, count), 1
    )
    hot = eye.astype(F32)
    lost = jnp.sum(total - jnp.sum(hot * logits, axis=-1, keepdims=True), axis=0, keepdims=True)
    grad = (jnp.exp(logits - total) - hot) * 0.5
    scale = jnp.sum(jnp.sum(grad * sims, axis=-1, keepdims=True), axis=0, keepdims=True)
    return lost, scale, mult * grad


def chain_kernel(lengths, log_mult, e_own_ref, e_oth_ref, vec, head_sl, act_sl, n2_sl, mix_sl, *rest):
    (proj_hbm, normf_hbm, invf_hbm, norm2_hbm, inv2_hbm, slope_hbm, keys_hbm, values_hbm, norm_hbm, probs_hbm,
     gv_hbm, z_hbm), rest = rest[:12], rest[12:]
    second, down = rest[:9], rest[9:18]
    outs, scratch = rest[18:37], rest[37:]
    (loss_out, scale_out, d_emb_hbm, d_down_hbm, d_fc_hbm, d_out_hbm, g_final, b_final, b_down, g_two, b_two, b_out, b_fc,
     mid_own, gm_out, gm_own, payload, gk_out, gq_out) = outs
    (w_out, w_fc, w_down, w_emb, gpre, mid_all, proj_v, normf_v, invf_v, norm2_v, inv2_v, slope, keys,
     values, norm_low, probs_v, gv_v, z_v, vec_grads, fcb_grads, d_emb, d_down, d_fc, d_out, sems, ins, ends) = scratch
    here = Place(lengths)
    owners = owner_table(here.dp)
    early = [
        copy(src, dst, ins.at[i])
        for i, (src, dst) in enumerate(
            ((proj_hbm, proj_v), (normf_hbm, normf_v), (invf_hbm, invf_v))
        )
    ]
    fetch(owners, second, 48, 32, w_emb, sems.at[0])
    fetch(owners, down, 0, 192, w_down, sems.at[1])
    slope_in = copy(slope_hbm, slope, ins.at[3])
    fetch(owners, second, 80, 192, w_fc, sems.at[2])
    later = [copy(norm2_hbm, norm2_v, ins.at[4]), copy(inv2_hbm, inv2_v, ins.at[5])]
    fetch(owners, second, 0, 48, w_out, sems.at[3])
    last = [
        copy(src, dst, ins.at[6 + i])
        for i, (src, dst) in enumerate(
            ((keys_hbm, keys), (values_hbm, values), (norm_hbm, norm_low), (probs_hbm, probs_v),
             (gv_hbm, gv_v), (z_hbm, z_v))
        )
    ]
    keep, winv = here.keep, here.winv
    text = here.text.astype(F32)
    mult = jnp.exp(jnp.full((1, 128), log_mult[0], F32))[:, 0:1]
    own, oth = e_own_ref[...].astype(F32), e_oth_ref[...].astype(F32)
    e_img = (own * (1.0 - text) + oth * text).astype(BF16)
    e_txt = (oth * (1.0 - text) + own * text).astype(BF16)
    lost_img, scale_img, grad_img = one_direction(e_img, e_txt, mult)
    lost_txt, scale_txt, grad_txt = one_direction(e_txt, e_img, mult)
    loss_out[...] = (lost_img + lost_txt) / (2.0 * N)
    scale_out[...] = mult * (scale_img + scale_txt)
    grad_own = (grad_img * (1.0 - text) + grad_txt * text).astype(BF16)
    grad_oth = (grad_txt * (1.0 - text) + grad_img * text).astype(BF16)
    oth_low = e_oth_ref[...]
    grad_e = dot(grad_own, oth_low) + dot(grad_oth, oth_low, 0, 0)
    for item in early:
        item.wait()
    drain(w_emb, sems.at[0])
    proj = proj_v[...]
    r = lax.rsqrt(jnp.sum(proj * proj, axis=-1, keepdims=True) + NORM_EPS)
    cross = jnp.sum(grad_e * proj, axis=-1, keepdims=True)
    grad_proj = (r * grad_e - proj * (r * r * r) * cross).astype(BF16)
    grad_head = dot(grad_proj, embed_matrix(w_emb[...]), 1, 1)
    normf = normf_v[...]
    grad_y = normalize_back(grad_head, vec[8:9, :], normf, invf_v[:, 0:1], keep, winv)
    branch = grad_y.astype(BF16)
    d_emb[...] = dot(head_sl[...], grad_proj, 0, 0)
    stored = [copy(d_emb, d_emb_hbm, ends.at[0])]
    vec_grads[0:1, :] = row_sum(grad_head * normf)
    vec_grads[1:2, :] = row_sum(grad_head)
    vec_grads[2:3, :] = row_sum(branch.astype(F32))
    d_down[...] = dot(act_sl[...], branch, 0, 0)
    stored.append(copy(d_down, d_down_hbm, ends.at[1]))
    drain(w_down, sems.at[1])
    slope_in.wait()
    for block in range(4):
        lanes = pl.ds(block * DI, DI)
        back = dot(branch, w_down[block * 4 : block * 4 + 4].reshape(DI, DI), 1, 1)
        low = (back * slope[:, lanes]).astype(BF16)
        gpre[:, lanes] = low
        fcb_grads[:, lanes] = jnp.broadcast_to(row_sum(low.astype(F32)), (8, DI))

    drain(w_fc, sems.at[2])
    grad_n2 = jnp.zeros((N, DI), F32)
    for block in range(4):
        weight = w_fc[:, block * 48 : block * 48 + 48, :].reshape(DI, DI)
        grad_n2 = grad_n2 + dot(gpre[:, block * DI : block * DI + DI], weight, 1, 1)
    for item in later:
        item.wait()
    norm2 = norm2_v[...]
    vec_grads[3:4, :] = row_sum(grad_n2 * norm2)
    vec_grads[4:5, :] = row_sum(grad_n2)
    grad_mid = grad_y + normalize_back(grad_n2, vec[5:6, :], norm2, inv2_v[:, 0:1], keep, winv)
    mid_all[...] = grad_mid
    own_rows = pl.ds(aligned(here.dp * 8, 8), 8)
    mid_own[...] = mid_all[own_rows, :]
    attn = grad_mid.astype(BF16)
    vec_grads[5:6, :] = row_sum(attn.astype(F32))
    drain(w_out, sems.at[3])
    gm_out[...] = dot(attn, w_out[...].reshape(DI, DI), 1, 1).astype(BF16).astype(F32)
    gm_own[...] = gm_out[own_rows, :]

    @pl.loop(0, 6)
    def _(j):
        lanes = pl.ds(aligned(j * 512, 512), 512)
        d_fc[:, lanes] = dot(n2_sl[...], gpre[:, lanes], 0, 0)

    d_out[...] = dot(mix_sl[...], attn, 0, 0)
    stored += [copy(d_fc, d_fc_hbm, ends.at[2]), copy(d_out, d_out_hbm, ends.at[3])]

    def mine(owner):
        lanes = slice(owner * 48, owner * 48 + 48)
        for at, dst in enumerate((g_final, b_final, b_down, g_two, b_two, b_out)):
            dst[...] = vec_grads[at : at + 1, lanes]
        b_fc[...] = fcb_grads[0:1, owner * 192 : owner * 192 + 192]

    here.mine(mine)
    for item in last:
        item.wait()
    m_rows = head_rows(gm_own[...])

    def path(width, count):
        rows = count * 8
        probs = probs_v[0:rows, :]
        grad_probs = dot(values[0:rows, 0:width], m_rows[:, 0:width], 1, 1)
        gk = (probs * (grad_probs - row_sum(probs * grad_probs))).astype(BF16)
        gv = gv_v[0:rows, :]
        gk_out[0:rows, :] = gk
        gq_low = own_heads(dot(gk, keys[0:rows, 0:width], 0, 0) * SCALE, width).astype(BF16)
        gq_out[...] = gq_low
        norm = norm_low[0:rows, :]
        z_key = dot(norm, gk, 0, 0).astype(BF16)
        z_value = z_v[...]
        sum_key = row_sum(gk.astype(F32))
        sum_value = row_sum(gv.astype(F32))
        key_high = sum_key.astype(BF16).astype(F32)
        value_high = sum_value.astype(BF16).astype(F32)
        row_id = lax.broadcasted_iota(jnp.int32, (16, 128), 0)
        sums = jnp.zeros((16, 128), F32)
        for at, value in enumerate((key_high, sum_key - key_high, value_high, sum_value - value_high)):
            sums = jnp.where(row_id == at, jnp.broadcast_to(value, (16, 128)), sums)
        sums = sums.astype(BF16)
        gq_tall = tall_rows(gq_low.astype(F32)).astype(BF16)
        for owner in range(ITEMS):
            base = owner * PAYLOAD
            payload[base : base + 48, :] = z_key[owner * 48 : owner * 48 + 48]
            payload[base + 48 : base + 64, :] = sums
            payload[base + 64 : base + 112, :] = z_value[owner * 48 : owner * 48 + 48]
            payload[base + 112 : base + 160, :] = gq_tall

    here.either(path, 56)
    for item in stored:
        item.wait()


def chain(lengths, log_mult, e_own, e_oth, vec, slices, saved, second, down):
    rows = saved[-2].shape[0]
    return call(
        chain_kernel,
        "chain",
        [(SMEM, lengths), (SMEM, log_mult)]
        + [(VMEM, item) for item in (e_own, e_oth, vec, *slices)]
        + [(ANY, r) for r in (*saved, *second, *down)],
        [
            (VMEM, (1, 1), F32),
            (VMEM, (1, 1), F32),
            (ANY, (48, EMB), F32),
            (ANY, (192, DI), F32),
            (ANY, (48, 4 * DI), F32),
            (ANY, (48, DI), F32),
        ]
        + [(VMEM, (1, 48), F32)] * 6
        + [
            (VMEM, (1, 192), F32),
            (VMEM, (8, DI), F32),
            (VMEM, (N, DI), F32),
            (VMEM, (8, DI), F32),
            (VMEM, (ITEMS * PAYLOAD, 128), BF16),
            (VMEM, (rows, 128), BF16),
            (VMEM, (8, DI), BF16),
        ],
        [
            pltpu.VMEM((ITEMS, 48, DI), BF16),
            pltpu.VMEM((ITEMS, 192, DI), BF16),
            pltpu.VMEM((ITEMS, 192, DI), BF16),
            pltpu.VMEM((ITEMS, 32, DI), BF16),
            pltpu.VMEM((N, 4 * DI), BF16),
            pltpu.VMEM((N, DI), F32),
            pltpu.VMEM((N, EMB), F32),
            pltpu.VMEM((N, DI), F32),
            pltpu.VMEM((N, 128), F32),
            pltpu.VMEM((N, DI), F32),
            pltpu.VMEM((N, 128), F32),
            pltpu.VMEM((N, 4 * DI), F32),
            pltpu.VMEM((rows, DI), BF16),
            pltpu.VMEM((rows, DI), BF16),
            pltpu.VMEM((rows, DI), BF16),
            pltpu.VMEM((rows, 128), F32),
            pltpu.VMEM((rows, 128), BF16),
            pltpu.VMEM((DI, 128), BF16),
            pltpu.VMEM((8, DI), F32),
            pltpu.VMEM((8, 4 * DI), F32),
            pltpu.VMEM((48, EMB), F32),
            pltpu.VMEM((192, DI), F32),
            pltpu.VMEM((48, 4 * DI), F32),
            pltpu.VMEM((48, DI), F32),
            pltpu.SemaphoreType.DMA((4,)),
            pltpu.SemaphoreType.DMA((12,)),
            pltpu.SemaphoreType.DMA((4,)),
        ],
        flops=15_000_000_000,
        touched=20_000_000,
    )


def close_kernel(lengths, tok, vec, gk, gv, q_own, gm_own, gq, mid_own, n2_hbm, middle_hbm, *rest):
    first, second, down = rest[:9], rest[9:18], rest[18:27]
    (block_out, out, q_out, norm_sl), scratch = rest[27:31], rest[31:]
    weights, w_fc, w_down, n2, act, middle, acc, xs, norm1_all, sems = scratch
    here = Place(lengths)
    owners = owner_table(here.dp)
    fetch(owners, first, 0, 144, weights, sems.at[0])
    fetch(owners, first, 144, 16, xs, sems.at[5])
    ready = copy(n2_hbm, n2, sems.at[1])
    fetch(owners, second, 80, 192, w_fc, sems.at[4])
    fetch(owners, down, 0, 192, w_down, sems.at[3])
    early = [copy(middle_hbm, middle, sems.at[2])]
    keep, winv = here.keep, here.winv
    q_rows = head_rows(q_own[...])
    m_rows = head_rows(gm_own[...])
    pool = here.column(here.pool)
    length = here.column(here.length)
    all_rows = out.shape[0]
    drain(weights, sems.at[0])
    u_key = (dot(q_rows, weights[:, 48:96, :].reshape(DI, DI), 1, 1) * SCALE).astype(BF16)
    u_value = dot(m_rows, weights[:, 96:144, :].reshape(DI, DI), 1, 1).astype(BF16)
    u_query = dot(gq[...], weights[:, 0:48, :].reshape(DI, DI), 1, 1)

    def path(width, count):
        rows = count * 8
        acc[0:rows, :] = dot(gk[0:rows, :], u_key) + dot(gv[0:rows, :], u_value)

        def back_chunk(position, row, count):
            at = pl.ds(row, count * 8)
            hit = lax.broadcasted_iota(jnp.int32, (count, 8, DI), 0) + position == pool
            norm, inv = normalize(tok[pl.ds(position, count)].astype(F32).reshape(count * 8, DI), keep, winv)
            total = acc[at, :] + jnp.where(hit, u_query[None], 0.0).reshape(count * 8, DI)
            back = normalize_back(total, vec[0:1, :], norm, inv, keep, winv)
            out[at, :] = back + jnp.where(hit, mid_own[...][None], 0.0).reshape(count * 8, DI)

        chunks(count, back_chunk)
        if rows < all_rows:
            out[rows:all_rows, :] = jnp.zeros((all_rows - rows, DI), F32)
        short = count if width == DT else IMG_ROWS
        rows = short * 8
        ready.wait()
        drain(w_fc, sems.at[4])
        for block in range(4):

            @pl.loop(0, 3 if width == DI else (3, 3, 2, 0)[block])
            def _(j, block=block):
                lanes = pl.ds(aligned(j * 256, 256), 256)
                wide = pl.ds(aligned(block * DI + j * 256, 256), 256)
                weight = w_fc[:, block * 48 : block * 48 + 48, lanes].reshape(DI, 256)[0:width]
                pre = dot(n2[0:rows, 0:width], weight) + vec[10 + block : 11 + block, lanes]
                act[0:rows, wide] = (pre * jax.nn.sigmoid(GELU_K * pre)).astype(BF16)

        for item in early:
            item.wait()
        drain(w_down, sems.at[3])

        @pl.loop(0, width // 256)
        def _(j):
            lanes = pl.ds(aligned(j * 256, 256), 256)
            weight = w_down[:, :, lanes].reshape(4 * DI, 256)[0 : 4 * width]
            total = dot(act[0:rows, 0 : 4 * width], weight)
            total = (total + vec[7:8, lanes] + middle[0:rows, lanes]).reshape(short, 8, 256)
            where = lax.broadcasted_iota(jnp.int32, (short, 8, 256), 0)
            block_out[0:rows, lanes] = jnp.where(where < length, total, 0.0).reshape(rows, 256).astype(BF16)

        if width < DI:
            block_out[:, width:DI] = jnp.zeros((all_rows, DI - width), BF16)
        if rows < all_rows:
            block_out[rows:all_rows, :] = jnp.zeros((all_rows - rows, DI), BF16)

    here.either(path, 56)
    drain(xs, sems.at[5])
    stream = xs[...].astype(F32)[:, :8, :].reshape(N, DI)
    norm1, _ = normalize(stream, keep, winv)
    norm1_all[...] = norm1.astype(BF16)
    n1 = (norm1 * vec[0:1, :] + vec[1:2, :]).astype(BF16)
    q_out[...] = (dot(n1, weights[:, 0:48, :].reshape(DI, DI)) + vec[2:3, :]).astype(BF16).astype(F32)

    def mine(owner):
        norm_sl[...] = norm1_all[:, owner * 48 : owner * 48 + 48]

    here.mine(mine)


def close(lengths, tok, vec, gk, gv, q_own, gm_own, gq, mid_own, n2, middle, first, second, down):
    rows = tok.shape[0] * tok.shape[1]
    return call(
        close_kernel,
        "close",
        [(SMEM, lengths)]
        + [(VMEM, item) for item in (tok, vec, gk, gv, q_own, gm_own, gq, mid_own)]
        + [(ANY, r) for r in (n2, middle, *first, *second, *down)],
        [(VMEM, (rows, DI), BF16), (VMEM, (rows, DI), F32), (VMEM, (N, DI), F32), (VMEM, (N, 48), BF16)],
        [
            pltpu.VMEM((ITEMS, 144, DI), BF16),
            pltpu.VMEM((ITEMS, 192, DI), BF16),
            pltpu.VMEM((ITEMS, 192, DI), BF16),
            pltpu.VMEM((rows, DI), BF16),
            pltpu.VMEM((rows, 4 * DI), BF16),
            pltpu.VMEM((rows, DI), F32),
            pltpu.VMEM((rows, DI), F32),
            pltpu.VMEM((ITEMS, 16, DI), BF16),
            pltpu.VMEM((N, DI), BF16),
            pltpu.SemaphoreType.DMA((6,)),
        ],
        flops=17_000_000_000,
        touched=18_000_000,
    )


def shard_kernel(got, q_all, gm_all, norm_sl, w_own, gain, bias, d_qkv, g_one, b_one, qv_out, turned, product):
    dp = lax.axis_index("dp")

    low_half = lax.broadcasted_iota(jnp.int32, (N, 128), 1) < HD

    def moments(start, source):
        for j in range(ITEMS):
            turned[j] = got[j, start : start + 64, :].astype(F32).T
        for pair in range(DI // 128):
            lanes = slice(pair * 128, pair * 128 + 128)
            rows = source[:, lanes]
            both = [jnp.where(low_half, rows, 0.0), jnp.where(low_half, 0.0, rows)]
            both = [half.reshape(ITEMS, 8, 128) for half in both]
            both = jnp.concatenate(both, axis=1).reshape(2 * N, 128).astype(BF16)
            part = turned[:, pair * 16 : pair * 16 + 16, :].reshape(2 * N, 64).astype(BF16)
            product[:, lanes] = dot(part, both, 0, 0)
        return product[...]

    def column(row):
        square = (48, 48)
        same = lax.broadcasted_iota(jnp.int32, square, 0) == lax.broadcasted_iota(jnp.int32, square, 1)
        return jnp.sum(jnp.where(same, row[...].astype(F32), 0.0), axis=1, keepdims=True)

    by_key = moments(0, q_all) * SCALE
    m_key, s_key = by_key[0:48], by_key[48:49] + by_key[49:50]
    by_value = moments(48, gm_all)
    m_value, s_value = by_value[16:64], by_value[2:3] + by_value[3:4]
    grad_q = wide_rows(got[:, 112:160, :])
    s_query = row_sum(grad_q)
    m_query = dot(norm_sl[...], grad_q.astype(BF16), 0, 0)
    gain_col, bias_col = column(gain), column(bias)
    by_gain = jnp.zeros((48, DI), F32)
    by_bias = jnp.zeros((48, DI), F32)
    for third, (moment, total) in enumerate(((m_query, s_query), (m_key, s_key), (m_value, s_value))):
        d_qkv[third] = gain_col * moment + bias_col * total
        weight = w_own[third].astype(F32)
        by_gain = by_gain + weight * moment
        by_bias = by_bias + weight * total
    ones = jnp.ones((8, DI), F32)
    line = (((1,), (1,)), ((), ()))
    for dst, item in ((g_one, by_gain), (b_one, by_bias)):
        dst[...] = lax.dot_general(
            ones, item, line, precision=lax.Precision.HIGHEST, preferred_element_type=F32
        )[0:1]
    for owner in range(ITEMS):

        @pl.when(dp == owner)
        def _(owner=owner):
            lanes = slice(owner * 48, owner * 48 + 48)
            qv_out[0:1, :] = s_query[:, lanes]
            qv_out[1:2, :] = s_value[:, lanes]


def shard_grads(got, q_all, gm_all, norm_sl, w_own, gain, bias):
    plain = (got, q_all, gm_all, norm_sl, w_own, gain, bias)
    return call(
        shard_kernel,
        "shard_grads",
        [(VMEM, item) for item in plain],
        [
            (VMEM, (3, 48, DI), F32),
            (VMEM, (1, 48), F32),
            (VMEM, (1, 48), F32),
            (VMEM, (2, 48), F32),
        ],
        [pltpu.VMEM((ITEMS, 128, 64), F32), pltpu.VMEM((64, DI), F32)],
        flops=5_000_000_000,
        touched=2_000_000,
    )


BOTH = ("tower", "dp")


def device(tower, place, core):
    return tower * 16 + (RING_Z[place] * 2 + RING_Y[place]) * 2 + core


def routes(towers):
    swap, turn = [], []
    for tower in range(towers):
        for place in range(8):
            for core, step in ((0, 1), (1, -1)):
                here = device(tower, place, core)
                swap.append((here, device(tower, place, 1 - core)))
                turn.append((here, device(tower, (place + step) % 8, core)))
    return swap, turn


def after(item, *earlier):
    return lax.optimization_barrier((item, *earlier))[0] if earlier else item


class Ring:
    def __init__(self, shard, swap, turn, first_core):
        other = lax.ppermute(shard, BOTH, swap)
        self.swap, self.turn, self.first_core = swap, turn, first_core
        held = jnp.stack([jnp.where(first_core, shard, other), jnp.where(first_core, other, shard)])
        self.items = [held]
        self.last = held
        self.hops = 0

    def step(self, *earlier, swap_after=(), later=False):
        held = self.last
        if self.hops == 3:
            held = jnp.where(self.first_core, held[0], held[1])
        held = lax.ppermute(after(held, *earlier), BOTH, self.turn)
        self.items += [held, None if later else lax.ppermute(after(held, *swap_after), BOTH, self.swap)]
        self.last = held
        self.hops += 1
        return held

    def finish(self, *earlier):
        for i, item in enumerate(self.items):
            if item is None:
                self.items[i] = lax.ppermute(after(self.items[i - 1], *earlier), BOTH, self.swap)
        return self.items


def ring_body(
    tokens,
    lengths,
    ln1_gain,
    ln1_bias,
    qkv_weight,
    qv_bias,
    out_weight,
    out_bias,
    ln2_gain,
    ln2_bias,
    fc_weight,
    fc_bias,
    down_weight,
    down_bias,
    final_gain,
    final_bias,
    embed_weight,
    logit_scale,
):
    towers = lax.axis_size("tower")
    dp_index = lax.axis_index("dp")
    swap, turn = routes(towers)
    tok = tokens[0].transpose(1, 0, 2)
    w_own = qkv_weight[0].transpose(1, 0, 2)
    vectors = (ln1_gain, ln1_bias, out_bias, ln2_gain, ln2_bias, down_bias, final_gain, final_bias)
    first_own = pack_first(lengths, w_own.reshape(144, DI), tok, vectors, qv_bias[0], fc_bias)
    second_own = pack_rest(out_weight[0], fc_weight[0], embed_weight[0])
    first_core = dp_index % 2 == 0

    qkv_ring = Ring(first_own, swap, turn, first_core)
    wide_ring = Ring(second_own, swap, turn, first_core)
    down_ring = Ring(down_weight[0], swap, turn, first_core)
    qkv_ring.step()
    d1 = down_ring.step()
    qkv_ring.step()
    q3 = qkv_ring.step(d1)
    wide_ring.step()
    qkv_ring.step()
    first = qkv_ring.items
    keys, values, norm_low, normed, vec, pooled, q_own, probs, gv = attend_pooled(lengths, tok, first)
    w2 = wide_ring.step(q3, swap_after=(q_own,))
    d2 = down_ring.step(q3, swap_after=(q_own,))
    mixes = lax.all_to_all(pooled, "dp", 0, 0, tiled=True)
    w3 = wide_ring.step(q_own)
    mixed, z_value = attend(lengths, vec, gv, after(normed, w2), keys, values, norm_low, first)
    wide_ring.step(z_value)
    d3 = down_ring.step(z_value, mixes)
    second = wide_ring.items
    down_ring.step()
    down = down_ring.items
    e_own, proj, normf, invf, norm2, inv2, slope, n2_sl, mix_sl, head_sl, act_sl = pooled_forward(
        lengths, vec, mixes, first, second, down
    )
    across = [(t * 16 + d, (1 - t) * 16 + d) for t in range(2) for d in range(16)]
    e_oth = lax.ppermute(e_own, BOTH, across)
    n2, middle = middle_part(lengths, tok, vec, after(mixed, e_own), second)
    (loss, scale, d_emb, d_down, d_fc, d_out, g_final, b_final, b_down, g_two, b_two, b_out, b_fc,
     mid_own, gm_all, gm_own, payload, gk, gq) = chain(
        lengths, logit_scale, after(e_own, n2), e_oth, vec, (head_sl, act_sl, n2_sl, mix_sl),
        (proj, normf, invf, norm2, inv2, slope, keys, values, norm_low, probs, gv, z_value), second, down,
    )
    got = lax.all_to_all(payload, "dp", 0, 0, tiled=True).reshape(ITEMS, PAYLOAD, 128)
    block_out, tokens_grad, q_all, norm_sl = close(
        lengths, tok, vec, gk, gv, q_own, gm_own, gq, mid_own, n2, middle, first, second, down
    )
    d_qkv, g_one, b_one, qv_sums = shard_grads(got, q_all, gm_all, norm_sl, w_own, ln1_gain, ln1_bias)
    seq = tok.shape[0]
    return (
        block_out.reshape(seq, 8, DI).transpose(1, 0, 2)[None],
        tokens_grad.reshape(seq, 8, DI).transpose(1, 0, 2)[None],
        loss.reshape(1),
        g_one,
        b_one,
        d_qkv.transpose(1, 0, 2)[None],
        qv_sums[None],
        d_out[None],
        b_out,
        g_two,
        b_two,
        d_fc[None],
        b_fc,
        d_down[None],
        b_down,
        g_final,
        b_final,
        d_emb[None],
        scale.reshape(1),
    )


def solution(mesh):
    fits = mesh.shape["dp"] == ITEMS and mesh.shape["tower"] == 2
    return jax.shard_map(
        ring_body if fits else body,
        mesh=mesh,
        in_specs=(
            P("tower", "dp", None, None),
            P("dp"),
            P("tower", "dp"),
            P("tower", "dp"),
            P("tower", "dp", None, None),
            P("tower", None, "dp"),
            P("tower", "dp", None),
            P("tower", "dp"),
            P("tower", "dp"),
            P("tower", "dp"),
            P("tower", "dp", None),
            P("tower", "dp"),
            P("tower", "dp", None),
            P("tower", "dp"),
            P("tower", "dp"),
            P("tower", "dp"),
            P("tower", "dp", None),
            P(),
        ),
        out_specs=(
            P("tower", "dp", None, None),
            P("tower", "dp", None, None),
            P(),
            P("tower", "dp"),
            P("tower", "dp"),
            P("tower", "dp", None, None),
            P("tower", None, "dp"),
            P("tower", "dp", None),
            P("tower", "dp"),
            P("tower", "dp"),
            P("tower", "dp"),
            P("tower", "dp", None),
            P("tower", "dp"),
            P("tower", "dp", None),
            P("tower", "dp"),
            P("tower", "dp"),
            P("tower", "dp"),
            P("tower", "dp", None),
            P(),
        ),
        check_vma=False,
    )
```

```python
import functools

import jax
import jax.numpy as jnp
from jax import lax
from jax.experimental import pallas as pl
from jax.experimental.pallas import tpu as pltpu
from jax.sharding import PartitionSpec as P

DI = 768
DT = 512
HD = 64
IMG_ROWS = 50
EMB = 512


EPS = 1e-05
NORM_EPS = 1e-06
GELU_K = 1.702
NEG_FILL = -1e30


def swapped(block, axis, stride):
    count = lax.axis_size(axis)
    route = []
    for low in range(count):
        high = low | 1 << stride
        if high != low and high < count:
            route += [(low, high), (high, low)]
    return lax.ppermute(block, axis, route)


def masked_norm(values, norm_gain, norm_bias, col_keep, width_real):
    row_mean = jnp.sum(values * col_keep, axis=-1, keepdims=True) / width_real
    centred = (values - row_mean) * col_keep
    row_var = jnp.sum(centred * centred, axis=-1, keepdims=True) / width_real
    inv_std = lax.rsqrt(row_var + EPS)
    normed = centred * inv_std
    return (normed * norm_gain + norm_bias, normed, inv_std)


def masked_norm_back(grad_out, norm_gain, normed, inv_std, col_keep, width_real):
    grad_normed = grad_out * norm_gain
    mean_grad = jnp.sum(grad_normed, axis=-1, keepdims=True) / width_real
    mean_cross = jnp.sum(grad_normed * normed, axis=-1, keepdims=True) / width_real
    grad_in = col_keep * inv_std * (grad_normed - mean_grad - normed * mean_cross)
    return (grad_in, jnp.sum(grad_out * normed, axis=0), jnp.sum(grad_out, axis=0))


def contract_rows(left_op, right_op):
    return lax.dot_general(
        left_op, right_op, (((0,), (0,)), ((), ())), preferred_element_type=jnp.float32
    )


def contract_cols(left_op, right_op):
    return lax.dot_general(
        left_op, right_op, (((1,), (1,)), ((), ())), preferred_element_type=jnp.float32
    )


def column_sum(values):
    return jnp.sum(values, axis=0, dtype=jnp.float32)


def body(
    tokens,
    lengths,
    ln1_gain,
    ln1_bias,
    qkv_weight,
    qv_bias,
    out_weight,
    out_bias,
    ln2_gain,
    ln2_bias,
    fc_weight,
    fc_bias,
    down_weight,
    down_bias,
    final_gain,
    final_bias,
    embed_weight,
    logit_scale,
):
    f32 = jnp.float32
    bf16 = jnp.bfloat16
    tower_index = lax.axis_index("tower")
    dp_index = lax.axis_index("dp")
    dp_count = lax.axis_size("dp")
    samples, seq_rows, width_all = (tokens.shape[1], tokens.shape[2], tokens.shape[3])
    head_count = width_all // HD
    sample_total = samples * dp_count
    flat_rows = samples * seq_rows
    is_text = tower_index == 1
    width_int = jnp.where(is_text, DT, DI)
    width_real = width_int.astype(f32)
    col_keep = (lax.broadcasted_iota(jnp.int32, (width_all,), 0) < width_int).astype(f32)
    seq_lens = jnp.where(is_text, lengths, IMG_ROWS)
    positions = lax.broadcasted_iota(jnp.int32, (samples, seq_rows), 1)
    row_keep = (positions < seq_lens[:, None]).astype(f32).reshape(flat_rows, 1)
    query_pos = lax.broadcasted_iota(jnp.int32, (seq_rows, seq_rows), 0)
    key_pos = lax.broadcasted_iota(jnp.int32, (seq_rows, seq_rows), 1)
    allowed = (key_pos[None] < seq_lens[:, None, None]) & (
        jnp.logical_not(is_text) | (key_pos <= query_pos)
    )[None]
    pool_pos = jnp.where(is_text, lengths - 1, 0)
    pool_hot = (positions == pool_pos[:, None]).astype(f32)
    score_mult = float(HD) ** (-0.5)
    gathered = (
        lax.all_gather(ln1_gain[0], "dp", axis=0, tiled=True),
        lax.all_gather(ln1_bias[0], "dp", axis=0, tiled=True),
        lax.all_gather(qkv_weight[0], "dp", axis=0, tiled=True),
        lax.all_gather(qv_bias[0], "dp", axis=1, tiled=True),
        lax.all_gather(out_weight[0], "dp", axis=0, tiled=True),
        lax.all_gather(out_bias[0], "dp", axis=0, tiled=True),
        lax.all_gather(ln2_gain[0], "dp", axis=0, tiled=True),
        lax.all_gather(ln2_bias[0], "dp", axis=0, tiled=True),
        lax.all_gather(fc_weight[0], "dp", axis=0, tiled=True),
        lax.all_gather(fc_bias[0], "dp", axis=0, tiled=True),
        lax.all_gather(down_weight[0], "dp", axis=0, tiled=True),
        lax.all_gather(down_bias[0], "dp", axis=0, tiled=True),
        lax.all_gather(final_gain[0], "dp", axis=0, tiled=True),
        lax.all_gather(final_bias[0], "dp", axis=0, tiled=True),
        lax.all_gather(embed_weight[0], "dp", axis=0, tiled=True),
    )
    (
        gain_one,
        bias_one,
        w_qkv,
        b_qv,
        w_out,
        b_out,
        gain_two,
        bias_two,
        w_fc,
        b_fc,
        w_down,
        b_down,
        gain_final,
        bias_final,
        w_embed,
    ) = gathered
    stream = tokens[0].astype(f32).reshape(flat_rows, width_all)
    normed_h1, norm_one, inv_one = masked_norm(
        stream, gain_one.astype(f32), bias_one.astype(f32), col_keep, width_real
    )
    normed_one = normed_h1.astype(bf16)
    qkv_bias = jnp.concatenate(
        [b_qv[0].astype(f32), jnp.zeros((width_all,), f32), b_qv[1].astype(f32)]
    )
    qkv_flat = (
        jnp.dot(normed_one, w_qkv.reshape(width_all, 3 * width_all), preferred_element_type=f32)
        + qkv_bias
    )
    qkv_low = qkv_flat.astype(bf16).reshape(samples, seq_rows, 3, head_count, HD)
    query_all = qkv_low[:, :, 0]
    key_all = qkv_low[:, :, 1]
    value_all = qkv_low[:, :, 2]

    def masked_scores():
        raw = (
            jnp.einsum("sqhd,skhd->shqk", query_all, key_all, preferred_element_type=f32)
            * score_mult
        )
        return jnp.where(allowed[:, None], raw, NEG_FILL)

    scores = masked_scores()
    row_top = jnp.max(scores, axis=-1, keepdims=True)
    exp_terms = jnp.exp(scores - row_top)
    exp_sum = jnp.sum(exp_terms, axis=-1, keepdims=True)
    log_total = row_top + jnp.log(exp_sum)
    attn_probs = (exp_terms / exp_sum).astype(bf16)
    head_mix = jnp.einsum("shqk,skhd->sqhd", attn_probs, value_all, preferred_element_type=f32)
    head_mix_low = head_mix.astype(bf16).reshape(flat_rows, width_all)
    attn_out = jnp.dot(head_mix_low, w_out, preferred_element_type=f32) + b_out.astype(f32)
    middle = stream + attn_out
    normed_h2, norm_two, inv_two = masked_norm(
        middle, gain_two.astype(f32), bias_two.astype(f32), col_keep, width_real
    )
    normed_two = normed_h2.astype(bf16)
    hidden_pre = jnp.dot(normed_two, w_fc, preferred_element_type=f32) + b_fc.astype(f32)
    gate_sig = jax.nn.sigmoid(GELU_K * hidden_pre)
    act_low = (hidden_pre * gate_sig).astype(bf16)
    branch = jnp.dot(act_low, w_down, preferred_element_type=f32) + b_down.astype(f32)
    block_rows = row_keep * (middle + branch)
    block_out = block_rows.astype(bf16).reshape(1, samples, seq_rows, width_all)
    block_three = block_rows.reshape(samples, seq_rows, width_all)
    pooled = jnp.take_along_axis(block_three, pool_pos[:, None, None], axis=1)[:, 0]
    normed_hf, norm_final, inv_final = masked_norm(
        pooled, gain_final.astype(f32), bias_final.astype(f32), col_keep, width_real
    )
    head_low = normed_hf.astype(bf16)
    projected = jnp.dot(head_low, w_embed, preferred_element_type=f32)
    inv_norm = lax.rsqrt(jnp.sum(projected * projected, axis=-1, keepdims=True) + NORM_EPS)
    embed_low = (projected * inv_norm).astype(bf16)
    own_all = lax.all_gather(embed_low, "dp", axis=0, tiled=True)
    others = swapped(own_all, "tower", 0)
    logit_mult = jnp.exp(logit_scale[0])
    similar = contract_cols(embed_low, others)
    logits = logit_mult * similar
    logit_top = jnp.max(logits, axis=-1, keepdims=True)
    logit_total = logit_top + jnp.log(jnp.sum(jnp.exp(logits - logit_top), axis=-1, keepdims=True))
    label_col = dp_index * samples + lax.broadcasted_iota(jnp.int32, (samples, 1), 0)
    label_hot = (lax.broadcasted_iota(jnp.int32, (samples, sample_total), 1) == label_col).astype(
        f32
    )
    diag_logit = jnp.sum(label_hot * logits, axis=-1, keepdims=True)
    loss_part = jnp.sum(logit_total - diag_logit) / (2.0 * sample_total)
    grad_logits = (jnp.exp(logits - logit_total) - label_hot) * 0.5
    scale_part = logit_mult * jnp.sum(grad_logits * similar)
    grad_sims = (logit_mult * grad_logits).astype(bf16)
    grad_own = jnp.dot(grad_sims, others, preferred_element_type=f32)
    grad_others = contract_rows(grad_sims, embed_low)
    sent_back = swapped(grad_others, "tower", 0)
    returned = lax.psum_scatter(sent_back, "dp", scatter_dimension=0, tiled=True)
    totals = lax.psum((loss_part, scale_part), ("tower", "dp"))
    grad_embed = grad_own + returned
    again = (
        lax.all_gather(ln1_gain[0], "dp", axis=0, tiled=True),
        lax.all_gather(qkv_weight[0], "dp", axis=0, tiled=True),
        lax.all_gather(out_weight[0], "dp", axis=0, tiled=True),
        lax.all_gather(ln2_gain[0], "dp", axis=0, tiled=True),
        lax.all_gather(fc_weight[0], "dp", axis=0, tiled=True),
        lax.all_gather(down_weight[0], "dp", axis=0, tiled=True),
        lax.all_gather(final_gain[0], "dp", axis=0, tiled=True),
        lax.all_gather(embed_weight[0], "dp", axis=0, tiled=True),
    )
    (
        back_gain_one,
        back_qkv,
        back_out,
        back_gain_two,
        back_fc,
        back_down,
        back_gain_final,
        back_embed,
    ) = again
    cross_term = jnp.sum(grad_embed * projected, axis=-1, keepdims=True)
    grad_proj = inv_norm * grad_embed - projected * inv_norm * inv_norm * inv_norm * cross_term
    grad_proj_low = grad_proj.astype(bf16)
    grad_head = contract_cols(grad_proj_low, back_embed)
    grad_pooled, d_gain_final, d_bias_final = masked_norm_back(
        grad_head, back_gain_final.astype(f32), norm_final, inv_final, col_keep, width_real
    )
    grad_rows = (pool_hot[:, :, None] * grad_pooled[:, None, :]).reshape(flat_rows, width_all)
    grad_branch_low = grad_rows.astype(bf16)
    d_down_b = column_sum(grad_branch_low)
    grad_act = contract_cols(grad_branch_low, back_down)
    grad_pre_low = (
        grad_act * (gate_sig + GELU_K * hidden_pre * gate_sig * (1.0 - gate_sig))
    ).astype(bf16)
    d_fc_b = column_sum(grad_pre_low)
    grad_norm_two = contract_cols(grad_pre_low, back_fc)
    grad_mid_norm, d_gain_two, d_bias_two = masked_norm_back(
        grad_norm_two, back_gain_two.astype(f32), norm_two, inv_two, col_keep, width_real
    )
    grad_middle = grad_rows + grad_mid_norm
    grad_attn_low = grad_middle.astype(bf16)
    d_out_b = column_sum(grad_attn_low)
    grad_mix_low = (
        contract_cols(grad_attn_low, back_out)
        .astype(bf16)
        .reshape(samples, seq_rows, head_count, HD)
    )
    probs_again = jnp.exp(masked_scores() - log_total)
    probs_low = probs_again.astype(bf16)
    grad_value = jnp.einsum("shqk,sqhd->skhd", probs_low, grad_mix_low, preferred_element_type=f32)
    grad_probs = jnp.einsum("sqhd,skhd->shqk", grad_mix_low, value_all, preferred_element_type=f32)
    grad_scores = probs_again * (
        grad_probs - jnp.sum(probs_again * grad_probs, axis=-1, keepdims=True)
    )
    grad_scores_low = grad_scores.astype(bf16)
    grad_query = (
        jnp.einsum("shqk,skhd->sqhd", grad_scores_low, key_all, preferred_element_type=f32)
        * score_mult
    )
    grad_key = (
        jnp.einsum("shqk,sqhd->skhd", grad_scores_low, query_all, preferred_element_type=f32)
        * score_mult
    )
    grad_qkv_low = (
        jnp.stack([grad_query, grad_key, grad_value], axis=2)
        .astype(bf16)
        .reshape(flat_rows, 3 * width_all)
    )
    d_qkv_w = contract_rows(normed_one, grad_qkv_low).reshape(width_all, 3, width_all)
    qkv_sums = column_sum(grad_qkv_low).reshape(3, width_all)
    d_qv_b = jnp.stack([qkv_sums[0], qkv_sums[2]])
    grad_norm_one = contract_cols(grad_qkv_low, back_qkv.reshape(width_all, 3 * width_all))
    grad_in_norm, d_gain_one, d_bias_one = masked_norm_back(
        grad_norm_one, back_gain_one.astype(f32), norm_one, inv_one, col_keep, width_real
    )
    tokens_grad = (grad_middle + grad_in_norm).reshape(1, samples, seq_rows, width_all)
    d_embed_w = contract_rows(head_low, grad_proj_low)
    d_down_w = contract_rows(act_low, grad_branch_low)
    d_fc_w = contract_rows(normed_two, grad_pre_low)
    d_out_w = contract_rows(head_mix_low, grad_attn_low)
    shares = (
        lax.psum_scatter(d_gain_one, "dp", scatter_dimension=0, tiled=True),
        lax.psum_scatter(d_bias_one, "dp", scatter_dimension=0, tiled=True),
        lax.psum_scatter(d_qkv_w, "dp", scatter_dimension=0, tiled=True),
        lax.psum_scatter(d_qv_b, "dp", scatter_dimension=1, tiled=True),
        lax.psum_scatter(d_out_w, "dp", scatter_dimension=0, tiled=True),
        lax.psum_scatter(d_out_b, "dp", scatter_dimension=0, tiled=True),
        lax.psum_scatter(d_gain_two, "dp", scatter_dimension=0, tiled=True),
        lax.psum_scatter(d_bias_two, "dp", scatter_dimension=0, tiled=True),
        lax.psum_scatter(d_fc_w, "dp", scatter_dimension=0, tiled=True),
        lax.psum_scatter(d_fc_b, "dp", scatter_dimension=0, tiled=True),
        lax.psum_scatter(d_down_w, "dp", scatter_dimension=0, tiled=True),
        lax.psum_scatter(d_down_b, "dp", scatter_dimension=0, tiled=True),
        lax.psum_scatter(d_gain_final, "dp", scatter_dimension=0, tiled=True),
        lax.psum_scatter(d_bias_final, "dp", scatter_dimension=0, tiled=True),
        lax.psum_scatter(d_embed_w, "dp", scatter_dimension=0, tiled=True),
    )
    results = list(shares)
    outputs = [item[None] for item in results]
    loss = totals[0].reshape(1)
    logit_scale_grad = totals[1].reshape(1)
    return (
        block_out,
        tokens_grad,
        loss,
        outputs[0],
        outputs[1],
        outputs[2],
        outputs[3],
        outputs[4],
        outputs[5],
        outputs[6],
        outputs[7],
        outputs[8],
        outputs[9],
        outputs[10],
        outputs[11],
        outputs[12],
        outputs[13],
        outputs[14],
        logit_scale_grad,
    )


RING_Z = (0, 1, 2, 3, 3, 2, 1, 0)
RING_Y = (0, 0, 0, 0, 1, 1, 1, 1)
ITEMS = 16
N = ITEMS * 8
F32 = jnp.float32
BF16 = jnp.bfloat16
ANY = pl.BlockSpec(memory_space=pl.ANY)
VMEM = pl.BlockSpec(memory_space=pltpu.VMEM)
SMEM = pl.BlockSpec(memory_space=pltpu.SMEM)
SCALE = float(HD) ** -0.5
PAYLOAD = 160


def call(kernel, name, ins, outs, scratch, flops=0, touched=0):
    return pl.pallas_call(
        kernel,
        name=name,
        out_shape=[jax.ShapeDtypeStruct(shape, dtype) for _, shape, dtype in outs],
        in_specs=[spec for spec, _ in ins],
        out_specs=[spec for spec, _, _ in outs],
        scratch_shapes=scratch,
        compiler_params=pltpu.CompilerParams(vmem_limit_bytes=67043328),
        cost_estimate=pl.CostEstimate(flops=flops, bytes_accessed=touched, transcendentals=0),
    )(*[item for _, item in ins])


def dot(left, right, left_dim=1, right_dim=0):
    return lax.dot_general(
        left, right, (((left_dim,), (right_dim,)), ((), ())), preferred_element_type=F32
    )


def aligned(index, size):
    return pl.multiple_of(index, size)


def owner_table(dp_index):
    core = dp_index % 2
    row = dp_index // 2 % 2
    depth = dp_index // 4
    place = jnp.where(row == 0, depth, 7 - depth)

    def chip(where):
        where = (where + 8) % 8
        z = jnp.where(where < 4, where, 7 - where)
        y = jnp.where(where < 4, 0, 1)
        return (z * 2 + y) * 2

    sign = jnp.where(core == 0, -1, 1)
    found = [chip(place)]
    for hop in range(1, 4):
        found += [chip(place + sign * hop), chip(place - sign * hop)]
    return found + [chip(place + 4) + core, chip(place + 4) + 1 - core]


class Place:
    def __init__(self, lengths):
        self.dp = lax.axis_index("dp")
        self.text = lax.axis_index("tower") == 1
        self.lengths = lengths
        self.keep = (
            lax.broadcasted_iota(jnp.int32, (1, DI), 1) < jnp.where(self.text, DT, DI)
        ).astype(F32)
        self.winv = jnp.where(self.text, 1.0 / DT, 1.0 / DI).astype(F32)

    def length(self, s):
        return jnp.where(self.text, self.lengths[s], IMG_ROWS)

    def pool(self, s):
        return jnp.where(self.text, self.lengths[s] - 1, 0)

    def column(self, pick):
        ids = lax.broadcasted_iota(jnp.int32, (1, 8, 1), 1)
        column = jnp.zeros((1, 8, 1), jnp.int32)
        for s in range(8):
            column = jnp.where(ids == s, pick(s), column)
        return column

    def either(self, path, image):
        @pl.when(self.text)
        def _():
            path(DT, 77)

        @pl.when(jnp.logical_not(self.text))
        def _():
            path(DI, image)

    def mine(self, visit):
        for owner in range(ITEMS):

            @pl.when(self.dp == owner)
            def _(owner=owner):
                visit(owner)


def copy(src, dst, sem):
    found = pltpu.make_async_copy(src, dst, sem)
    found.start()
    return found


def drain(dst, sem):
    pltpu.make_async_copy(dst, dst, sem).wait()


def fetch(owners, refs, row, rows, dst, sem):
    for owner, ref in zip(owners, refs):
        if len(ref.shape) == 3:
            copy(ref.at[:, pl.ds(row, rows), :], dst.at[pl.ds(owner, 2)], sem)
        else:
            copy(ref.at[pl.ds(row, rows), :], dst.at[owner], sem)


def embed_matrix(packed):
    tail = jnp.concatenate([packed[:, 0:16, EMB:DI], packed[:, 16:32, EMB:DI]], axis=2)
    return jnp.concatenate([packed[:, :, 0:EMB], tail], axis=1).reshape(DI, EMB)


def normalize(values, keep, winv):
    mean = jnp.sum(values, axis=-1, keepdims=True) * winv
    centred = (values - mean) * keep
    var = jnp.sum(centred * centred, axis=-1, keepdims=True) * winv
    inv = lax.rsqrt(var + EPS)
    return centred * inv, inv


def normalize_back(grad_out, gain, normed, inv, keep, winv):
    grad_normed = grad_out * gain
    mean_grad = jnp.sum(grad_normed, axis=-1, keepdims=True) * winv
    mean_cross = jnp.sum(grad_normed * normed, axis=-1, keepdims=True) * winv
    return keep * inv * (grad_normed - mean_grad - normed * mean_cross)


def row_sum(values):
    return jnp.sum(values, axis=0, keepdims=True)


def head_rows(rows):
    heads = lax.broadcasted_iota(jnp.int32, rows.shape, 1) // HD
    parts = [jnp.where(heads == head, rows, 0.0) for head in range(16)]
    return jnp.concatenate(parts, axis=0).astype(BF16)


def chunks(count, visit):
    @pl.loop(0, count // 14)
    def _(i):
        visit(i * 14, aligned(i * 112, 16), 14)

    if count % 14:
        at = count - count % 14
        visit(at, at * 8, count % 14)


def pack_first_kernel(lengths, qkv, tok, *rest):
    here = Place(lengths)
    vectors, (qv_bias, fc_bias, out) = rest[:8], rest[8:]
    out[0:144, :] = qkv[...]
    sub = lax.broadcasted_iota(jnp.int32, (8, DI), 0)
    pooled = jnp.zeros((8, DI), F32)
    for s in range(8):
        pooled = jnp.where(sub == s, tok[here.pool(s)].astype(F32), pooled)
    out[144:152, :] = pooled.astype(BF16)
    lane = lax.broadcasted_iota(jnp.int32, (1, DI), 1) // 48 == here.dp
    short = [v[...].astype(F32) for v in vectors]
    pair = qv_bias[...].astype(F32)
    short[2:2] = [pair[0:1], pair[1:2]]
    rows = [jnp.where(lane, jnp.concatenate([v] * ITEMS, axis=1), 0.0) for v in short]
    wide = lax.broadcasted_iota(jnp.int32, (1, 4 * DI), 1) // 192 == here.dp
    fc = jnp.where(wide, jnp.concatenate([fc_bias[...].astype(F32)] * ITEMS, axis=1), 0.0)
    rows += [fc[:, i * DI : (i + 1) * DI] for i in range(4)]
    row_id = lax.broadcasted_iota(jnp.int32, (16, DI), 0)
    small = jnp.zeros((16, DI), F32)
    for at, row in enumerate(rows):
        small = jnp.where(row_id == at, jnp.broadcast_to(row, (16, DI)), small)
    out[152:168, :] = small.astype(BF16)


def pack_first(lengths, qkv, tok, vectors, qv_bias, fc_bias):
    return call(
        pack_first_kernel,
        "pack_first",
        [(SMEM, lengths)] + [(VMEM, item) for item in (qkv, tok, *vectors, qv_bias, fc_bias)],
        [(VMEM, (168, DI), BF16)],
        [],
        touched=1_500_000,
    )[0]


def pack_rest_kernel(w_out, w_fc, w_emb, out):
    out[0:48, :] = w_out[...]
    out[48:80, 0:EMB] = w_emb[0:32, :]
    out[48:64, EMB:DI] = w_emb[32:48, 0:256]
    out[64:80, EMB:DI] = w_emb[32:48, 256:EMB]
    for block in range(4):
        out[80 + 48 * block : 128 + 48 * block, :] = w_fc[:, block * DI : (block + 1) * DI]


def pack_rest(w_out, w_fc, w_emb):
    return call(
        pack_rest_kernel,
        "pack_rest",
        [(VMEM, item) for item in (w_out, w_fc, w_emb)],
        [(VMEM, (272, DI), BF16)],
        [],
        touched=1_500_000,
    )[0]


def sample_limits(here):
    lane_sample = lax.broadcasted_iota(jnp.int32, (1, 128), 1) % 8
    limit = jnp.zeros((1, 128), jnp.int32)
    for s in range(8):
        limit = jnp.where(lane_sample == s, here.length(s), limit)
    return limit


def own_heads(tall, width):
    heads = lax.broadcasted_iota(jnp.int32, (8, width), 1) // HD
    total = jnp.zeros((8, width), F32)
    for head in range(width // HD):
        total = total + jnp.where(heads == head, tall[head * 8 : head * 8 + 8], 0.0)
    if width < DI:
        total = jnp.concatenate([total, jnp.zeros((8, DI - width), F32)], axis=1)
    return total


def tall_rows(rows):
    return jnp.concatenate([rows[:, i * 128 : (i + 1) * 128] for i in range(DI // 128)], axis=0)


def wide_rows(tall):
    tall = tall.astype(F32)
    return jnp.concatenate(
        [tall[:, i * 8 : i * 8 + 8, :].reshape(N, 128) for i in range(DI // 128)], axis=1
    )


def pooled_kernel(lengths, tok, *rest):
    first, outs, scratch = rest[:9], rest[9:18], rest[18:]
    keys_hbm, values_hbm, norm_hbm, normed_hbm, vec, pooled, q_own, probs_out, gv_out = outs
    weights, small, normed, keys, values, norm_low, sems, ends = scratch
    here = Place(lengths)
    owners = owner_table(here.dp)
    fetch(owners, first, 152, 16, small, sems.at[0])
    fetch(owners, first, 0, 144, weights, sems.at[1])
    keep, winv = here.keep, here.winv
    drain(small, sems.at[0])
    vec[...] = jnp.sum(small[...].astype(F32), axis=0)
    limit = sample_limits(here)
    sub = lax.broadcasted_iota(jnp.int32, (8, DI), 0)
    picked = jnp.zeros((8, DI), F32)
    for s in range(8):
        picked = jnp.where(sub == s, tok[here.pool(s)].astype(F32), picked)
    pooled_norm, _ = normalize(picked, keep, winv)
    pooled_normed = (pooled_norm * vec[0:1, :] + vec[1:2, :]).astype(BF16)

    def norm_chunk(position, row, count):
        x = tok[pl.ds(position, count)].astype(F32).reshape(count * 8, DI)
        norm, _ = normalize(x, keep, winv)
        norm_low[pl.ds(row, count * 8), :] = norm.astype(BF16)
        normed[pl.ds(row, count * 8), :] = (norm * vec[0:1, :] + vec[1:2, :]).astype(BF16)

    def path(width, count):
        rows = count * 8
        chunks(count, norm_chunk)
        saved = [copy(norm_low, norm_hbm, ends.at[0]), copy(normed, normed_hbm, ends.at[1])]
        drain(weights, sems.at[1])
        for third, low, bias in ((1, keys, None), (2, values, 3)):

            @pl.loop(0, width // 256)
            def _(j, third=third, low=low, bias=bias):
                lanes = pl.ds(aligned(j * 256, 256), 256)
                weight = weights[:, third * 48 : third * 48 + 48, lanes].reshape(DI, 256)
                prod = dot(normed[0:rows, 0:width], weight[0:width])
                if bias is not None:
                    prod = prod + vec[bias : bias + 1, lanes]
                low[0:rows, lanes] = prod.astype(BF16)

        saved += [copy(keys, keys_hbm, ends.at[2]), copy(values, values_hbm, ends.at[3])]
        query = dot(pooled_normed, weights[:, 0:48, :].reshape(DI, DI)) + vec[2:3, :]
        query = query.astype(BF16).astype(F32)
        q_own[...] = query
        q_rows = head_rows(query)
        raw = dot(keys[0:rows, 0:width], q_rows[:, 0:width], 1, 1) * SCALE
        row = lax.broadcasted_iota(jnp.int32, (rows, 128), 0)
        lane = lax.broadcasted_iota(jnp.int32, (rows, 128), 1)
        valid = (lane % 8 == row % 8) & (row // 8 < limit) & (lane < width // 8)
        raw = jnp.where(valid, raw, NEG_FILL)
        terms = jnp.where(valid, jnp.exp(raw - jnp.max(raw, axis=0, keepdims=True)), 0.0)
        probs = terms / jnp.maximum(row_sum(terms), 1e-30)
        low_probs = probs.astype(BF16)
        probs_out[0:rows, :] = probs
        gv_out[0:rows, :] = low_probs
        mixed = own_heads(dot(low_probs, values[0:rows, 0:width], 0, 0), width)
        tall = tall_rows(mixed).astype(BF16)
        for owner in range(ITEMS):
            pooled[owner] = tall
        for item in saved:
            item.wait()

    here.either(path, 56)


def attend_pooled(lengths, tok, first):
    rows = tok.shape[0] * tok.shape[1]
    return call(
        pooled_kernel,
        "attend_pooled",
        [(SMEM, lengths), (VMEM, tok)] + [(ANY, r) for r in first],
        [(ANY, (rows, DI), BF16)] * 4
        + [
            (VMEM, (16, DI), F32),
            (VMEM, (ITEMS, 48, 128), BF16),
            (VMEM, (8, DI), F32),
            (VMEM, (rows, 128), F32),
            (VMEM, (rows, 128), BF16),
        ],
        [
            pltpu.VMEM((ITEMS, 144, DI), BF16),
            pltpu.VMEM((ITEMS, 16, DI), BF16),
            pltpu.VMEM((rows, DI), BF16),
            pltpu.VMEM((rows, DI), BF16),
            pltpu.VMEM((rows, DI), BF16),
            pltpu.VMEM((rows, DI), BF16),
            pltpu.SemaphoreType.DMA((2,)),
            pltpu.SemaphoreType.DMA((4,)),
        ],
        flops=7_000_000_000,
        touched=10_000_000,
    )


def attend_kernel(lengths, vec, gv, normed_hbm, keys_hbm, values_hbm, norm_hbm, *rest):
    first, (mixed, z_value), scratch = rest[:9], rest[9:11], rest[11:]
    weights, normed, keys, values, norm_low, qf, kf, vf, mf, sems = scratch
    here = Place(lengths)
    owners = owner_table(here.dp)
    fetch(owners, first, 0, 48, weights, sems.at[0])
    early = [
        copy(src, dst, sems.at[1 + i])
        for i, (src, dst) in enumerate(
            ((normed_hbm, normed), (keys_hbm, keys), (values_hbm, values), (norm_hbm, norm_low))
        )
    ]
    drain(weights, sems.at[0])
    for item in early:
        item.wait()

    def path(width, count):
        rows = count * 8
        span = 80 if count == 77 else count
        if span > count:
            for dst in (qf, kf, vf):
                dst[:, rows : span * 8, :] = jnp.zeros((6, span * 8 - rows, 128), F32)

        @pl.loop(0, width // 256)
        def _(j):
            lanes = pl.ds(aligned(j * 256, 256), 256)
            weight = weights[:, :, lanes].reshape(DI, 256)
            prod = dot(normed[0:rows, 0:width], weight[0:width]) + vec[2:3, lanes]
            prod = prod.astype(BF16).astype(F32) * SCALE
            for dst, item in ((qf, prod), (kf, keys[0:rows, lanes].astype(F32)), (vf, values[0:rows, lanes].astype(F32))):
                dst[2 * j, 0:rows, :] = item[:, 0:128]
                dst[2 * j + 1, 0:rows, :] = item[:, 128:256]

        key_pos = lax.broadcasted_iota(jnp.int32, (span, 2 * span), 0)
        query_pos = lax.broadcasted_iota(jnp.int32, (span, 2 * span), 1) % span
        low_half = lax.broadcasted_iota(jnp.int32, (span, 128), 1) < HD

        @pl.loop(0, 8)
        def _(s):
            at = pl.ds(s, span, stride=8)
            allowed = key_pos < here.length(s)
            if width == DT:
                allowed = allowed & (key_pos <= query_pos)
            pairs = range(width // 128)
            raws = []
            for pair in pairs:
                query, key = qf.at[pair][at, :], kf.at[pair][at, :].astype(BF16)
                spread = [jnp.where(low_half, query, 0.0), jnp.where(low_half, 0.0, query)]
                spread = jnp.concatenate(spread, axis=0).astype(BF16)
                raws.append(dot(key, spread, 1, 1))
            probs = []
            for raw in raws:
                raw = jnp.where(allowed, raw, NEG_FILL)
                terms = jnp.exp(raw - jnp.max(raw, axis=0, keepdims=True))
                probs.append((terms / jnp.sum(terms, axis=0, keepdims=True)).astype(BF16))
            for pair in pairs:
                out = dot(probs[pair], vf.at[pair][at, :].astype(BF16), 0, 0)
                mf.at[pair][at, :] = jnp.where(low_half, out[0:span], out[span : 2 * span])

        for i in range(width // 128):
            mixed[0:rows, 128 * i : 128 * i + 128] = mf[i, 0:rows, :].astype(BF16)
        z_value[...] = dot(norm_low[0:rows, :], gv[0:rows, :], 0, 0).astype(BF16)

    here.either(path, 56)


def attend(lengths, vec, gv, normed, keys, values, norm_low, first):
    rows = keys.shape[0]
    high = rows + 24
    return call(
        attend_kernel,
        "attend",
        [(SMEM, lengths), (VMEM, vec), (VMEM, gv)]
        + [(ANY, r) for r in (normed, keys, values, norm_low, *first)],
        [(VMEM, (rows, DI), BF16), (VMEM, (DI, 128), BF16)],
        [
            pltpu.VMEM((ITEMS, 48, DI), BF16),
            pltpu.VMEM((rows, DI), BF16),
            pltpu.VMEM((rows, DI), BF16),
            pltpu.VMEM((rows, DI), BF16),
            pltpu.VMEM((rows, DI), BF16),
            pltpu.VMEM((6, high, 128), F32),
            pltpu.VMEM((6, high, 128), F32),
            pltpu.VMEM((6, high, 128), F32),
            pltpu.VMEM((6, high, 128), F32),
            pltpu.SemaphoreType.DMA((5,)),
        ],
        flops=9_000_000_000,
        touched=10_000_000,
    )


def forward_kernel(lengths, vec, mixes, *rest):
    first, second, down = rest[:9], rest[9:18], rest[18:27]
    outs, scratch = rest[27:38], rest[38:]
    (e_out, proj_out, normf_out, invf_out, norm2_out, inv2_out, slope_out, n2_sl, mix_sl, head_sl,
     act_sl) = outs
    w_out, w_fc, w_down, w_emb, xs, mix, n2, act, head_all, sems = scratch
    here = Place(lengths)
    owners = owner_table(here.dp)
    fetch(owners, second, 0, 48, w_out, sems.at[1])
    fetch(owners, first, 144, 8, xs, sems.at[0])
    fetch(owners, second, 80, 192, w_fc, sems.at[2])
    keep, winv = here.keep, here.winv
    mix[...] = wide_rows(mixes[...]).astype(BF16)
    drain(w_out, sems.at[1])
    drain(xs, sems.at[0])
    fetch(owners, down, 0, 192, w_down, sems.at[3])
    fetch(owners, second, 48, 32, w_emb, sems.at[4])
    stream = xs[...].astype(F32).reshape(N, DI)
    middle = stream + dot(mix[...], w_out[...].reshape(DI, DI)) + vec[4:5, :]
    norm2, inv2 = normalize(middle, keep, winv)
    n2[...] = (norm2 * vec[5:6, :] + vec[6:7, :]).astype(BF16)
    norm2_out[...] = norm2
    inv2_out[...] = jnp.broadcast_to(inv2, (N, 128))
    drain(w_fc, sems.at[2])
    for block in range(4):
        lanes = pl.ds(block * DI, DI)
        weight = w_fc[:, block * 48 : block * 48 + 48, :].reshape(DI, DI)
        pre = dot(n2[...], weight) + vec[10 + block : 11 + block, :]
        gate = jax.nn.sigmoid(GELU_K * pre)
        act[:, lanes] = (pre * gate).astype(BF16)
        slope_out[:, lanes] = gate + GELU_K * pre * gate * (1.0 - gate)

    drain(w_down, sems.at[3])
    last = middle + dot(act[...], w_down[...].reshape(4 * DI, DI)) + vec[7:8, :]
    normf, invf = normalize(last, keep, winv)
    normf_out[...] = normf
    invf_out[...] = jnp.broadcast_to(invf, (N, 128))
    head_all[...] = (normf * vec[8:9, :] + vec[9:10, :]).astype(BF16)
    drain(w_emb, sems.at[4])
    proj = dot(head_all[...], embed_matrix(w_emb[...]))
    proj_out[...] = proj
    scale = lax.rsqrt(jnp.sum(proj * proj, axis=-1, keepdims=True) + NORM_EPS)
    e_out[...] = (proj * scale).astype(BF16)

    def mine(owner):
        lanes = slice(owner * 48, owner * 48 + 48)
        n2_sl[...] = n2[:, lanes]
        mix_sl[...] = mix[:, lanes]
        head_sl[...] = head_all[:, lanes]
        act_sl[...] = act[:, owner * 192 : owner * 192 + 192]

    here.mine(mine)


def pooled_forward(lengths, vec, mixes, first, second, down):
    return call(
        forward_kernel,
        "pooled_forward",
        [(SMEM, lengths), (VMEM, vec), (VMEM, mixes)] + [(ANY, r) for r in (*first, *second, *down)],
        [
            (VMEM, (N, EMB), BF16),
            (VMEM, (N, EMB), F32),
            (VMEM, (N, DI), F32),
            (VMEM, (N, 128), F32),
            (VMEM, (N, DI), F32),
            (VMEM, (N, 128), F32),
            (VMEM, (N, 4 * DI), F32),
            (VMEM, (N, 48), BF16),
            (VMEM, (N, 48), BF16),
            (VMEM, (N, 48), BF16),
            (VMEM, (N, 192), BF16),
        ],
        [
            pltpu.VMEM((ITEMS, 48, DI), BF16),
            pltpu.VMEM((ITEMS, 192, DI), BF16),
            pltpu.VMEM((ITEMS, 192, DI), BF16),
            pltpu.VMEM((ITEMS, 32, DI), BF16),
            pltpu.VMEM((ITEMS, 8, DI), BF16),
            pltpu.VMEM((N, DI), BF16),
            pltpu.VMEM((N, DI), BF16),
            pltpu.VMEM((N, 4 * DI), BF16),
            pltpu.VMEM((N, DI), BF16),
            pltpu.SemaphoreType.DMA((5,)),
        ],
        flops=11_000_000_000,
        touched=16_000_000,
    )


def middle_kernel(lengths, tok_hbm, vec, mixed_hbm, *rest):
    second = rest[:9]
    (n2_hbm, middle_hbm), scratch = rest[9:11], rest[11:]
    w_out, middle, tok, mixed, n2, sems = scratch
    here = Place(lengths)
    owners = owner_table(here.dp)
    rows_in = copy(mixed_hbm, mixed, sems.at[1])
    fetch(owners, second, 0, 48, w_out, sems.at[0])
    tok_in = copy(tok_hbm, tok, sems.at[2])
    keep, winv = here.keep, here.winv
    rows_in.wait()
    drain(w_out, sems.at[0])

    def norm_chunk(position, row, count):
        at = pl.ds(row, count * 8)
        total = middle[at, :] + tok[pl.ds(position, count)].astype(F32).reshape(count * 8, DI)
        middle[at, :] = total
        norm, _ = normalize(total, keep, winv)
        n2[at, :] = (norm * vec[5:6, :] + vec[6:7, :]).astype(BF16)
        copy(middle.at[at, :], middle_hbm.at[at, :], sems.at[3])
        copy(n2.at[at, :], n2_hbm.at[at, :], sems.at[4])

    def path(width, count):
        rows = count * 8

        @pl.loop(0, width // 256)
        def _(j):
            lanes = pl.ds(aligned(j * 256, 256), 256)
            weight = w_out[:, :, lanes].reshape(DI, 256)[0:width]
            middle[0:rows, lanes] = dot(mixed[0:rows, 0:width], weight) + vec[4:5, lanes]

        if width < DI:
            middle[0:rows, width:DI] = jnp.zeros((rows, DI - width), F32)
        tok_in.wait()
        chunks(count, norm_chunk)
        drain(middle.at[pl.ds(0, rows), :], sems.at[3])
        drain(n2.at[pl.ds(0, rows), :], sems.at[4])

    here.either(path, 56)


def middle_part(lengths, tok, vec, mixed, second):
    rows = mixed.shape[0]
    return call(
        middle_kernel,
        "middle_part",
        [(SMEM, lengths), (ANY, tok), (VMEM, vec), (ANY, mixed)] + [(ANY, r) for r in second],
        [(ANY, (rows, DI), BF16), (ANY, (rows, DI), F32)],
        [
            pltpu.VMEM((ITEMS, 48, DI), BF16),
            pltpu.VMEM((rows, DI), F32),
            pltpu.VMEM(tok.shape, BF16),
            pltpu.VMEM((rows, DI), BF16),
            pltpu.VMEM((rows, DI), BF16),
            pltpu.SemaphoreType.DMA((5,)),
        ],
        flops=5_000_000_000,
        touched=8_000_000,
    )


def one_direction(left, right, mult):
    sims = dot(left, right, 1, 1)
    logits = mult * sims
    top = jnp.max(logits, axis=-1, keepdims=True)
    total = top + jnp.log(jnp.sum(jnp.exp(logits - top), axis=-1, keepdims=True))
    count = sims.shape[0]
    eye = lax.broadcasted_iota(jnp.int32, (count, count), 0) == lax.broadcasted_iota(
        jnp.int32, (count, count), 1
    )
    hot = eye.astype(F32)
    lost = jnp.sum(total - jnp.sum(hot * logits, axis=-1, keepdims=True), axis=0, keepdims=True)
    grad = (jnp.exp(logits - total) - hot) * 0.5
    scale = jnp.sum(jnp.sum(grad * sims, axis=-1, keepdims=True), axis=0, keepdims=True)
    return lost, scale, mult * grad


def chain_kernel(lengths, log_mult, e_own_ref, e_oth_ref, vec, head_sl, act_sl, n2_sl, mix_sl, *rest):
    (proj_hbm, normf_hbm, invf_hbm, norm2_hbm, inv2_hbm, slope_hbm, keys_hbm, values_hbm, norm_hbm, probs_hbm,
     gv_hbm, z_hbm), rest = rest[:12], rest[12:]
    second, down = rest[:9], rest[9:18]
    outs, scratch = rest[18:37], rest[37:]
    (loss_out, scale_out, d_emb_hbm, d_down_hbm, d_fc_hbm, d_out_hbm, g_final, b_final, b_down, g_two, b_two, b_out, b_fc,
     mid_own, gm_out, gm_own, payload, gk_out, gq_out) = outs
    (w_out, w_fc, w_down, w_emb, gpre, mid_all, proj_v, normf_v, invf_v, norm2_v, inv2_v, slope, keys,
     values, norm_low, probs_v, gv_v, z_v, vec_grads, fcb_grads, d_emb, d_down, d_fc, d_out, sems, ins, ends) = scratch
    here = Place(lengths)
    owners = owner_table(here.dp)
    early = [
        copy(src, dst, ins.at[i])
        for i, (src, dst) in enumerate(
            ((proj_hbm, proj_v), (normf_hbm, normf_v), (invf_hbm, invf_v))
        )
    ]
    fetch(owners, second, 48, 32, w_emb, sems.at[0])
    fetch(owners, down, 0, 192, w_down, sems.at[1])
    slope_in = copy(slope_hbm, slope, ins.at[3])
    fetch(owners, second, 80, 192, w_fc, sems.at[2])
    later = [copy(norm2_hbm, norm2_v, ins.at[4]), copy(inv2_hbm, inv2_v, ins.at[5])]
    fetch(owners, second, 0, 48, w_out, sems.at[3])
    last = [
        copy(src, dst, ins.at[6 + i])
        for i, (src, dst) in enumerate(
            ((keys_hbm, keys), (values_hbm, values), (norm_hbm, norm_low), (probs_hbm, probs_v),
             (gv_hbm, gv_v), (z_hbm, z_v))
        )
    ]
    keep, winv = here.keep, here.winv
    text = here.text.astype(F32)
    mult = jnp.exp(jnp.full((1, 128), log_mult[0], F32))[:, 0:1]
    own, oth = e_own_ref[...].astype(F32), e_oth_ref[...].astype(F32)
    e_img = (own * (1.0 - text) + oth * text).astype(BF16)
    e_txt = (oth * (1.0 - text) + own * text).astype(BF16)
    lost_img, scale_img, grad_img = one_direction(e_img, e_txt, mult)
    lost_txt, scale_txt, grad_txt = one_direction(e_txt, e_img, mult)
    loss_out[...] = (lost_img + lost_txt) / (2.0 * N)
    scale_out[...] = mult * (scale_img + scale_txt)
    grad_own = (grad_img * (1.0 - text) + grad_txt * text).astype(BF16)
    grad_oth = (grad_txt * (1.0 - text) + grad_img * text).astype(BF16)
    oth_low = e_oth_ref[...]
    grad_e = dot(grad_own, oth_low) + dot(grad_oth, oth_low, 0, 0)
    for item in early:
        item.wait()
    drain(w_emb, sems.at[0])
    proj = proj_v[...]
    r = lax.rsqrt(jnp.sum(proj * proj, axis=-1, keepdims=True) + NORM_EPS)
    cross = jnp.sum(grad_e * proj, axis=-1, keepdims=True)
    grad_proj = (r * grad_e - proj * (r * r * r) * cross).astype(BF16)
    grad_head = dot(grad_proj, embed_matrix(w_emb[...]), 1, 1)
    normf = normf_v[...]
    grad_y = normalize_back(grad_head, vec[8:9, :], normf, invf_v[:, 0:1], keep, winv)
    branch = grad_y.astype(BF16)
    d_emb[...] = dot(head_sl[...], grad_proj, 0, 0)
    stored = [copy(d_emb, d_emb_hbm, ends.at[0])]
    vec_grads[0:1, :] = row_sum(grad_head * normf)
    vec_grads[1:2, :] = row_sum(grad_head)
    vec_grads[2:3, :] = row_sum(branch.astype(F32))
    d_down[...] = dot(act_sl[...], branch, 0, 0)
    stored.append(copy(d_down, d_down_hbm, ends.at[1]))
    drain(w_down, sems.at[1])
    slope_in.wait()
    for block in range(4):
        lanes = pl.ds(block * DI, DI)
        back = dot(branch, w_down[block * 4 : block * 4 + 4].reshape(DI, DI), 1, 1)
        low = (back * slope[:, lanes]).astype(BF16)
        gpre[:, lanes] = low
        fcb_grads[:, lanes] = jnp.broadcast_to(row_sum(low.astype(F32)), (8, DI))

    drain(w_fc, sems.at[2])
    grad_n2 = jnp.zeros((N, DI), F32)
    for block in range(4):
        weight = w_fc[:, block * 48 : block * 48 + 48, :].reshape(DI, DI)
        grad_n2 = grad_n2 + dot(gpre[:, block * DI : block * DI + DI], weight, 1, 1)
    for item in later:
        item.wait()
    norm2 = norm2_v[...]
    vec_grads[3:4, :] = row_sum(grad_n2 * norm2)
    vec_grads[4:5, :] = row_sum(grad_n2)
    grad_mid = grad_y + normalize_back(grad_n2, vec[5:6, :], norm2, inv2_v[:, 0:1], keep, winv)
    mid_all[...] = grad_mid
    own_rows = pl.ds(aligned(here.dp * 8, 8), 8)
    mid_own[...] = mid_all[own_rows, :]
    attn = grad_mid.astype(BF16)
    vec_grads[5:6, :] = row_sum(attn.astype(F32))
    drain(w_out, sems.at[3])
    gm_out[...] = dot(attn, w_out[...].reshape(DI, DI), 1, 1).astype(BF16).astype(F32)
    gm_own[...] = gm_out[own_rows, :]

    @pl.loop(0, 6)
    def _(j):
        lanes = pl.ds(aligned(j * 512, 512), 512)
        d_fc[:, lanes] = dot(n2_sl[...], gpre[:, lanes], 0, 0)

    d_out[...] = dot(mix_sl[...], attn, 0, 0)
    stored += [copy(d_fc, d_fc_hbm, ends.at[2]), copy(d_out, d_out_hbm, ends.at[3])]

    def mine(owner):
        lanes = slice(owner * 48, owner * 48 + 48)
        for at, dst in enumerate((g_final, b_final, b_down, g_two, b_two, b_out)):
            dst[...] = vec_grads[at : at + 1, lanes]
        b_fc[...] = fcb_grads[0:1, owner * 192 : owner * 192 + 192]

    here.mine(mine)
    for item in last:
        item.wait()
    m_rows = head_rows(gm_own[...])

    def path(width, count):
        rows = count * 8
        probs = probs_v[0:rows, :]
        grad_probs = dot(values[0:rows, 0:width], m_rows[:, 0:width], 1, 1)
        gk = (probs * (grad_probs - row_sum(probs * grad_probs))).astype(BF16)
        gv = gv_v[0:rows, :]
        gk_out[0:rows, :] = gk
        gq_low = own_heads(dot(gk, keys[0:rows, 0:width], 0, 0) * SCALE, width).astype(BF16)
        gq_out[...] = gq_low
        norm = norm_low[0:rows, :]
        z_key = dot(norm, gk, 0, 0).astype(BF16)
        z_value = z_v[...]
        sum_key = row_sum(gk.astype(F32))
        sum_value = row_sum(gv.astype(F32))
        key_high = sum_key.astype(BF16).astype(F32)
        value_high = sum_value.astype(BF16).astype(F32)
        row_id = lax.broadcasted_iota(jnp.int32, (16, 128), 0)
        sums = jnp.zeros((16, 128), F32)
        for at, value in enumerate((key_high, sum_key - key_high, value_high, sum_value - value_high)):
            sums = jnp.where(row_id == at, jnp.broadcast_to(value, (16, 128)), sums)
        sums = sums.astype(BF16)
        gq_tall = tall_rows(gq_low.astype(F32)).astype(BF16)
        for owner in range(ITEMS):
            base = owner * PAYLOAD
            payload[base : base + 48, :] = z_key[owner * 48 : owner * 48 + 48]
            payload[base + 48 : base + 64, :] = sums
            payload[base + 64 : base + 112, :] = z_value[owner * 48 : owner * 48 + 48]
            payload[base + 112 : base + 160, :] = gq_tall

    here.either(path, 56)
    for item in stored:
        item.wait()


def chain(lengths, log_mult, e_own, e_oth, vec, slices, saved, second, down):
    rows = saved[-2].shape[0]
    return call(
        chain_kernel,
        "chain",
        [(SMEM, lengths), (SMEM, log_mult)]
        + [(VMEM, item) for item in (e_own, e_oth, vec, *slices)]
        + [(ANY, r) for r in (*saved, *second, *down)],
        [
            (VMEM, (1, 1), F32),
            (VMEM, (1, 1), F32),
            (ANY, (48, EMB), F32),
            (ANY, (192, DI), F32),
            (ANY, (48, 4 * DI), F32),
            (ANY, (48, DI), F32),
        ]
        + [(VMEM, (1, 48), F32)] * 6
        + [
            (VMEM, (1, 192), F32),
            (VMEM, (8, DI), F32),
            (VMEM, (N, DI), F32),
            (VMEM, (8, DI), F32),
            (VMEM, (ITEMS * PAYLOAD, 128), BF16),
            (VMEM, (rows, 128), BF16),
            (VMEM, (8, DI), BF16),
        ],
        [
            pltpu.VMEM((ITEMS, 48, DI), BF16),
            pltpu.VMEM((ITEMS, 192, DI), BF16),
            pltpu.VMEM((ITEMS, 192, DI), BF16),
            pltpu.VMEM((ITEMS, 32, DI), BF16),
            pltpu.VMEM((N, 4 * DI), BF16),
            pltpu.VMEM((N, DI), F32),
            pltpu.VMEM((N, EMB), F32),
            pltpu.VMEM((N, DI), F32),
            pltpu.VMEM((N, 128), F32),
            pltpu.VMEM((N, DI), F32),
            pltpu.VMEM((N, 128), F32),
            pltpu.VMEM((N, 4 * DI), F32),
            pltpu.VMEM((rows, DI), BF16),
            pltpu.VMEM((rows, DI), BF16),
            pltpu.VMEM((rows, DI), BF16),
            pltpu.VMEM((rows, 128), F32),
            pltpu.VMEM((rows, 128), BF16),
            pltpu.VMEM((DI, 128), BF16),
            pltpu.VMEM((8, DI), F32),
            pltpu.VMEM((8, 4 * DI), F32),
            pltpu.VMEM((48, EMB), F32),
            pltpu.VMEM((192, DI), F32),
            pltpu.VMEM((48, 4 * DI), F32),
            pltpu.VMEM((48, DI), F32),
            pltpu.SemaphoreType.DMA((4,)),
            pltpu.SemaphoreType.DMA((12,)),
            pltpu.SemaphoreType.DMA((4,)),
        ],
        flops=15_000_000_000,
        touched=20_000_000,
    )


def close_kernel(lengths, tok, vec, gk, gv, q_own, gm_own, gq, mid_own, n2_hbm, middle_hbm, *rest):
    first, second, down = rest[:9], rest[9:18], rest[18:27]
    (block_out, out, q_out, norm_sl), scratch = rest[27:31], rest[31:]
    weights, w_fc, w_down, n2, act, middle, acc, xs, norm1_all, sems = scratch
    here = Place(lengths)
    owners = owner_table(here.dp)
    fetch(owners, first, 0, 144, weights, sems.at[0])
    fetch(owners, first, 144, 8, xs, sems.at[5])
    ready = copy(n2_hbm, n2, sems.at[1])
    fetch(owners, second, 80, 192, w_fc, sems.at[4])
    fetch(owners, down, 0, 192, w_down, sems.at[3])
    early = [copy(middle_hbm, middle, sems.at[2])]
    keep, winv = here.keep, here.winv
    q_rows = head_rows(q_own[...])
    m_rows = head_rows(gm_own[...])
    pool = here.column(here.pool)
    length = here.column(here.length)
    all_rows = out.shape[0]
    drain(weights, sems.at[0])
    u_key = (dot(q_rows, weights[:, 48:96, :].reshape(DI, DI), 1, 1) * SCALE).astype(BF16)
    u_value = dot(m_rows, weights[:, 96:144, :].reshape(DI, DI), 1, 1).astype(BF16)
    u_query = dot(gq[...], weights[:, 0:48, :].reshape(DI, DI), 1, 1)

    def path(width, count):
        rows = count * 8
        acc[0:rows, :] = dot(gk[0:rows, :], u_key) + dot(gv[0:rows, :], u_value)

        def back_chunk(position, row, count):
            at = pl.ds(row, count * 8)
            hit = lax.broadcasted_iota(jnp.int32, (count, 8, DI), 0) + position == pool
            norm, inv = normalize(tok[pl.ds(position, count)].astype(F32).reshape(count * 8, DI), keep, winv)
            total = acc[at, :] + jnp.where(hit, u_query[None], 0.0).reshape(count * 8, DI)
            back = normalize_back(total, vec[0:1, :], norm, inv, keep, winv)
            out[at, :] = back + jnp.where(hit, mid_own[...][None], 0.0).reshape(count * 8, DI)

        chunks(count, back_chunk)
        if rows < all_rows:
            out[rows:all_rows, :] = jnp.zeros((all_rows - rows, DI), F32)
        short = count if width == DT else IMG_ROWS
        rows = short * 8
        ready.wait()
        drain(w_fc, sems.at[4])
        for block in range(4):

            @pl.loop(0, 3 if width == DI else (3, 3, 2, 0)[block])
            def _(j, block=block):
                lanes = pl.ds(aligned(j * 256, 256), 256)
                wide = pl.ds(aligned(block * DI + j * 256, 256), 256)
                weight = w_fc[:, block * 48 : block * 48 + 48, lanes].reshape(DI, 256)[0:width]
                pre = dot(n2[0:rows, 0:width], weight) + vec[10 + block : 11 + block, lanes]
                act[0:rows, wide] = (pre * jax.nn.sigmoid(GELU_K * pre)).astype(BF16)

        for item in early:
            item.wait()
        drain(w_down, sems.at[3])

        @pl.loop(0, width // 256)
        def _(j):
            lanes = pl.ds(aligned(j * 256, 256), 256)
            weight = w_down[:, :, lanes].reshape(4 * DI, 256)[0 : 4 * width]
            total = dot(act[0:rows, 0 : 4 * width], weight)
            total = (total + vec[7:8, lanes] + middle[0:rows, lanes]).reshape(short, 8, 256)
            where = lax.broadcasted_iota(jnp.int32, (short, 8, 256), 0)
            block_out[0:rows, lanes] = jnp.where(where < length, total, 0.0).reshape(rows, 256).astype(BF16)

        if width < DI:
            block_out[:, width:DI] = jnp.zeros((all_rows, DI - width), BF16)
        if rows < all_rows:
            block_out[rows:all_rows, :] = jnp.zeros((all_rows - rows, DI), BF16)

    here.either(path, 56)
    drain(xs, sems.at[5])
    stream = xs[...].astype(F32).reshape(N, DI)
    norm1, _ = normalize(stream, keep, winv)
    norm1_all[...] = norm1.astype(BF16)
    n1 = (norm1 * vec[0:1, :] + vec[1:2, :]).astype(BF16)
    q_out[...] = (dot(n1, weights[:, 0:48, :].reshape(DI, DI)) + vec[2:3, :]).astype(BF16).astype(F32)

    def mine(owner):
        norm_sl[...] = norm1_all[:, owner * 48 : owner * 48 + 48]

    here.mine(mine)


def close(lengths, tok, vec, gk, gv, q_own, gm_own, gq, mid_own, n2, middle, first, second, down):
    rows = tok.shape[0] * tok.shape[1]
    return call(
        close_kernel,
        "close",
        [(SMEM, lengths)]
        + [(VMEM, item) for item in (tok, vec, gk, gv, q_own, gm_own, gq, mid_own)]
        + [(ANY, r) for r in (n2, middle, *first, *second, *down)],
        [(VMEM, (rows, DI), BF16), (VMEM, (rows, DI), F32), (VMEM, (N, DI), F32), (VMEM, (N, 48), BF16)],
        [
            pltpu.VMEM((ITEMS, 144, DI), BF16),
            pltpu.VMEM((ITEMS, 192, DI), BF16),
            pltpu.VMEM((ITEMS, 192, DI), BF16),
            pltpu.VMEM((rows, DI), BF16),
            pltpu.VMEM((rows, 4 * DI), BF16),
            pltpu.VMEM((rows, DI), F32),
            pltpu.VMEM((rows, DI), F32),
            pltpu.VMEM((ITEMS, 8, DI), BF16),
            pltpu.VMEM((N, DI), BF16),
            pltpu.SemaphoreType.DMA((6,)),
        ],
        flops=17_000_000_000,
        touched=18_000_000,
    )


def shard_kernel(got, q_all, gm_all, norm_sl, w_own, gain, bias, d_qkv, g_one, b_one, qv_out, turned, product):
    dp = lax.axis_index("dp")

    low_half = lax.broadcasted_iota(jnp.int32, (N, 128), 1) < HD

    def moments(start, source):
        for j in range(ITEMS):
            turned[j] = got[j, start : start + 64, :].astype(F32).T
        for pair in range(DI // 128):
            lanes = slice(pair * 128, pair * 128 + 128)
            rows = source[:, lanes]
            both = [jnp.where(low_half, rows, 0.0), jnp.where(low_half, 0.0, rows)]
            both = [half.reshape(ITEMS, 8, 128) for half in both]
            both = jnp.concatenate(both, axis=1).reshape(2 * N, 128).astype(BF16)
            part = turned[:, pair * 16 : pair * 16 + 16, :].reshape(2 * N, 64).astype(BF16)
            product[:, lanes] = dot(part, both, 0, 0)
        return product[...]

    def column(row):
        square = (48, 48)
        same = lax.broadcasted_iota(jnp.int32, square, 0) == lax.broadcasted_iota(jnp.int32, square, 1)
        return jnp.sum(jnp.where(same, row[...].astype(F32), 0.0), axis=1, keepdims=True)

    by_key = moments(0, q_all) * SCALE
    m_key, s_key = by_key[0:48], by_key[48:49] + by_key[49:50]
    by_value = moments(48, gm_all)
    m_value, s_value = by_value[16:64], by_value[2:3] + by_value[3:4]
    grad_q = wide_rows(got[:, 112:160, :])
    s_query = row_sum(grad_q)
    m_query = dot(norm_sl[...], grad_q.astype(BF16), 0, 0)
    gain_col, bias_col = column(gain), column(bias)
    by_gain = jnp.zeros((48, DI), F32)
    by_bias = jnp.zeros((48, DI), F32)
    for third, (moment, total) in enumerate(((m_query, s_query), (m_key, s_key), (m_value, s_value))):
        d_qkv[third] = gain_col * moment + bias_col * total
        weight = w_own[third].astype(F32)
        by_gain = by_gain + weight * moment
        by_bias = by_bias + weight * total
    ones = jnp.ones((8, DI), F32)
    line = (((1,), (1,)), ((), ()))
    for dst, item in ((g_one, by_gain), (b_one, by_bias)):
        dst[...] = lax.dot_general(
            ones, item, line, precision=lax.Precision.HIGHEST, preferred_element_type=F32
        )[0:1]
    for owner in range(ITEMS):

        @pl.when(dp == owner)
        def _(owner=owner):
            lanes = slice(owner * 48, owner * 48 + 48)
            qv_out[0:1, :] = s_query[:, lanes]
            qv_out[1:2, :] = s_value[:, lanes]


def shard_grads(got, q_all, gm_all, norm_sl, w_own, gain, bias):
    plain = (got, q_all, gm_all, norm_sl, w_own, gain, bias)
    return call(
        shard_kernel,
        "shard_grads",
        [(VMEM, item) for item in plain],
        [
            (VMEM, (3, 48, DI), F32),
            (VMEM, (1, 48), F32),
            (VMEM, (1, 48), F32),
            (VMEM, (2, 48), F32),
        ],
        [pltpu.VMEM((ITEMS, 128, 64), F32), pltpu.VMEM((64, DI), F32)],
        flops=5_000_000_000,
        touched=2_000_000,
    )


BOTH = ("tower", "dp")


def device(tower, place, core):
    return tower * 16 + (RING_Z[place] * 2 + RING_Y[place]) * 2 + core


def routes(towers):
    swap, turn = [], []
    for tower in range(towers):
        for place in range(8):
            for core, step in ((0, 1), (1, -1)):
                here = device(tower, place, core)
                swap.append((here, device(tower, place, 1 - core)))
                turn.append((here, device(tower, (place + step) % 8, core)))
    return swap, turn


def after(item, *earlier):
    return lax.optimization_barrier((item, *earlier))[0] if earlier else item


class Ring:
    def __init__(self, shard, swap, turn, first_core):
        self.swap, self.turn, self.first_core = swap, turn, first_core
        self.shard, self.other = shard, lax.ppermute(shard, BOTH, swap)
        self.last = self.joined(shard, self.other)
        self.items = [self.last]
        self.hops = 0

    def joined(self, own, other):
        return jnp.stack([jnp.where(self.first_core, own, other), jnp.where(self.first_core, other, own)])

    def first_step(self):
        held = self.joined(*(lax.ppermute(item, BOTH, self.turn) for item in (self.shard, self.other)))
        self.items += [held, lax.ppermute(held, BOTH, self.swap)]
        self.last = held
        self.hops += 1
        return held

    def step(self, *earlier, swap_after=(), later=False):
        held = self.last
        if self.hops == 3:
            held = jnp.where(self.first_core, held[0], held[1])
        held = lax.ppermute(after(held, *earlier), BOTH, self.turn)
        self.items += [held, None if later else lax.ppermute(after(held, *swap_after), BOTH, self.swap)]
        self.last = held
        self.hops += 1
        return held

    def finish(self, *earlier):
        for i, item in enumerate(self.items):
            if item is None:
                self.items[i] = lax.ppermute(after(self.items[i - 1], *earlier), BOTH, self.swap)
        return self.items


def ring_body(
    tokens,
    lengths,
    ln1_gain,
    ln1_bias,
    qkv_weight,
    qv_bias,
    out_weight,
    out_bias,
    ln2_gain,
    ln2_bias,
    fc_weight,
    fc_bias,
    down_weight,
    down_bias,
    final_gain,
    final_bias,
    embed_weight,
    logit_scale,
):
    towers = lax.axis_size("tower")
    dp_index = lax.axis_index("dp")
    swap, turn = routes(towers)
    tok = tokens[0].transpose(1, 0, 2)
    w_own = qkv_weight[0].transpose(1, 0, 2)
    vectors = (ln1_gain, ln1_bias, out_bias, ln2_gain, ln2_bias, down_bias, final_gain, final_bias)
    first_own = pack_first(lengths, w_own.reshape(144, DI), tok, vectors, qv_bias[0], fc_bias)
    second_own = pack_rest(out_weight[0], fc_weight[0], embed_weight[0])
    first_core = dp_index % 2 == 0

    qkv_ring = Ring(first_own, swap, turn, first_core)
    wide_ring = Ring(second_own, swap, turn, first_core)
    down_ring = Ring(down_weight[0], swap, turn, first_core)
    qkv_ring.first_step()
    d1 = down_ring.step()
    qkv_ring.step()
    q3 = qkv_ring.step(d1)
    wide_ring.step()
    qkv_ring.step()
    first = qkv_ring.items
    keys, values, norm_low, normed, vec, pooled, q_own, probs, gv = attend_pooled(lengths, tok, first)
    w2 = wide_ring.step(q3, swap_after=(q_own,))
    d2 = down_ring.step(q3, swap_after=(q_own,))
    mixes = lax.all_to_all(pooled, "dp", 0, 0, tiled=True)
    w3 = wide_ring.step(q_own)
    mixed, z_value = attend(lengths, vec, gv, after(normed, w2), keys, values, norm_low, first)
    wide_ring.step(z_value)
    d3 = down_ring.step(z_value, mixes)
    second = wide_ring.items
    down_ring.step()
    down = down_ring.items
    e_own, proj, normf, invf, norm2, inv2, slope, n2_sl, mix_sl, head_sl, act_sl = pooled_forward(
        lengths, vec, mixes, first, second, down
    )
    across = [(t * 16 + d, (1 - t) * 16 + d) for t in range(2) for d in range(16)]
    e_oth = lax.ppermute(e_own, BOTH, across)
    n2, middle = middle_part(lengths, tok, vec, after(mixed, e_own), second)
    (loss, scale, d_emb, d_down, d_fc, d_out, g_final, b_final, b_down, g_two, b_two, b_out, b_fc,
     mid_own, gm_all, gm_own, payload, gk, gq) = chain(
        lengths, logit_scale, after(e_own, n2), e_oth, vec, (head_sl, act_sl, n2_sl, mix_sl),
        (proj, normf, invf, norm2, inv2, slope, keys, values, norm_low, probs, gv, z_value), second, down,
    )
    got = lax.all_to_all(payload, "dp", 0, 0, tiled=True).reshape(ITEMS, PAYLOAD, 128)
    block_out, tokens_grad, q_all, norm_sl = close(
        lengths, tok, vec, gk, gv, q_own, gm_own, gq, mid_own, n2, middle, first, second, down
    )
    d_qkv, g_one, b_one, qv_sums = shard_grads(got, q_all, gm_all, norm_sl, w_own, ln1_gain, ln1_bias)
    seq = tok.shape[0]
    return (
        block_out.reshape(seq, 8, DI).transpose(1, 0, 2)[None],
        tokens_grad.reshape(seq, 8, DI).transpose(1, 0, 2)[None],
        loss.reshape(1),
        g_one,
        b_one,
        d_qkv.transpose(1, 0, 2)[None],
        qv_sums[None],
        d_out[None],
        b_out,
        g_two,
        b_two,
        d_fc[None],
        b_fc,
        d_down[None],
        b_down,
        g_final,
        b_final,
        d_emb[None],
        scale.reshape(1),
    )


def solution(mesh):
    fits = mesh.shape["dp"] == ITEMS and mesh.shape["tower"] == 2
    return jax.shard_map(
        ring_body if fits else body,
        mesh=mesh,
        in_specs=(
            P("tower", "dp", None, None),
            P("dp"),
            P("tower", "dp"),
            P("tower", "dp"),
            P("tower", "dp", None, None),
            P("tower", None, "dp"),
            P("tower", "dp", None),
            P("tower", "dp"),
            P("tower", "dp"),
            P("tower", "dp"),
            P("tower", "dp", None),
            P("tower", "dp"),
            P("tower", "dp", None),
            P("tower", "dp"),
            P("tower", "dp"),
            P("tower", "dp"),
            P("tower", "dp", None),
            P(),
        ),
        out_specs=(
            P("tower", "dp", None, None),
            P("tower", "dp", None, None),
            P(),
            P("tower", "dp"),
            P("tower", "dp"),
            P("tower", "dp", None, None),
            P("tower", None, "dp"),
            P("tower", "dp", None),
            P("tower", "dp"),
            P("tower", "dp"),
            P("tower", "dp"),
            P("tower", "dp", None),
            P("tower", "dp"),
            P("tower", "dp", None),
            P("tower", "dp"),
            P("tower", "dp"),
            P("tower", "dp"),
            P("tower", "dp", None),
            P(),
        ),
        check_vma=False,
    )
```

```python
import functools

import jax
import jax.numpy as jnp
from jax import lax
from jax.experimental import pallas as pl
from jax.experimental.pallas import tpu as pltpu
from jax.sharding import PartitionSpec as P

DI = 768
DT = 512
HD = 64
IMG_ROWS = 50
EMB = 512


EPS = 1e-05
NORM_EPS = 1e-06
GELU_K = 1.702
NEG_FILL = -1e30


def swapped(block, axis, stride):
    count = lax.axis_size(axis)
    route = []
    for low in range(count):
        high = low | 1 << stride
        if high != low and high < count:
            route += [(low, high), (high, low)]
    return lax.ppermute(block, axis, route)


def masked_norm(values, norm_gain, norm_bias, col_keep, width_real):
    row_mean = jnp.sum(values * col_keep, axis=-1, keepdims=True) / width_real
    centred = (values - row_mean) * col_keep
    row_var = jnp.sum(centred * centred, axis=-1, keepdims=True) / width_real
    inv_std = lax.rsqrt(row_var + EPS)
    normed = centred * inv_std
    return (normed * norm_gain + norm_bias, normed, inv_std)


def masked_norm_back(grad_out, norm_gain, normed, inv_std, col_keep, width_real):
    grad_normed = grad_out * norm_gain
    mean_grad = jnp.sum(grad_normed, axis=-1, keepdims=True) / width_real
    mean_cross = jnp.sum(grad_normed * normed, axis=-1, keepdims=True) / width_real
    grad_in = col_keep * inv_std * (grad_normed - mean_grad - normed * mean_cross)
    return (grad_in, jnp.sum(grad_out * normed, axis=0), jnp.sum(grad_out, axis=0))


def contract_rows(left_op, right_op):
    return lax.dot_general(
        left_op, right_op, (((0,), (0,)), ((), ())), preferred_element_type=jnp.float32
    )


def contract_cols(left_op, right_op):
    return lax.dot_general(
        left_op, right_op, (((1,), (1,)), ((), ())), preferred_element_type=jnp.float32
    )


def column_sum(values):
    return jnp.sum(values, axis=0, dtype=jnp.float32)


def body(
    tokens,
    lengths,
    ln1_gain,
    ln1_bias,
    qkv_weight,
    qv_bias,
    out_weight,
    out_bias,
    ln2_gain,
    ln2_bias,
    fc_weight,
    fc_bias,
    down_weight,
    down_bias,
    final_gain,
    final_bias,
    embed_weight,
    logit_scale,
):
    f32 = jnp.float32
    bf16 = jnp.bfloat16
    tower_index = lax.axis_index("tower")
    dp_index = lax.axis_index("dp")
    dp_count = lax.axis_size("dp")
    samples, seq_rows, width_all = (tokens.shape[1], tokens.shape[2], tokens.shape[3])
    head_count = width_all // HD
    sample_total = samples * dp_count
    flat_rows = samples * seq_rows
    is_text = tower_index == 1
    width_int = jnp.where(is_text, DT, DI)
    width_real = width_int.astype(f32)
    col_keep = (lax.broadcasted_iota(jnp.int32, (width_all,), 0) < width_int).astype(f32)
    seq_lens = jnp.where(is_text, lengths, IMG_ROWS)
    positions = lax.broadcasted_iota(jnp.int32, (samples, seq_rows), 1)
    row_keep = (positions < seq_lens[:, None]).astype(f32).reshape(flat_rows, 1)
    query_pos = lax.broadcasted_iota(jnp.int32, (seq_rows, seq_rows), 0)
    key_pos = lax.broadcasted_iota(jnp.int32, (seq_rows, seq_rows), 1)
    allowed = (key_pos[None] < seq_lens[:, None, None]) & (
        jnp.logical_not(is_text) | (key_pos <= query_pos)
    )[None]
    pool_pos = jnp.where(is_text, lengths - 1, 0)
    pool_hot = (positions == pool_pos[:, None]).astype(f32)
    score_mult = float(HD) ** (-0.5)
    gathered = (
        lax.all_gather(ln1_gain[0], "dp", axis=0, tiled=True),
        lax.all_gather(ln1_bias[0], "dp", axis=0, tiled=True),
        lax.all_gather(qkv_weight[0], "dp", axis=0, tiled=True),
        lax.all_gather(qv_bias[0], "dp", axis=1, tiled=True),
        lax.all_gather(out_weight[0], "dp", axis=0, tiled=True),
        lax.all_gather(out_bias[0], "dp", axis=0, tiled=True),
        lax.all_gather(ln2_gain[0], "dp", axis=0, tiled=True),
        lax.all_gather(ln2_bias[0], "dp", axis=0, tiled=True),
        lax.all_gather(fc_weight[0], "dp", axis=0, tiled=True),
        lax.all_gather(fc_bias[0], "dp", axis=0, tiled=True),
        lax.all_gather(down_weight[0], "dp", axis=0, tiled=True),
        lax.all_gather(down_bias[0], "dp", axis=0, tiled=True),
        lax.all_gather(final_gain[0], "dp", axis=0, tiled=True),
        lax.all_gather(final_bias[0], "dp", axis=0, tiled=True),
        lax.all_gather(embed_weight[0], "dp", axis=0, tiled=True),
    )
    (
        gain_one,
        bias_one,
        w_qkv,
        b_qv,
        w_out,
        b_out,
        gain_two,
        bias_two,
        w_fc,
        b_fc,
        w_down,
        b_down,
        gain_final,
        bias_final,
        w_embed,
    ) = gathered
    stream = tokens[0].astype(f32).reshape(flat_rows, width_all)
    normed_h1, norm_one, inv_one = masked_norm(
        stream, gain_one.astype(f32), bias_one.astype(f32), col_keep, width_real
    )
    normed_one = normed_h1.astype(bf16)
    qkv_bias = jnp.concatenate(
        [b_qv[0].astype(f32), jnp.zeros((width_all,), f32), b_qv[1].astype(f32)]
    )
    qkv_flat = (
        jnp.dot(normed_one, w_qkv.reshape(width_all, 3 * width_all), preferred_element_type=f32)
        + qkv_bias
    )
    qkv_low = qkv_flat.astype(bf16).reshape(samples, seq_rows, 3, head_count, HD)
    query_all = qkv_low[:, :, 0]
    key_all = qkv_low[:, :, 1]
    value_all = qkv_low[:, :, 2]

    def masked_scores():
        raw = (
            jnp.einsum("sqhd,skhd->shqk", query_all, key_all, preferred_element_type=f32)
            * score_mult
        )
        return jnp.where(allowed[:, None], raw, NEG_FILL)

    scores = masked_scores()
    row_top = jnp.max(scores, axis=-1, keepdims=True)
    exp_terms = jnp.exp(scores - row_top)
    exp_sum = jnp.sum(exp_terms, axis=-1, keepdims=True)
    log_total = row_top + jnp.log(exp_sum)
    attn_probs = (exp_terms / exp_sum).astype(bf16)
    head_mix = jnp.einsum("shqk,skhd->sqhd", attn_probs, value_all, preferred_element_type=f32)
    head_mix_low = head_mix.astype(bf16).reshape(flat_rows, width_all)
    attn_out = jnp.dot(head_mix_low, w_out, preferred_element_type=f32) + b_out.astype(f32)
    middle = stream + attn_out
    normed_h2, norm_two, inv_two = masked_norm(
        middle, gain_two.astype(f32), bias_two.astype(f32), col_keep, width_real
    )
    normed_two = normed_h2.astype(bf16)
    hidden_pre = jnp.dot(normed_two, w_fc, preferred_element_type=f32) + b_fc.astype(f32)
    gate_sig = jax.nn.sigmoid(GELU_K * hidden_pre)
    act_low = (hidden_pre * gate_sig).astype(bf16)
    branch = jnp.dot(act_low, w_down, preferred_element_type=f32) + b_down.astype(f32)
    block_rows = row_keep * (middle + branch)
    block_out = block_rows.astype(bf16).reshape(1, samples, seq_rows, width_all)
    block_three = block_rows.reshape(samples, seq_rows, width_all)
    pooled = jnp.take_along_axis(block_three, pool_pos[:, None, None], axis=1)[:, 0]
    normed_hf, norm_final, inv_final = masked_norm(
        pooled, gain_final.astype(f32), bias_final.astype(f32), col_keep, width_real
    )
    head_low = normed_hf.astype(bf16)
    projected = jnp.dot(head_low, w_embed, preferred_element_type=f32)
    inv_norm = lax.rsqrt(jnp.sum(projected * projected, axis=-1, keepdims=True) + NORM_EPS)
    embed_low = (projected * inv_norm).astype(bf16)
    own_all = lax.all_gather(embed_low, "dp", axis=0, tiled=True)
    others = swapped(own_all, "tower", 0)
    logit_mult = jnp.exp(logit_scale[0])
    similar = contract_cols(embed_low, others)
    logits = logit_mult * similar
    logit_top = jnp.max(logits, axis=-1, keepdims=True)
    logit_total = logit_top + jnp.log(jnp.sum(jnp.exp(logits - logit_top), axis=-1, keepdims=True))
    label_col = dp_index * samples + lax.broadcasted_iota(jnp.int32, (samples, 1), 0)
    label_hot = (lax.broadcasted_iota(jnp.int32, (samples, sample_total), 1) == label_col).astype(
        f32
    )
    diag_logit = jnp.sum(label_hot * logits, axis=-1, keepdims=True)
    loss_part = jnp.sum(logit_total - diag_logit) / (2.0 * sample_total)
    grad_logits = (jnp.exp(logits - logit_total) - label_hot) * 0.5
    scale_part = logit_mult * jnp.sum(grad_logits * similar)
    grad_sims = (logit_mult * grad_logits).astype(bf16)
    grad_own = jnp.dot(grad_sims, others, preferred_element_type=f32)
    grad_others = contract_rows(grad_sims, embed_low)
    sent_back = swapped(grad_others, "tower", 0)
    returned = lax.psum_scatter(sent_back, "dp", scatter_dimension=0, tiled=True)
    totals = lax.psum((loss_part, scale_part), ("tower", "dp"))
    grad_embed = grad_own + returned
    again = (
        lax.all_gather(ln1_gain[0], "dp", axis=0, tiled=True),
        lax.all_gather(qkv_weight[0], "dp", axis=0, tiled=True),
        lax.all_gather(out_weight[0], "dp", axis=0, tiled=True),
        lax.all_gather(ln2_gain[0], "dp", axis=0, tiled=True),
        lax.all_gather(fc_weight[0], "dp", axis=0, tiled=True),
        lax.all_gather(down_weight[0], "dp", axis=0, tiled=True),
        lax.all_gather(final_gain[0], "dp", axis=0, tiled=True),
        lax.all_gather(embed_weight[0], "dp", axis=0, tiled=True),
    )
    (
        back_gain_one,
        back_qkv,
        back_out,
        back_gain_two,
        back_fc,
        back_down,
        back_gain_final,
        back_embed,
    ) = again
    cross_term = jnp.sum(grad_embed * projected, axis=-1, keepdims=True)
    grad_proj = inv_norm * grad_embed - projected * inv_norm * inv_norm * inv_norm * cross_term
    grad_proj_low = grad_proj.astype(bf16)
    grad_head = contract_cols(grad_proj_low, back_embed)
    grad_pooled, d_gain_final, d_bias_final = masked_norm_back(
        grad_head, back_gain_final.astype(f32), norm_final, inv_final, col_keep, width_real
    )
    grad_rows = (pool_hot[:, :, None] * grad_pooled[:, None, :]).reshape(flat_rows, width_all)
    grad_branch_low = grad_rows.astype(bf16)
    d_down_b = column_sum(grad_branch_low)
    grad_act = contract_cols(grad_branch_low, back_down)
    grad_pre_low = (
        grad_act * (gate_sig + GELU_K * hidden_pre * gate_sig * (1.0 - gate_sig))
    ).astype(bf16)
    d_fc_b = column_sum(grad_pre_low)
    grad_norm_two = contract_cols(grad_pre_low, back_fc)
    grad_mid_norm, d_gain_two, d_bias_two = masked_norm_back(
        grad_norm_two, back_gain_two.astype(f32), norm_two, inv_two, col_keep, width_real
    )
    grad_middle = grad_rows + grad_mid_norm
    grad_attn_low = grad_middle.astype(bf16)
    d_out_b = column_sum(grad_attn_low)
    grad_mix_low = (
        contract_cols(grad_attn_low, back_out)
        .astype(bf16)
        .reshape(samples, seq_rows, head_count, HD)
    )
    probs_again = jnp.exp(masked_scores() - log_total)
    probs_low = probs_again.astype(bf16)
    grad_value = jnp.einsum("shqk,sqhd->skhd", probs_low, grad_mix_low, preferred_element_type=f32)
    grad_probs = jnp.einsum("sqhd,skhd->shqk", grad_mix_low, value_all, preferred_element_type=f32)
    grad_scores = probs_again * (
        grad_probs - jnp.sum(probs_again * grad_probs, axis=-1, keepdims=True)
    )
    grad_scores_low = grad_scores.astype(bf16)
    grad_query = (
        jnp.einsum("shqk,skhd->sqhd", grad_scores_low, key_all, preferred_element_type=f32)
        * score_mult
    )
    grad_key = (
        jnp.einsum("shqk,sqhd->skhd", grad_scores_low, query_all, preferred_element_type=f32)
        * score_mult
    )
    grad_qkv_low = (
        jnp.stack([grad_query, grad_key, grad_value], axis=2)
        .astype(bf16)
        .reshape(flat_rows, 3 * width_all)
    )
    d_qkv_w = contract_rows(normed_one, grad_qkv_low).reshape(width_all, 3, width_all)
    qkv_sums = column_sum(grad_qkv_low).reshape(3, width_all)
    d_qv_b = jnp.stack([qkv_sums[0], qkv_sums[2]])
    grad_norm_one = contract_cols(grad_qkv_low, back_qkv.reshape(width_all, 3 * width_all))
    grad_in_norm, d_gain_one, d_bias_one = masked_norm_back(
        grad_norm_one, back_gain_one.astype(f32), norm_one, inv_one, col_keep, width_real
    )
    tokens_grad = (grad_middle + grad_in_norm).reshape(1, samples, seq_rows, width_all)
    d_embed_w = contract_rows(head_low, grad_proj_low)
    d_down_w = contract_rows(act_low, grad_branch_low)
    d_fc_w = contract_rows(normed_two, grad_pre_low)
    d_out_w = contract_rows(head_mix_low, grad_attn_low)
    shares = (
        lax.psum_scatter(d_gain_one, "dp", scatter_dimension=0, tiled=True),
        lax.psum_scatter(d_bias_one, "dp", scatter_dimension=0, tiled=True),
        lax.psum_scatter(d_qkv_w, "dp", scatter_dimension=0, tiled=True),
        lax.psum_scatter(d_qv_b, "dp", scatter_dimension=1, tiled=True),
        lax.psum_scatter(d_out_w, "dp", scatter_dimension=0, tiled=True),
        lax.psum_scatter(d_out_b, "dp", scatter_dimension=0, tiled=True),
        lax.psum_scatter(d_gain_two, "dp", scatter_dimension=0, tiled=True),
        lax.psum_scatter(d_bias_two, "dp", scatter_dimension=0, tiled=True),
        lax.psum_scatter(d_fc_w, "dp", scatter_dimension=0, tiled=True),
        lax.psum_scatter(d_fc_b, "dp", scatter_dimension=0, tiled=True),
        lax.psum_scatter(d_down_w, "dp", scatter_dimension=0, tiled=True),
        lax.psum_scatter(d_down_b, "dp", scatter_dimension=0, tiled=True),
        lax.psum_scatter(d_gain_final, "dp", scatter_dimension=0, tiled=True),
        lax.psum_scatter(d_bias_final, "dp", scatter_dimension=0, tiled=True),
        lax.psum_scatter(d_embed_w, "dp", scatter_dimension=0, tiled=True),
    )
    results = list(shares)
    outputs = [item[None] for item in results]
    loss = totals[0].reshape(1)
    logit_scale_grad = totals[1].reshape(1)
    return (
        block_out,
        tokens_grad,
        loss,
        outputs[0],
        outputs[1],
        outputs[2],
        outputs[3],
        outputs[4],
        outputs[5],
        outputs[6],
        outputs[7],
        outputs[8],
        outputs[9],
        outputs[10],
        outputs[11],
        outputs[12],
        outputs[13],
        outputs[14],
        logit_scale_grad,
    )


RING_Z = (0, 1, 2, 3, 3, 2, 1, 0)
RING_Y = (0, 0, 0, 0, 1, 1, 1, 1)
ITEMS = 16
N = ITEMS * 8
F32 = jnp.float32
BF16 = jnp.bfloat16
ANY = pl.BlockSpec(memory_space=pl.ANY)
VMEM = pl.BlockSpec(memory_space=pltpu.VMEM)
SMEM = pl.BlockSpec(memory_space=pltpu.SMEM)
SCALE = float(HD) ** -0.5
PAYLOAD = 128


def call(kernel, name, ins, outs, scratch, flops=0, touched=0):
    return pl.pallas_call(
        kernel,
        name=name,
        out_shape=[jax.ShapeDtypeStruct(shape, dtype) for _, shape, dtype in outs],
        in_specs=[spec for spec, _ in ins],
        out_specs=[spec for spec, _, _ in outs],
        scratch_shapes=scratch,
        compiler_params=pltpu.CompilerParams(vmem_limit_bytes=67043328),
        cost_estimate=pl.CostEstimate(flops=flops, bytes_accessed=touched, transcendentals=0),
    )(*[item for _, item in ins])


def dot(left, right, left_dim=1, right_dim=0):
    return lax.dot_general(
        left, right, (((left_dim,), (right_dim,)), ((), ())), preferred_element_type=F32
    )


def aligned(index, size):
    return pl.multiple_of(index, size)


def owner_table(dp_index):
    core = dp_index % 2
    row = dp_index // 2 % 2
    depth = dp_index // 4
    place = jnp.where(row == 0, depth, 7 - depth)

    def chip(where):
        where = (where + 8) % 8
        z = jnp.where(where < 4, where, 7 - where)
        y = jnp.where(where < 4, 0, 1)
        return (z * 2 + y) * 2

    sign = jnp.where(core == 0, -1, 1)
    found = [chip(place)]
    for hop in range(1, 4):
        found += [chip(place + sign * hop), chip(place - sign * hop)]
    return found + [chip(place + 4) + core, chip(place + 4) + 1 - core]


class Place:
    def __init__(self, lengths):
        self.dp = lax.axis_index("dp")
        self.text = lax.axis_index("tower") == 1
        self.lengths = lengths
        self.keep = (
            lax.broadcasted_iota(jnp.int32, (1, DI), 1) < jnp.where(self.text, DT, DI)
        ).astype(F32)
        self.winv = jnp.where(self.text, 1.0 / DT, 1.0 / DI).astype(F32)

    def length(self, s):
        return jnp.where(self.text, self.lengths[s], IMG_ROWS)

    def pool(self, s):
        return jnp.where(self.text, self.lengths[s] - 1, 0)

    def column(self, pick):
        ids = lax.broadcasted_iota(jnp.int32, (1, 8, 1), 1)
        column = jnp.zeros((1, 8, 1), jnp.int32)
        for s in range(8):
            column = jnp.where(ids == s, pick(s), column)
        return column

    def either(self, path, image):
        @pl.when(self.text)
        def _():
            path(DT, 77)

        @pl.when(jnp.logical_not(self.text))
        def _():
            path(DI, image)

    def mine(self, visit):
        for owner in range(ITEMS):

            @pl.when(self.dp == owner)
            def _(owner=owner):
                visit(owner)


def copy(src, dst, sem):
    found = pltpu.make_async_copy(src, dst, sem)
    found.start()
    return found


def drain(dst, sem):
    pltpu.make_async_copy(dst, dst, sem).wait()


def fetch(owners, refs, row, rows, dst, sem):
    for owner, ref in zip(owners, refs):
        if len(ref.shape) == 3:
            copy(ref.at[:, pl.ds(row, rows), :], dst.at[pl.ds(owner, 2)], sem)
        else:
            copy(ref.at[pl.ds(row, rows), :], dst.at[owner], sem)


def embed_matrix(packed):
    tail = jnp.concatenate([packed[:, 0:16, EMB:DI], packed[:, 16:32, EMB:DI]], axis=2)
    return jnp.concatenate([packed[:, :, 0:EMB], tail], axis=1).reshape(DI, EMB)


def normalize(values, keep, winv):
    mean = jnp.sum(values, axis=-1, keepdims=True) * winv
    centred = (values - mean) * keep
    var = jnp.sum(centred * centred, axis=-1, keepdims=True) * winv
    inv = lax.rsqrt(var + EPS)
    return centred * inv, inv


def normalize_back(grad_out, gain, normed, inv, keep, winv):
    grad_normed = grad_out * gain
    mean_grad = jnp.sum(grad_normed, axis=-1, keepdims=True) * winv
    mean_cross = jnp.sum(grad_normed * normed, axis=-1, keepdims=True) * winv
    return keep * inv * (grad_normed - mean_grad - normed * mean_cross)


def row_sum(values):
    return jnp.sum(values, axis=0, keepdims=True)


def head_rows(rows):
    heads = lax.broadcasted_iota(jnp.int32, rows.shape, 1) // HD
    parts = [jnp.where(heads == head, rows, 0.0) for head in range(16)]
    return jnp.concatenate(parts, axis=0).astype(BF16)


def chunks(count, visit):
    @pl.loop(0, count // 14)
    def _(i):
        visit(i * 14, aligned(i * 112, 16), 14)

    if count % 14:
        at = count - count % 14
        visit(at, at * 8, count % 14)


def pack_first_kernel(lengths, qkv, tok, *rest):
    here = Place(lengths)
    vectors, (qv_bias, fc_bias, out) = rest[:8], rest[8:]
    out[0:144, :] = qkv[...]
    sub = lax.broadcasted_iota(jnp.int32, (8, DI), 0)
    pooled = jnp.zeros((8, DI), F32)
    for s in range(8):
        pooled = jnp.where(sub == s, tok[here.pool(s)].astype(F32), pooled)
    out[144:152, :] = pooled.astype(BF16)
    lane = lax.broadcasted_iota(jnp.int32, (1, DI), 1) // 48 == here.dp
    short = [v[...].astype(F32) for v in vectors]
    pair = qv_bias[...].astype(F32)
    short[2:2] = [pair[0:1], pair[1:2]]
    rows = [jnp.where(lane, jnp.concatenate([v] * ITEMS, axis=1), 0.0) for v in short]
    wide = lax.broadcasted_iota(jnp.int32, (1, 4 * DI), 1) // 192 == here.dp
    fc = jnp.where(wide, jnp.concatenate([fc_bias[...].astype(F32)] * ITEMS, axis=1), 0.0)
    rows += [fc[:, i * DI : (i + 1) * DI] for i in range(4)]
    row_id = lax.broadcasted_iota(jnp.int32, (16, DI), 0)
    small = jnp.zeros((16, DI), F32)
    for at, row in enumerate(rows):
        small = jnp.where(row_id == at, jnp.broadcast_to(row, (16, DI)), small)
    out[152:168, :] = small.astype(BF16)


def pack_first(lengths, qkv, tok, vectors, qv_bias, fc_bias):
    return call(
        pack_first_kernel,
        "pack_first",
        [(SMEM, lengths)] + [(VMEM, item) for item in (qkv, tok, *vectors, qv_bias, fc_bias)],
        [(VMEM, (168, DI), BF16)],
        [],
        touched=1_500_000,
    )[0]


def pack_rest_kernel(w_out, w_fc, w_emb, out):
    out[0:48, :] = w_out[...]
    out[48:80, 0:EMB] = w_emb[0:32, :]
    out[48:64, EMB:DI] = w_emb[32:48, 0:256]
    out[64:80, EMB:DI] = w_emb[32:48, 256:EMB]
    for block in range(4):
        out[80 + 48 * block : 128 + 48 * block, :] = w_fc[:, block * DI : (block + 1) * DI]


def pack_rest(w_out, w_fc, w_emb):
    return call(
        pack_rest_kernel,
        "pack_rest",
        [(VMEM, item) for item in (w_out, w_fc, w_emb)],
        [(VMEM, (272, DI), BF16)],
        [],
        touched=1_500_000,
    )[0]


def sample_limits(here):
    lane_sample = lax.broadcasted_iota(jnp.int32, (1, 128), 1) % 8
    limit = jnp.zeros((1, 128), jnp.int32)
    for s in range(8):
        limit = jnp.where(lane_sample == s, here.length(s), limit)
    return limit


def own_heads(tall, width):
    heads = lax.broadcasted_iota(jnp.int32, (8, width), 1) // HD
    total = jnp.zeros((8, width), F32)
    for head in range(width // HD):
        total = total + jnp.where(heads == head, tall[head * 8 : head * 8 + 8], 0.0)
    if width < DI:
        total = jnp.concatenate([total, jnp.zeros((8, DI - width), F32)], axis=1)
    return total


def tall_rows(rows):
    return jnp.concatenate([rows[:, i * 128 : (i + 1) * 128] for i in range(DI // 128)], axis=0)


def wide_rows(tall):
    tall = tall.astype(F32)
    return jnp.concatenate(
        [tall[:, i * 8 : i * 8 + 8, :].reshape(N, 128) for i in range(DI // 128)], axis=1
    )


def pooled_kernel(lengths, tok_hbm, *rest):
    first, outs, scratch = rest[:9], rest[9:18], rest[18:]
    keys_hbm, values_hbm, norm_hbm, normed_hbm, vec, pooled, q_own, probs_out, gv_out = outs
    weights, small, tok, normed, keys, values, norm_low, sems, ends = scratch
    here = Place(lengths)
    owners = owner_table(here.dp)
    tok_in = copy(tok_hbm, tok, sems.at[2])
    fetch(owners, first, 152, 16, small, sems.at[0])
    fetch(owners, first, 0, 144, weights, sems.at[1])
    keep, winv = here.keep, here.winv
    drain(small, sems.at[0])
    vec[...] = jnp.sum(small[...].astype(F32), axis=0)
    limit = sample_limits(here)
    tok_in.wait()
    sub = lax.broadcasted_iota(jnp.int32, (8, DI), 0)
    picked = jnp.zeros((8, DI), F32)
    for s in range(8):
        picked = jnp.where(sub == s, tok[here.pool(s)].astype(F32), picked)
    pooled_norm, _ = normalize(picked, keep, winv)
    pooled_normed = (pooled_norm * vec[0:1, :] + vec[1:2, :]).astype(BF16)

    def norm_chunk(position, row, count):
        x = tok[pl.ds(position, count)].astype(F32).reshape(count * 8, DI)
        norm, _ = normalize(x, keep, winv)
        norm_low[pl.ds(row, count * 8), :] = norm.astype(BF16)
        normed[pl.ds(row, count * 8), :] = (norm * vec[0:1, :] + vec[1:2, :]).astype(BF16)

    def path(width, count):
        rows = count * 8
        chunks(count, norm_chunk)
        saved = [copy(norm_low, norm_hbm, ends.at[0]), copy(normed, normed_hbm, ends.at[1])]
        drain(weights, sems.at[1])
        for third, low, bias in ((1, keys, None), (2, values, 3)):

            @pl.loop(0, width // 256)
            def _(j, third=third, low=low, bias=bias):
                lanes = pl.ds(aligned(j * 256, 256), 256)
                weight = weights[:, third * 48 : third * 48 + 48, lanes].reshape(DI, 256)
                prod = dot(normed[0:rows, 0:width], weight[0:width])
                if bias is not None:
                    prod = prod + vec[bias : bias + 1, lanes]
                low[0:rows, lanes] = prod.astype(BF16)

        saved += [copy(keys, keys_hbm, ends.at[2]), copy(values, values_hbm, ends.at[3])]
        query = dot(pooled_normed, weights[:, 0:48, :].reshape(DI, DI)) + vec[2:3, :]
        query = query.astype(BF16).astype(F32)
        q_own[...] = query
        q_rows = head_rows(query)
        raw = dot(keys[0:rows, 0:width], q_rows[:, 0:width], 1, 1) * SCALE
        row = lax.broadcasted_iota(jnp.int32, (rows, 128), 0)
        lane = lax.broadcasted_iota(jnp.int32, (rows, 128), 1)
        valid = (lane % 8 == row % 8) & (row // 8 < limit) & (lane < width // 8)
        raw = jnp.where(valid, raw, NEG_FILL)
        terms = jnp.where(valid, jnp.exp(raw - jnp.max(raw, axis=0, keepdims=True)), 0.0)
        probs = terms / jnp.maximum(row_sum(terms), 1e-30)
        low_probs = probs.astype(BF16)
        probs_out[0:rows, :] = probs
        gv_out[0:rows, :] = low_probs
        mixed = own_heads(dot(low_probs, values[0:rows, 0:width], 0, 0), width)
        tall = tall_rows(mixed).astype(BF16)
        for owner in range(ITEMS):
            pooled[owner] = tall
        for item in saved:
            item.wait()

    here.either(path, 56)


def attend_pooled(lengths, tok, first):
    rows = tok.shape[0] * tok.shape[1]
    return call(
        pooled_kernel,
        "attend_pooled",
        [(SMEM, lengths), (ANY, tok)] + [(ANY, r) for r in first],
        [(ANY, (rows, DI), BF16)] * 4
        + [
            (VMEM, (16, DI), F32),
            (VMEM, (ITEMS, 48, 128), BF16),
            (VMEM, (8, DI), F32),
            (VMEM, (rows, 128), F32),
            (VMEM, (rows, 128), BF16),
        ],
        [
            pltpu.VMEM((ITEMS, 144, DI), BF16),
            pltpu.VMEM((ITEMS, 16, DI), BF16),
            pltpu.VMEM(tok.shape, BF16),
            pltpu.VMEM((rows, DI), BF16),
            pltpu.VMEM((rows, DI), BF16),
            pltpu.VMEM((rows, DI), BF16),
            pltpu.VMEM((rows, DI), BF16),
            pltpu.SemaphoreType.DMA((3,)),
            pltpu.SemaphoreType.DMA((4,)),
        ],
        flops=7_000_000_000,
        touched=10_000_000,
    )


def attend_kernel(lengths, vec, gv, normed_hbm, keys_hbm, values_hbm, norm_hbm, *rest):
    first, (mixed_hbm, z_value), scratch = rest[:9], rest[9:11], rest[11:]
    weights, normed, keys, values, norm_low, mixed, qf, kf, vf, mf, sems = scratch
    here = Place(lengths)
    owners = owner_table(here.dp)
    fetch(owners, first, 0, 48, weights, sems.at[0])
    early = [
        copy(src, dst, sems.at[1 + i])
        for i, (src, dst) in enumerate(
            ((normed_hbm, normed), (keys_hbm, keys), (values_hbm, values), (norm_hbm, norm_low))
        )
    ]
    drain(weights, sems.at[0])
    early[0].wait()
    early[1].wait()
    early[2].wait()

    def path(width, count):
        rows = count * 8
        span = 80 if count == 77 else count
        if span > count:
            for dst in (qf, kf, vf):
                dst[:, rows : span * 8, :] = jnp.zeros((6, span * 8 - rows, 128), F32)

        @pl.loop(0, width // 256)
        def _(j):
            lanes = pl.ds(aligned(j * 256, 256), 256)
            weight = weights[:, :, lanes].reshape(DI, 256)
            prod = dot(normed[0:rows, 0:width], weight[0:width]) + vec[2:3, lanes]
            prod = prod.astype(BF16).astype(F32) * SCALE
            for dst, item in ((qf, prod), (kf, keys[0:rows, lanes].astype(F32)), (vf, values[0:rows, lanes].astype(F32))):
                dst[2 * j, 0:rows, :] = item[:, 0:128]
                dst[2 * j + 1, 0:rows, :] = item[:, 128:256]

        key_pos = lax.broadcasted_iota(jnp.int32, (span, 2 * span), 0)
        query_pos = lax.broadcasted_iota(jnp.int32, (span, 2 * span), 1) % span
        low_half = lax.broadcasted_iota(jnp.int32, (span, 128), 1) < HD

        @pl.loop(0, 8)
        def _(s):
            at = pl.ds(s, span, stride=8)
            allowed = key_pos < here.length(s)
            if width == DT:
                allowed = allowed & (key_pos <= query_pos)
            pairs = range(width // 128)
            raws = []
            for pair in pairs:
                query, key = qf.at[pair][at, :], kf.at[pair][at, :].astype(BF16)
                spread = [jnp.where(low_half, query, 0.0), jnp.where(low_half, 0.0, query)]
                spread = jnp.concatenate(spread, axis=0).astype(BF16)
                raws.append(dot(key, spread, 1, 1))
            probs = []
            for raw in raws:
                raw = jnp.where(allowed, raw, NEG_FILL)
                terms = jnp.exp(raw - jnp.max(raw, axis=0, keepdims=True))
                probs.append((terms / jnp.sum(terms, axis=0, keepdims=True)).astype(BF16))
            for pair in pairs:
                out = dot(probs[pair], vf.at[pair][at, :].astype(BF16), 0, 0)
                mf.at[pair][at, :] = jnp.where(low_half, out[0:span], out[span : 2 * span])

        stored = []
        for i in range(width // 128):
            lanes = pl.ds(128 * i, 128)
            mixed[0:rows, lanes] = mf[i, 0:rows, :].astype(BF16)
            stored.append(copy(mixed.at[0:rows, lanes], mixed_hbm.at[0:rows, lanes], sems.at[5 + i]))
        early[3].wait()
        z_value[...] = pltpu.roll(dot(norm_low[0:rows, :], gv[0:rows, :], 0, 0), 96, 1).astype(BF16)
        for item in stored:
            item.wait()

    here.either(path, 56)


def attend(lengths, vec, gv, normed, keys, values, norm_low, first):
    rows = keys.shape[0]
    high = rows + 24
    return call(
        attend_kernel,
        "attend",
        [(SMEM, lengths), (VMEM, vec), (VMEM, gv)]
        + [(ANY, r) for r in (normed, keys, values, norm_low, *first)],
        [(ANY, (rows, DI), BF16), (VMEM, (DI, 128), BF16)],
        [
            pltpu.VMEM((ITEMS, 48, DI), BF16),
            pltpu.VMEM((rows, DI), BF16),
            pltpu.VMEM((rows, DI), BF16),
            pltpu.VMEM((rows, DI), BF16),
            pltpu.VMEM((rows, DI), BF16),
            pltpu.VMEM((rows, DI), BF16),
            pltpu.VMEM((6, high, 128), F32),
            pltpu.VMEM((6, high, 128), F32),
            pltpu.VMEM((6, high, 128), F32),
            pltpu.VMEM((6, high, 128), F32),
            pltpu.SemaphoreType.DMA((11,)),
        ],
        flops=9_000_000_000,
        touched=10_000_000,
    )


def forward_kernel(lengths, vec, mixes, *rest):
    first, second, down = rest[:9], rest[9:18], rest[18:27]
    outs, scratch = rest[27:38], rest[38:]
    (e_out, proj_out, normf_out, invf_out, norm2_out, inv2_out, slope_out, n2_sl, mix_sl, head_sl,
     act_sl) = outs
    w_out, w_fc, w_down, w_emb, xs, mix, n2, act, head_all, sems = scratch
    here = Place(lengths)
    owners = owner_table(here.dp)
    fetch(owners, second, 0, 48, w_out, sems.at[1])
    fetch(owners, first, 144, 8, xs, sems.at[0])
    fetch(owners, second, 80, 192, w_fc, sems.at[2])
    keep, winv = here.keep, here.winv
    mix[...] = wide_rows(mixes[...]).astype(BF16)
    drain(w_out, sems.at[1])
    drain(xs, sems.at[0])
    fetch(owners, down, 0, 192, w_down, sems.at[3])
    fetch(owners, second, 48, 32, w_emb, sems.at[4])
    stream = xs[...].astype(F32).reshape(N, DI)
    middle = stream + dot(mix[...], w_out[...].reshape(DI, DI)) + vec[4:5, :]
    norm2, inv2 = normalize(middle, keep, winv)
    n2[...] = (norm2 * vec[5:6, :] + vec[6:7, :]).astype(BF16)
    norm2_out[...] = norm2
    inv2_out[...] = jnp.broadcast_to(inv2, (N, 128))
    drain(w_fc, sems.at[2])
    for block in range(4):
        lanes = pl.ds(block * DI, DI)
        weight = w_fc[:, block * 48 : block * 48 + 48, :].reshape(DI, DI)
        pre = dot(n2[...], weight) + vec[10 + block : 11 + block, :]
        gate = jax.nn.sigmoid(GELU_K * pre)
        act[:, lanes] = (pre * gate).astype(BF16)
        slope_out[:, lanes] = gate + GELU_K * pre * gate * (1.0 - gate)

    drain(w_down, sems.at[3])
    last = middle + dot(act[...], w_down[...].reshape(4 * DI, DI)) + vec[7:8, :]
    normf, invf = normalize(last, keep, winv)
    normf_out[...] = normf
    invf_out[...] = jnp.broadcast_to(invf, (N, 128))
    head_all[...] = (normf * vec[8:9, :] + vec[9:10, :]).astype(BF16)
    drain(w_emb, sems.at[4])
    proj = dot(head_all[...], embed_matrix(w_emb[...]))
    proj_out[...] = proj
    scale = lax.rsqrt(jnp.sum(proj * proj, axis=-1, keepdims=True) + NORM_EPS)
    e_out[...] = (proj * scale).astype(BF16)

    def mine(owner):
        lanes = slice(owner * 48, owner * 48 + 48)
        n2_sl[...] = n2[:, lanes]
        mix_sl[...] = mix[:, lanes]
        head_sl[...] = head_all[:, lanes]
        act_sl[...] = act[:, owner * 192 : owner * 192 + 192]

    here.mine(mine)


def pooled_forward(lengths, vec, mixes, first, second, down):
    return call(
        forward_kernel,
        "pooled_forward",
        [(SMEM, lengths), (VMEM, vec), (VMEM, mixes)] + [(ANY, r) for r in (*first, *second, *down)],
        [
            (VMEM, (N, EMB), BF16),
            (VMEM, (N, EMB), F32),
            (VMEM, (N, DI), F32),
            (VMEM, (N, 128), F32),
            (VMEM, (N, DI), F32),
            (VMEM, (N, 128), F32),
            (VMEM, (N, 4 * DI), F32),
            (VMEM, (N, 48), BF16),
            (VMEM, (N, 48), BF16),
            (VMEM, (N, 48), BF16),
            (VMEM, (N, 192), BF16),
        ],
        [
            pltpu.VMEM((ITEMS, 48, DI), BF16),
            pltpu.VMEM((ITEMS, 192, DI), BF16),
            pltpu.VMEM((ITEMS, 192, DI), BF16),
            pltpu.VMEM((ITEMS, 32, DI), BF16),
            pltpu.VMEM((ITEMS, 8, DI), BF16),
            pltpu.VMEM((N, DI), BF16),
            pltpu.VMEM((N, DI), BF16),
            pltpu.VMEM((N, 4 * DI), BF16),
            pltpu.VMEM((N, DI), BF16),
            pltpu.SemaphoreType.DMA((5,)),
        ],
        flops=11_000_000_000,
        touched=16_000_000,
    )


def middle_kernel(lengths, tok_hbm, vec, mixed_hbm, *rest):
    second = rest[:9]
    (n2_hbm, middle_hbm), scratch = rest[9:11], rest[11:]
    w_out, middle, tok, mixed, n2, sems = scratch
    here = Place(lengths)
    owners = owner_table(here.dp)
    rows_in = copy(mixed_hbm, mixed, sems.at[1])
    fetch(owners, second, 0, 48, w_out, sems.at[0])
    tok_in = copy(tok_hbm, tok, sems.at[2])
    keep, winv = here.keep, here.winv
    rows_in.wait()
    drain(w_out, sems.at[0])

    def norm_chunk(position, row, count):
        at = pl.ds(row, count * 8)
        total = middle[at, :] + tok[pl.ds(position, count)].astype(F32).reshape(count * 8, DI)
        middle[at, :] = total
        norm, _ = normalize(total, keep, winv)
        n2[at, :] = (norm * vec[5:6, :] + vec[6:7, :]).astype(BF16)
        copy(middle.at[at, :], middle_hbm.at[at, :], sems.at[3])
        copy(n2.at[at, :], n2_hbm.at[at, :], sems.at[4])

    def path(width, count):
        rows = count * 8

        @pl.loop(0, width // 256)
        def _(j):
            lanes = pl.ds(aligned(j * 256, 256), 256)
            weight = w_out[:, :, lanes].reshape(DI, 256)[0:width]
            middle[0:rows, lanes] = dot(mixed[0:rows, 0:width], weight) + vec[4:5, lanes]

        if width < DI:
            middle[0:rows, width:DI] = jnp.zeros((rows, DI - width), F32)
        tok_in.wait()
        chunks(count, norm_chunk)
        drain(middle.at[pl.ds(0, rows), :], sems.at[3])
        drain(n2.at[pl.ds(0, rows), :], sems.at[4])

    here.either(path, 56)


def middle_part(lengths, tok, vec, mixed, second):
    rows = mixed.shape[0]
    return call(
        middle_kernel,
        "middle_part",
        [(SMEM, lengths), (ANY, tok), (VMEM, vec), (ANY, mixed)] + [(ANY, r) for r in second],
        [(ANY, (rows, DI), BF16), (ANY, (rows, DI), F32)],
        [
            pltpu.VMEM((ITEMS, 48, DI), BF16),
            pltpu.VMEM((rows, DI), F32),
            pltpu.VMEM(tok.shape, BF16),
            pltpu.VMEM((rows, DI), BF16),
            pltpu.VMEM((rows, DI), BF16),
            pltpu.SemaphoreType.DMA((5,)),
        ],
        flops=5_000_000_000,
        touched=8_000_000,
    )


def one_direction(left, right, mult):
    sims = dot(left, right, 1, 1)
    logits = mult * sims
    top = jnp.max(logits, axis=-1, keepdims=True)
    total = top + jnp.log(jnp.sum(jnp.exp(logits - top), axis=-1, keepdims=True))
    count = sims.shape[0]
    eye = lax.broadcasted_iota(jnp.int32, (count, count), 0) == lax.broadcasted_iota(
        jnp.int32, (count, count), 1
    )
    hot = eye.astype(F32)
    lost = jnp.sum(total - jnp.sum(hot * logits, axis=-1, keepdims=True), axis=0, keepdims=True)
    grad = (jnp.exp(logits - total) - hot) * 0.5
    scale = jnp.sum(jnp.sum(grad * sims, axis=-1, keepdims=True), axis=0, keepdims=True)
    return lost, scale, mult * grad


def pack_payload(payload, z_key, z_value, sum_key, sum_value, grad_q):
    lane = lax.broadcasted_iota(jnp.int32, (1, 128), 1)
    upper = jnp.where(lane < 96, z_key, z_value).astype(BF16)
    blocks = [grad_q[:, i * 128 : (i + 1) * 128] for i in range(6)]
    beside = jnp.concatenate(
        [half for block in blocks[:3] for half in (pltpu.roll(block, 64, 1), block)], axis=0
    )
    key_high = sum_key.astype(BF16).astype(F32)
    value_high = sum_value.astype(BF16).astype(F32)
    row_id = lax.broadcasted_iota(jnp.int32, (8, 128), 0)
    sums = jnp.zeros((8, 128), F32)
    for at, value in enumerate((key_high, sum_key - key_high, value_high, sum_value - value_high)):
        sums = jnp.where(row_id == at, jnp.broadcast_to(value, (8, 128)), sums)
    last = jnp.concatenate([*blocks[3:], sums], axis=0).astype(BF16)
    for owner in range(ITEMS):
        base, rows = owner * PAYLOAD, slice(owner * 48, owner * 48 + 48)
        payload[base : base + 48, :] = upper[rows]
        payload[base + 48 : base + 96, :] = jnp.where(lane < 64, z_value[rows], beside).astype(BF16)
        payload[base + 96 : base + 128, :] = last


def chain_kernel(lengths, log_mult, e_own_ref, e_oth_ref, vec, head_sl, act_sl, n2_sl, mix_sl, *rest):
    (proj_hbm, normf_hbm, invf_hbm, norm2_hbm, inv2_hbm, slope_hbm, keys_hbm, values_hbm, norm_hbm, probs_hbm,
     gv_hbm, z_hbm), rest = rest[:12], rest[12:]
    second, down = rest[:9], rest[9:18]
    outs, scratch = rest[18:37], rest[37:]
    (loss_out, scale_out, d_emb_hbm, d_down_hbm, d_fc_hbm, d_out_hbm, g_final, b_final, b_down, g_two, b_two, b_out, b_fc,
     mid_own, gm_out, gm_own, payload, gk_out, gq_out) = outs
    (w_out, w_fc, w_down, w_emb, gpre, mid_all, proj_v, normf_v, invf_v, norm2_v, inv2_v, slope, keys,
     values, norm_low, probs_v, gv_v, z_v, vec_grads, fcb_grads, d_emb, d_down, d_fc, d_out, sems, ins, ends) = scratch
    here = Place(lengths)
    owners = owner_table(here.dp)
    early = [
        copy(src, dst, ins.at[i])
        for i, (src, dst) in enumerate(
            ((proj_hbm, proj_v), (normf_hbm, normf_v), (invf_hbm, invf_v))
        )
    ]
    fetch(owners, second, 48, 32, w_emb, sems.at[0])
    fetch(owners, down, 0, 192, w_down, sems.at[1])
    slope_in = copy(slope_hbm, slope, ins.at[3])
    fetch(owners, second, 80, 192, w_fc, sems.at[2])
    later = [copy(norm2_hbm, norm2_v, ins.at[4]), copy(inv2_hbm, inv2_v, ins.at[5])]
    fetch(owners, second, 0, 48, w_out, sems.at[3])
    last = [
        copy(src, dst, ins.at[6 + i])
        for i, (src, dst) in enumerate(
            ((keys_hbm, keys), (values_hbm, values), (norm_hbm, norm_low), (probs_hbm, probs_v),
             (gv_hbm, gv_v), (z_hbm, z_v))
        )
    ]
    keep, winv = here.keep, here.winv
    text = here.text.astype(F32)
    mult = jnp.exp(jnp.full((1, 128), log_mult[0], F32))[:, 0:1]
    own, oth = e_own_ref[...].astype(F32), e_oth_ref[...].astype(F32)
    e_img = (own * (1.0 - text) + oth * text).astype(BF16)
    e_txt = (oth * (1.0 - text) + own * text).astype(BF16)
    lost_img, scale_img, grad_img = one_direction(e_img, e_txt, mult)
    lost_txt, scale_txt, grad_txt = one_direction(e_txt, e_img, mult)
    loss_out[...] = (lost_img + lost_txt) / (2.0 * N)
    scale_out[...] = mult * (scale_img + scale_txt)
    grad_own = (grad_img * (1.0 - text) + grad_txt * text).astype(BF16)
    grad_oth = (grad_txt * (1.0 - text) + grad_img * text).astype(BF16)
    oth_low = e_oth_ref[...]
    grad_e = dot(grad_own, oth_low) + dot(grad_oth, oth_low, 0, 0)
    for item in early:
        item.wait()
    drain(w_emb, sems.at[0])
    proj = proj_v[...]
    r = lax.rsqrt(jnp.sum(proj * proj, axis=-1, keepdims=True) + NORM_EPS)
    cross = jnp.sum(grad_e * proj, axis=-1, keepdims=True)
    grad_proj = (r * grad_e - proj * (r * r * r) * cross).astype(BF16)
    grad_head = dot(grad_proj, embed_matrix(w_emb[...]), 1, 1)
    normf = normf_v[...]
    grad_y = normalize_back(grad_head, vec[8:9, :], normf, invf_v[:, 0:1], keep, winv)
    branch = grad_y.astype(BF16)
    d_emb[...] = dot(head_sl[...], grad_proj, 0, 0)
    stored = [copy(d_emb, d_emb_hbm, ends.at[0])]
    vec_grads[0:1, :] = row_sum(grad_head * normf)
    vec_grads[1:2, :] = row_sum(grad_head)
    vec_grads[2:3, :] = row_sum(branch.astype(F32))
    d_down[...] = dot(act_sl[...], branch, 0, 0)
    stored.append(copy(d_down, d_down_hbm, ends.at[1]))
    drain(w_down, sems.at[1])
    slope_in.wait()
    for block in range(4):
        lanes = pl.ds(block * DI, DI)
        back = dot(branch, w_down[block * 4 : block * 4 + 4].reshape(DI, DI), 1, 1)
        low = (back * slope[:, lanes]).astype(BF16)
        gpre[:, lanes] = low
        fcb_grads[:, lanes] = jnp.broadcast_to(row_sum(low.astype(F32)), (8, DI))

    drain(w_fc, sems.at[2])
    grad_n2 = jnp.zeros((N, DI), F32)
    for block in range(4):
        weight = w_fc[:, block * 48 : block * 48 + 48, :].reshape(DI, DI)
        grad_n2 = grad_n2 + dot(gpre[:, block * DI : block * DI + DI], weight, 1, 1)
    for item in later:
        item.wait()
    norm2 = norm2_v[...]
    vec_grads[3:4, :] = row_sum(grad_n2 * norm2)
    vec_grads[4:5, :] = row_sum(grad_n2)
    grad_mid = grad_y + normalize_back(grad_n2, vec[5:6, :], norm2, inv2_v[:, 0:1], keep, winv)
    mid_all[...] = grad_mid
    own_rows = pl.ds(aligned(here.dp * 8, 8), 8)
    mid_own[...] = mid_all[own_rows, :]
    attn = grad_mid.astype(BF16)
    vec_grads[5:6, :] = row_sum(attn.astype(F32))
    drain(w_out, sems.at[3])
    gm_out[...] = dot(attn, w_out[...].reshape(DI, DI), 1, 1).astype(BF16).astype(F32)
    gm_own[...] = gm_out[own_rows, :]

    @pl.loop(0, 6)
    def _(j):
        lanes = pl.ds(aligned(j * 512, 512), 512)
        d_fc[:, lanes] = dot(n2_sl[...], gpre[:, lanes], 0, 0)

    d_out[...] = dot(mix_sl[...], attn, 0, 0)
    stored += [copy(d_fc, d_fc_hbm, ends.at[2]), copy(d_out, d_out_hbm, ends.at[3])]

    def mine(owner):
        lanes = slice(owner * 48, owner * 48 + 48)
        for at, dst in enumerate((g_final, b_final, b_down, g_two, b_two, b_out)):
            dst[...] = vec_grads[at : at + 1, lanes]
        b_fc[...] = fcb_grads[0:1, owner * 192 : owner * 192 + 192]

    here.mine(mine)
    for item in last:
        item.wait()
    m_rows = head_rows(gm_own[...])

    def path(width, count):
        rows = count * 8
        probs = probs_v[0:rows, :]
        grad_probs = dot(values[0:rows, 0:width], m_rows[:, 0:width], 1, 1)
        gk = (probs * (grad_probs - row_sum(probs * grad_probs))).astype(BF16)
        gv = gv_v[0:rows, :]
        gk_out[0:rows, :] = gk
        gq_low = own_heads(dot(gk, keys[0:rows, 0:width], 0, 0) * SCALE, width).astype(BF16)
        gq_out[...] = gq_low
        z_key = dot(norm_low[0:rows, :], gk, 0, 0)
        pack_payload(
            payload,
            z_key,
            z_v[...].astype(F32),
            row_sum(gk.astype(F32)),
            pltpu.roll(jnp.broadcast_to(row_sum(gv.astype(F32)), (8, 128)), 96, 1)[0:1],
            gq_low.astype(F32),
        )

    here.either(path, 56)
    for item in stored:
        item.wait()


def chain(lengths, log_mult, e_own, e_oth, vec, slices, saved, second, down):
    rows = saved[-2].shape[0]
    return call(
        chain_kernel,
        "chain",
        [(SMEM, lengths), (SMEM, log_mult)]
        + [(VMEM, item) for item in (e_own, e_oth, vec, *slices)]
        + [(ANY, r) for r in (*saved, *second, *down)],
        [
            (VMEM, (1, 1), F32),
            (VMEM, (1, 1), F32),
            (ANY, (48, EMB), F32),
            (ANY, (192, DI), F32),
            (ANY, (48, 4 * DI), F32),
            (ANY, (48, DI), F32),
        ]
        + [(VMEM, (1, 48), F32)] * 6
        + [
            (VMEM, (1, 192), F32),
            (VMEM, (8, DI), F32),
            (VMEM, (N, DI), F32),
            (VMEM, (8, DI), F32),
            (VMEM, (ITEMS * PAYLOAD, 128), BF16),
            (VMEM, (rows, 128), BF16),
            (VMEM, (8, DI), BF16),
        ],
        [
            pltpu.VMEM((ITEMS, 48, DI), BF16),
            pltpu.VMEM((ITEMS, 192, DI), BF16),
            pltpu.VMEM((ITEMS, 192, DI), BF16),
            pltpu.VMEM((ITEMS, 32, DI), BF16),
            pltpu.VMEM((N, 4 * DI), BF16),
            pltpu.VMEM((N, DI), F32),
            pltpu.VMEM((N, EMB), F32),
            pltpu.VMEM((N, DI), F32),
            pltpu.VMEM((N, 128), F32),
            pltpu.VMEM((N, DI), F32),
            pltpu.VMEM((N, 128), F32),
            pltpu.VMEM((N, 4 * DI), F32),
            pltpu.VMEM((rows, DI), BF16),
            pltpu.VMEM((rows, DI), BF16),
            pltpu.VMEM((rows, DI), BF16),
            pltpu.VMEM((rows, 128), F32),
            pltpu.VMEM((rows, 128), BF16),
            pltpu.VMEM((DI, 128), BF16),
            pltpu.VMEM((8, DI), F32),
            pltpu.VMEM((8, 4 * DI), F32),
            pltpu.VMEM((48, EMB), F32),
            pltpu.VMEM((192, DI), F32),
            pltpu.VMEM((48, 4 * DI), F32),
            pltpu.VMEM((48, DI), F32),
            pltpu.SemaphoreType.DMA((4,)),
            pltpu.SemaphoreType.DMA((12,)),
            pltpu.SemaphoreType.DMA((4,)),
        ],
        flops=15_000_000_000,
        touched=20_000_000,
    )


def close_kernel(lengths, tok, vec, gk, gv, q_own, gm_own, gq, mid_own, n2_hbm, middle_hbm, *rest):
    first, second, down = rest[:9], rest[9:18], rest[18:27]
    (block_out, out_hbm, q_out, norm_sl), scratch = rest[27:31], rest[31:]
    weights, w_fc, w_down, n2, act, middle, acc, xs, norm1_all, out, sems = scratch
    here = Place(lengths)
    owners = owner_table(here.dp)
    fetch(owners, first, 0, 144, weights, sems.at[0])
    fetch(owners, first, 144, 8, xs, sems.at[5])
    ready = copy(n2_hbm, n2, sems.at[1])
    fetch(owners, second, 80, 192, w_fc, sems.at[4])
    fetch(owners, down, 0, 192, w_down, sems.at[3])
    early = [copy(middle_hbm, middle, sems.at[2])]
    keep, winv = here.keep, here.winv
    q_rows = head_rows(q_own[...])
    m_rows = head_rows(gm_own[...])
    pool = here.column(here.pool)
    length = here.column(here.length)
    all_rows = out.shape[0]
    drain(weights, sems.at[0])
    u_key = (dot(q_rows, weights[:, 48:96, :].reshape(DI, DI), 1, 1) * SCALE).astype(BF16)
    u_value = dot(m_rows, weights[:, 96:144, :].reshape(DI, DI), 1, 1).astype(BF16)
    u_query = dot(gq[...], weights[:, 0:48, :].reshape(DI, DI), 1, 1)

    def path(width, count):
        rows = count * 8
        acc[0:rows, :] = dot(gk[0:rows, :], u_key) + dot(gv[0:rows, :], u_value)

        def back_chunk(position, row, count):
            at = pl.ds(row, count * 8)
            hit = lax.broadcasted_iota(jnp.int32, (count, 8, DI), 0) + position == pool
            norm, inv = normalize(tok[pl.ds(position, count)].astype(F32).reshape(count * 8, DI), keep, winv)
            total = acc[at, :] + jnp.where(hit, u_query[None], 0.0).reshape(count * 8, DI)
            back = normalize_back(total, vec[0:1, :], norm, inv, keep, winv)
            out[at, :] = back + jnp.where(hit, mid_own[...][None], 0.0).reshape(count * 8, DI)

        if rows < all_rows:
            out[rows:all_rows, :] = jnp.zeros((all_rows - rows, DI), F32)
        chunks(count, back_chunk)
        stored = copy(out, out_hbm, sems.at[6])
        short = count if width == DT else IMG_ROWS
        rows = short * 8
        ready.wait()
        drain(w_fc, sems.at[4])
        for block in range(4):

            @pl.loop(0, 3 if width == DI else (3, 3, 2, 0)[block])
            def _(j, block=block):
                lanes = pl.ds(aligned(j * 256, 256), 256)
                wide = pl.ds(aligned(block * DI + j * 256, 256), 256)
                weight = w_fc[:, block * 48 : block * 48 + 48, lanes].reshape(DI, 256)[0:width]
                pre = dot(n2[0:rows, 0:width], weight) + vec[10 + block : 11 + block, lanes]
                act[0:rows, wide] = (pre * jax.nn.sigmoid(GELU_K * pre)).astype(BF16)

        for item in early:
            item.wait()
        drain(w_down, sems.at[3])

        @pl.loop(0, width // 256)
        def _(j):
            lanes = pl.ds(aligned(j * 256, 256), 256)
            weight = w_down[:, :, lanes].reshape(4 * DI, 256)[0 : 4 * width]
            total = dot(act[0:rows, 0 : 4 * width], weight)
            total = (total + vec[7:8, lanes] + middle[0:rows, lanes]).reshape(short, 8, 256)
            where = lax.broadcasted_iota(jnp.int32, (short, 8, 256), 0)
            block_out[0:rows, lanes] = jnp.where(where < length, total, 0.0).reshape(rows, 256).astype(BF16)

        if width < DI:
            block_out[:, width:DI] = jnp.zeros((all_rows, DI - width), BF16)
        if rows < all_rows:
            block_out[rows:all_rows, :] = jnp.zeros((all_rows - rows, DI), BF16)
        stored.wait()

    here.either(path, 56)
    drain(xs, sems.at[5])
    stream = xs[...].astype(F32).reshape(N, DI)
    norm1, _ = normalize(stream, keep, winv)
    norm1_all[...] = norm1.astype(BF16)
    n1 = (norm1 * vec[0:1, :] + vec[1:2, :]).astype(BF16)
    q_out[...] = (dot(n1, weights[:, 0:48, :].reshape(DI, DI)) + vec[2:3, :]).astype(BF16).astype(F32)

    def mine(owner):
        norm_sl[...] = norm1_all[:, owner * 48 : owner * 48 + 48]

    here.mine(mine)


def close(lengths, tok, vec, gk, gv, q_own, gm_own, gq, mid_own, n2, middle, first, second, down):
    rows = tok.shape[0] * tok.shape[1]
    return call(
        close_kernel,
        "close",
        [(SMEM, lengths)]
        + [(VMEM, item) for item in (tok, vec, gk, gv, q_own, gm_own, gq, mid_own)]
        + [(ANY, r) for r in (n2, middle, *first, *second, *down)],
        [(VMEM, (rows, DI), BF16), (ANY, (rows, DI), F32), (VMEM, (N, DI), F32), (VMEM, (N, 48), BF16)],
        [
            pltpu.VMEM((ITEMS, 144, DI), BF16),
            pltpu.VMEM((ITEMS, 192, DI), BF16),
            pltpu.VMEM((ITEMS, 192, DI), BF16),
            pltpu.VMEM((rows, DI), BF16),
            pltpu.VMEM((rows, 4 * DI), BF16),
            pltpu.VMEM((rows, DI), F32),
            pltpu.VMEM((rows, DI), F32),
            pltpu.VMEM((ITEMS, 8, DI), BF16),
            pltpu.VMEM((N, DI), BF16),
            pltpu.VMEM((rows, DI), F32),
            pltpu.SemaphoreType.DMA((7,)),
        ],
        flops=17_000_000_000,
        touched=18_000_000,
    )


def shard_kernel(got, q_all, gm_all, norm_sl, w_own, gain, bias, d_qkv, g_one, b_one, qv_out, by_keys, by_values, product):
    dp = lax.axis_index("dp")

    low_half = lax.broadcasted_iota(jnp.int32, (N, 128), 1) < HD

    for j in range(ITEMS):
        found = got[j].astype(F32)
        upper = jnp.concatenate([found[0:48], found[120:128]], axis=0).T
        lower = jnp.concatenate([found[48:96], found[120:128]], axis=0).T
        by_keys[j] = upper[0:96]
        by_values[j, 0:32, :] = upper[96:128]
        by_values[j, 32:96, :] = lower[0:64]

    def moments(turned, source):
        for pair in range(DI // 128):
            lanes = slice(pair * 128, pair * 128 + 128)
            rows = source[:, lanes]
            both = [jnp.where(low_half, rows, 0.0), jnp.where(low_half, 0.0, rows)]
            both = [half.reshape(ITEMS, 8, 128) for half in both]
            both = jnp.concatenate(both, axis=1).reshape(2 * N, 128).astype(BF16)
            part = turned[:, pair * 16 : pair * 16 + 16, :].reshape(2 * N, 56).astype(BF16)
            product[:, lanes] = dot(part, both, 0, 0)
        return product[...]

    def column(row):
        square = (48, 48)
        same = lax.broadcasted_iota(jnp.int32, square, 0) == lax.broadcasted_iota(jnp.int32, square, 1)
        return jnp.sum(jnp.where(same, row[...].astype(F32), 0.0), axis=1, keepdims=True)

    by_key = moments(by_keys, q_all) * SCALE
    m_key, s_key = by_key[0:48], by_key[48:49] + by_key[49:50]
    by_value = moments(by_values, gm_all)
    m_value, s_value = by_value[0:48], by_value[50:51] + by_value[51:52]
    beside = got[:, 48:96, :].astype(F32)
    last = got[:, 96:128, :].astype(F32)
    lane = lax.broadcasted_iota(jnp.int32, (1, 1, 128), 2)
    blocks = []
    for i in range(3):
        low = pltpu.roll(beside[:, 16 * i : 16 * i + 8, :], 64, 2)
        blocks.append(jnp.where(lane < 64, low, beside[:, 16 * i + 8 : 16 * i + 16, :]).reshape(N, 128))
    blocks += [last[:, 8 * i : 8 * i + 8, :].reshape(N, 128) for i in range(3)]
    grad_q = jnp.concatenate(blocks, axis=1)
    s_query = row_sum(grad_q)
    m_query = dot(norm_sl[...], grad_q.astype(BF16), 0, 0)
    gain_col, bias_col = column(gain), column(bias)
    by_gain = jnp.zeros((48, DI), F32)
    by_bias = jnp.zeros((48, DI), F32)
    for third, (moment, total) in enumerate(((m_query, s_query), (m_key, s_key), (m_value, s_value))):
        d_qkv[third] = gain_col * moment + bias_col * total
        weight = w_own[third].astype(F32)
        by_gain = by_gain + weight * moment
        by_bias = by_bias + weight * total
    ones = jnp.ones((8, DI), F32)
    line = (((1,), (1,)), ((), ()))
    for dst, item in ((g_one, by_gain), (b_one, by_bias)):
        dst[...] = lax.dot_general(
            ones, item, line, precision=lax.Precision.HIGHEST, preferred_element_type=F32
        )[0:1]
    for owner in range(ITEMS):

        @pl.when(dp == owner)
        def _(owner=owner):
            lanes = slice(owner * 48, owner * 48 + 48)
            qv_out[0:1, :] = s_query[:, lanes]
            qv_out[1:2, :] = s_value[:, lanes]


def shard_grads(got, q_all, gm_all, norm_sl, w_own, gain, bias):
    plain = (got, q_all, gm_all, norm_sl, w_own, gain, bias)
    return call(
        shard_kernel,
        "shard_grads",
        [(VMEM, item) for item in plain],
        [
            (VMEM, (3, 48, DI), F32),
            (VMEM, (1, 48), F32),
            (VMEM, (1, 48), F32),
            (VMEM, (2, 48), F32),
        ],
        [
            pltpu.VMEM((ITEMS, 96, 56), F32),
            pltpu.VMEM((ITEMS, 96, 56), F32),
            pltpu.VMEM((56, DI), F32),
        ],
        flops=5_000_000_000,
        touched=2_000_000,
    )


BOTH = ("tower", "dp")


def device(tower, place, core):
    return tower * 16 + (RING_Z[place] * 2 + RING_Y[place]) * 2 + core


def routes(towers):
    swap, turn = [], []
    for tower in range(towers):
        for place in range(8):
            for core, step in ((0, 1), (1, -1)):
                here = device(tower, place, core)
                swap.append((here, device(tower, place, 1 - core)))
                turn.append((here, device(tower, (place + step) % 8, core)))
    return swap, turn


def after(item, *earlier):
    return lax.optimization_barrier((item, *earlier))[0] if earlier else item


class Ring:
    def __init__(self, shard, swap, turn, first_core):
        self.swap, self.turn, self.first_core = swap, turn, first_core
        self.shard, self.other = shard, lax.ppermute(shard, BOTH, swap)
        self.last = self.joined(shard, self.other)
        self.items = [self.last]
        self.hops = 0

    def joined(self, own, other):
        return jnp.stack([jnp.where(self.first_core, own, other), jnp.where(self.first_core, other, own)])

    def first_step(self):
        held = self.joined(*(lax.ppermute(item, BOTH, self.turn) for item in (self.shard, self.other)))
        self.items += [held, lax.ppermute(held, BOTH, self.swap)]
        self.last = held
        self.hops += 1
        return held

    def step(self, *earlier, swap_after=(), later=False):
        held = self.last
        if self.hops == 3:
            held = jnp.where(self.first_core, held[0], held[1])
        held = lax.ppermute(after(held, *earlier), BOTH, self.turn)
        self.items += [held, None if later else lax.ppermute(after(held, *swap_after), BOTH, self.swap)]
        self.last = held
        self.hops += 1
        return held

    def finish(self, *earlier):
        for i, item in enumerate(self.items):
            if item is None:
                self.items[i] = lax.ppermute(after(self.items[i - 1], *earlier), BOTH, self.swap)
        return self.items


def ring_body(
    tokens,
    lengths,
    ln1_gain,
    ln1_bias,
    qkv_weight,
    qv_bias,
    out_weight,
    out_bias,
    ln2_gain,
    ln2_bias,
    fc_weight,
    fc_bias,
    down_weight,
    down_bias,
    final_gain,
    final_bias,
    embed_weight,
    logit_scale,
):
    towers = lax.axis_size("tower")
    dp_index = lax.axis_index("dp")
    swap, turn = routes(towers)
    tok = tokens[0].transpose(1, 0, 2)
    w_own = qkv_weight[0].transpose(1, 0, 2)
    vectors = (ln1_gain, ln1_bias, out_bias, ln2_gain, ln2_bias, down_bias, final_gain, final_bias)
    first_own = pack_first(lengths, w_own.reshape(144, DI), tok, vectors, qv_bias[0], fc_bias)
    second_own = pack_rest(out_weight[0], fc_weight[0], embed_weight[0])
    first_core = dp_index % 2 == 0

    qkv_ring = Ring(first_own, swap, turn, first_core)
    wide_ring = Ring(second_own, swap, turn, first_core)
    down_ring = Ring(down_weight[0], swap, turn, first_core)
    qkv_ring.first_step()
    d1 = down_ring.step()
    qkv_ring.step()
    q3 = qkv_ring.step(d1)
    wide_ring.step()
    qkv_ring.step()
    first = qkv_ring.items
    keys, values, norm_low, normed, vec, pooled, q_own, probs, gv = attend_pooled(lengths, tok, first)
    w2 = wide_ring.step(q3, swap_after=(q_own,))
    d2 = down_ring.step(q3, swap_after=(q_own,))
    mixes = lax.all_to_all(pooled, "dp", 0, 0, tiled=True)
    w3 = wide_ring.step(q_own)
    mixed, z_value = attend(lengths, vec, gv, after(normed, w2), keys, values, norm_low, first)
    wide_ring.step(z_value)
    d3 = down_ring.step(z_value, mixes)
    second = wide_ring.items
    down_ring.step()
    down = down_ring.items
    e_own, proj, normf, invf, norm2, inv2, slope, n2_sl, mix_sl, head_sl, act_sl = pooled_forward(
        lengths, vec, mixes, first, second, down
    )
    across = [(t * 16 + d, (1 - t) * 16 + d) for t in range(2) for d in range(16)]
    e_oth = lax.ppermute(e_own, BOTH, across)
    n2, middle = middle_part(lengths, tok, vec, after(mixed, e_own), second)
    (loss, scale, d_emb, d_down, d_fc, d_out, g_final, b_final, b_down, g_two, b_two, b_out, b_fc,
     mid_own, gm_all, gm_own, payload, gk, gq) = chain(
        lengths, logit_scale, after(e_own, n2), e_oth, vec, (head_sl, act_sl, n2_sl, mix_sl),
        (proj, normf, invf, norm2, inv2, slope, keys, values, norm_low, probs, gv, z_value), second, down,
    )
    got = lax.all_to_all(payload, "dp", 0, 0, tiled=True).reshape(ITEMS, PAYLOAD, 128)
    block_out, tokens_grad, q_all, norm_sl = close(
        lengths, tok, vec, gk, gv, q_own, gm_own, gq, mid_own, n2, middle, first, second, down
    )
    d_qkv, g_one, b_one, qv_sums = shard_grads(got, q_all, gm_all, norm_sl, w_own, ln1_gain, ln1_bias)
    seq = tok.shape[0]
    return (
        block_out.reshape(seq, 8, DI).transpose(1, 0, 2)[None],
        tokens_grad.reshape(seq, 8, DI).transpose(1, 0, 2)[None],
        loss.reshape(1),
        g_one,
        b_one,
        d_qkv.transpose(1, 0, 2)[None],
        qv_sums[None],
        d_out[None],
        b_out,
        g_two,
        b_two,
        d_fc[None],
        b_fc,
        d_down[None],
        b_down,
        g_final,
        b_final,
        d_emb[None],
        scale.reshape(1),
    )


def solution(mesh):
    fits = mesh.shape["dp"] == ITEMS and mesh.shape["tower"] == 2
    return jax.shard_map(
        ring_body if fits else body,
        mesh=mesh,
        in_specs=(
            P("tower", "dp", None, None),
            P("dp"),
            P("tower", "dp"),
            P("tower", "dp"),
            P("tower", "dp", None, None),
            P("tower", None, "dp"),
            P("tower", "dp", None),
            P("tower", "dp"),
            P("tower", "dp"),
            P("tower", "dp"),
            P("tower", "dp", None),
            P("tower", "dp"),
            P("tower", "dp", None),
            P("tower", "dp"),
            P("tower", "dp"),
            P("tower", "dp"),
            P("tower", "dp", None),
            P(),
        ),
        out_specs=(
            P("tower", "dp", None, None),
            P("tower", "dp", None, None),
            P(),
            P("tower", "dp"),
            P("tower", "dp"),
            P("tower", "dp", None, None),
            P("tower", None, "dp"),
            P("tower", "dp", None),
            P("tower", "dp"),
            P("tower", "dp"),
            P("tower", "dp"),
            P("tower", "dp", None),
            P("tower", "dp"),
            P("tower", "dp", None),
            P("tower", "dp"),
            P("tower", "dp"),
            P("tower", "dp"),
            P("tower", "dp", None),
            P(),
        ),
        check_vma=False,
    )
```

```python
import functools

import jax
import jax.numpy as jnp
from jax import lax
from jax.experimental import pallas as pl
from jax.experimental.pallas import tpu as pltpu
from jax.sharding import PartitionSpec as P

DI = 768
DT = 512
HD = 64
IMG_ROWS = 50
EMB = 512


EPS = 1e-05
NORM_EPS = 1e-06
GELU_K = 1.702
NEG_FILL = -1e30


def swapped(block, axis, stride):
    count = lax.axis_size(axis)
    route = []
    for low in range(count):
        high = low | 1 << stride
        if high != low and high < count:
            route += [(low, high), (high, low)]
    return lax.ppermute(block, axis, route)


def masked_norm(values, norm_gain, norm_bias, col_keep, width_real):
    row_mean = jnp.sum(values * col_keep, axis=-1, keepdims=True) / width_real
    centred = (values - row_mean) * col_keep
    row_var = jnp.sum(centred * centred, axis=-1, keepdims=True) / width_real
    inv_std = lax.rsqrt(row_var + EPS)
    normed = centred * inv_std
    return (normed * norm_gain + norm_bias, normed, inv_std)


def masked_norm_back(grad_out, norm_gain, normed, inv_std, col_keep, width_real):
    grad_normed = grad_out * norm_gain
    mean_grad = jnp.sum(grad_normed, axis=-1, keepdims=True) / width_real
    mean_cross = jnp.sum(grad_normed * normed, axis=-1, keepdims=True) / width_real
    grad_in = col_keep * inv_std * (grad_normed - mean_grad - normed * mean_cross)
    return (grad_in, jnp.sum(grad_out * normed, axis=0), jnp.sum(grad_out, axis=0))


def contract_rows(left_op, right_op):
    return lax.dot_general(
        left_op, right_op, (((0,), (0,)), ((), ())), preferred_element_type=jnp.float32
    )


def contract_cols(left_op, right_op):
    return lax.dot_general(
        left_op, right_op, (((1,), (1,)), ((), ())), preferred_element_type=jnp.float32
    )


def column_sum(values):
    return jnp.sum(values, axis=0, dtype=jnp.float32)


def body(
    tokens,
    lengths,
    ln1_gain,
    ln1_bias,
    qkv_weight,
    qv_bias,
    out_weight,
    out_bias,
    ln2_gain,
    ln2_bias,
    fc_weight,
    fc_bias,
    down_weight,
    down_bias,
    final_gain,
    final_bias,
    embed_weight,
    logit_scale,
):
    f32 = jnp.float32
    bf16 = jnp.bfloat16
    tower_index = lax.axis_index("tower")
    dp_index = lax.axis_index("dp")
    dp_count = lax.axis_size("dp")
    samples, seq_rows, width_all = (tokens.shape[1], tokens.shape[2], tokens.shape[3])
    head_count = width_all // HD
    sample_total = samples * dp_count
    flat_rows = samples * seq_rows
    is_text = tower_index == 1
    width_int = jnp.where(is_text, DT, DI)
    width_real = width_int.astype(f32)
    col_keep = (lax.broadcasted_iota(jnp.int32, (width_all,), 0) < width_int).astype(f32)
    seq_lens = jnp.where(is_text, lengths, IMG_ROWS)
    positions = lax.broadcasted_iota(jnp.int32, (samples, seq_rows), 1)
    row_keep = (positions < seq_lens[:, None]).astype(f32).reshape(flat_rows, 1)
    query_pos = lax.broadcasted_iota(jnp.int32, (seq_rows, seq_rows), 0)
    key_pos = lax.broadcasted_iota(jnp.int32, (seq_rows, seq_rows), 1)
    allowed = (key_pos[None] < seq_lens[:, None, None]) & (
        jnp.logical_not(is_text) | (key_pos <= query_pos)
    )[None]
    pool_pos = jnp.where(is_text, lengths - 1, 0)
    pool_hot = (positions == pool_pos[:, None]).astype(f32)
    score_mult = float(HD) ** (-0.5)
    gathered = (
        lax.all_gather(ln1_gain[0], "dp", axis=0, tiled=True),
        lax.all_gather(ln1_bias[0], "dp", axis=0, tiled=True),
        lax.all_gather(qkv_weight[0], "dp", axis=0, tiled=True),
        lax.all_gather(qv_bias[0], "dp", axis=1, tiled=True),
        lax.all_gather(out_weight[0], "dp", axis=0, tiled=True),
        lax.all_gather(out_bias[0], "dp", axis=0, tiled=True),
        lax.all_gather(ln2_gain[0], "dp", axis=0, tiled=True),
        lax.all_gather(ln2_bias[0], "dp", axis=0, tiled=True),
        lax.all_gather(fc_weight[0], "dp", axis=0, tiled=True),
        lax.all_gather(fc_bias[0], "dp", axis=0, tiled=True),
        lax.all_gather(down_weight[0], "dp", axis=0, tiled=True),
        lax.all_gather(down_bias[0], "dp", axis=0, tiled=True),
        lax.all_gather(final_gain[0], "dp", axis=0, tiled=True),
        lax.all_gather(final_bias[0], "dp", axis=0, tiled=True),
        lax.all_gather(embed_weight[0], "dp", axis=0, tiled=True),
    )
    (
        gain_one,
        bias_one,
        w_qkv,
        b_qv,
        w_out,
        b_out,
        gain_two,
        bias_two,
        w_fc,
        b_fc,
        w_down,
        b_down,
        gain_final,
        bias_final,
        w_embed,
    ) = gathered
    stream = tokens[0].astype(f32).reshape(flat_rows, width_all)
    normed_h1, norm_one, inv_one = masked_norm(
        stream, gain_one.astype(f32), bias_one.astype(f32), col_keep, width_real
    )
    normed_one = normed_h1.astype(bf16)
    qkv_bias = jnp.concatenate(
        [b_qv[0].astype(f32), jnp.zeros((width_all,), f32), b_qv[1].astype(f32)]
    )
    qkv_flat = (
        jnp.dot(normed_one, w_qkv.reshape(width_all, 3 * width_all), preferred_element_type=f32)
        + qkv_bias
    )
    qkv_low = qkv_flat.astype(bf16).reshape(samples, seq_rows, 3, head_count, HD)
    query_all = qkv_low[:, :, 0]
    key_all = qkv_low[:, :, 1]
    value_all = qkv_low[:, :, 2]

    def masked_scores():
        raw = (
            jnp.einsum("sqhd,skhd->shqk", query_all, key_all, preferred_element_type=f32)
            * score_mult
        )
        return jnp.where(allowed[:, None], raw, NEG_FILL)

    scores = masked_scores()
    row_top = jnp.max(scores, axis=-1, keepdims=True)
    exp_terms = jnp.exp(scores - row_top)
    exp_sum = jnp.sum(exp_terms, axis=-1, keepdims=True)
    log_total = row_top + jnp.log(exp_sum)
    attn_probs = (exp_terms / exp_sum).astype(bf16)
    head_mix = jnp.einsum("shqk,skhd->sqhd", attn_probs, value_all, preferred_element_type=f32)
    head_mix_low = head_mix.astype(bf16).reshape(flat_rows, width_all)
    attn_out = jnp.dot(head_mix_low, w_out, preferred_element_type=f32) + b_out.astype(f32)
    middle = stream + attn_out
    normed_h2, norm_two, inv_two = masked_norm(
        middle, gain_two.astype(f32), bias_two.astype(f32), col_keep, width_real
    )
    normed_two = normed_h2.astype(bf16)
    hidden_pre = jnp.dot(normed_two, w_fc, preferred_element_type=f32) + b_fc.astype(f32)
    gate_sig = jax.nn.sigmoid(GELU_K * hidden_pre)
    act_low = (hidden_pre * gate_sig).astype(bf16)
    branch = jnp.dot(act_low, w_down, preferred_element_type=f32) + b_down.astype(f32)
    block_rows = row_keep * (middle + branch)
    block_out = block_rows.astype(bf16).reshape(1, samples, seq_rows, width_all)
    block_three = block_rows.reshape(samples, seq_rows, width_all)
    pooled = jnp.take_along_axis(block_three, pool_pos[:, None, None], axis=1)[:, 0]
    normed_hf, norm_final, inv_final = masked_norm(
        pooled, gain_final.astype(f32), bias_final.astype(f32), col_keep, width_real
    )
    head_low = normed_hf.astype(bf16)
    projected = jnp.dot(head_low, w_embed, preferred_element_type=f32)
    inv_norm = lax.rsqrt(jnp.sum(projected * projected, axis=-1, keepdims=True) + NORM_EPS)
    embed_low = (projected * inv_norm).astype(bf16)
    own_all = lax.all_gather(embed_low, "dp", axis=0, tiled=True)
    others = swapped(own_all, "tower", 0)
    logit_mult = jnp.exp(logit_scale[0])
    similar = contract_cols(embed_low, others)
    logits = logit_mult * similar
    logit_top = jnp.max(logits, axis=-1, keepdims=True)
    logit_total = logit_top + jnp.log(jnp.sum(jnp.exp(logits - logit_top), axis=-1, keepdims=True))
    label_col = dp_index * samples + lax.broadcasted_iota(jnp.int32, (samples, 1), 0)
    label_hot = (lax.broadcasted_iota(jnp.int32, (samples, sample_total), 1) == label_col).astype(
        f32
    )
    diag_logit = jnp.sum(label_hot * logits, axis=-1, keepdims=True)
    loss_part = jnp.sum(logit_total - diag_logit) / (2.0 * sample_total)
    grad_logits = (jnp.exp(logits - logit_total) - label_hot) * 0.5
    scale_part = logit_mult * jnp.sum(grad_logits * similar)
    grad_sims = (logit_mult * grad_logits).astype(bf16)
    grad_own = jnp.dot(grad_sims, others, preferred_element_type=f32)
    grad_others = contract_rows(grad_sims, embed_low)
    sent_back = swapped(grad_others, "tower", 0)
    returned = lax.psum_scatter(sent_back, "dp", scatter_dimension=0, tiled=True)
    totals = lax.psum((loss_part, scale_part), ("tower", "dp"))
    grad_embed = grad_own + returned
    again = (
        lax.all_gather(ln1_gain[0], "dp", axis=0, tiled=True),
        lax.all_gather(qkv_weight[0], "dp", axis=0, tiled=True),
        lax.all_gather(out_weight[0], "dp", axis=0, tiled=True),
        lax.all_gather(ln2_gain[0], "dp", axis=0, tiled=True),
        lax.all_gather(fc_weight[0], "dp", axis=0, tiled=True),
        lax.all_gather(down_weight[0], "dp", axis=0, tiled=True),
        lax.all_gather(final_gain[0], "dp", axis=0, tiled=True),
        lax.all_gather(embed_weight[0], "dp", axis=0, tiled=True),
    )
    (
        back_gain_one,
        back_qkv,
        back_out,
        back_gain_two,
        back_fc,
        back_down,
        back_gain_final,
        back_embed,
    ) = again
    cross_term = jnp.sum(grad_embed * projected, axis=-1, keepdims=True)
    grad_proj = inv_norm * grad_embed - projected * inv_norm * inv_norm * inv_norm * cross_term
    grad_proj_low = grad_proj.astype(bf16)
    grad_head = contract_cols(grad_proj_low, back_embed)
    grad_pooled, d_gain_final, d_bias_final = masked_norm_back(
        grad_head, back_gain_final.astype(f32), norm_final, inv_final, col_keep, width_real
    )
    grad_rows = (pool_hot[:, :, None] * grad_pooled[:, None, :]).reshape(flat_rows, width_all)
    grad_branch_low = grad_rows.astype(bf16)
    d_down_b = column_sum(grad_branch_low)
    grad_act = contract_cols(grad_branch_low, back_down)
    grad_pre_low = (
        grad_act * (gate_sig + GELU_K * hidden_pre * gate_sig * (1.0 - gate_sig))
    ).astype(bf16)
    d_fc_b = column_sum(grad_pre_low)
    grad_norm_two = contract_cols(grad_pre_low, back_fc)
    grad_mid_norm, d_gain_two, d_bias_two = masked_norm_back(
        grad_norm_two, back_gain_two.astype(f32), norm_two, inv_two, col_keep, width_real
    )
    grad_middle = grad_rows + grad_mid_norm
    grad_attn_low = grad_middle.astype(bf16)
    d_out_b = column_sum(grad_attn_low)
    grad_mix_low = (
        contract_cols(grad_attn_low, back_out)
        .astype(bf16)
        .reshape(samples, seq_rows, head_count, HD)
    )
    probs_again = jnp.exp(masked_scores() - log_total)
    probs_low = probs_again.astype(bf16)
    grad_value = jnp.einsum("shqk,sqhd->skhd", probs_low, grad_mix_low, preferred_element_type=f32)
    grad_probs = jnp.einsum("sqhd,skhd->shqk", grad_mix_low, value_all, preferred_element_type=f32)
    grad_scores = probs_again * (
        grad_probs - jnp.sum(probs_again * grad_probs, axis=-1, keepdims=True)
    )
    grad_scores_low = grad_scores.astype(bf16)
    grad_query = (
        jnp.einsum("shqk,skhd->sqhd", grad_scores_low, key_all, preferred_element_type=f32)
        * score_mult
    )
    grad_key = (
        jnp.einsum("shqk,sqhd->skhd", grad_scores_low, query_all, preferred_element_type=f32)
        * score_mult
    )
    grad_qkv_low = (
        jnp.stack([grad_query, grad_key, grad_value], axis=2)
        .astype(bf16)
        .reshape(flat_rows, 3 * width_all)
    )
    d_qkv_w = contract_rows(normed_one, grad_qkv_low).reshape(width_all, 3, width_all)
    qkv_sums = column_sum(grad_qkv_low).reshape(3, width_all)
    d_qv_b = jnp.stack([qkv_sums[0], qkv_sums[2]])
    grad_norm_one = contract_cols(grad_qkv_low, back_qkv.reshape(width_all, 3 * width_all))
    grad_in_norm, d_gain_one, d_bias_one = masked_norm_back(
        grad_norm_one, back_gain_one.astype(f32), norm_one, inv_one, col_keep, width_real
    )
    tokens_grad = (grad_middle + grad_in_norm).reshape(1, samples, seq_rows, width_all)
    d_embed_w = contract_rows(head_low, grad_proj_low)
    d_down_w = contract_rows(act_low, grad_branch_low)
    d_fc_w = contract_rows(normed_two, grad_pre_low)
    d_out_w = contract_rows(head_mix_low, grad_attn_low)
    shares = (
        lax.psum_scatter(d_gain_one, "dp", scatter_dimension=0, tiled=True),
        lax.psum_scatter(d_bias_one, "dp", scatter_dimension=0, tiled=True),
        lax.psum_scatter(d_qkv_w, "dp", scatter_dimension=0, tiled=True),
        lax.psum_scatter(d_qv_b, "dp", scatter_dimension=1, tiled=True),
        lax.psum_scatter(d_out_w, "dp", scatter_dimension=0, tiled=True),
        lax.psum_scatter(d_out_b, "dp", scatter_dimension=0, tiled=True),
        lax.psum_scatter(d_gain_two, "dp", scatter_dimension=0, tiled=True),
        lax.psum_scatter(d_bias_two, "dp", scatter_dimension=0, tiled=True),
        lax.psum_scatter(d_fc_w, "dp", scatter_dimension=0, tiled=True),
        lax.psum_scatter(d_fc_b, "dp", scatter_dimension=0, tiled=True),
        lax.psum_scatter(d_down_w, "dp", scatter_dimension=0, tiled=True),
        lax.psum_scatter(d_down_b, "dp", scatter_dimension=0, tiled=True),
        lax.psum_scatter(d_gain_final, "dp", scatter_dimension=0, tiled=True),
        lax.psum_scatter(d_bias_final, "dp", scatter_dimension=0, tiled=True),
        lax.psum_scatter(d_embed_w, "dp", scatter_dimension=0, tiled=True),
    )
    results = list(shares)
    outputs = [item[None] for item in results]
    loss = totals[0].reshape(1)
    logit_scale_grad = totals[1].reshape(1)
    return (
        block_out,
        tokens_grad,
        loss,
        outputs[0],
        outputs[1],
        outputs[2],
        outputs[3],
        outputs[4],
        outputs[5],
        outputs[6],
        outputs[7],
        outputs[8],
        outputs[9],
        outputs[10],
        outputs[11],
        outputs[12],
        outputs[13],
        outputs[14],
        logit_scale_grad,
    )


RING_Z = (0, 1, 2, 3, 3, 2, 1, 0)
RING_Y = (0, 0, 0, 0, 1, 1, 1, 1)
ITEMS = 16
N = ITEMS * 8
F32 = jnp.float32
BF16 = jnp.bfloat16
ANY = pl.BlockSpec(memory_space=pl.ANY)
VMEM = pl.BlockSpec(memory_space=pltpu.VMEM)
SMEM = pl.BlockSpec(memory_space=pltpu.SMEM)
SCALE = float(HD) ** -0.5
PAYLOAD = 128


def call(kernel, name, ins, outs, scratch, flops=0, touched=0):
    return pl.pallas_call(
        kernel,
        name=name,
        out_shape=[jax.ShapeDtypeStruct(shape, dtype) for _, shape, dtype in outs],
        in_specs=[spec for spec, _ in ins],
        out_specs=[spec for spec, _, _ in outs],
        scratch_shapes=scratch,
        compiler_params=pltpu.CompilerParams(vmem_limit_bytes=67043328),
        cost_estimate=pl.CostEstimate(flops=flops, bytes_accessed=touched, transcendentals=0),
    )(*[item for _, item in ins])


def dot(left, right, left_dim=1, right_dim=0):
    return lax.dot_general(
        left, right, (((left_dim,), (right_dim,)), ((), ())), preferred_element_type=F32
    )


def aligned(index, size):
    return pl.multiple_of(index, size)


def owner_table(dp_index):
    core = dp_index % 2
    row = dp_index // 2 % 2
    depth = dp_index // 4
    place = jnp.where(row == 0, depth, 7 - depth)

    def chip(where):
        where = (where + 8) % 8
        z = jnp.where(where < 4, where, 7 - where)
        y = jnp.where(where < 4, 0, 1)
        return (z * 2 + y) * 2

    sign = jnp.where(core == 0, -1, 1)
    found = [chip(place)]
    for hop in range(1, 4):
        found += [chip(place + sign * hop), chip(place - sign * hop)]
    return found + [chip(place + 4) + core, chip(place + 4) + 1 - core]


class Place:
    def __init__(self, lengths):
        self.dp = lax.axis_index("dp")
        self.text = lax.axis_index("tower") == 1
        self.lengths = lengths
        self.keep = (
            lax.broadcasted_iota(jnp.int32, (1, DI), 1) < jnp.where(self.text, DT, DI)
        ).astype(F32)
        self.winv = jnp.where(self.text, 1.0 / DT, 1.0 / DI).astype(F32)

    def length(self, s):
        return jnp.where(self.text, self.lengths[s], IMG_ROWS)

    def pool(self, s):
        return jnp.where(self.text, self.lengths[s] - 1, 0)

    def column(self, pick):
        ids = lax.broadcasted_iota(jnp.int32, (1, 8, 1), 1)
        column = jnp.zeros((1, 8, 1), jnp.int32)
        for s in range(8):
            column = jnp.where(ids == s, pick(s), column)
        return column

    def either(self, path, image):
        @pl.when(self.text)
        def _():
            path(DT, 77)

        @pl.when(jnp.logical_not(self.text))
        def _():
            path(DI, image)

    def mine(self, visit):
        for owner in range(ITEMS):

            @pl.when(self.dp == owner)
            def _(owner=owner):
                visit(owner)


def copy(src, dst, sem):
    found = pltpu.make_async_copy(src, dst, sem)
    found.start()
    return found


def drain(dst, sem):
    pltpu.make_async_copy(dst, dst, sem).wait()


def fetch(owners, refs, row, rows, dst, sem):
    for owner, ref in zip(owners, refs):
        if len(ref.shape) == 3:
            copy(ref.at[:, pl.ds(row, rows), :], dst.at[pl.ds(owner, 2)], sem)
        else:
            copy(ref.at[pl.ds(row, rows), :], dst.at[owner], sem)


def embed_matrix(packed):
    tail = jnp.concatenate([packed[:, 0:16, EMB:DI], packed[:, 16:32, EMB:DI]], axis=2)
    return jnp.concatenate([packed[:, :, 0:EMB], tail], axis=1).reshape(DI, EMB)


def normalize(values, keep, winv):
    mean = jnp.sum(values, axis=-1, keepdims=True) * winv
    centred = (values - mean) * keep
    var = jnp.sum(centred * centred, axis=-1, keepdims=True) * winv
    inv = lax.rsqrt(var + EPS)
    return centred * inv, inv


def normalize_back(grad_out, gain, normed, inv, keep, winv):
    grad_normed = grad_out * gain
    mean_grad = jnp.sum(grad_normed, axis=-1, keepdims=True) * winv
    mean_cross = jnp.sum(grad_normed * normed, axis=-1, keepdims=True) * winv
    return keep * inv * (grad_normed - mean_grad - normed * mean_cross)


def row_sum(values):
    return jnp.sum(values, axis=0, keepdims=True)


def head_rows(rows):
    heads = lax.broadcasted_iota(jnp.int32, rows.shape, 1) // HD
    parts = [jnp.where(heads == head, rows, 0.0) for head in range(16)]
    return jnp.concatenate(parts, axis=0).astype(BF16)


def chunks(count, visit):
    @pl.loop(0, count // 14)
    def _(i):
        visit(i * 14, aligned(i * 112, 16), 14)

    if count % 14:
        at = count - count % 14
        visit(at, at * 8, count % 14)


def pack_first_kernel(lengths, qkv, tok, *rest):
    here = Place(lengths)
    vectors, (qv_bias, fc_bias, out) = rest[:8], rest[8:]
    out[0:144, :] = qkv[...]
    sub = lax.broadcasted_iota(jnp.int32, (8, DI), 0)
    pooled = jnp.zeros((8, DI), F32)
    for s in range(8):
        pooled = jnp.where(sub == s, tok[here.pool(s)].astype(F32), pooled)
    out[144:152, :] = pooled.astype(BF16)
    lane = lax.broadcasted_iota(jnp.int32, (1, DI), 1) // 48 == here.dp
    short = [v[...].astype(F32) for v in vectors]
    pair = qv_bias[...].astype(F32)
    short[2:2] = [pair[0:1], pair[1:2]]
    rows = [jnp.where(lane, jnp.concatenate([v] * ITEMS, axis=1), 0.0) for v in short]
    wide = lax.broadcasted_iota(jnp.int32, (1, 4 * DI), 1) // 192 == here.dp
    fc = jnp.where(wide, jnp.concatenate([fc_bias[...].astype(F32)] * ITEMS, axis=1), 0.0)
    rows += [fc[:, i * DI : (i + 1) * DI] for i in range(4)]
    row_id = lax.broadcasted_iota(jnp.int32, (16, DI), 0)
    small = jnp.zeros((16, DI), F32)
    for at, row in enumerate(rows):
        small = jnp.where(row_id == at, jnp.broadcast_to(row, (16, DI)), small)
    out[152:168, :] = small.astype(BF16)


def pack_first(lengths, qkv, tok, vectors, qv_bias, fc_bias):
    return call(
        pack_first_kernel,
        "pack_first",
        [(SMEM, lengths)] + [(VMEM, item) for item in (qkv, tok, *vectors, qv_bias, fc_bias)],
        [(VMEM, (168, DI), BF16)],
        [],
        touched=1_500_000,
    )[0]


def pack_rest_kernel(w_out, w_fc, w_emb, out):
    out[0:48, :] = w_out[...]
    out[48:80, 0:EMB] = w_emb[0:32, :]
    out[48:64, EMB:DI] = w_emb[32:48, 0:256]
    out[64:80, EMB:DI] = w_emb[32:48, 256:EMB]
    for block in range(4):
        out[80 + 48 * block : 128 + 48 * block, :] = w_fc[:, block * DI : (block + 1) * DI]


def pack_rest(w_out, w_fc, w_emb):
    return call(
        pack_rest_kernel,
        "pack_rest",
        [(VMEM, item) for item in (w_out, w_fc, w_emb)],
        [(VMEM, (272, DI), BF16)],
        [],
        touched=1_500_000,
    )[0]


def sample_limits(here):
    lane_sample = lax.broadcasted_iota(jnp.int32, (1, 128), 1) % 8
    limit = jnp.zeros((1, 128), jnp.int32)
    for s in range(8):
        limit = jnp.where(lane_sample == s, here.length(s), limit)
    return limit


def own_heads(tall, width):
    heads = lax.broadcasted_iota(jnp.int32, (8, width), 1) // HD
    total = jnp.zeros((8, width), F32)
    for head in range(width // HD):
        total = total + jnp.where(heads == head, tall[head * 8 : head * 8 + 8], 0.0)
    if width < DI:
        total = jnp.concatenate([total, jnp.zeros((8, DI - width), F32)], axis=1)
    return total


def tall_rows(rows):
    return jnp.concatenate([rows[:, i * 128 : (i + 1) * 128] for i in range(DI // 128)], axis=0)


def wide_rows(tall):
    tall = tall.astype(F32)
    return jnp.concatenate(
        [tall[:, i * 8 : i * 8 + 8, :].reshape(N, 128) for i in range(DI // 128)], axis=1
    )


def pooled_kernel(lengths, tok_hbm, *rest):
    first, outs, scratch = rest[:9], rest[9:18], rest[18:]
    keys_hbm, values_hbm, norm_hbm, normed_hbm, vec, pooled, q_own, probs_out, gv_out = outs
    weights, small, tok, normed, keys, values, norm_low, sems, ends = scratch
    here = Place(lengths)
    owners = owner_table(here.dp)
    tok_in = copy(tok_hbm, tok, sems.at[2])
    fetch(owners, first, 152, 16, small, sems.at[0])
    fetch(owners, first, 0, 144, weights, sems.at[1])
    keep, winv = here.keep, here.winv
    drain(small, sems.at[0])
    vec[...] = jnp.sum(small[...].astype(F32), axis=0)
    limit = sample_limits(here)
    tok_in.wait()
    sub = lax.broadcasted_iota(jnp.int32, (8, DI), 0)
    picked = jnp.zeros((8, DI), F32)
    for s in range(8):
        picked = jnp.where(sub == s, tok[here.pool(s)].astype(F32), picked)
    pooled_norm, _ = normalize(picked, keep, winv)
    pooled_normed = (pooled_norm * vec[0:1, :] + vec[1:2, :]).astype(BF16)

    def norm_chunk(position, row, count):
        x = tok[pl.ds(position, count)].astype(F32).reshape(count * 8, DI)
        norm, _ = normalize(x, keep, winv)
        norm_low[pl.ds(row, count * 8), :] = norm.astype(BF16)
        normed[pl.ds(row, count * 8), :] = (norm * vec[0:1, :] + vec[1:2, :]).astype(BF16)

    def path(width, count):
        rows = count * 8
        chunks(count, norm_chunk)
        saved = [copy(norm_low, norm_hbm, ends.at[0]), copy(normed, normed_hbm, ends.at[1])]
        drain(weights, sems.at[1])
        for third, low, bias in ((1, keys, None), (2, values, 3)):

            weight = weights[:, third * 48 : third * 48 + 48, 0:width].reshape(DI, width)[0:width]
            prod = dot(normed[0:rows, 0:width], weight)
            if bias is not None:
                prod = prod + vec[bias : bias + 1, 0:width]
            low[0:rows, 0:width] = prod.astype(BF16)

        saved += [copy(keys, keys_hbm, ends.at[2]), copy(values, values_hbm, ends.at[3])]
        query = dot(pooled_normed, weights[:, 0:48, :].reshape(DI, DI)) + vec[2:3, :]
        query = query.astype(BF16).astype(F32)
        q_own[...] = query
        q_rows = head_rows(query)
        raw = dot(keys[0:rows, 0:width], q_rows[:, 0:width], 1, 1) * SCALE
        row = lax.broadcasted_iota(jnp.int32, (rows, 128), 0)
        lane = lax.broadcasted_iota(jnp.int32, (rows, 128), 1)
        valid = (lane % 8 == row % 8) & (row // 8 < limit) & (lane < width // 8)
        raw = jnp.where(valid, raw, NEG_FILL)
        terms = jnp.where(valid, jnp.exp(raw - jnp.max(raw, axis=0, keepdims=True)), 0.0)
        probs = terms / jnp.maximum(row_sum(terms), 1e-30)
        low_probs = probs.astype(BF16)
        probs_out[0:rows, :] = probs
        gv_out[0:rows, :] = low_probs
        mixed = own_heads(dot(low_probs, values[0:rows, 0:width], 0, 0), width)
        tall = tall_rows(mixed).astype(BF16)
        for owner in range(ITEMS):
            pooled[owner] = tall
        for item in saved:
            item.wait()

    here.either(path, 56)


def attend_pooled(lengths, tok, first):
    rows = tok.shape[0] * tok.shape[1]
    return call(
        pooled_kernel,
        "attend_pooled",
        [(SMEM, lengths), (ANY, tok)] + [(ANY, r) for r in first],
        [(ANY, (rows, DI), BF16)] * 4
        + [
            (VMEM, (16, DI), F32),
            (VMEM, (ITEMS, 48, 128), BF16),
            (VMEM, (8, DI), F32),
            (VMEM, (rows, 128), F32),
            (VMEM, (rows, 128), BF16),
        ],
        [
            pltpu.VMEM((ITEMS, 144, DI), BF16),
            pltpu.VMEM((ITEMS, 16, DI), BF16),
            pltpu.VMEM(tok.shape, BF16),
            pltpu.VMEM((rows, DI), BF16),
            pltpu.VMEM((rows, DI), BF16),
            pltpu.VMEM((rows, DI), BF16),
            pltpu.VMEM((rows, DI), BF16),
            pltpu.SemaphoreType.DMA((3,)),
            pltpu.SemaphoreType.DMA((4,)),
        ],
        flops=7_000_000_000,
        touched=10_000_000,
    )


def attend_kernel(lengths, vec, gv, normed_hbm, keys_hbm, values_hbm, norm_hbm, *rest):
    first, (mixed_hbm, z_value), scratch = rest[:9], rest[9:11], rest[11:]
    weights, normed, keys, values, norm_low, mixed, qf, kf, vf, mf, sems = scratch
    here = Place(lengths)
    owners = owner_table(here.dp)
    fetch(owners, first, 0, 48, weights, sems.at[0])
    early = [
        copy(src, dst, sems.at[1 + i])
        for i, (src, dst) in enumerate(
            ((normed_hbm, normed), (keys_hbm, keys), (values_hbm, values), (norm_hbm, norm_low))
        )
    ]
    drain(weights, sems.at[0])
    early[0].wait()
    early[1].wait()
    early[2].wait()

    def path(width, count):
        rows = count * 8
        span = 80 if count == 77 else count
        if span > count:
            for dst in (qf, kf, vf):
                dst[:, rows : span * 8, :] = jnp.zeros((6, span * 8 - rows, 128), F32)

        weight = weights[:, :, 0:width].reshape(DI, width)[0:width]
        prod = dot(normed[0:rows, 0:width], weight) + vec[2:3, 0:width]
        prod = prod.astype(BF16).astype(F32) * SCALE
        for pair in range(width // 128):
            lanes = pl.ds(pair * 128, 128)
            qf[pair, 0:rows, :] = prod[:, pair * 128 : pair * 128 + 128]
            kf[pair, 0:rows, :] = keys[0:rows, lanes].astype(F32)
            vf[pair, 0:rows, :] = values[0:rows, lanes].astype(F32)

        key_pos = lax.broadcasted_iota(jnp.int32, (span, 2 * span), 0)
        query_pos = lax.broadcasted_iota(jnp.int32, (span, 2 * span), 1) % span
        low_half = lax.broadcasted_iota(jnp.int32, (span, 128), 1) < HD

        @pl.loop(0, 8, unroll=2)
        def _(s):
            at = pl.ds(s, span, stride=8)
            allowed = key_pos < here.length(s)
            if width == DT:
                allowed = allowed & (key_pos <= query_pos)
            pairs = range(width // 128)
            raws = []
            for pair in pairs:
                query, key = qf.at[pair][at, :], kf.at[pair][at, :].astype(BF16)
                spread = [jnp.where(low_half, query, 0.0), jnp.where(low_half, 0.0, query)]
                spread = jnp.concatenate(spread, axis=0).astype(BF16)
                raws.append(dot(key, spread, 1, 1))
            probs = []
            for raw in raws:
                raw = jnp.where(allowed, raw, NEG_FILL)
                terms = jnp.exp(raw - jnp.max(raw, axis=0, keepdims=True))
                probs.append((terms / jnp.sum(terms, axis=0, keepdims=True)).astype(BF16))
            for pair in pairs:
                out = dot(probs[pair], vf.at[pair][at, :].astype(BF16), 0, 0)
                mf.at[pair][at, :] = jnp.where(low_half, out[0:span], out[span : 2 * span])

        stored = []
        for i in range(width // 128):
            lanes = pl.ds(128 * i, 128)
            mixed[0:rows, lanes] = mf[i, 0:rows, :].astype(BF16)
            stored.append(copy(mixed.at[0:rows, lanes], mixed_hbm.at[0:rows, lanes], sems.at[5 + i]))
        early[3].wait()
        z_value[...] = pltpu.roll(dot(norm_low[0:rows, :], gv[0:rows, :], 0, 0), 96, 1).astype(BF16)
        for item in stored:
            item.wait()

    here.either(path, 56)


def attend(lengths, vec, gv, normed, keys, values, norm_low, first):
    rows = keys.shape[0]
    high = rows + 24
    return call(
        attend_kernel,
        "attend",
        [(SMEM, lengths), (VMEM, vec), (VMEM, gv)]
        + [(ANY, r) for r in (normed, keys, values, norm_low, *first)],
        [(ANY, (rows, DI), BF16), (VMEM, (DI, 128), BF16)],
        [
            pltpu.VMEM((ITEMS, 48, DI), BF16),
            pltpu.VMEM((rows, DI), BF16),
            pltpu.VMEM((rows, DI), BF16),
            pltpu.VMEM((rows, DI), BF16),
            pltpu.VMEM((rows, DI), BF16),
            pltpu.VMEM((rows, DI), BF16),
            pltpu.VMEM((6, high, 128), F32),
            pltpu.VMEM((6, high, 128), F32),
            pltpu.VMEM((6, high, 128), F32),
            pltpu.VMEM((6, high, 128), F32),
            pltpu.SemaphoreType.DMA((11,)),
        ],
        flops=9_000_000_000,
        touched=10_000_000,
    )


def forward_kernel(lengths, vec, mixes, *rest):
    first, second, down = rest[:9], rest[9:18], rest[18:27]
    outs, scratch = rest[27:38], rest[38:]
    (e_out, proj_out, normf_out, invf_out, norm2_out, inv2_out, slope_out, n2_sl, mix_sl, head_sl,
     act_sl) = outs
    w_out, w_fc, w_down, w_emb, xs, mix, n2, act, head_all, sems = scratch
    here = Place(lengths)
    owners = owner_table(here.dp)
    fetch(owners, second, 0, 48, w_out, sems.at[1])
    fetch(owners, first, 144, 8, xs, sems.at[0])
    fetch(owners, second, 80, 192, w_fc, sems.at[2])
    keep, winv = here.keep, here.winv
    mix[...] = wide_rows(mixes[...]).astype(BF16)
    drain(w_out, sems.at[1])
    drain(xs, sems.at[0])
    fetch(owners, down, 0, 192, w_down, sems.at[3])
    fetch(owners, second, 48, 32, w_emb, sems.at[4])
    stream = xs[...].astype(F32).reshape(N, DI)
    middle = stream + dot(mix[...], w_out[...].reshape(DI, DI)) + vec[4:5, :]
    norm2, inv2 = normalize(middle, keep, winv)
    n2[...] = (norm2 * vec[5:6, :] + vec[6:7, :]).astype(BF16)
    norm2_out[...] = norm2
    inv2_out[...] = jnp.broadcast_to(inv2, (N, 128))
    drain(w_fc, sems.at[2])
    for block in range(4):
        lanes = pl.ds(block * DI, DI)
        weight = w_fc[:, block * 48 : block * 48 + 48, :].reshape(DI, DI)
        pre = dot(n2[...], weight) + vec[10 + block : 11 + block, :]
        gate = jax.nn.sigmoid(GELU_K * pre)
        act[:, lanes] = (pre * gate).astype(BF16)
        slope_out[:, lanes] = gate + GELU_K * pre * gate * (1.0 - gate)

    drain(w_down, sems.at[3])
    last = middle + dot(act[...], w_down[...].reshape(4 * DI, DI)) + vec[7:8, :]
    normf, invf = normalize(last, keep, winv)
    normf_out[...] = normf
    invf_out[...] = jnp.broadcast_to(invf, (N, 128))
    head_all[...] = (normf * vec[8:9, :] + vec[9:10, :]).astype(BF16)
    drain(w_emb, sems.at[4])
    proj = dot(head_all[...], embed_matrix(w_emb[...]))
    proj_out[...] = proj
    scale = lax.rsqrt(jnp.sum(proj * proj, axis=-1, keepdims=True) + NORM_EPS)
    e_out[...] = (proj * scale).astype(BF16)

    def mine(owner):
        lanes = slice(owner * 48, owner * 48 + 48)
        n2_sl[...] = n2[:, lanes]
        mix_sl[...] = mix[:, lanes]
        head_sl[...] = head_all[:, lanes]
        act_sl[...] = act[:, owner * 192 : owner * 192 + 192]

    here.mine(mine)


def pooled_forward(lengths, vec, mixes, first, second, down):
    return call(
        forward_kernel,
        "pooled_forward",
        [(SMEM, lengths), (VMEM, vec), (VMEM, mixes)] + [(ANY, r) for r in (*first, *second, *down)],
        [
            (VMEM, (N, EMB), BF16),
            (VMEM, (N, EMB), F32),
            (VMEM, (N, DI), F32),
            (VMEM, (N, 128), F32),
            (VMEM, (N, DI), F32),
            (VMEM, (N, 128), F32),
            (VMEM, (N, 4 * DI), F32),
            (VMEM, (N, 48), BF16),
            (VMEM, (N, 48), BF16),
            (VMEM, (N, 48), BF16),
            (VMEM, (N, 192), BF16),
        ],
        [
            pltpu.VMEM((ITEMS, 48, DI), BF16),
            pltpu.VMEM((ITEMS, 192, DI), BF16),
            pltpu.VMEM((ITEMS, 192, DI), BF16),
            pltpu.VMEM((ITEMS, 32, DI), BF16),
            pltpu.VMEM((ITEMS, 8, DI), BF16),
            pltpu.VMEM((N, DI), BF16),
            pltpu.VMEM((N, DI), BF16),
            pltpu.VMEM((N, 4 * DI), BF16),
            pltpu.VMEM((N, DI), BF16),
            pltpu.SemaphoreType.DMA((5,)),
        ],
        flops=11_000_000_000,
        touched=16_000_000,
    )


def middle_kernel(lengths, tok_hbm, vec, mixed_hbm, *rest):
    second = rest[:9]
    (n2_hbm, middle_hbm), scratch = rest[9:11], rest[11:]
    w_out, middle, tok, mixed, n2, sems = scratch
    here = Place(lengths)
    owners = owner_table(here.dp)
    rows_in = copy(mixed_hbm, mixed, sems.at[1])
    fetch(owners, second, 0, 48, w_out, sems.at[0])
    tok_in = copy(tok_hbm, tok, sems.at[2])
    keep, winv = here.keep, here.winv
    rows_in.wait()
    drain(w_out, sems.at[0])

    def norm_chunk(position, row, count):
        at = pl.ds(row, count * 8)
        total = middle[at, :] + tok[pl.ds(position, count)].astype(F32).reshape(count * 8, DI)
        middle[at, :] = total
        norm, _ = normalize(total, keep, winv)
        n2[at, :] = (norm * vec[5:6, :] + vec[6:7, :]).astype(BF16)
        copy(middle.at[at, :], middle_hbm.at[at, :], sems.at[3])
        copy(n2.at[at, :], n2_hbm.at[at, :], sems.at[4])

    def path(width, count):
        rows = count * 8

        weight = w_out[:, :, 0:width].reshape(DI, width)[0:width]
        middle[0:rows, 0:width] = dot(mixed[0:rows, 0:width], weight) + vec[4:5, 0:width]
        if width < DI:
            middle[0:rows, width:DI] = jnp.zeros((rows, DI - width), F32)
        tok_in.wait()
        chunks(count, norm_chunk)
        drain(middle.at[pl.ds(0, rows), :], sems.at[3])
        drain(n2.at[pl.ds(0, rows), :], sems.at[4])

    here.either(path, 56)


def middle_part(lengths, tok, vec, mixed, second):
    rows = mixed.shape[0]
    return call(
        middle_kernel,
        "middle_part",
        [(SMEM, lengths), (ANY, tok), (VMEM, vec), (ANY, mixed)] + [(ANY, r) for r in second],
        [(ANY, (rows, DI), BF16), (ANY, (rows, DI), F32)],
        [
            pltpu.VMEM((ITEMS, 48, DI), BF16),
            pltpu.VMEM((rows, DI), F32),
            pltpu.VMEM(tok.shape, BF16),
            pltpu.VMEM((rows, DI), BF16),
            pltpu.VMEM((rows, DI), BF16),
            pltpu.SemaphoreType.DMA((5,)),
        ],
        flops=5_000_000_000,
        touched=8_000_000,
    )


def one_direction(left, right, mult):
    sims = dot(left, right, 1, 1)
    logits = mult * sims
    top = jnp.max(logits, axis=-1, keepdims=True)
    total = top + jnp.log(jnp.sum(jnp.exp(logits - top), axis=-1, keepdims=True))
    count = sims.shape[0]
    eye = lax.broadcasted_iota(jnp.int32, (count, count), 0) == lax.broadcasted_iota(
        jnp.int32, (count, count), 1
    )
    hot = eye.astype(F32)
    lost = jnp.sum(total - jnp.sum(hot * logits, axis=-1, keepdims=True), axis=0, keepdims=True)
    grad = (jnp.exp(logits - total) - hot) * 0.5
    scale = jnp.sum(jnp.sum(grad * sims, axis=-1, keepdims=True), axis=0, keepdims=True)
    return lost, scale, mult * grad


def pack_payload(payload, z_key, z_value, sum_key, sum_value, grad_q):
    lane = lax.broadcasted_iota(jnp.int32, (1, 128), 1)
    upper = jnp.where(lane < 96, z_key, z_value).astype(BF16)
    blocks = [grad_q[:, i * 128 : (i + 1) * 128] for i in range(6)]
    beside = jnp.concatenate(
        [half for block in blocks[:3] for half in (pltpu.roll(block, 64, 1), block)], axis=0
    )
    key_high = sum_key.astype(BF16).astype(F32)
    value_high = sum_value.astype(BF16).astype(F32)
    row_id = lax.broadcasted_iota(jnp.int32, (8, 128), 0)
    sums = jnp.zeros((8, 128), F32)
    for at, value in enumerate((key_high, sum_key - key_high, value_high, sum_value - value_high)):
        sums = jnp.where(row_id == at, jnp.broadcast_to(value, (8, 128)), sums)
    last = jnp.concatenate([*blocks[3:], sums], axis=0).astype(BF16)
    for owner in range(ITEMS):
        base, rows = owner * PAYLOAD, slice(owner * 48, owner * 48 + 48)
        payload[base : base + 48, :] = upper[rows]
        payload[base + 48 : base + 96, :] = jnp.where(lane < 64, z_value[rows], beside).astype(BF16)
        payload[base + 96 : base + 128, :] = last


def chain_kernel(lengths, log_mult, e_own_ref, e_oth_ref, vec, head_sl, act_sl, n2_sl, mix_sl, *rest):
    (proj_hbm, normf_hbm, invf_hbm, norm2_hbm, inv2_hbm, slope_hbm, keys_hbm, values_hbm, norm_hbm, probs_hbm,
     gv_hbm, z_hbm), rest = rest[:12], rest[12:]
    second, down = rest[:9], rest[9:18]
    outs, scratch = rest[18:37], rest[37:]
    (loss_out, scale_out, d_emb_hbm, d_down_hbm, d_fc_hbm, d_out_hbm, g_final, b_final, b_down, g_two, b_two, b_out, b_fc,
     mid_own, gm_out, gm_own, payload, gk_out, gq_out) = outs
    (w_out, w_fc, w_down, w_emb, gpre, mid_all, proj_v, normf_v, invf_v, norm2_v, inv2_v, slope, keys,
     values, norm_low, probs_v, gv_v, z_v, vec_grads, fcb_grads, d_emb, d_down, d_fc, d_out, sems, ins, ends) = scratch
    here = Place(lengths)
    owners = owner_table(here.dp)
    early = [
        copy(src, dst, ins.at[i])
        for i, (src, dst) in enumerate(
            ((proj_hbm, proj_v), (normf_hbm, normf_v), (invf_hbm, invf_v))
        )
    ]
    fetch(owners, second, 48, 32, w_emb, sems.at[0])
    fetch(owners, down, 0, 192, w_down, sems.at[1])
    slope_in = copy(slope_hbm, slope, ins.at[3])
    fetch(owners, second, 80, 192, w_fc, sems.at[2])
    later = [copy(norm2_hbm, norm2_v, ins.at[4]), copy(inv2_hbm, inv2_v, ins.at[5])]
    fetch(owners, second, 0, 48, w_out, sems.at[3])
    last = [
        copy(src, dst, ins.at[6 + i])
        for i, (src, dst) in enumerate(
            ((keys_hbm, keys), (values_hbm, values), (norm_hbm, norm_low), (probs_hbm, probs_v),
             (gv_hbm, gv_v), (z_hbm, z_v))
        )
    ]
    keep, winv = here.keep, here.winv
    text = here.text.astype(F32)
    mult = jnp.exp(jnp.full((1, 128), log_mult[0], F32))[:, 0:1]
    own, oth = e_own_ref[...].astype(F32), e_oth_ref[...].astype(F32)
    e_img = (own * (1.0 - text) + oth * text).astype(BF16)
    e_txt = (oth * (1.0 - text) + own * text).astype(BF16)
    lost_img, scale_img, grad_img = one_direction(e_img, e_txt, mult)
    lost_txt, scale_txt, grad_txt = one_direction(e_txt, e_img, mult)
    loss_out[...] = (lost_img + lost_txt) / (2.0 * N)
    scale_out[...] = mult * (scale_img + scale_txt)
    grad_own = (grad_img * (1.0 - text) + grad_txt * text).astype(BF16)
    grad_oth = (grad_txt * (1.0 - text) + grad_img * text).astype(BF16)
    oth_low = e_oth_ref[...]
    grad_e = dot(grad_own, oth_low) + dot(grad_oth, oth_low, 0, 0)
    for item in early:
        item.wait()
    drain(w_emb, sems.at[0])
    proj = proj_v[...]
    r = lax.rsqrt(jnp.sum(proj * proj, axis=-1, keepdims=True) + NORM_EPS)
    cross = jnp.sum(grad_e * proj, axis=-1, keepdims=True)
    grad_proj = (r * grad_e - proj * (r * r * r) * cross).astype(BF16)
    grad_head = dot(grad_proj, embed_matrix(w_emb[...]), 1, 1)
    normf = normf_v[...]
    grad_y = normalize_back(grad_head, vec[8:9, :], normf, invf_v[:, 0:1], keep, winv)
    branch = grad_y.astype(BF16)
    d_emb[...] = dot(head_sl[...], grad_proj, 0, 0)
    stored = [copy(d_emb, d_emb_hbm, ends.at[0])]
    vec_grads[0:1, :] = row_sum(grad_head * normf)
    vec_grads[1:2, :] = row_sum(grad_head)
    vec_grads[2:3, :] = row_sum(branch.astype(F32))
    d_down[...] = dot(act_sl[...], branch, 0, 0)
    stored.append(copy(d_down, d_down_hbm, ends.at[1]))
    drain(w_down, sems.at[1])
    slope_in.wait()
    for block in range(4):
        lanes = pl.ds(block * DI, DI)
        back = dot(branch, w_down[block * 4 : block * 4 + 4].reshape(DI, DI), 1, 1)
        low = (back * slope[:, lanes]).astype(BF16)
        gpre[:, lanes] = low
        fcb_grads[:, lanes] = jnp.broadcast_to(row_sum(low.astype(F32)), (8, DI))

    drain(w_fc, sems.at[2])
    grad_n2 = jnp.zeros((N, DI), F32)
    for block in range(4):
        weight = w_fc[:, block * 48 : block * 48 + 48, :].reshape(DI, DI)
        grad_n2 = grad_n2 + dot(gpre[:, block * DI : block * DI + DI], weight, 1, 1)
    for item in later:
        item.wait()
    norm2 = norm2_v[...]
    vec_grads[3:4, :] = row_sum(grad_n2 * norm2)
    vec_grads[4:5, :] = row_sum(grad_n2)
    grad_mid = grad_y + normalize_back(grad_n2, vec[5:6, :], norm2, inv2_v[:, 0:1], keep, winv)
    mid_all[...] = grad_mid
    own_rows = pl.ds(aligned(here.dp * 8, 8), 8)
    mid_own[...] = mid_all[own_rows, :]
    attn = grad_mid.astype(BF16)
    vec_grads[5:6, :] = row_sum(attn.astype(F32))
    drain(w_out, sems.at[3])
    gm_out[...] = dot(attn, w_out[...].reshape(DI, DI), 1, 1).astype(BF16).astype(F32)
    gm_own[...] = gm_out[own_rows, :]

    @pl.loop(0, 6)
    def _(j):
        lanes = pl.ds(aligned(j * 512, 512), 512)
        d_fc[:, lanes] = dot(n2_sl[...], gpre[:, lanes], 0, 0)

    d_out[...] = dot(mix_sl[...], attn, 0, 0)
    stored += [copy(d_fc, d_fc_hbm, ends.at[2]), copy(d_out, d_out_hbm, ends.at[3])]

    def mine(owner):
        lanes = slice(owner * 48, owner * 48 + 48)
        for at, dst in enumerate((g_final, b_final, b_down, g_two, b_two, b_out)):
            dst[...] = vec_grads[at : at + 1, lanes]
        b_fc[...] = fcb_grads[0:1, owner * 192 : owner * 192 + 192]

    here.mine(mine)
    for item in last:
        item.wait()
    m_rows = head_rows(gm_own[...])

    def path(width, count):
        rows = count * 8
        probs = probs_v[0:rows, :]
        grad_probs = dot(values[0:rows, 0:width], m_rows[:, 0:width], 1, 1)
        gk = (probs * (grad_probs - row_sum(probs * grad_probs))).astype(BF16)
        gv = gv_v[0:rows, :]
        gk_out[0:rows, :] = gk
        gq_low = own_heads(dot(gk, keys[0:rows, 0:width], 0, 0) * SCALE, width).astype(BF16)
        gq_out[...] = gq_low
        z_key = dot(norm_low[0:rows, :], gk, 0, 0)
        pack_payload(
            payload,
            z_key,
            z_v[...].astype(F32),
            row_sum(gk.astype(F32)),
            pltpu.roll(jnp.broadcast_to(row_sum(gv.astype(F32)), (8, 128)), 96, 1)[0:1],
            gq_low.astype(F32),
        )

    here.either(path, 56)
    for item in stored:
        item.wait()


def chain(lengths, log_mult, e_own, e_oth, vec, slices, saved, second, down):
    rows = saved[-2].shape[0]
    return call(
        chain_kernel,
        "chain",
        [(SMEM, lengths), (SMEM, log_mult)]
        + [(VMEM, item) for item in (e_own, e_oth, vec, *slices)]
        + [(ANY, r) for r in (*saved, *second, *down)],
        [
            (VMEM, (1, 1), F32),
            (VMEM, (1, 1), F32),
            (ANY, (48, EMB), F32),
            (ANY, (192, DI), F32),
            (ANY, (48, 4 * DI), F32),
            (ANY, (48, DI), F32),
        ]
        + [(VMEM, (1, 48), F32)] * 6
        + [
            (VMEM, (1, 192), F32),
            (VMEM, (8, DI), F32),
            (VMEM, (N, DI), F32),
            (VMEM, (8, DI), F32),
            (VMEM, (ITEMS * PAYLOAD, 128), BF16),
            (VMEM, (rows, 128), BF16),
            (VMEM, (8, DI), BF16),
        ],
        [
            pltpu.VMEM((ITEMS, 48, DI), BF16),
            pltpu.VMEM((ITEMS, 192, DI), BF16),
            pltpu.VMEM((ITEMS, 192, DI), BF16),
            pltpu.VMEM((ITEMS, 32, DI), BF16),
            pltpu.VMEM((N, 4 * DI), BF16),
            pltpu.VMEM((N, DI), F32),
            pltpu.VMEM((N, EMB), F32),
            pltpu.VMEM((N, DI), F32),
            pltpu.VMEM((N, 128), F32),
            pltpu.VMEM((N, DI), F32),
            pltpu.VMEM((N, 128), F32),
            pltpu.VMEM((N, 4 * DI), F32),
            pltpu.VMEM((rows, DI), BF16),
            pltpu.VMEM((rows, DI), BF16),
            pltpu.VMEM((rows, DI), BF16),
            pltpu.VMEM((rows, 128), F32),
            pltpu.VMEM((rows, 128), BF16),
            pltpu.VMEM((DI, 128), BF16),
            pltpu.VMEM((8, DI), F32),
            pltpu.VMEM((8, 4 * DI), F32),
            pltpu.VMEM((48, EMB), F32),
            pltpu.VMEM((192, DI), F32),
            pltpu.VMEM((48, 4 * DI), F32),
            pltpu.VMEM((48, DI), F32),
            pltpu.SemaphoreType.DMA((4,)),
            pltpu.SemaphoreType.DMA((12,)),
            pltpu.SemaphoreType.DMA((4,)),
        ],
        flops=15_000_000_000,
        touched=20_000_000,
    )


def close_kernel(lengths, tok, vec, gk, gv, q_own, gm_own, gq, mid_own, n2_hbm, middle_hbm, *rest):
    first, second, down = rest[:9], rest[9:18], rest[18:27]
    (block_out, out_hbm, q_out, norm_sl), scratch = rest[27:31], rest[31:]
    weights, w_fc, w_down, n2, act, middle, acc, xs, norm1_all, out, sems = scratch
    here = Place(lengths)
    owners = owner_table(here.dp)
    fetch(owners, first, 0, 144, weights, sems.at[0])
    fetch(owners, first, 144, 8, xs, sems.at[5])
    ready = copy(n2_hbm, n2, sems.at[1])
    fetch(owners, second, 80, 192, w_fc, sems.at[4])
    fetch(owners, down, 0, 192, w_down, sems.at[3])
    early = [copy(middle_hbm, middle, sems.at[2])]
    keep, winv = here.keep, here.winv
    q_rows = head_rows(q_own[...])
    m_rows = head_rows(gm_own[...])
    pool = here.column(here.pool)
    length = here.column(here.length)
    all_rows = out.shape[0]
    drain(weights, sems.at[0])
    u_key = (dot(q_rows, weights[:, 48:96, :].reshape(DI, DI), 1, 1) * SCALE).astype(BF16)
    u_value = dot(m_rows, weights[:, 96:144, :].reshape(DI, DI), 1, 1).astype(BF16)
    u_query = dot(gq[...], weights[:, 0:48, :].reshape(DI, DI), 1, 1)

    def path(width, count):
        rows = count * 8
        acc[0:rows, :] = dot(gk[0:rows, :], u_key) + dot(gv[0:rows, :], u_value)

        def back_chunk(position, row, count):
            at = pl.ds(row, count * 8)
            hit = lax.broadcasted_iota(jnp.int32, (count, 8, DI), 0) + position == pool
            norm, inv = normalize(tok[pl.ds(position, count)].astype(F32).reshape(count * 8, DI), keep, winv)
            total = acc[at, :] + jnp.where(hit, u_query[None], 0.0).reshape(count * 8, DI)
            back = normalize_back(total, vec[0:1, :], norm, inv, keep, winv)
            out[at, :] = back + jnp.where(hit, mid_own[...][None], 0.0).reshape(count * 8, DI)

        if rows < all_rows:
            out[rows:all_rows, :] = jnp.zeros((all_rows - rows, DI), F32)
        chunks(count, back_chunk)
        stored = copy(out, out_hbm, sems.at[6])
        short = count if width == DT else IMG_ROWS
        rows = short * 8
        ready.wait()
        drain(w_fc, sems.at[4])
        for block in range(4):
            size = min(DI, 4 * width - block * DI)
            if size > 0:
                weight = w_fc[:, block * 48 : block * 48 + 48, 0:size].reshape(DI, size)[0:width]
                pre = dot(n2[0:rows, 0:width], weight) + vec[10 + block : 11 + block, 0:size]
                low = (pre * jax.nn.sigmoid(GELU_K * pre)).astype(BF16)
                act[0:rows, block * DI : block * DI + size] = low

        for item in early:
            item.wait()
        drain(w_down, sems.at[3])

        weight = w_down[:, :, 0:width].reshape(4 * DI, width)[0 : 4 * width]
        total = dot(act[0:rows, 0 : 4 * width], weight)
        total = (total + vec[7:8, 0:width] + middle[0:rows, 0:width]).reshape(short, 8, width)
        where = lax.broadcasted_iota(jnp.int32, (short, 8, width), 0)
        block_out[0:rows, 0:width] = jnp.where(where < length, total, 0.0).reshape(rows, width).astype(BF16)

        if width < DI:
            block_out[:, width:DI] = jnp.zeros((all_rows, DI - width), BF16)
        if rows < all_rows:
            block_out[rows:all_rows, :] = jnp.zeros((all_rows - rows, DI), BF16)
        stored.wait()

    here.either(path, 56)
    drain(xs, sems.at[5])
    stream = xs[...].astype(F32).reshape(N, DI)
    norm1, _ = normalize(stream, keep, winv)
    norm1_all[...] = norm1.astype(BF16)
    n1 = (norm1 * vec[0:1, :] + vec[1:2, :]).astype(BF16)
    q_out[...] = (dot(n1, weights[:, 0:48, :].reshape(DI, DI)) + vec[2:3, :]).astype(BF16).astype(F32)

    def mine(owner):
        norm_sl[...] = norm1_all[:, owner * 48 : owner * 48 + 48]

    here.mine(mine)


def close(lengths, tok, vec, gk, gv, q_own, gm_own, gq, mid_own, n2, middle, first, second, down):
    rows = tok.shape[0] * tok.shape[1]
    return call(
        close_kernel,
        "close",
        [(SMEM, lengths)]
        + [(VMEM, item) for item in (tok, vec, gk, gv, q_own, gm_own, gq, mid_own)]
        + [(ANY, r) for r in (n2, middle, *first, *second, *down)],
        [(VMEM, (rows, DI), BF16), (ANY, (rows, DI), F32), (VMEM, (N, DI), F32), (VMEM, (N, 48), BF16)],
        [
            pltpu.VMEM((ITEMS, 144, DI), BF16),
            pltpu.VMEM((ITEMS, 192, DI), BF16),
            pltpu.VMEM((ITEMS, 192, DI), BF16),
            pltpu.VMEM((rows, DI), BF16),
            pltpu.VMEM((rows, 4 * DI), BF16),
            pltpu.VMEM((rows, DI), F32),
            pltpu.VMEM((rows, DI), F32),
            pltpu.VMEM((ITEMS, 8, DI), BF16),
            pltpu.VMEM((N, DI), BF16),
            pltpu.VMEM((rows, DI), F32),
            pltpu.SemaphoreType.DMA((7,)),
        ],
        flops=17_000_000_000,
        touched=18_000_000,
    )


def shard_kernel(got, q_all, gm_all, norm_sl, w_own, gain, bias, d_qkv, g_one, b_one, qv_out, by_keys, by_values, product):
    dp = lax.axis_index("dp")

    low_half = lax.broadcasted_iota(jnp.int32, (N, 128), 1) < HD

    for j in range(ITEMS):
        found = got[j].astype(F32)
        upper = jnp.concatenate([found[0:48], found[120:128]], axis=0).T
        lower = jnp.concatenate([found[48:96], found[120:128]], axis=0).T
        by_keys[j] = upper[0:96]
        by_values[j, 0:32, :] = upper[96:128]
        by_values[j, 32:96, :] = lower[0:64]

    def moments(turned, source):
        for pair in range(DI // 128):
            lanes = slice(pair * 128, pair * 128 + 128)
            rows = source[:, lanes]
            both = [jnp.where(low_half, rows, 0.0), jnp.where(low_half, 0.0, rows)]
            both = [half.reshape(ITEMS, 8, 128) for half in both]
            both = jnp.concatenate(both, axis=1).reshape(2 * N, 128).astype(BF16)
            part = turned[:, pair * 16 : pair * 16 + 16, :].reshape(2 * N, 56).astype(BF16)
            product[:, lanes] = dot(part, both, 0, 0)
        return product[...]

    def column(row):
        square = (48, 48)
        same = lax.broadcasted_iota(jnp.int32, square, 0) == lax.broadcasted_iota(jnp.int32, square, 1)
        return jnp.sum(jnp.where(same, row[...].astype(F32), 0.0), axis=1, keepdims=True)

    by_key = moments(by_keys, q_all) * SCALE
    m_key, s_key = by_key[0:48], by_key[48:49] + by_key[49:50]
    by_value = moments(by_values, gm_all)
    m_value, s_value = by_value[0:48], by_value[50:51] + by_value[51:52]
    beside = got[:, 48:96, :].astype(F32)
    last = got[:, 96:128, :].astype(F32)
    lane = lax.broadcasted_iota(jnp.int32, (1, 1, 128), 2)
    blocks = []
    for i in range(3):
        low = pltpu.roll(beside[:, 16 * i : 16 * i + 8, :], 64, 2)
        blocks.append(jnp.where(lane < 64, low, beside[:, 16 * i + 8 : 16 * i + 16, :]).reshape(N, 128))
    blocks += [last[:, 8 * i : 8 * i + 8, :].reshape(N, 128) for i in range(3)]
    grad_q = jnp.concatenate(blocks, axis=1)
    s_query = row_sum(grad_q)
    m_query = dot(norm_sl[...], grad_q.astype(BF16), 0, 0)
    gain_col, bias_col = column(gain), column(bias)
    by_gain = jnp.zeros((48, DI), F32)
    by_bias = jnp.zeros((48, DI), F32)
    for third, (moment, total) in enumerate(((m_query, s_query), (m_key, s_key), (m_value, s_value))):
        d_qkv[third] = gain_col * moment + bias_col * total
        weight = w_own[third].astype(F32)
        by_gain = by_gain + weight * moment
        by_bias = by_bias + weight * total
    ones = jnp.ones((8, DI), F32)
    line = (((1,), (1,)), ((), ()))
    for dst, item in ((g_one, by_gain), (b_one, by_bias)):
        dst[...] = lax.dot_general(
            ones, item, line, precision=lax.Precision.HIGHEST, preferred_element_type=F32
        )[0:1]
    for owner in range(ITEMS):

        @pl.when(dp == owner)
        def _(owner=owner):
            lanes = slice(owner * 48, owner * 48 + 48)
            qv_out[0:1, :] = s_query[:, lanes]
            qv_out[1:2, :] = s_value[:, lanes]


def shard_grads(got, q_all, gm_all, norm_sl, w_own, gain, bias):
    plain = (got, q_all, gm_all, norm_sl, w_own, gain, bias)
    return call(
        shard_kernel,
        "shard_grads",
        [(VMEM, item) for item in plain],
        [
            (VMEM, (3, 48, DI), F32),
            (VMEM, (1, 48), F32),
            (VMEM, (1, 48), F32),
            (VMEM, (2, 48), F32),
        ],
        [
            pltpu.VMEM((ITEMS, 96, 56), F32),
            pltpu.VMEM((ITEMS, 96, 56), F32),
            pltpu.VMEM((56, DI), F32),
        ],
        flops=5_000_000_000,
        touched=2_000_000,
    )


BOTH = ("tower", "dp")


def device(tower, place, core):
    return tower * 16 + (RING_Z[place] * 2 + RING_Y[place]) * 2 + core


def routes(towers):
    swap, turn = [], []
    for tower in range(towers):
        for place in range(8):
            for core, step in ((0, 1), (1, -1)):
                here = device(tower, place, core)
                swap.append((here, device(tower, place, 1 - core)))
                turn.append((here, device(tower, (place + step) % 8, core)))
    return swap, turn


def after(item, *earlier):
    return lax.optimization_barrier((item, *earlier))[0] if earlier else item


class Ring:
    def __init__(self, shard, swap, turn, first_core):
        self.swap, self.turn, self.first_core = swap, turn, first_core
        self.shard, self.other = shard, lax.ppermute(shard, BOTH, swap)
        self.last = self.joined(shard, self.other)
        self.items = [self.last]
        self.hops = 0

    def joined(self, own, other):
        return jnp.stack([jnp.where(self.first_core, own, other), jnp.where(self.first_core, other, own)])

    def first_step(self):
        held = self.joined(*(lax.ppermute(item, BOTH, self.turn) for item in (self.shard, self.other)))
        self.items += [held, lax.ppermute(held, BOTH, self.swap)]
        self.last = held
        self.hops += 1
        return held

    def step(self, *earlier, swap_after=(), later=False):
        held = self.last
        if self.hops == 3:
            held = jnp.where(self.first_core, held[0], held[1])
        held = lax.ppermute(after(held, *earlier), BOTH, self.turn)
        self.items += [held, None if later else lax.ppermute(after(held, *swap_after), BOTH, self.swap)]
        self.last = held
        self.hops += 1
        return held

    def finish(self, *earlier):
        for i, item in enumerate(self.items):
            if item is None:
                self.items[i] = lax.ppermute(after(self.items[i - 1], *earlier), BOTH, self.swap)
        return self.items


def ring_body(
    tokens,
    lengths,
    ln1_gain,
    ln1_bias,
    qkv_weight,
    qv_bias,
    out_weight,
    out_bias,
    ln2_gain,
    ln2_bias,
    fc_weight,
    fc_bias,
    down_weight,
    down_bias,
    final_gain,
    final_bias,
    embed_weight,
    logit_scale,
):
    towers = lax.axis_size("tower")
    dp_index = lax.axis_index("dp")
    swap, turn = routes(towers)
    tok = tokens[0].transpose(1, 0, 2)
    w_own = qkv_weight[0].transpose(1, 0, 2)
    vectors = (ln1_gain, ln1_bias, out_bias, ln2_gain, ln2_bias, down_bias, final_gain, final_bias)
    first_own = pack_first(lengths, w_own.reshape(144, DI), tok, vectors, qv_bias[0], fc_bias)
    second_own = pack_rest(out_weight[0], fc_weight[0], embed_weight[0])
    first_core = dp_index % 2 == 0

    qkv_ring = Ring(first_own, swap, turn, first_core)
    wide_ring = Ring(second_own, swap, turn, first_core)
    down_ring = Ring(down_weight[0], swap, turn, first_core)
    qkv_ring.first_step()
    d1 = down_ring.step()
    qkv_ring.step()
    q3 = qkv_ring.step(d1)
    wide_ring.step()
    qkv_ring.step()
    first = qkv_ring.items
    keys, values, norm_low, normed, vec, pooled, q_own, probs, gv = attend_pooled(lengths, tok, first)
    w2 = wide_ring.step(q3, swap_after=(q_own,))
    d2 = down_ring.step(q3, swap_after=(q_own,))
    mixes = lax.all_to_all(pooled, "dp", 0, 0, tiled=True)
    w3 = wide_ring.step(q_own)
    mixed, z_value = attend(lengths, vec, gv, after(normed, w2), keys, values, norm_low, first)
    wide_ring.step(z_value)
    d3 = down_ring.step(z_value, mixes)
    second = wide_ring.items
    down_ring.step()
    down = down_ring.items
    e_own, proj, normf, invf, norm2, inv2, slope, n2_sl, mix_sl, head_sl, act_sl = pooled_forward(
        lengths, vec, mixes, first, second, down
    )
    across = [(t * 16 + d, (1 - t) * 16 + d) for t in range(2) for d in range(16)]
    e_oth = lax.ppermute(e_own, BOTH, across)
    n2, middle = middle_part(lengths, tok, vec, after(mixed, e_own), second)
    (loss, scale, d_emb, d_down, d_fc, d_out, g_final, b_final, b_down, g_two, b_two, b_out, b_fc,
     mid_own, gm_all, gm_own, payload, gk, gq) = chain(
        lengths, logit_scale, after(e_own, n2), e_oth, vec, (head_sl, act_sl, n2_sl, mix_sl),
        (proj, normf, invf, norm2, inv2, slope, keys, values, norm_low, probs, gv, z_value), second, down,
    )
    got = lax.all_to_all(payload, "dp", 0, 0, tiled=True).reshape(ITEMS, PAYLOAD, 128)
    block_out, tokens_grad, q_all, norm_sl = close(
        lengths, tok, vec, gk, gv, q_own, gm_own, gq, mid_own, n2, middle, first, second, down
    )
    d_qkv, g_one, b_one, qv_sums = shard_grads(got, q_all, gm_all, norm_sl, w_own, ln1_gain, ln1_bias)
    seq = tok.shape[0]
    return (
        block_out.reshape(seq, 8, DI).transpose(1, 0, 2)[None],
        tokens_grad.reshape(seq, 8, DI).transpose(1, 0, 2)[None],
        loss.reshape(1),
        g_one,
        b_one,
        d_qkv.transpose(1, 0, 2)[None],
        qv_sums[None],
        d_out[None],
        b_out,
        g_two,
        b_two,
        d_fc[None],
        b_fc,
        d_down[None],
        b_down,
        g_final,
        b_final,
        d_emb[None],
        scale.reshape(1),
    )


def solution(mesh):
    fits = mesh.shape["dp"] == ITEMS and mesh.shape["tower"] == 2
    return jax.shard_map(
        ring_body if fits else body,
        mesh=mesh,
        in_specs=(
            P("tower", "dp", None, None),
            P("dp"),
            P("tower", "dp"),
            P("tower", "dp"),
            P("tower", "dp", None, None),
            P("tower", None, "dp"),
            P("tower", "dp", None),
            P("tower", "dp"),
            P("tower", "dp"),
            P("tower", "dp"),
            P("tower", "dp", None),
            P("tower", "dp"),
            P("tower", "dp", None),
            P("tower", "dp"),
            P("tower", "dp"),
            P("tower", "dp"),
            P("tower", "dp", None),
            P(),
        ),
        out_specs=(
            P("tower", "dp", None, None),
            P("tower", "dp", None, None),
            P(),
            P("tower", "dp"),
            P("tower", "dp"),
            P("tower", "dp", None, None),
            P("tower", None, "dp"),
            P("tower", "dp", None),
            P("tower", "dp"),
            P("tower", "dp"),
            P("tower", "dp"),
            P("tower", "dp", None),
            P("tower", "dp"),
            P("tower", "dp", None),
            P("tower", "dp"),
            P("tower", "dp"),
            P("tower", "dp"),
            P("tower", "dp", None),
            P(),
        ),
        check_vma=False,
    )
```

```python
import functools

import jax
import jax.numpy as jnp
from jax import lax
from jax.experimental import pallas as pl
from jax.experimental.pallas import tpu as pltpu
from jax.sharding import PartitionSpec as P

DI = 768
DT = 512
HD = 64
IMG_ROWS = 50
EMB = 512


EPS = 1e-05
NORM_EPS = 1e-06
GELU_K = 1.702
NEG_FILL = -1e30


def swapped(block, axis, stride):
    count = lax.axis_size(axis)
    route = []
    for low in range(count):
        high = low | 1 << stride
        if high != low and high < count:
            route += [(low, high), (high, low)]
    return lax.ppermute(block, axis, route)


def masked_norm(values, norm_gain, norm_bias, col_keep, width_real):
    row_mean = jnp.sum(values * col_keep, axis=-1, keepdims=True) / width_real
    centred = (values - row_mean) * col_keep
    row_var = jnp.sum(centred * centred, axis=-1, keepdims=True) / width_real
    inv_std = lax.rsqrt(row_var + EPS)
    normed = centred * inv_std
    return (normed * norm_gain + norm_bias, normed, inv_std)


def masked_norm_back(grad_out, norm_gain, normed, inv_std, col_keep, width_real):
    grad_normed = grad_out * norm_gain
    mean_grad = jnp.sum(grad_normed, axis=-1, keepdims=True) / width_real
    mean_cross = jnp.sum(grad_normed * normed, axis=-1, keepdims=True) / width_real
    grad_in = col_keep * inv_std * (grad_normed - mean_grad - normed * mean_cross)
    return (grad_in, jnp.sum(grad_out * normed, axis=0), jnp.sum(grad_out, axis=0))


def contract_rows(left_op, right_op):
    return lax.dot_general(
        left_op, right_op, (((0,), (0,)), ((), ())), preferred_element_type=jnp.float32
    )


def contract_cols(left_op, right_op):
    return lax.dot_general(
        left_op, right_op, (((1,), (1,)), ((), ())), preferred_element_type=jnp.float32
    )


def column_sum(values):
    return jnp.sum(values, axis=0, dtype=jnp.float32)


def body(
    tokens,
    lengths,
    ln1_gain,
    ln1_bias,
    qkv_weight,
    qv_bias,
    out_weight,
    out_bias,
    ln2_gain,
    ln2_bias,
    fc_weight,
    fc_bias,
    down_weight,
    down_bias,
    final_gain,
    final_bias,
    embed_weight,
    logit_scale,
):
    f32 = jnp.float32
    bf16 = jnp.bfloat16
    tower_index = lax.axis_index("tower")
    dp_index = lax.axis_index("dp")
    dp_count = lax.axis_size("dp")
    samples, seq_rows, width_all = (tokens.shape[1], tokens.shape[2], tokens.shape[3])
    head_count = width_all // HD
    sample_total = samples * dp_count
    flat_rows = samples * seq_rows
    is_text = tower_index == 1
    width_int = jnp.where(is_text, DT, DI)
    width_real = width_int.astype(f32)
    col_keep = (lax.broadcasted_iota(jnp.int32, (width_all,), 0) < width_int).astype(f32)
    seq_lens = jnp.where(is_text, lengths, IMG_ROWS)
    positions = lax.broadcasted_iota(jnp.int32, (samples, seq_rows), 1)
    row_keep = (positions < seq_lens[:, None]).astype(f32).reshape(flat_rows, 1)
    query_pos = lax.broadcasted_iota(jnp.int32, (seq_rows, seq_rows), 0)
    key_pos = lax.broadcasted_iota(jnp.int32, (seq_rows, seq_rows), 1)
    allowed = (key_pos[None] < seq_lens[:, None, None]) & (
        jnp.logical_not(is_text) | (key_pos <= query_pos)
    )[None]
    pool_pos = jnp.where(is_text, lengths - 1, 0)
    pool_hot = (positions == pool_pos[:, None]).astype(f32)
    score_mult = float(HD) ** (-0.5)
    gathered = (
        lax.all_gather(ln1_gain[0], "dp", axis=0, tiled=True),
        lax.all_gather(ln1_bias[0], "dp", axis=0, tiled=True),
        lax.all_gather(qkv_weight[0], "dp", axis=0, tiled=True),
        lax.all_gather(qv_bias[0], "dp", axis=1, tiled=True),
        lax.all_gather(out_weight[0], "dp", axis=0, tiled=True),
        lax.all_gather(out_bias[0], "dp", axis=0, tiled=True),
        lax.all_gather(ln2_gain[0], "dp", axis=0, tiled=True),
        lax.all_gather(ln2_bias[0], "dp", axis=0, tiled=True),
        lax.all_gather(fc_weight[0], "dp", axis=0, tiled=True),
        lax.all_gather(fc_bias[0], "dp", axis=0, tiled=True),
        lax.all_gather(down_weight[0], "dp", axis=0, tiled=True),
        lax.all_gather(down_bias[0], "dp", axis=0, tiled=True),
        lax.all_gather(final_gain[0], "dp", axis=0, tiled=True),
        lax.all_gather(final_bias[0], "dp", axis=0, tiled=True),
        lax.all_gather(embed_weight[0], "dp", axis=0, tiled=True),
    )
    (
        gain_one,
        bias_one,
        w_qkv,
        b_qv,
        w_out,
        b_out,
        gain_two,
        bias_two,
        w_fc,
        b_fc,
        w_down,
        b_down,
        gain_final,
        bias_final,
        w_embed,
    ) = gathered
    stream = tokens[0].astype(f32).reshape(flat_rows, width_all)
    normed_h1, norm_one, inv_one = masked_norm(
        stream, gain_one.astype(f32), bias_one.astype(f32), col_keep, width_real
    )
    normed_one = normed_h1.astype(bf16)
    qkv_bias = jnp.concatenate(
        [b_qv[0].astype(f32), jnp.zeros((width_all,), f32), b_qv[1].astype(f32)]
    )
    qkv_flat = (
        jnp.dot(normed_one, w_qkv.reshape(width_all, 3 * width_all), preferred_element_type=f32)
        + qkv_bias
    )
    qkv_low = qkv_flat.astype(bf16).reshape(samples, seq_rows, 3, head_count, HD)
    query_all = qkv_low[:, :, 0]
    key_all = qkv_low[:, :, 1]
    value_all = qkv_low[:, :, 2]

    def masked_scores():
        raw = (
            jnp.einsum("sqhd,skhd->shqk", query_all, key_all, preferred_element_type=f32)
            * score_mult
        )
        return jnp.where(allowed[:, None], raw, NEG_FILL)

    scores = masked_scores()
    row_top = jnp.max(scores, axis=-1, keepdims=True)
    exp_terms = jnp.exp(scores - row_top)
    exp_sum = jnp.sum(exp_terms, axis=-1, keepdims=True)
    log_total = row_top + jnp.log(exp_sum)
    attn_probs = (exp_terms / exp_sum).astype(bf16)
    head_mix = jnp.einsum("shqk,skhd->sqhd", attn_probs, value_all, preferred_element_type=f32)
    head_mix_low = head_mix.astype(bf16).reshape(flat_rows, width_all)
    attn_out = jnp.dot(head_mix_low, w_out, preferred_element_type=f32) + b_out.astype(f32)
    middle = stream + attn_out
    normed_h2, norm_two, inv_two = masked_norm(
        middle, gain_two.astype(f32), bias_two.astype(f32), col_keep, width_real
    )
    normed_two = normed_h2.astype(bf16)
    hidden_pre = jnp.dot(normed_two, w_fc, preferred_element_type=f32) + b_fc.astype(f32)
    gate_sig = jax.nn.sigmoid(GELU_K * hidden_pre)
    act_low = (hidden_pre * gate_sig).astype(bf16)
    branch = jnp.dot(act_low, w_down, preferred_element_type=f32) + b_down.astype(f32)
    block_rows = row_keep * (middle + branch)
    block_out = block_rows.astype(bf16).reshape(1, samples, seq_rows, width_all)
    block_three = block_rows.reshape(samples, seq_rows, width_all)
    pooled = jnp.take_along_axis(block_three, pool_pos[:, None, None], axis=1)[:, 0]
    normed_hf, norm_final, inv_final = masked_norm(
        pooled, gain_final.astype(f32), bias_final.astype(f32), col_keep, width_real
    )
    head_low = normed_hf.astype(bf16)
    projected = jnp.dot(head_low, w_embed, preferred_element_type=f32)
    inv_norm = lax.rsqrt(jnp.sum(projected * projected, axis=-1, keepdims=True) + NORM_EPS)
    embed_low = (projected * inv_norm).astype(bf16)
    own_all = lax.all_gather(embed_low, "dp", axis=0, tiled=True)
    others = swapped(own_all, "tower", 0)
    logit_mult = jnp.exp(logit_scale[0])
    similar = contract_cols(embed_low, others)
    logits = logit_mult * similar
    logit_top = jnp.max(logits, axis=-1, keepdims=True)
    logit_total = logit_top + jnp.log(jnp.sum(jnp.exp(logits - logit_top), axis=-1, keepdims=True))
    label_col = dp_index * samples + lax.broadcasted_iota(jnp.int32, (samples, 1), 0)
    label_hot = (lax.broadcasted_iota(jnp.int32, (samples, sample_total), 1) == label_col).astype(
        f32
    )
    diag_logit = jnp.sum(label_hot * logits, axis=-1, keepdims=True)
    loss_part = jnp.sum(logit_total - diag_logit) / (2.0 * sample_total)
    grad_logits = (jnp.exp(logits - logit_total) - label_hot) * 0.5
    scale_part = logit_mult * jnp.sum(grad_logits * similar)
    grad_sims = (logit_mult * grad_logits).astype(bf16)
    grad_own = jnp.dot(grad_sims, others, preferred_element_type=f32)
    grad_others = contract_rows(grad_sims, embed_low)
    sent_back = swapped(grad_others, "tower", 0)
    returned = lax.psum_scatter(sent_back, "dp", scatter_dimension=0, tiled=True)
    totals = lax.psum((loss_part, scale_part), ("tower", "dp"))
    grad_embed = grad_own + returned
    again = (
        lax.all_gather(ln1_gain[0], "dp", axis=0, tiled=True),
        lax.all_gather(qkv_weight[0], "dp", axis=0, tiled=True),
        lax.all_gather(out_weight[0], "dp", axis=0, tiled=True),
        lax.all_gather(ln2_gain[0], "dp", axis=0, tiled=True),
        lax.all_gather(fc_weight[0], "dp", axis=0, tiled=True),
        lax.all_gather(down_weight[0], "dp", axis=0, tiled=True),
        lax.all_gather(final_gain[0], "dp", axis=0, tiled=True),
        lax.all_gather(embed_weight[0], "dp", axis=0, tiled=True),
    )
    (
        back_gain_one,
        back_qkv,
        back_out,
        back_gain_two,
        back_fc,
        back_down,
        back_gain_final,
        back_embed,
    ) = again
    cross_term = jnp.sum(grad_embed * projected, axis=-1, keepdims=True)
    grad_proj = inv_norm * grad_embed - projected * inv_norm * inv_norm * inv_norm * cross_term
    grad_proj_low = grad_proj.astype(bf16)
    grad_head = contract_cols(grad_proj_low, back_embed)
    grad_pooled, d_gain_final, d_bias_final = masked_norm_back(
        grad_head, back_gain_final.astype(f32), norm_final, inv_final, col_keep, width_real
    )
    grad_rows = (pool_hot[:, :, None] * grad_pooled[:, None, :]).reshape(flat_rows, width_all)
    grad_branch_low = grad_rows.astype(bf16)
    d_down_b = column_sum(grad_branch_low)
    grad_act = contract_cols(grad_branch_low, back_down)
    grad_pre_low = (
        grad_act * (gate_sig + GELU_K * hidden_pre * gate_sig * (1.0 - gate_sig))
    ).astype(bf16)
    d_fc_b = column_sum(grad_pre_low)
    grad_norm_two = contract_cols(grad_pre_low, back_fc)
    grad_mid_norm, d_gain_two, d_bias_two = masked_norm_back(
        grad_norm_two, back_gain_two.astype(f32), norm_two, inv_two, col_keep, width_real
    )
    grad_middle = grad_rows + grad_mid_norm
    grad_attn_low = grad_middle.astype(bf16)
    d_out_b = column_sum(grad_attn_low)
    grad_mix_low = (
        contract_cols(grad_attn_low, back_out)
        .astype(bf16)
        .reshape(samples, seq_rows, head_count, HD)
    )
    probs_again = jnp.exp(masked_scores() - log_total)
    probs_low = probs_again.astype(bf16)
    grad_value = jnp.einsum("shqk,sqhd->skhd", probs_low, grad_mix_low, preferred_element_type=f32)
    grad_probs = jnp.einsum("sqhd,skhd->shqk", grad_mix_low, value_all, preferred_element_type=f32)
    grad_scores = probs_again * (
        grad_probs - jnp.sum(probs_again * grad_probs, axis=-1, keepdims=True)
    )
    grad_scores_low = grad_scores.astype(bf16)
    grad_query = (
        jnp.einsum("shqk,skhd->sqhd", grad_scores_low, key_all, preferred_element_type=f32)
        * score_mult
    )
    grad_key = (
        jnp.einsum("shqk,sqhd->skhd", grad_scores_low, query_all, preferred_element_type=f32)
        * score_mult
    )
    grad_qkv_low = (
        jnp.stack([grad_query, grad_key, grad_value], axis=2)
        .astype(bf16)
        .reshape(flat_rows, 3 * width_all)
    )
    d_qkv_w = contract_rows(normed_one, grad_qkv_low).reshape(width_all, 3, width_all)
    qkv_sums = column_sum(grad_qkv_low).reshape(3, width_all)
    d_qv_b = jnp.stack([qkv_sums[0], qkv_sums[2]])
    grad_norm_one = contract_cols(grad_qkv_low, back_qkv.reshape(width_all, 3 * width_all))
    grad_in_norm, d_gain_one, d_bias_one = masked_norm_back(
        grad_norm_one, back_gain_one.astype(f32), norm_one, inv_one, col_keep, width_real
    )
    tokens_grad = (grad_middle + grad_in_norm).reshape(1, samples, seq_rows, width_all)
    d_embed_w = contract_rows(head_low, grad_proj_low)
    d_down_w = contract_rows(act_low, grad_branch_low)
    d_fc_w = contract_rows(normed_two, grad_pre_low)
    d_out_w = contract_rows(head_mix_low, grad_attn_low)
    shares = (
        lax.psum_scatter(d_gain_one, "dp", scatter_dimension=0, tiled=True),
        lax.psum_scatter(d_bias_one, "dp", scatter_dimension=0, tiled=True),
        lax.psum_scatter(d_qkv_w, "dp", scatter_dimension=0, tiled=True),
        lax.psum_scatter(d_qv_b, "dp", scatter_dimension=1, tiled=True),
        lax.psum_scatter(d_out_w, "dp", scatter_dimension=0, tiled=True),
        lax.psum_scatter(d_out_b, "dp", scatter_dimension=0, tiled=True),
        lax.psum_scatter(d_gain_two, "dp", scatter_dimension=0, tiled=True),
        lax.psum_scatter(d_bias_two, "dp", scatter_dimension=0, tiled=True),
        lax.psum_scatter(d_fc_w, "dp", scatter_dimension=0, tiled=True),
        lax.psum_scatter(d_fc_b, "dp", scatter_dimension=0, tiled=True),
        lax.psum_scatter(d_down_w, "dp", scatter_dimension=0, tiled=True),
        lax.psum_scatter(d_down_b, "dp", scatter_dimension=0, tiled=True),
        lax.psum_scatter(d_gain_final, "dp", scatter_dimension=0, tiled=True),
        lax.psum_scatter(d_bias_final, "dp", scatter_dimension=0, tiled=True),
        lax.psum_scatter(d_embed_w, "dp", scatter_dimension=0, tiled=True),
    )
    results = list(shares)
    outputs = [item[None] for item in results]
    loss = totals[0].reshape(1)
    logit_scale_grad = totals[1].reshape(1)
    return (
        block_out,
        tokens_grad,
        loss,
        outputs[0],
        outputs[1],
        outputs[2],
        outputs[3],
        outputs[4],
        outputs[5],
        outputs[6],
        outputs[7],
        outputs[8],
        outputs[9],
        outputs[10],
        outputs[11],
        outputs[12],
        outputs[13],
        outputs[14],
        logit_scale_grad,
    )


RING_Z = (0, 1, 2, 3, 3, 2, 1, 0)
RING_Y = (0, 0, 0, 0, 1, 1, 1, 1)
ITEMS = 16
N = ITEMS * 8
F32 = jnp.float32
BF16 = jnp.bfloat16
ANY = pl.BlockSpec(memory_space=pl.ANY)
VMEM = pl.BlockSpec(memory_space=pltpu.VMEM)
SMEM = pl.BlockSpec(memory_space=pltpu.SMEM)
SCALE = float(HD) ** -0.5
PAYLOAD = 128


def call(kernel, name, ins, outs, scratch, flops=0, touched=0, limit=67043328):
    return pl.pallas_call(
        kernel,
        name=name,
        out_shape=[jax.ShapeDtypeStruct(shape, dtype) for _, shape, dtype in outs],
        in_specs=[spec for spec, _ in ins],
        out_specs=[spec for spec, _, _ in outs],
        scratch_shapes=scratch,
        compiler_params=pltpu.CompilerParams(vmem_limit_bytes=limit),
        cost_estimate=pl.CostEstimate(flops=flops, bytes_accessed=touched, transcendentals=0),
    )(*[item for _, item in ins])


def dot(left, right, left_dim=1, right_dim=0):
    return lax.dot_general(
        left, right, (((left_dim,), (right_dim,)), ((), ())), preferred_element_type=F32
    )


def aligned(index, size):
    return pl.multiple_of(index, size)


def owner_table(dp_index):
    core = dp_index % 2
    row = dp_index // 2 % 2
    depth = dp_index // 4
    place = jnp.where(row == 0, depth, 7 - depth)

    def chip(where):
        where = (where + 8) % 8
        z = jnp.where(where < 4, where, 7 - where)
        y = jnp.where(where < 4, 0, 1)
        return (z * 2 + y) * 2

    sign = jnp.where(core == 0, -1, 1)
    found = [chip(place)]
    for hop in range(1, 4):
        found += [chip(place + sign * hop), chip(place - sign * hop)]
    return found + [chip(place + 4) + core, chip(place + 4) + 1 - core]


class Place:
    def __init__(self, lengths):
        self.dp = lax.axis_index("dp")
        self.text = lax.axis_index("tower") == 1
        self.lengths = lengths
        self.keep = (
            lax.broadcasted_iota(jnp.int32, (1, DI), 1) < jnp.where(self.text, DT, DI)
        ).astype(F32)
        self.winv = jnp.where(self.text, 1.0 / DT, 1.0 / DI).astype(F32)

    def length(self, s):
        return jnp.where(self.text, self.lengths[s], IMG_ROWS)

    def pool(self, s):
        return jnp.where(self.text, self.lengths[s] - 1, 0)

    def column(self, pick):
        ids = lax.broadcasted_iota(jnp.int32, (1, 8, 1), 1)
        column = jnp.zeros((1, 8, 1), jnp.int32)
        for s in range(8):
            column = jnp.where(ids == s, pick(s), column)
        return column

    def either(self, path, image):
        @pl.when(self.text)
        def _():
            path(DT, 77)

        @pl.when(jnp.logical_not(self.text))
        def _():
            path(DI, image)

    def mine(self, visit):
        for owner in range(ITEMS):

            @pl.when(self.dp == owner)
            def _(owner=owner):
                visit(owner)


def copy(src, dst, sem):
    found = pltpu.make_async_copy(src, dst, sem)
    found.start()
    return found


def drain(dst, sem):
    pltpu.make_async_copy(dst, dst, sem).wait()


def fetch(owners, refs, row, rows, dst, sem):
    for owner, ref in zip(owners, refs):
        if len(ref.shape) == 3:
            copy(ref.at[:, pl.ds(row, rows), :], dst.at[pl.ds(owner, 2)], sem)
        else:
            copy(ref.at[pl.ds(row, rows), :], dst.at[owner], sem)


def embed_matrix(packed):
    tail = jnp.concatenate([packed[:, 0:16, EMB:DI], packed[:, 16:32, EMB:DI]], axis=2)
    return jnp.concatenate([packed[:, :, 0:EMB], tail], axis=1).reshape(DI, EMB)


def normalize(values, keep, winv):
    mean = jnp.sum(values, axis=-1, keepdims=True) * winv
    centred = (values - mean) * keep
    var = jnp.sum(centred * centred, axis=-1, keepdims=True) * winv
    inv = lax.rsqrt(var + EPS)
    return centred * inv, inv


def normalize_back(grad_out, gain, normed, inv, keep, winv):
    grad_normed = grad_out * gain
    mean_grad = jnp.sum(grad_normed, axis=-1, keepdims=True) * winv
    mean_cross = jnp.sum(grad_normed * normed, axis=-1, keepdims=True) * winv
    return keep * inv * (grad_normed - mean_grad - normed * mean_cross)


def row_sum(values):
    return jnp.sum(values, axis=0, keepdims=True)


def head_rows(rows):
    heads = lax.broadcasted_iota(jnp.int32, rows.shape, 1) // HD
    parts = [jnp.where(heads == head, rows, 0.0) for head in range(16)]
    return jnp.concatenate(parts, axis=0).astype(BF16)


def chunks(count, visit):
    @pl.loop(0, count // 14)
    def _(i):
        visit(i * 14, aligned(i * 112, 16), 14)

    if count % 14:
        at = count - count % 14
        visit(at, at * 8, count % 14)


def pack_first_kernel(lengths, qkv, tok, *rest):
    here = Place(lengths)
    vectors, (qv_bias, fc_bias, out) = rest[:8], rest[8:]
    out[0:144, :] = qkv[...]
    sub = lax.broadcasted_iota(jnp.int32, (8, DI), 0)
    pooled = jnp.zeros((8, DI), F32)
    for s in range(8):
        pooled = jnp.where(sub == s, tok[here.pool(s)].astype(F32), pooled)
    out[144:152, :] = pooled.astype(BF16)
    lane = lax.broadcasted_iota(jnp.int32, (1, DI), 1) // 48 == here.dp
    short = [v[...].astype(F32) for v in vectors]
    pair = qv_bias[...].astype(F32)
    short[2:2] = [pair[0:1], pair[1:2]]
    rows = [jnp.where(lane, jnp.concatenate([v] * ITEMS, axis=1), 0.0) for v in short]
    wide = lax.broadcasted_iota(jnp.int32, (1, 4 * DI), 1) // 192 == here.dp
    fc = jnp.where(wide, jnp.concatenate([fc_bias[...].astype(F32)] * ITEMS, axis=1), 0.0)
    rows += [fc[:, i * DI : (i + 1) * DI] for i in range(4)]
    row_id = lax.broadcasted_iota(jnp.int32, (16, DI), 0)
    small = jnp.zeros((16, DI), F32)
    for at, row in enumerate(rows):
        small = jnp.where(row_id == at, jnp.broadcast_to(row, (16, DI)), small)
    out[152:168, :] = small.astype(BF16)


def pack_first(lengths, qkv, tok, vectors, qv_bias, fc_bias):
    return call(
        pack_first_kernel,
        "pack_first",
        [(SMEM, lengths)] + [(VMEM, item) for item in (qkv, tok, *vectors, qv_bias, fc_bias)],
        [(VMEM, (168, DI), BF16)],
        [],
        touched=1_500_000,
    )[0]


def pack_rest_kernel(w_out, w_fc, w_emb, out):
    out[0:48, :] = w_out[...]
    out[48:80, 0:EMB] = w_emb[0:32, :]
    out[48:64, EMB:DI] = w_emb[32:48, 0:256]
    out[64:80, EMB:DI] = w_emb[32:48, 256:EMB]
    for block in range(4):
        out[80 + 48 * block : 128 + 48 * block, :] = w_fc[:, block * DI : (block + 1) * DI]


def pack_rest(w_out, w_fc, w_emb):
    return call(
        pack_rest_kernel,
        "pack_rest",
        [(VMEM, item) for item in (w_out, w_fc, w_emb)],
        [(VMEM, (272, DI), BF16)],
        [],
        touched=1_500_000,
    )[0]


def sample_limits(here):
    lane_sample = lax.broadcasted_iota(jnp.int32, (1, 128), 1) % 8
    limit = jnp.zeros((1, 128), jnp.int32)
    for s in range(8):
        limit = jnp.where(lane_sample == s, here.length(s), limit)
    return limit


def own_heads(tall, width):
    heads = lax.broadcasted_iota(jnp.int32, (8, width), 1) // HD
    total = jnp.zeros((8, width), F32)
    for head in range(width // HD):
        total = total + jnp.where(heads == head, tall[head * 8 : head * 8 + 8], 0.0)
    if width < DI:
        total = jnp.concatenate([total, jnp.zeros((8, DI - width), F32)], axis=1)
    return total


def tall_rows(rows):
    return jnp.concatenate([rows[:, i * 128 : (i + 1) * 128] for i in range(DI // 128)], axis=0)


def wide_rows(tall):
    tall = tall.astype(F32)
    return jnp.concatenate(
        [tall[:, i * 8 : i * 8 + 8, :].reshape(N, 128) for i in range(DI // 128)], axis=1
    )


def pooled_kernel(lengths, tok_hbm, *rest):
    first, outs, scratch = rest[:9], rest[9:18], rest[18:]
    keys_hbm, values_hbm, norm_hbm, normed_hbm, vec, pooled, q_own, probs_out, gv_out = outs
    weights, small, tok, normed, keys, values, norm_low, sems, ends = scratch
    here = Place(lengths)
    owners = owner_table(here.dp)
    tok_in = copy(tok_hbm, tok, sems.at[2])
    fetch(owners, first, 152, 16, small, sems.at[0])
    fetch(owners, first, 0, 144, weights, sems.at[1])
    keep, winv = here.keep, here.winv
    drain(small, sems.at[0])
    vec[...] = jnp.sum(small[...].astype(F32), axis=0)
    limit = sample_limits(here)
    tok_in.wait()
    sub = lax.broadcasted_iota(jnp.int32, (8, DI), 0)
    picked = jnp.zeros((8, DI), F32)
    for s in range(8):
        picked = jnp.where(sub == s, tok[here.pool(s)].astype(F32), picked)
    pooled_norm, _ = normalize(picked, keep, winv)
    pooled_normed = (pooled_norm * vec[0:1, :] + vec[1:2, :]).astype(BF16)

    def norm_chunk(position, row, count):
        x = tok[pl.ds(position, count)].astype(F32).reshape(count * 8, DI)
        norm, _ = normalize(x, keep, winv)
        norm_low[pl.ds(row, count * 8), :] = norm.astype(BF16)
        normed[pl.ds(row, count * 8), :] = (norm * vec[0:1, :] + vec[1:2, :]).astype(BF16)

    def path(width, count):
        rows = count * 8
        chunks(count, norm_chunk)
        saved = [copy(norm_low, norm_hbm, ends.at[0]), copy(normed, normed_hbm, ends.at[1])]
        drain(weights, sems.at[1])
        for third, low, bias in ((1, keys, None), (2, values, 3)):

            weight = weights[:, third * 48 : third * 48 + 48, 0:width].reshape(DI, width)[0:width]
            prod = dot(normed[0:rows, 0:width], weight)
            if bias is not None:
                prod = prod + vec[bias : bias + 1, 0:width]
            low[0:rows, 0:width] = prod.astype(BF16)

        saved += [copy(keys, keys_hbm, ends.at[2]), copy(values, values_hbm, ends.at[3])]
        query = dot(pooled_normed, weights[:, 0:48, :].reshape(DI, DI)) + vec[2:3, :]
        query = query.astype(BF16).astype(F32)
        q_own[...] = query
        q_rows = head_rows(query)
        raw = dot(keys[0:rows, 0:width], q_rows[:, 0:width], 1, 1) * SCALE
        row = lax.broadcasted_iota(jnp.int32, (rows, 128), 0)
        lane = lax.broadcasted_iota(jnp.int32, (rows, 128), 1)
        valid = (lane % 8 == row % 8) & (row // 8 < limit) & (lane < width // 8)
        raw = jnp.where(valid, raw, NEG_FILL)
        terms = jnp.where(valid, jnp.exp(raw - jnp.max(raw, axis=0, keepdims=True)), 0.0)
        probs = terms / jnp.maximum(row_sum(terms), 1e-30)
        low_probs = probs.astype(BF16)
        probs_out[0:rows, :] = probs
        gv_out[0:rows, :] = low_probs
        mixed = own_heads(dot(low_probs, values[0:rows, 0:width], 0, 0), width)
        tall = tall_rows(mixed).astype(BF16)
        for owner in range(ITEMS):
            pooled[owner] = tall
        for item in saved:
            item.wait()

    here.either(path, 56)


def attend_pooled(lengths, tok, first):
    rows = tok.shape[0] * tok.shape[1]
    return call(
        pooled_kernel,
        "attend_pooled",
        [(SMEM, lengths), (ANY, tok)] + [(ANY, r) for r in first],
        [(ANY, (rows, DI), BF16)] * 4
        + [
            (VMEM, (16, DI), F32),
            (VMEM, (ITEMS, 48, 128), BF16),
            (VMEM, (8, DI), F32),
            (VMEM, (rows, 128), F32),
            (VMEM, (rows, 128), BF16),
        ],
        [
            pltpu.VMEM((ITEMS, 144, DI), BF16),
            pltpu.VMEM((ITEMS, 16, DI), BF16),
            pltpu.VMEM(tok.shape, BF16),
            pltpu.VMEM((rows, DI), BF16),
            pltpu.VMEM((rows, DI), BF16),
            pltpu.VMEM((rows, DI), BF16),
            pltpu.VMEM((rows, DI), BF16),
            pltpu.SemaphoreType.DMA((3,)),
            pltpu.SemaphoreType.DMA((4,)),
        ],
        flops=7_000_000_000,
        touched=10_000_000,
    )


def attend_kernel(lengths, vec, gv, normed_hbm, keys_hbm, values_hbm, norm_hbm, *rest):
    first, (mixed_hbm, z_value), scratch = rest[:9], rest[9:11], rest[11:]
    weights, normed, keys, values, norm_low, mixed, qf, kf, vf, mf, sems = scratch
    here = Place(lengths)
    owners = owner_table(here.dp)
    fetch(owners, first, 0, 48, weights, sems.at[0])
    early = [
        copy(src, dst, sems.at[1 + i])
        for i, (src, dst) in enumerate(
            ((normed_hbm, normed), (keys_hbm, keys), (values_hbm, values), (norm_hbm, norm_low))
        )
    ]
    drain(weights, sems.at[0])
    early[0].wait()
    early[1].wait()
    early[2].wait()

    def path(width, count):
        rows = count * 8
        span = 80 if count == 77 else count
        if span > count:
            for dst in (qf, kf, vf):
                dst[:, rows : span * 8, :] = jnp.zeros((6, span * 8 - rows, 128), F32)

        weight = weights[:, :, 0:width].reshape(DI, width)[0:width]
        prod = dot(normed[0:rows, 0:width], weight) + vec[2:3, 0:width]
        prod = prod.astype(BF16).astype(F32) * SCALE
        for pair in range(width // 128):
            lanes = pl.ds(pair * 128, 128)
            qf[pair, 0:rows, :] = prod[:, pair * 128 : pair * 128 + 128]
            kf[pair, 0:rows, :] = keys[0:rows, lanes].astype(F32)
            vf[pair, 0:rows, :] = values[0:rows, lanes].astype(F32)

        key_pos = lax.broadcasted_iota(jnp.int32, (span, 2 * span), 0)
        query_pos = lax.broadcasted_iota(jnp.int32, (span, 2 * span), 1) % span
        low_half = lax.broadcasted_iota(jnp.int32, (span, 128), 1) < HD

        @pl.loop(0, 8, unroll=2)
        def _(s):
            at = pl.ds(s, span, stride=8)
            allowed = key_pos < here.length(s)
            if width == DT:
                allowed = allowed & (key_pos <= query_pos)
            pairs = range(width // 128)
            raws = []
            for pair in pairs:
                query, key = qf.at[pair][at, :], kf.at[pair][at, :].astype(BF16)
                spread = [jnp.where(low_half, query, 0.0), jnp.where(low_half, 0.0, query)]
                spread = jnp.concatenate(spread, axis=0).astype(BF16)
                raws.append(dot(key, spread, 1, 1))
            probs = []
            for raw in raws:
                raw = jnp.where(allowed, raw, NEG_FILL)
                terms = jnp.exp(raw - jnp.max(raw, axis=0, keepdims=True))
                probs.append((terms / jnp.sum(terms, axis=0, keepdims=True)).astype(BF16))
            for pair in pairs:
                out = dot(probs[pair], vf.at[pair][at, :].astype(BF16), 0, 0)
                mf.at[pair][at, :] = jnp.where(low_half, out[0:span], out[span : 2 * span])

        stored = []
        for i in range(width // 128):
            lanes = pl.ds(128 * i, 128)
            mixed[0:rows, lanes] = mf[i, 0:rows, :].astype(BF16)
            stored.append(copy(mixed.at[0:rows, lanes], mixed_hbm.at[0:rows, lanes], sems.at[5 + i]))
        early[3].wait()
        z_value[...] = pltpu.roll(dot(norm_low[0:rows, :], gv[0:rows, :], 0, 0), 96, 1).astype(BF16)
        for item in stored:
            item.wait()

    here.either(path, 56)


def attend(lengths, vec, gv, normed, keys, values, norm_low, first):
    rows = keys.shape[0]
    high = rows + 24
    return call(
        attend_kernel,
        "attend",
        [(SMEM, lengths), (VMEM, vec), (VMEM, gv)]
        + [(ANY, r) for r in (normed, keys, values, norm_low, *first)],
        [(ANY, (rows, DI), BF16), (VMEM, (DI, 128), BF16)],
        [
            pltpu.VMEM((ITEMS, 48, DI), BF16),
            pltpu.VMEM((rows, DI), BF16),
            pltpu.VMEM((rows, DI), BF16),
            pltpu.VMEM((rows, DI), BF16),
            pltpu.VMEM((rows, DI), BF16),
            pltpu.VMEM((rows, DI), BF16),
            pltpu.VMEM((6, high, 128), F32),
            pltpu.VMEM((6, high, 128), F32),
            pltpu.VMEM((6, high, 128), F32),
            pltpu.VMEM((6, high, 128), F32),
            pltpu.SemaphoreType.DMA((11,)),
        ],
        flops=9_000_000_000,
        touched=10_000_000,
    )


def forward_kernel(lengths, vec, mixes, *rest):
    first, second, down = rest[:9], rest[9:18], rest[18:27]
    outs, scratch = rest[27:38], rest[38:]
    (e_out, proj_out, normf_out, invf_out, norm2_out, inv2_out, slope_out, n2_sl, mix_sl, head_sl,
     act_sl) = outs
    w_out, w_fc, w_down, w_emb, xs, mix, n2, act, head_all, sems = scratch
    here = Place(lengths)
    owners = owner_table(here.dp)
    fetch(owners, second, 0, 48, w_out, sems.at[1])
    fetch(owners, first, 144, 8, xs, sems.at[0])
    fetch(owners, second, 80, 192, w_fc, sems.at[2])
    keep, winv = here.keep, here.winv
    mix[...] = wide_rows(mixes[...]).astype(BF16)
    drain(w_out, sems.at[1])
    drain(xs, sems.at[0])
    fetch(owners, down, 0, 192, w_down, sems.at[3])
    fetch(owners, second, 48, 32, w_emb, sems.at[4])
    stream = xs[...].astype(F32).reshape(N, DI)
    middle = stream + dot(mix[...], w_out[...].reshape(DI, DI)) + vec[4:5, :]
    norm2, inv2 = normalize(middle, keep, winv)
    n2[...] = (norm2 * vec[5:6, :] + vec[6:7, :]).astype(BF16)
    norm2_out[...] = norm2
    inv2_out[...] = jnp.broadcast_to(inv2, (N, 128))
    drain(w_fc, sems.at[2])
    for block in range(4):
        lanes = pl.ds(block * DI, DI)
        weight = w_fc[:, block * 48 : block * 48 + 48, :].reshape(DI, DI)
        pre = dot(n2[...], weight) + vec[10 + block : 11 + block, :]
        gate = jax.nn.sigmoid(GELU_K * pre)
        act[:, lanes] = (pre * gate).astype(BF16)
        slope_out[:, lanes] = gate + GELU_K * pre * gate * (1.0 - gate)

    drain(w_down, sems.at[3])
    last = middle + dot(act[...], w_down[...].reshape(4 * DI, DI)) + vec[7:8, :]
    normf, invf = normalize(last, keep, winv)
    normf_out[...] = normf
    invf_out[...] = jnp.broadcast_to(invf, (N, 128))
    head_all[...] = (normf * vec[8:9, :] + vec[9:10, :]).astype(BF16)
    drain(w_emb, sems.at[4])
    proj = dot(head_all[...], embed_matrix(w_emb[...]))
    proj_out[...] = proj
    scale = lax.rsqrt(jnp.sum(proj * proj, axis=-1, keepdims=True) + NORM_EPS)
    e_out[...] = (proj * scale).astype(BF16)

    def mine(owner):
        lanes = slice(owner * 48, owner * 48 + 48)
        n2_sl[...] = n2[:, lanes]
        mix_sl[...] = mix[:, lanes]
        head_sl[...] = head_all[:, lanes]
        act_sl[...] = act[:, owner * 192 : owner * 192 + 192]

    here.mine(mine)


def pooled_forward(lengths, vec, mixes, first, second, down):
    return call(
        forward_kernel,
        "pooled_forward",
        [(SMEM, lengths), (VMEM, vec), (VMEM, mixes)] + [(ANY, r) for r in (*first, *second, *down)],
        [
            (VMEM, (N, EMB), BF16),
            (VMEM, (N, EMB), F32),
            (VMEM, (N, DI), F32),
            (VMEM, (N, 128), F32),
            (VMEM, (N, DI), F32),
            (VMEM, (N, 128), F32),
            (VMEM, (N, 4 * DI), F32),
            (VMEM, (N, 48), BF16),
            (VMEM, (N, 48), BF16),
            (VMEM, (N, 48), BF16),
            (VMEM, (N, 192), BF16),
        ],
        [
            pltpu.VMEM((ITEMS, 48, DI), BF16),
            pltpu.VMEM((ITEMS, 192, DI), BF16),
            pltpu.VMEM((ITEMS, 192, DI), BF16),
            pltpu.VMEM((ITEMS, 32, DI), BF16),
            pltpu.VMEM((ITEMS, 8, DI), BF16),
            pltpu.VMEM((N, DI), BF16),
            pltpu.VMEM((N, DI), BF16),
            pltpu.VMEM((N, 4 * DI), BF16),
            pltpu.VMEM((N, DI), BF16),
            pltpu.SemaphoreType.DMA((5,)),
        ],
        flops=11_000_000_000,
        touched=16_000_000,
        limit=50 * 1024 * 1024,
    )


def middle_kernel(lengths, tok_hbm, vec, mixed_hbm, *rest):
    second = rest[:9]
    (n2_hbm, middle_hbm), scratch = rest[9:11], rest[11:]
    w_out, middle, tok, mixed, n2, sems = scratch
    here = Place(lengths)
    owners = owner_table(here.dp)
    rows_in = copy(mixed_hbm, mixed, sems.at[1])
    fetch(owners, second, 0, 48, w_out, sems.at[0])
    tok_in = copy(tok_hbm, tok, sems.at[2])
    keep, winv = here.keep, here.winv
    rows_in.wait()
    drain(w_out, sems.at[0])

    def norm_chunk(position, row, count):
        at = pl.ds(row, count * 8)
        total = middle[at, :] + tok[pl.ds(position, count)].astype(F32).reshape(count * 8, DI)
        middle[at, :] = total
        norm, _ = normalize(total, keep, winv)
        n2[at, :] = (norm * vec[5:6, :] + vec[6:7, :]).astype(BF16)
        copy(middle.at[at, :], middle_hbm.at[at, :], sems.at[3])
        copy(n2.at[at, :], n2_hbm.at[at, :], sems.at[4])

    def path(width, count):
        rows = count * 8

        weight = w_out[:, :, 0:width].reshape(DI, width)[0:width]
        middle[0:rows, 0:width] = dot(mixed[0:rows, 0:width], weight) + vec[4:5, 0:width]
        if width < DI:
            middle[0:rows, width:DI] = jnp.zeros((rows, DI - width), F32)
        tok_in.wait()
        chunks(count, norm_chunk)
        drain(middle.at[pl.ds(0, rows), :], sems.at[3])
        drain(n2.at[pl.ds(0, rows), :], sems.at[4])

    here.either(path, 56)


def middle_part(lengths, tok, vec, mixed, second):
    rows = mixed.shape[0]
    return call(
        middle_kernel,
        "middle_part",
        [(SMEM, lengths), (ANY, tok), (VMEM, vec), (ANY, mixed)] + [(ANY, r) for r in second],
        [(ANY, (rows, DI), BF16), (ANY, (rows, DI), F32)],
        [
            pltpu.VMEM((ITEMS, 48, DI), BF16),
            pltpu.VMEM((rows, DI), F32),
            pltpu.VMEM(tok.shape, BF16),
            pltpu.VMEM((rows, DI), BF16),
            pltpu.VMEM((rows, DI), BF16),
            pltpu.SemaphoreType.DMA((5,)),
        ],
        flops=5_000_000_000,
        touched=8_000_000,
        limit=50 * 1024 * 1024,
    )


def one_direction(left, right, mult):
    sims = dot(left, right, 1, 1)
    logits = mult * sims
    top = jnp.max(logits, axis=-1, keepdims=True)
    total = top + jnp.log(jnp.sum(jnp.exp(logits - top), axis=-1, keepdims=True))
    count = sims.shape[0]
    eye = lax.broadcasted_iota(jnp.int32, (count, count), 0) == lax.broadcasted_iota(
        jnp.int32, (count, count), 1
    )
    hot = eye.astype(F32)
    lost = jnp.sum(total - jnp.sum(hot * logits, axis=-1, keepdims=True), axis=0, keepdims=True)
    grad = (jnp.exp(logits - total) - hot) * 0.5
    scale = jnp.sum(jnp.sum(grad * sims, axis=-1, keepdims=True), axis=0, keepdims=True)
    return lost, scale, mult * grad


def pack_payload(payload, z_key, z_value, sum_key, sum_value, grad_q):
    lane = lax.broadcasted_iota(jnp.int32, (1, 128), 1)
    upper = jnp.where(lane < 96, z_key, z_value).astype(BF16)
    blocks = [grad_q[:, i * 128 : (i + 1) * 128] for i in range(6)]
    beside = jnp.concatenate(
        [half for block in blocks[:3] for half in (pltpu.roll(block, 64, 1), block)], axis=0
    )
    key_high = sum_key.astype(BF16).astype(F32)
    value_high = sum_value.astype(BF16).astype(F32)
    row_id = lax.broadcasted_iota(jnp.int32, (8, 128), 0)
    sums = jnp.zeros((8, 128), F32)
    for at, value in enumerate((key_high, sum_key - key_high, value_high, sum_value - value_high)):
        sums = jnp.where(row_id == at, jnp.broadcast_to(value, (8, 128)), sums)
    last = jnp.concatenate([*blocks[3:], sums], axis=0).astype(BF16)
    for owner in range(ITEMS):
        base, rows = owner * PAYLOAD, slice(owner * 48, owner * 48 + 48)
        payload[base : base + 48, :] = upper[rows]
        payload[base + 48 : base + 96, :] = jnp.where(lane < 64, z_value[rows], beside).astype(BF16)
        payload[base + 96 : base + 128, :] = last


def chain_kernel(lengths, log_mult, e_own_ref, e_oth_ref, vec, head_sl, act_sl, n2_sl, mix_sl, *rest):
    (proj_hbm, normf_hbm, invf_hbm, norm2_hbm, inv2_hbm, slope_hbm, keys_hbm, values_hbm, norm_hbm, probs_hbm,
     gv_hbm, z_hbm), rest = rest[:12], rest[12:]
    second, down = rest[:9], rest[9:18]
    outs, scratch = rest[18:37], rest[37:]
    (loss_out, scale_out, d_emb_hbm, d_down_hbm, d_fc_hbm, d_out_hbm, g_final, b_final, b_down, g_two, b_two, b_out, b_fc,
     mid_own, gm_out, gm_own, payload, gk_out, gq_out) = outs
    (w_out, w_fc, w_down, w_emb, gpre, mid_all, proj_v, normf_v, invf_v, norm2_v, inv2_v, slope, keys,
     values, norm_low, probs_v, gv_v, z_v, vec_grads, fcb_grads, d_emb, d_down, d_fc, d_out, sems, ins, ends) = scratch
    here = Place(lengths)
    owners = owner_table(here.dp)
    early = [
        copy(src, dst, ins.at[i])
        for i, (src, dst) in enumerate(
            ((proj_hbm, proj_v), (normf_hbm, normf_v), (invf_hbm, invf_v))
        )
    ]
    fetch(owners, second, 48, 32, w_emb, sems.at[0])
    fetch(owners, down, 0, 192, w_down, sems.at[1])
    slope_in = copy(slope_hbm, slope, ins.at[3])
    fetch(owners, second, 80, 192, w_fc, sems.at[2])
    later = [copy(norm2_hbm, norm2_v, ins.at[4]), copy(inv2_hbm, inv2_v, ins.at[5])]
    fetch(owners, second, 0, 48, w_out, sems.at[3])
    last = [
        copy(src, dst, ins.at[6 + i])
        for i, (src, dst) in enumerate(
            ((keys_hbm, keys), (values_hbm, values), (norm_hbm, norm_low), (probs_hbm, probs_v),
             (gv_hbm, gv_v), (z_hbm, z_v))
        )
    ]
    keep, winv = here.keep, here.winv
    text = here.text.astype(F32)
    mult = jnp.exp(jnp.full((1, 128), log_mult[0], F32))[:, 0:1]
    own, oth = e_own_ref[...].astype(F32), e_oth_ref[...].astype(F32)
    e_img = (own * (1.0 - text) + oth * text).astype(BF16)
    e_txt = (oth * (1.0 - text) + own * text).astype(BF16)
    lost_img, scale_img, grad_img = one_direction(e_img, e_txt, mult)
    lost_txt, scale_txt, grad_txt = one_direction(e_txt, e_img, mult)
    loss_out[...] = (lost_img + lost_txt) / (2.0 * N)
    scale_out[...] = mult * (scale_img + scale_txt)
    grad_own = (grad_img * (1.0 - text) + grad_txt * text).astype(BF16)
    grad_oth = (grad_txt * (1.0 - text) + grad_img * text).astype(BF16)
    oth_low = e_oth_ref[...]
    grad_e = dot(grad_own, oth_low) + dot(grad_oth, oth_low, 0, 0)
    for item in early:
        item.wait()
    drain(w_emb, sems.at[0])
    proj = proj_v[...]
    r = lax.rsqrt(jnp.sum(proj * proj, axis=-1, keepdims=True) + NORM_EPS)
    cross = jnp.sum(grad_e * proj, axis=-1, keepdims=True)
    grad_proj = (r * grad_e - proj * (r * r * r) * cross).astype(BF16)
    grad_head = dot(grad_proj, embed_matrix(w_emb[...]), 1, 1)
    normf = normf_v[...]
    grad_y = normalize_back(grad_head, vec[8:9, :], normf, invf_v[:, 0:1], keep, winv)
    branch = grad_y.astype(BF16)
    d_emb[...] = dot(head_sl[...], grad_proj, 0, 0)
    stored = [copy(d_emb, d_emb_hbm, ends.at[0])]
    vec_grads[0:1, :] = row_sum(grad_head * normf)
    vec_grads[1:2, :] = row_sum(grad_head)
    vec_grads[2:3, :] = row_sum(branch.astype(F32))
    d_down[...] = dot(act_sl[...], branch, 0, 0)
    stored.append(copy(d_down, d_down_hbm, ends.at[1]))
    drain(w_down, sems.at[1])
    slope_in.wait()
    for block in range(4):
        lanes = pl.ds(block * DI, DI)
        back = dot(branch, w_down[block * 4 : block * 4 + 4].reshape(DI, DI), 1, 1)
        low = (back * slope[:, lanes]).astype(BF16)
        gpre[:, lanes] = low
        fcb_grads[:, lanes] = jnp.broadcast_to(row_sum(low.astype(F32)), (8, DI))

    drain(w_fc, sems.at[2])
    grad_n2 = jnp.zeros((N, DI), F32)
    for block in range(4):
        weight = w_fc[:, block * 48 : block * 48 + 48, :].reshape(DI, DI)
        grad_n2 = grad_n2 + dot(gpre[:, block * DI : block * DI + DI], weight, 1, 1)
    for item in later:
        item.wait()
    norm2 = norm2_v[...]
    vec_grads[3:4, :] = row_sum(grad_n2 * norm2)
    vec_grads[4:5, :] = row_sum(grad_n2)
    grad_mid = grad_y + normalize_back(grad_n2, vec[5:6, :], norm2, inv2_v[:, 0:1], keep, winv)
    mid_all[...] = grad_mid
    own_rows = pl.ds(aligned(here.dp * 8, 8), 8)
    mid_own[...] = mid_all[own_rows, :]
    attn = grad_mid.astype(BF16)
    vec_grads[5:6, :] = row_sum(attn.astype(F32))
    drain(w_out, sems.at[3])
    gm_out[...] = dot(attn, w_out[...].reshape(DI, DI), 1, 1).astype(BF16).astype(F32)
    gm_own[...] = gm_out[own_rows, :]

    @pl.loop(0, 6)
    def _(j):
        lanes = pl.ds(aligned(j * 512, 512), 512)
        d_fc[:, lanes] = dot(n2_sl[...], gpre[:, lanes], 0, 0)

    d_out[...] = dot(mix_sl[...], attn, 0, 0)
    stored += [copy(d_fc, d_fc_hbm, ends.at[2]), copy(d_out, d_out_hbm, ends.at[3])]

    def mine(owner):
        lanes = slice(owner * 48, owner * 48 + 48)
        for at, dst in enumerate((g_final, b_final, b_down, g_two, b_two, b_out)):
            dst[...] = vec_grads[at : at + 1, lanes]
        b_fc[...] = fcb_grads[0:1, owner * 192 : owner * 192 + 192]

    here.mine(mine)
    for item in last:
        item.wait()
    m_rows = head_rows(gm_own[...])

    def path(width, count):
        rows = count * 8
        probs = probs_v[0:rows, :]
        grad_probs = dot(values[0:rows, 0:width], m_rows[:, 0:width], 1, 1)
        gk = (probs * (grad_probs - row_sum(probs * grad_probs))).astype(BF16)
        gv = gv_v[0:rows, :]
        gk_out[0:rows, :] = gk
        gq_low = own_heads(dot(gk, keys[0:rows, 0:width], 0, 0) * SCALE, width).astype(BF16)
        gq_out[...] = gq_low
        z_key = dot(norm_low[0:rows, :], gk, 0, 0)
        pack_payload(
            payload,
            z_key,
            z_v[...].astype(F32),
            row_sum(gk.astype(F32)),
            pltpu.roll(jnp.broadcast_to(row_sum(gv.astype(F32)), (8, 128)), 96, 1)[0:1],
            gq_low.astype(F32),
        )

    here.either(path, 56)
    for item in stored:
        item.wait()


def chain(lengths, log_mult, e_own, e_oth, vec, slices, saved, second, down):
    rows = saved[-2].shape[0]
    return call(
        chain_kernel,
        "chain",
        [(SMEM, lengths), (SMEM, log_mult)]
        + [(VMEM, item) for item in (e_own, e_oth, vec, *slices)]
        + [(ANY, r) for r in (*saved, *second, *down)],
        [
            (VMEM, (1, 1), F32),
            (VMEM, (1, 1), F32),
            (ANY, (48, EMB), F32),
            (ANY, (192, DI), F32),
            (ANY, (48, 4 * DI), F32),
            (ANY, (48, DI), F32),
        ]
        + [(VMEM, (1, 48), F32)] * 6
        + [
            (VMEM, (1, 192), F32),
            (VMEM, (8, DI), F32),
            (VMEM, (N, DI), F32),
            (VMEM, (8, DI), F32),
            (VMEM, (ITEMS * PAYLOAD, 128), BF16),
            (VMEM, (rows, 128), BF16),
            (VMEM, (8, DI), BF16),
        ],
        [
            pltpu.VMEM((ITEMS, 48, DI), BF16),
            pltpu.VMEM((ITEMS, 192, DI), BF16),
            pltpu.VMEM((ITEMS, 192, DI), BF16),
            pltpu.VMEM((ITEMS, 32, DI), BF16),
            pltpu.VMEM((N, 4 * DI), BF16),
            pltpu.VMEM((N, DI), F32),
            pltpu.VMEM((N, EMB), F32),
            pltpu.VMEM((N, DI), F32),
            pltpu.VMEM((N, 128), F32),
            pltpu.VMEM((N, DI), F32),
            pltpu.VMEM((N, 128), F32),
            pltpu.VMEM((N, 4 * DI), F32),
            pltpu.VMEM((rows, DI), BF16),
            pltpu.VMEM((rows, DI), BF16),
            pltpu.VMEM((rows, DI), BF16),
            pltpu.VMEM((rows, 128), F32),
            pltpu.VMEM((rows, 128), BF16),
            pltpu.VMEM((DI, 128), BF16),
            pltpu.VMEM((8, DI), F32),
            pltpu.VMEM((8, 4 * DI), F32),
            pltpu.VMEM((48, EMB), F32),
            pltpu.VMEM((192, DI), F32),
            pltpu.VMEM((48, 4 * DI), F32),
            pltpu.VMEM((48, DI), F32),
            pltpu.SemaphoreType.DMA((4,)),
            pltpu.SemaphoreType.DMA((12,)),
            pltpu.SemaphoreType.DMA((4,)),
        ],
        flops=15_000_000_000,
        touched=20_000_000,
        limit=50 * 1024 * 1024,
    )


def close_kernel(lengths, tok, vec, gk, gv, q_own, gm_own, gq, mid_own, n2_hbm, middle_hbm, *rest):
    first, second, down = rest[:9], rest[9:18], rest[18:27]
    (block_out, out_hbm, q_out, norm_sl), scratch = rest[27:31], rest[31:]
    weights, w_fc, w_down, n2, act, middle, acc, xs, norm1_all, out, sems = scratch
    here = Place(lengths)
    owners = owner_table(here.dp)
    fetch(owners, first, 0, 144, weights, sems.at[0])
    fetch(owners, first, 144, 8, xs, sems.at[5])
    ready = copy(n2_hbm, n2, sems.at[1])
    fetch(owners, second, 80, 192, w_fc, sems.at[4])
    fetch(owners, down, 0, 192, w_down, sems.at[3])
    early = [copy(middle_hbm, middle, sems.at[2])]
    keep, winv = here.keep, here.winv
    q_rows = head_rows(q_own[...])
    m_rows = head_rows(gm_own[...])
    pool = here.column(here.pool)
    length = here.column(here.length)
    all_rows = out.shape[0]
    drain(weights, sems.at[0])
    u_key = (dot(q_rows, weights[:, 48:96, :].reshape(DI, DI), 1, 1) * SCALE).astype(BF16)
    u_value = dot(m_rows, weights[:, 96:144, :].reshape(DI, DI), 1, 1).astype(BF16)
    u_query = dot(gq[...], weights[:, 0:48, :].reshape(DI, DI), 1, 1)

    def path(width, count):
        rows = count * 8
        acc[0:rows, :] = dot(gk[0:rows, :], u_key) + dot(gv[0:rows, :], u_value)

        def back_chunk(position, row, count):
            at = pl.ds(row, count * 8)
            hit = lax.broadcasted_iota(jnp.int32, (count, 8, DI), 0) + position == pool
            norm, inv = normalize(tok[pl.ds(position, count)].astype(F32).reshape(count * 8, DI), keep, winv)
            total = acc[at, :] + jnp.where(hit, u_query[None], 0.0).reshape(count * 8, DI)
            back = normalize_back(total, vec[0:1, :], norm, inv, keep, winv)
            out[at, :] = back + jnp.where(hit, mid_own[...][None], 0.0).reshape(count * 8, DI)

        if rows < all_rows:
            out[rows:all_rows, :] = jnp.zeros((all_rows - rows, DI), F32)
        chunks(count, back_chunk)
        stored = copy(out, out_hbm, sems.at[6])
        short = count if width == DT else IMG_ROWS
        rows = short * 8
        ready.wait()
        drain(w_fc, sems.at[4])
        for block in range(4):
            size = min(DI, 4 * width - block * DI)
            if size > 0:
                weight = w_fc[:, block * 48 : block * 48 + 48, 0:size].reshape(DI, size)[0:width]
                pre = dot(n2[0:rows, 0:width], weight) + vec[10 + block : 11 + block, 0:size]
                low = (pre * jax.nn.sigmoid(GELU_K * pre)).astype(BF16)
                act[0:rows, block * DI : block * DI + size] = low

        for item in early:
            item.wait()
        drain(w_down, sems.at[3])

        weight = w_down[:, :, 0:width].reshape(4 * DI, width)[0 : 4 * width]
        total = dot(act[0:rows, 0 : 4 * width], weight)
        total = (total + vec[7:8, 0:width] + middle[0:rows, 0:width]).reshape(short, 8, width)
        where = lax.broadcasted_iota(jnp.int32, (short, 8, width), 0)
        block_out[0:rows, 0:width] = jnp.where(where < length, total, 0.0).reshape(rows, width).astype(BF16)

        if width < DI:
            block_out[:, width:DI] = jnp.zeros((all_rows, DI - width), BF16)
        if rows < all_rows:
            block_out[rows:all_rows, :] = jnp.zeros((all_rows - rows, DI), BF16)
        stored.wait()

    here.either(path, 56)
    drain(xs, sems.at[5])
    stream = xs[...].astype(F32).reshape(N, DI)
    norm1, _ = normalize(stream, keep, winv)
    norm1_all[...] = norm1.astype(BF16)
    n1 = (norm1 * vec[0:1, :] + vec[1:2, :]).astype(BF16)
    q_out[...] = (dot(n1, weights[:, 0:48, :].reshape(DI, DI)) + vec[2:3, :]).astype(BF16).astype(F32)

    def mine(owner):
        norm_sl[...] = norm1_all[:, owner * 48 : owner * 48 + 48]

    here.mine(mine)


def close(lengths, tok, vec, gk, gv, q_own, gm_own, gq, mid_own, n2, middle, first, second, down):
    rows = tok.shape[0] * tok.shape[1]
    return call(
        close_kernel,
        "close",
        [(SMEM, lengths)]
        + [(VMEM, item) for item in (tok, vec, gk, gv, q_own, gm_own, gq, mid_own)]
        + [(ANY, r) for r in (n2, middle, *first, *second, *down)],
        [(VMEM, (rows, DI), BF16), (ANY, (rows, DI), F32), (VMEM, (N, DI), F32), (VMEM, (N, 48), BF16)],
        [
            pltpu.VMEM((ITEMS, 144, DI), BF16),
            pltpu.VMEM((ITEMS, 192, DI), BF16),
            pltpu.VMEM((ITEMS, 192, DI), BF16),
            pltpu.VMEM((rows, DI), BF16),
            pltpu.VMEM((rows, 4 * DI), BF16),
            pltpu.VMEM((rows, DI), F32),
            pltpu.VMEM((rows, DI), F32),
            pltpu.VMEM((ITEMS, 8, DI), BF16),
            pltpu.VMEM((N, DI), BF16),
            pltpu.VMEM((rows, DI), F32),
            pltpu.SemaphoreType.DMA((7,)),
        ],
        flops=17_000_000_000,
        touched=18_000_000,
        limit=50 * 1024 * 1024,
    )


def shard_kernel(got, q_all, gm_all, norm_sl, w_own, gain, bias, d_qkv, g_one, b_one, qv_out, by_keys, by_values, product):
    dp = lax.axis_index("dp")

    low_half = lax.broadcasted_iota(jnp.int32, (N, 128), 1) < HD

    for j in range(ITEMS):
        found = got[j].astype(F32)
        upper = jnp.concatenate([found[0:48], found[120:128]], axis=0).T
        lower = jnp.concatenate([found[48:96], found[120:128]], axis=0).T
        by_keys[j] = upper[0:96]
        by_values[j, 0:32, :] = upper[96:128]
        by_values[j, 32:96, :] = lower[0:64]

    def moments(turned, source):
        for pair in range(DI // 128):
            lanes = slice(pair * 128, pair * 128 + 128)
            rows = source[:, lanes]
            both = [jnp.where(low_half, rows, 0.0), jnp.where(low_half, 0.0, rows)]
            both = [half.reshape(ITEMS, 8, 128) for half in both]
            both = jnp.concatenate(both, axis=1).reshape(2 * N, 128).astype(BF16)
            part = turned[:, pair * 16 : pair * 16 + 16, :].reshape(2 * N, 56).astype(BF16)
            product[:, lanes] = dot(part, both, 0, 0)
        return product[...]

    def column(row):
        square = (48, 48)
        same = lax.broadcasted_iota(jnp.int32, square, 0) == lax.broadcasted_iota(jnp.int32, square, 1)
        return jnp.sum(jnp.where(same, row[...].astype(F32), 0.0), axis=1, keepdims=True)

    by_key = moments(by_keys, q_all) * SCALE
    m_key, s_key = by_key[0:48], by_key[48:49] + by_key[49:50]
    by_value = moments(by_values, gm_all)
    m_value, s_value = by_value[0:48], by_value[50:51] + by_value[51:52]
    beside = got[:, 48:96, :].astype(F32)
    last = got[:, 96:128, :].astype(F32)
    lane = lax.broadcasted_iota(jnp.int32, (1, 1, 128), 2)
    blocks = []
    for i in range(3):
        low = pltpu.roll(beside[:, 16 * i : 16 * i + 8, :], 64, 2)
        blocks.append(jnp.where(lane < 64, low, beside[:, 16 * i + 8 : 16 * i + 16, :]).reshape(N, 128))
    blocks += [last[:, 8 * i : 8 * i + 8, :].reshape(N, 128) for i in range(3)]
    grad_q = jnp.concatenate(blocks, axis=1)
    s_query = row_sum(grad_q)
    m_query = dot(norm_sl[...], grad_q.astype(BF16), 0, 0)
    gain_col, bias_col = column(gain), column(bias)
    by_gain = jnp.zeros((48, DI), F32)
    by_bias = jnp.zeros((48, DI), F32)
    for third, (moment, total) in enumerate(((m_query, s_query), (m_key, s_key), (m_value, s_value))):
        d_qkv[third] = gain_col * moment + bias_col * total
        weight = w_own[third].astype(F32)
        by_gain = by_gain + weight * moment
        by_bias = by_bias + weight * total
    ones = jnp.ones((8, DI), F32)
    line = (((1,), (1,)), ((), ()))
    for dst, item in ((g_one, by_gain), (b_one, by_bias)):
        dst[...] = lax.dot_general(
            ones, item, line, precision=lax.Precision.HIGHEST, preferred_element_type=F32
        )[0:1]
    for owner in range(ITEMS):

        @pl.when(dp == owner)
        def _(owner=owner):
            lanes = slice(owner * 48, owner * 48 + 48)
            qv_out[0:1, :] = s_query[:, lanes]
            qv_out[1:2, :] = s_value[:, lanes]


def shard_grads(got, q_all, gm_all, norm_sl, w_own, gain, bias):
    plain = (got, q_all, gm_all, norm_sl, w_own, gain, bias)
    return call(
        shard_kernel,
        "shard_grads",
        [(VMEM, item) for item in plain],
        [
            (VMEM, (3, 48, DI), F32),
            (VMEM, (1, 48), F32),
            (VMEM, (1, 48), F32),
            (VMEM, (2, 48), F32),
        ],
        [
            pltpu.VMEM((ITEMS, 96, 56), F32),
            pltpu.VMEM((ITEMS, 96, 56), F32),
            pltpu.VMEM((56, DI), F32),
        ],
        flops=5_000_000_000,
        touched=2_000_000,
        limit=50 * 1024 * 1024,
    )


BOTH = ("tower", "dp")


def device(tower, place, core):
    return tower * 16 + (RING_Z[place] * 2 + RING_Y[place]) * 2 + core


def routes(towers):
    swap, turn = [], []
    for tower in range(towers):
        for place in range(8):
            for core, step in ((0, 1), (1, -1)):
                here = device(tower, place, core)
                swap.append((here, device(tower, place, 1 - core)))
                turn.append((here, device(tower, (place + step) % 8, core)))
    return swap, turn


def after(item, *earlier):
    return lax.optimization_barrier((item, *earlier))[0] if earlier else item


class Ring:
    def __init__(self, shard, swap, turn, first_core):
        self.swap, self.turn, self.first_core = swap, turn, first_core
        self.shard, self.other = shard, lax.ppermute(shard, BOTH, swap)
        self.last = self.joined(shard, self.other)
        self.items = [self.last]
        self.hops = 0

    def joined(self, own, other):
        return jnp.stack([jnp.where(self.first_core, own, other), jnp.where(self.first_core, other, own)])

    def first_step(self):
        held = self.joined(*(lax.ppermute(item, BOTH, self.turn) for item in (self.shard, self.other)))
        self.items += [held, lax.ppermute(held, BOTH, self.swap)]
        self.last = held
        self.hops += 1
        return held

    def step(self, *earlier, swap_after=(), later=False):
        held = self.last
        if self.hops == 3:
            held = jnp.where(self.first_core, held[0], held[1])
        held = lax.ppermute(after(held, *earlier), BOTH, self.turn)
        self.items += [held, None if later else lax.ppermute(after(held, *swap_after), BOTH, self.swap)]
        self.last = held
        self.hops += 1
        return held

    def finish(self, *earlier):
        for i, item in enumerate(self.items):
            if item is None:
                self.items[i] = lax.ppermute(after(self.items[i - 1], *earlier), BOTH, self.swap)
        return self.items


def ring_body(
    tokens,
    lengths,
    ln1_gain,
    ln1_bias,
    qkv_weight,
    qv_bias,
    out_weight,
    out_bias,
    ln2_gain,
    ln2_bias,
    fc_weight,
    fc_bias,
    down_weight,
    down_bias,
    final_gain,
    final_bias,
    embed_weight,
    logit_scale,
):
    towers = lax.axis_size("tower")
    dp_index = lax.axis_index("dp")
    swap, turn = routes(towers)
    tok = tokens[0].transpose(1, 0, 2)
    w_own = qkv_weight[0].transpose(1, 0, 2)
    vectors = (ln1_gain, ln1_bias, out_bias, ln2_gain, ln2_bias, down_bias, final_gain, final_bias)
    first_own = pack_first(lengths, w_own.reshape(144, DI), tok, vectors, qv_bias[0], fc_bias)
    second_own = pack_rest(out_weight[0], fc_weight[0], embed_weight[0])
    first_core = dp_index % 2 == 0

    qkv_ring = Ring(first_own, swap, turn, first_core)
    wide_ring = Ring(second_own, swap, turn, first_core)
    down_ring = Ring(down_weight[0], swap, turn, first_core)
    qkv_ring.first_step()
    d1 = down_ring.step()
    qkv_ring.step()
    q3 = qkv_ring.step(d1)
    wide_ring.step()
    qkv_ring.step()
    first = qkv_ring.items
    keys, values, norm_low, normed, vec, pooled, q_own, probs, gv = attend_pooled(lengths, tok, first)
    w2 = wide_ring.step(q3, swap_after=(q_own,))
    d2 = down_ring.step(q3, swap_after=(q_own,))
    mixes = lax.all_to_all(pooled, "dp", 0, 0, tiled=True)
    w3 = wide_ring.step(q_own)
    mixed, z_value = attend(lengths, vec, gv, after(normed, w2), keys, values, norm_low, first)
    wide_ring.step(z_value)
    d3 = down_ring.step(z_value, mixes)
    second = wide_ring.items
    down_ring.step()
    down = down_ring.items
    e_own, proj, normf, invf, norm2, inv2, slope, n2_sl, mix_sl, head_sl, act_sl = pooled_forward(
        lengths, vec, mixes, first, second, down
    )
    across = [(t * 16 + d, (1 - t) * 16 + d) for t in range(2) for d in range(16)]
    e_oth = lax.ppermute(e_own, BOTH, across)
    n2, middle = middle_part(lengths, tok, vec, after(mixed, e_own), second)
    (loss, scale, d_emb, d_down, d_fc, d_out, g_final, b_final, b_down, g_two, b_two, b_out, b_fc,
     mid_own, gm_all, gm_own, payload, gk, gq) = chain(
        lengths, logit_scale, after(e_own, n2), e_oth, vec, (head_sl, act_sl, n2_sl, mix_sl),
        (proj, normf, invf, norm2, inv2, slope, keys, values, norm_low, probs, gv, z_value), second, down,
    )
    got = lax.all_to_all(payload, "dp", 0, 0, tiled=True).reshape(ITEMS, PAYLOAD, 128)
    block_out, tokens_grad, q_all, norm_sl = close(
        lengths, tok, vec, gk, gv, q_own, gm_own, gq, mid_own, n2, middle, first, second, down
    )
    d_qkv, g_one, b_one, qv_sums = shard_grads(got, q_all, gm_all, norm_sl, w_own, ln1_gain, ln1_bias)
    seq = tok.shape[0]
    return (
        block_out.reshape(seq, 8, DI).transpose(1, 0, 2)[None],
        tokens_grad.reshape(seq, 8, DI).transpose(1, 0, 2)[None],
        loss.reshape(1),
        g_one,
        b_one,
        d_qkv.transpose(1, 0, 2)[None],
        qv_sums[None],
        d_out[None],
        b_out,
        g_two,
        b_two,
        d_fc[None],
        b_fc,
        d_down[None],
        b_down,
        g_final,
        b_final,
        d_emb[None],
        scale.reshape(1),
    )


def solution(mesh):
    fits = mesh.shape["dp"] == ITEMS and mesh.shape["tower"] == 2
    return jax.shard_map(
        ring_body if fits else body,
        mesh=mesh,
        in_specs=(
            P("tower", "dp", None, None),
            P("dp"),
            P("tower", "dp"),
            P("tower", "dp"),
            P("tower", "dp", None, None),
            P("tower", None, "dp"),
            P("tower", "dp", None),
            P("tower", "dp"),
            P("tower", "dp"),
            P("tower", "dp"),
            P("tower", "dp", None),
            P("tower", "dp"),
            P("tower", "dp", None),
            P("tower", "dp"),
            P("tower", "dp"),
            P("tower", "dp"),
            P("tower", "dp", None),
            P(),
        ),
        out_specs=(
            P("tower", "dp", None, None),
            P("tower", "dp", None, None),
            P(),
            P("tower", "dp"),
            P("tower", "dp"),
            P("tower", "dp", None, None),
            P("tower", None, "dp"),
            P("tower", "dp", None),
            P("tower", "dp"),
            P("tower", "dp"),
            P("tower", "dp"),
            P("tower", "dp", None),
            P("tower", "dp"),
            P("tower", "dp", None),
            P("tower", "dp"),
            P("tower", "dp"),
            P("tower", "dp"),
            P("tower", "dp", None),
            P(),
        ),
        check_vma=False,
    )
```

```python
import functools

import jax
import jax.numpy as jnp
from jax import lax
from jax.experimental import pallas as pl
from jax.experimental.pallas import tpu as pltpu
from jax.sharding import PartitionSpec as P

DI = 768
DT = 512
HD = 64
IMG_ROWS = 50
EMB = 512


EPS = 1e-05
NORM_EPS = 1e-06
GELU_K = 1.702
NEG_FILL = -1e30


def swapped(block, axis, stride):
    count = lax.axis_size(axis)
    route = []
    for low in range(count):
        high = low | 1 << stride
        if high != low and high < count:
            route += [(low, high), (high, low)]
    return lax.ppermute(block, axis, route)


def masked_norm(values, norm_gain, norm_bias, col_keep, width_real):
    row_mean = jnp.sum(values * col_keep, axis=-1, keepdims=True) / width_real
    centred = (values - row_mean) * col_keep
    row_var = jnp.sum(centred * centred, axis=-1, keepdims=True) / width_real
    inv_std = lax.rsqrt(row_var + EPS)
    normed = centred * inv_std
    return (normed * norm_gain + norm_bias, normed, inv_std)


def masked_norm_back(grad_out, norm_gain, normed, inv_std, col_keep, width_real):
    grad_normed = grad_out * norm_gain
    mean_grad = jnp.sum(grad_normed, axis=-1, keepdims=True) / width_real
    mean_cross = jnp.sum(grad_normed * normed, axis=-1, keepdims=True) / width_real
    grad_in = col_keep * inv_std * (grad_normed - mean_grad - normed * mean_cross)
    return (grad_in, jnp.sum(grad_out * normed, axis=0), jnp.sum(grad_out, axis=0))


def contract_rows(left_op, right_op):
    return lax.dot_general(
        left_op, right_op, (((0,), (0,)), ((), ())), preferred_element_type=jnp.float32
    )


def contract_cols(left_op, right_op):
    return lax.dot_general(
        left_op, right_op, (((1,), (1,)), ((), ())), preferred_element_type=jnp.float32
    )


def column_sum(values):
    return jnp.sum(values, axis=0, dtype=jnp.float32)


def body(
    tokens,
    lengths,
    ln1_gain,
    ln1_bias,
    qkv_weight,
    qv_bias,
    out_weight,
    out_bias,
    ln2_gain,
    ln2_bias,
    fc_weight,
    fc_bias,
    down_weight,
    down_bias,
    final_gain,
    final_bias,
    embed_weight,
    logit_scale,
):
    f32 = jnp.float32
    bf16 = jnp.bfloat16
    tower_index = lax.axis_index("tower")
    dp_index = lax.axis_index("dp")
    dp_count = lax.axis_size("dp")
    samples, seq_rows, width_all = (tokens.shape[1], tokens.shape[2], tokens.shape[3])
    head_count = width_all // HD
    sample_total = samples * dp_count
    flat_rows = samples * seq_rows
    is_text = tower_index == 1
    width_int = jnp.where(is_text, DT, DI)
    width_real = width_int.astype(f32)
    col_keep = (lax.broadcasted_iota(jnp.int32, (width_all,), 0) < width_int).astype(f32)
    seq_lens = jnp.where(is_text, lengths, IMG_ROWS)
    positions = lax.broadcasted_iota(jnp.int32, (samples, seq_rows), 1)
    row_keep = (positions < seq_lens[:, None]).astype(f32).reshape(flat_rows, 1)
    query_pos = lax.broadcasted_iota(jnp.int32, (seq_rows, seq_rows), 0)
    key_pos = lax.broadcasted_iota(jnp.int32, (seq_rows, seq_rows), 1)
    allowed = (key_pos[None] < seq_lens[:, None, None]) & (
        jnp.logical_not(is_text) | (key_pos <= query_pos)
    )[None]
    pool_pos = jnp.where(is_text, lengths - 1, 0)
    pool_hot = (positions == pool_pos[:, None]).astype(f32)
    score_mult = float(HD) ** (-0.5)
    gathered = (
        lax.all_gather(ln1_gain[0], "dp", axis=0, tiled=True),
        lax.all_gather(ln1_bias[0], "dp", axis=0, tiled=True),
        lax.all_gather(qkv_weight[0], "dp", axis=0, tiled=True),
        lax.all_gather(qv_bias[0], "dp", axis=1, tiled=True),
        lax.all_gather(out_weight[0], "dp", axis=0, tiled=True),
        lax.all_gather(out_bias[0], "dp", axis=0, tiled=True),
        lax.all_gather(ln2_gain[0], "dp", axis=0, tiled=True),
        lax.all_gather(ln2_bias[0], "dp", axis=0, tiled=True),
        lax.all_gather(fc_weight[0], "dp", axis=0, tiled=True),
        lax.all_gather(fc_bias[0], "dp", axis=0, tiled=True),
        lax.all_gather(down_weight[0], "dp", axis=0, tiled=True),
        lax.all_gather(down_bias[0], "dp", axis=0, tiled=True),
        lax.all_gather(final_gain[0], "dp", axis=0, tiled=True),
        lax.all_gather(final_bias[0], "dp", axis=0, tiled=True),
        lax.all_gather(embed_weight[0], "dp", axis=0, tiled=True),
    )
    (
        gain_one,
        bias_one,
        w_qkv,
        b_qv,
        w_out,
        b_out,
        gain_two,
        bias_two,
        w_fc,
        b_fc,
        w_down,
        b_down,
        gain_final,
        bias_final,
        w_embed,
    ) = gathered
    stream = tokens[0].astype(f32).reshape(flat_rows, width_all)
    normed_h1, norm_one, inv_one = masked_norm(
        stream, gain_one.astype(f32), bias_one.astype(f32), col_keep, width_real
    )
    normed_one = normed_h1.astype(bf16)
    qkv_bias = jnp.concatenate(
        [b_qv[0].astype(f32), jnp.zeros((width_all,), f32), b_qv[1].astype(f32)]
    )
    qkv_flat = (
        jnp.dot(normed_one, w_qkv.reshape(width_all, 3 * width_all), preferred_element_type=f32)
        + qkv_bias
    )
    qkv_low = qkv_flat.astype(bf16).reshape(samples, seq_rows, 3, head_count, HD)
    query_all = qkv_low[:, :, 0]
    key_all = qkv_low[:, :, 1]
    value_all = qkv_low[:, :, 2]

    def masked_scores():
        raw = (
            jnp.einsum("sqhd,skhd->shqk", query_all, key_all, preferred_element_type=f32)
            * score_mult
        )
        return jnp.where(allowed[:, None], raw, NEG_FILL)

    scores = masked_scores()
    row_top = jnp.max(scores, axis=-1, keepdims=True)
    exp_terms = jnp.exp(scores - row_top)
    exp_sum = jnp.sum(exp_terms, axis=-1, keepdims=True)
    log_total = row_top + jnp.log(exp_sum)
    attn_probs = (exp_terms / exp_sum).astype(bf16)
    head_mix = jnp.einsum("shqk,skhd->sqhd", attn_probs, value_all, preferred_element_type=f32)
    head_mix_low = head_mix.astype(bf16).reshape(flat_rows, width_all)
    attn_out = jnp.dot(head_mix_low, w_out, preferred_element_type=f32) + b_out.astype(f32)
    middle = stream + attn_out
    normed_h2, norm_two, inv_two = masked_norm(
        middle, gain_two.astype(f32), bias_two.astype(f32), col_keep, width_real
    )
    normed_two = normed_h2.astype(bf16)
    hidden_pre = jnp.dot(normed_two, w_fc, preferred_element_type=f32) + b_fc.astype(f32)
    gate_sig = jax.nn.sigmoid(GELU_K * hidden_pre)
    act_low = (hidden_pre * gate_sig).astype(bf16)
    branch = jnp.dot(act_low, w_down, preferred_element_type=f32) + b_down.astype(f32)
    block_rows = row_keep * (middle + branch)
    block_out = block_rows.astype(bf16).reshape(1, samples, seq_rows, width_all)
    block_three = block_rows.reshape(samples, seq_rows, width_all)
    pooled = jnp.take_along_axis(block_three, pool_pos[:, None, None], axis=1)[:, 0]
    normed_hf, norm_final, inv_final = masked_norm(
        pooled, gain_final.astype(f32), bias_final.astype(f32), col_keep, width_real
    )
    head_low = normed_hf.astype(bf16)
    projected = jnp.dot(head_low, w_embed, preferred_element_type=f32)
    inv_norm = lax.rsqrt(jnp.sum(projected * projected, axis=-1, keepdims=True) + NORM_EPS)
    embed_low = (projected * inv_norm).astype(bf16)
    own_all = lax.all_gather(embed_low, "dp", axis=0, tiled=True)
    others = swapped(own_all, "tower", 0)
    logit_mult = jnp.exp(logit_scale[0])
    similar = contract_cols(embed_low, others)
    logits = logit_mult * similar
    logit_top = jnp.max(logits, axis=-1, keepdims=True)
    logit_total = logit_top + jnp.log(jnp.sum(jnp.exp(logits - logit_top), axis=-1, keepdims=True))
    label_col = dp_index * samples + lax.broadcasted_iota(jnp.int32, (samples, 1), 0)
    label_hot = (lax.broadcasted_iota(jnp.int32, (samples, sample_total), 1) == label_col).astype(
        f32
    )
    diag_logit = jnp.sum(label_hot * logits, axis=-1, keepdims=True)
    loss_part = jnp.sum(logit_total - diag_logit) / (2.0 * sample_total)
    grad_logits = (jnp.exp(logits - logit_total) - label_hot) * 0.5
    scale_part = logit_mult * jnp.sum(grad_logits * similar)
    grad_sims = (logit_mult * grad_logits).astype(bf16)
    grad_own = jnp.dot(grad_sims, others, preferred_element_type=f32)
    grad_others = contract_rows(grad_sims, embed_low)
    sent_back = swapped(grad_others, "tower", 0)
    returned = lax.psum_scatter(sent_back, "dp", scatter_dimension=0, tiled=True)
    totals = lax.psum((loss_part, scale_part), ("tower", "dp"))
    grad_embed = grad_own + returned
    again = (
        lax.all_gather(ln1_gain[0], "dp", axis=0, tiled=True),
        lax.all_gather(qkv_weight[0], "dp", axis=0, tiled=True),
        lax.all_gather(out_weight[0], "dp", axis=0, tiled=True),
        lax.all_gather(ln2_gain[0], "dp", axis=0, tiled=True),
        lax.all_gather(fc_weight[0], "dp", axis=0, tiled=True),
        lax.all_gather(down_weight[0], "dp", axis=0, tiled=True),
        lax.all_gather(final_gain[0], "dp", axis=0, tiled=True),
        lax.all_gather(embed_weight[0], "dp", axis=0, tiled=True),
    )
    (
        back_gain_one,
        back_qkv,
        back_out,
        back_gain_two,
        back_fc,
        back_down,
        back_gain_final,
        back_embed,
    ) = again
    cross_term = jnp.sum(grad_embed * projected, axis=-1, keepdims=True)
    grad_proj = inv_norm * grad_embed - projected * inv_norm * inv_norm * inv_norm * cross_term
    grad_proj_low = grad_proj.astype(bf16)
    grad_head = contract_cols(grad_proj_low, back_embed)
    grad_pooled, d_gain_final, d_bias_final = masked_norm_back(
        grad_head, back_gain_final.astype(f32), norm_final, inv_final, col_keep, width_real
    )
    grad_rows = (pool_hot[:, :, None] * grad_pooled[:, None, :]).reshape(flat_rows, width_all)
    grad_branch_low = grad_rows.astype(bf16)
    d_down_b = column_sum(grad_branch_low)
    grad_act = contract_cols(grad_branch_low, back_down)
    grad_pre_low = (
        grad_act * (gate_sig + GELU_K * hidden_pre * gate_sig * (1.0 - gate_sig))
    ).astype(bf16)
    d_fc_b = column_sum(grad_pre_low)
    grad_norm_two = contract_cols(grad_pre_low, back_fc)
    grad_mid_norm, d_gain_two, d_bias_two = masked_norm_back(
        grad_norm_two, back_gain_two.astype(f32), norm_two, inv_two, col_keep, width_real
    )
    grad_middle = grad_rows + grad_mid_norm
    grad_attn_low = grad_middle.astype(bf16)
    d_out_b = column_sum(grad_attn_low)
    grad_mix_low = (
        contract_cols(grad_attn_low, back_out)
        .astype(bf16)
        .reshape(samples, seq_rows, head_count, HD)
    )
    probs_again = jnp.exp(masked_scores() - log_total)
    probs_low = probs_again.astype(bf16)
    grad_value = jnp.einsum("shqk,sqhd->skhd", probs_low, grad_mix_low, preferred_element_type=f32)
    grad_probs = jnp.einsum("sqhd,skhd->shqk", grad_mix_low, value_all, preferred_element_type=f32)
    grad_scores = probs_again * (
        grad_probs - jnp.sum(probs_again * grad_probs, axis=-1, keepdims=True)
    )
    grad_scores_low = grad_scores.astype(bf16)
    grad_query = (
        jnp.einsum("shqk,skhd->sqhd", grad_scores_low, key_all, preferred_element_type=f32)
        * score_mult
    )
    grad_key = (
        jnp.einsum("shqk,sqhd->skhd", grad_scores_low, query_all, preferred_element_type=f32)
        * score_mult
    )
    grad_qkv_low = (
        jnp.stack([grad_query, grad_key, grad_value], axis=2)
        .astype(bf16)
        .reshape(flat_rows, 3 * width_all)
    )
    d_qkv_w = contract_rows(normed_one, grad_qkv_low).reshape(width_all, 3, width_all)
    qkv_sums = column_sum(grad_qkv_low).reshape(3, width_all)
    d_qv_b = jnp.stack([qkv_sums[0], qkv_sums[2]])
    grad_norm_one = contract_cols(grad_qkv_low, back_qkv.reshape(width_all, 3 * width_all))
    grad_in_norm, d_gain_one, d_bias_one = masked_norm_back(
        grad_norm_one, back_gain_one.astype(f32), norm_one, inv_one, col_keep, width_real
    )
    tokens_grad = (grad_middle + grad_in_norm).reshape(1, samples, seq_rows, width_all)
    d_embed_w = contract_rows(head_low, grad_proj_low)
    d_down_w = contract_rows(act_low, grad_branch_low)
    d_fc_w = contract_rows(normed_two, grad_pre_low)
    d_out_w = contract_rows(head_mix_low, grad_attn_low)
    shares = (
        lax.psum_scatter(d_gain_one, "dp", scatter_dimension=0, tiled=True),
        lax.psum_scatter(d_bias_one, "dp", scatter_dimension=0, tiled=True),
        lax.psum_scatter(d_qkv_w, "dp", scatter_dimension=0, tiled=True),
        lax.psum_scatter(d_qv_b, "dp", scatter_dimension=1, tiled=True),
        lax.psum_scatter(d_out_w, "dp", scatter_dimension=0, tiled=True),
        lax.psum_scatter(d_out_b, "dp", scatter_dimension=0, tiled=True),
        lax.psum_scatter(d_gain_two, "dp", scatter_dimension=0, tiled=True),
        lax.psum_scatter(d_bias_two, "dp", scatter_dimension=0, tiled=True),
        lax.psum_scatter(d_fc_w, "dp", scatter_dimension=0, tiled=True),
        lax.psum_scatter(d_fc_b, "dp", scatter_dimension=0, tiled=True),
        lax.psum_scatter(d_down_w, "dp", scatter_dimension=0, tiled=True),
        lax.psum_scatter(d_down_b, "dp", scatter_dimension=0, tiled=True),
        lax.psum_scatter(d_gain_final, "dp", scatter_dimension=0, tiled=True),
        lax.psum_scatter(d_bias_final, "dp", scatter_dimension=0, tiled=True),
        lax.psum_scatter(d_embed_w, "dp", scatter_dimension=0, tiled=True),
    )
    results = list(shares)
    outputs = [item[None] for item in results]
    loss = totals[0].reshape(1)
    logit_scale_grad = totals[1].reshape(1)
    return (
        block_out,
        tokens_grad,
        loss,
        outputs[0],
        outputs[1],
        outputs[2],
        outputs[3],
        outputs[4],
        outputs[5],
        outputs[6],
        outputs[7],
        outputs[8],
        outputs[9],
        outputs[10],
        outputs[11],
        outputs[12],
        outputs[13],
        outputs[14],
        logit_scale_grad,
    )


RING_Z = (0, 1, 2, 3, 3, 2, 1, 0)
RING_Y = (0, 0, 0, 0, 1, 1, 1, 1)
ITEMS = 16
N = ITEMS * 8
F32 = jnp.float32
BF16 = jnp.bfloat16
ANY = pl.BlockSpec(memory_space=pl.ANY)
VMEM = pl.BlockSpec(memory_space=pltpu.VMEM)
SMEM = pl.BlockSpec(memory_space=pltpu.SMEM)
SCALE = float(HD) ** -0.5
PAYLOAD = 128


def call(kernel, name, ins, outs, scratch, flops=0, touched=0, limit=67043328):
    return pl.pallas_call(
        kernel,
        name=name,
        out_shape=[jax.ShapeDtypeStruct(shape, dtype) for _, shape, dtype in outs],
        in_specs=[spec for spec, _ in ins],
        out_specs=[spec for spec, _, _ in outs],
        scratch_shapes=scratch,
        compiler_params=pltpu.CompilerParams(vmem_limit_bytes=limit),
        cost_estimate=pl.CostEstimate(flops=flops, bytes_accessed=touched, transcendentals=0),
    )(*[item for _, item in ins])


def dot(left, right, left_dim=1, right_dim=0):
    return lax.dot_general(
        left, right, (((left_dim,), (right_dim,)), ((), ())), preferred_element_type=F32
    )


def aligned(index, size):
    return pl.multiple_of(index, size)


def owner_table(dp_index):
    core = dp_index % 2
    row = dp_index // 2 % 2
    depth = dp_index // 4
    place = jnp.where(row == 0, depth, 7 - depth)

    def chip(where):
        where = (where + 8) % 8
        z = jnp.where(where < 4, where, 7 - where)
        y = jnp.where(where < 4, 0, 1)
        return (z * 2 + y) * 2

    sign = jnp.where(core == 0, -1, 1)
    found = [chip(place)]
    for hop in range(1, 4):
        found += [chip(place + sign * hop), chip(place - sign * hop)]
    return found + [chip(place + 4) + core, chip(place + 4) + 1 - core]


class Place:
    def __init__(self, lengths):
        self.dp = lax.axis_index("dp")
        self.text = lax.axis_index("tower") == 1
        self.lengths = lengths
        self.keep = (
            lax.broadcasted_iota(jnp.int32, (1, DI), 1) < jnp.where(self.text, DT, DI)
        ).astype(F32)
        self.winv = jnp.where(self.text, 1.0 / DT, 1.0 / DI).astype(F32)

    def length(self, s):
        return jnp.where(self.text, self.lengths[s], IMG_ROWS)

    def pool(self, s):
        return jnp.where(self.text, self.lengths[s] - 1, 0)

    def column(self, pick):
        ids = lax.broadcasted_iota(jnp.int32, (1, 8, 1), 1)
        column = jnp.zeros((1, 8, 1), jnp.int32)
        for s in range(8):
            column = jnp.where(ids == s, pick(s), column)
        return column

    def either(self, path, image):
        @pl.when(self.text)
        def _():
            path(DT, 77)

        @pl.when(jnp.logical_not(self.text))
        def _():
            path(DI, image)

    def mine(self, visit):
        for owner in range(ITEMS):

            @pl.when(self.dp == owner)
            def _(owner=owner):
                visit(owner)


def copy(src, dst, sem):
    found = pltpu.make_async_copy(src, dst, sem)
    found.start()
    return found


def drain(dst, sem):
    pltpu.make_async_copy(dst, dst, sem).wait()


def fetch(owners, refs, row, rows, dst, sem):
    for owner, ref in zip(owners, refs):
        if len(ref.shape) == 3:
            copy(ref.at[:, pl.ds(row, rows), :], dst.at[pl.ds(owner, 2)], sem)
        else:
            copy(ref.at[pl.ds(row, rows), :], dst.at[owner], sem)


def embed_matrix(packed):
    tail = jnp.concatenate([packed[:, 0:16, EMB:DI], packed[:, 16:32, EMB:DI]], axis=2)
    return jnp.concatenate([packed[:, :, 0:EMB], tail], axis=1).reshape(DI, EMB)


def normalize(values, keep, winv):
    mean = jnp.sum(values, axis=-1, keepdims=True) * winv
    centred = (values - mean) * keep
    var = jnp.sum(centred * centred, axis=-1, keepdims=True) * winv
    inv = lax.rsqrt(var + EPS)
    return centred * inv, inv


def normalize_back(grad_out, gain, normed, inv, keep, winv):
    grad_normed = grad_out * gain
    mean_grad = jnp.sum(grad_normed, axis=-1, keepdims=True) * winv
    mean_cross = jnp.sum(grad_normed * normed, axis=-1, keepdims=True) * winv
    return keep * inv * (grad_normed - mean_grad - normed * mean_cross)


def row_sum(values):
    return jnp.sum(values, axis=0, keepdims=True)


def head_rows(rows):
    heads = lax.broadcasted_iota(jnp.int32, rows.shape, 1) // HD
    parts = [jnp.where(heads == head, rows, 0.0) for head in range(16)]
    return jnp.concatenate(parts, axis=0).astype(BF16)


def chunks(count, visit):
    @pl.loop(0, count // 28)
    def _(i):
        visit(i * 28, aligned(i * 224, 16), 28)

    if count % 28:
        at = count - count % 28
        visit(at, at * 8, count % 28)


def pack_first_kernel(lengths, qkv, tok, *rest):
    here = Place(lengths)
    vectors, (qv_bias, fc_bias, out) = rest[:8], rest[8:]
    out[0:144, :] = qkv[...]
    sub = lax.broadcasted_iota(jnp.int32, (8, DI), 0)
    pooled = jnp.zeros((8, DI), F32)
    for s in range(8):
        pooled = jnp.where(sub == s, tok[here.pool(s)].astype(F32), pooled)
    out[144:152, :] = pooled.astype(BF16)
    lane = lax.broadcasted_iota(jnp.int32, (1, DI), 1) // 48 == here.dp
    short = [v[...].astype(F32) for v in vectors]
    pair = qv_bias[...].astype(F32)
    short[2:2] = [pair[0:1], pair[1:2]]
    rows = [jnp.where(lane, jnp.concatenate([v] * ITEMS, axis=1), 0.0) for v in short]
    wide = lax.broadcasted_iota(jnp.int32, (1, 4 * DI), 1) // 192 == here.dp
    fc = jnp.where(wide, jnp.concatenate([fc_bias[...].astype(F32)] * ITEMS, axis=1), 0.0)
    rows += [fc[:, i * DI : (i + 1) * DI] for i in range(4)]
    row_id = lax.broadcasted_iota(jnp.int32, (16, DI), 0)
    small = jnp.zeros((16, DI), F32)
    for at, row in enumerate(rows):
        small = jnp.where(row_id == at, jnp.broadcast_to(row, (16, DI)), small)
    out[152:168, :] = small.astype(BF16)


def pack_first(lengths, qkv, tok, vectors, qv_bias, fc_bias):
    return call(
        pack_first_kernel,
        "pack_first",
        [(SMEM, lengths)] + [(VMEM, item) for item in (qkv, tok, *vectors, qv_bias, fc_bias)],
        [(VMEM, (168, DI), BF16)],
        [],
        touched=1_500_000,
    )[0]


def pack_rest_kernel(w_out, w_fc, w_emb, out):
    out[0:48, :] = w_out[...]
    out[48:80, 0:EMB] = w_emb[0:32, :]
    out[48:64, EMB:DI] = w_emb[32:48, 0:256]
    out[64:80, EMB:DI] = w_emb[32:48, 256:EMB]
    for block in range(4):
        out[80 + 48 * block : 128 + 48 * block, :] = w_fc[:, block * DI : (block + 1) * DI]


def pack_rest(w_out, w_fc, w_emb):
    return call(
        pack_rest_kernel,
        "pack_rest",
        [(VMEM, item) for item in (w_out, w_fc, w_emb)],
        [(VMEM, (272, DI), BF16)],
        [],
        touched=1_500_000,
    )[0]


def sample_limits(here):
    lane_sample = lax.broadcasted_iota(jnp.int32, (1, 128), 1) % 8
    limit = jnp.zeros((1, 128), jnp.int32)
    for s in range(8):
        limit = jnp.where(lane_sample == s, here.length(s), limit)
    return limit


def own_heads(tall, width):
    heads = lax.broadcasted_iota(jnp.int32, (8, width), 1) // HD
    total = jnp.zeros((8, width), F32)
    for head in range(width // HD):
        total = total + jnp.where(heads == head, tall[head * 8 : head * 8 + 8], 0.0)
    if width < DI:
        total = jnp.concatenate([total, jnp.zeros((8, DI - width), F32)], axis=1)
    return total


def tall_rows(rows):
    return jnp.concatenate([rows[:, i * 128 : (i + 1) * 128] for i in range(DI // 128)], axis=0)


def wide_rows(tall):
    tall = tall.astype(F32)
    return jnp.concatenate(
        [tall[:, i * 8 : i * 8 + 8, :].reshape(N, 128) for i in range(DI // 128)], axis=1
    )


def pooled_kernel(lengths, tok_hbm, *rest):
    first, outs, scratch = rest[:9], rest[9:18], rest[18:]
    keys_hbm, values_hbm, norm_hbm, normed_hbm, vec, pooled, q_own, probs_out, gv_out = outs
    weights, small, tok, normed, keys, values, norm_low, sems, ends = scratch
    here = Place(lengths)
    owners = owner_table(here.dp)
    tok_in = copy(tok_hbm, tok, sems.at[2])
    fetch(owners, first, 152, 16, small, sems.at[0])
    fetch(owners, first, 0, 144, weights, sems.at[1])
    keep, winv = here.keep, here.winv
    drain(small, sems.at[0])
    vec[...] = jnp.sum(small[...].astype(F32), axis=0)
    limit = sample_limits(here)
    tok_in.wait()
    sub = lax.broadcasted_iota(jnp.int32, (8, DI), 0)
    picked = jnp.zeros((8, DI), F32)
    for s in range(8):
        picked = jnp.where(sub == s, tok[here.pool(s)].astype(F32), picked)
    pooled_norm, _ = normalize(picked, keep, winv)
    pooled_normed = (pooled_norm * vec[0:1, :] + vec[1:2, :]).astype(BF16)

    def norm_chunk(position, row, count):
        x = tok[pl.ds(position, count)].astype(F32).reshape(count * 8, DI)
        norm, _ = normalize(x, keep, winv)
        norm_low[pl.ds(row, count * 8), :] = norm.astype(BF16)
        normed[pl.ds(row, count * 8), :] = (norm * vec[0:1, :] + vec[1:2, :]).astype(BF16)

    def path(width, count):
        rows = count * 8
        chunks(count, norm_chunk)
        saved = [copy(norm_low, norm_hbm, ends.at[0]), copy(normed, normed_hbm, ends.at[1])]
        drain(weights, sems.at[1])
        for third, low, bias in ((1, keys, None), (2, values, 3)):

            weight = weights[:, third * 48 : third * 48 + 48, 0:width].reshape(DI, width)[0:width]
            prod = dot(normed[0:rows, 0:width], weight)
            if bias is not None:
                prod = prod + vec[bias : bias + 1, 0:width]
            low[0:rows, 0:width] = prod.astype(BF16)

        saved += [copy(keys, keys_hbm, ends.at[2]), copy(values, values_hbm, ends.at[3])]
        query = dot(pooled_normed, weights[:, 0:48, :].reshape(DI, DI)) + vec[2:3, :]
        query = query.astype(BF16).astype(F32)
        q_own[...] = query
        q_rows = head_rows(query)
        raw = dot(keys[0:rows, 0:width], q_rows[:, 0:width], 1, 1) * SCALE
        row = lax.broadcasted_iota(jnp.int32, (rows, 128), 0)
        lane = lax.broadcasted_iota(jnp.int32, (rows, 128), 1)
        valid = (lane % 8 == row % 8) & (row // 8 < limit) & (lane < width // 8)
        raw = jnp.where(valid, raw, NEG_FILL)
        terms = jnp.where(valid, jnp.exp(raw - jnp.max(raw, axis=0, keepdims=True)), 0.0)
        probs = terms / jnp.maximum(row_sum(terms), 1e-30)
        low_probs = probs.astype(BF16)
        probs_out[0:rows, :] = probs
        gv_out[0:rows, :] = low_probs
        mixed = own_heads(dot(low_probs, values[0:rows, 0:width], 0, 0), width)
        tall = tall_rows(mixed).astype(BF16)
        for owner in range(ITEMS):
            pooled[owner] = tall
        for item in saved:
            item.wait()

    here.either(path, 56)


def attend_pooled(lengths, tok, first):
    rows = tok.shape[0] * tok.shape[1]
    return call(
        pooled_kernel,
        "attend_pooled",
        [(SMEM, lengths), (ANY, tok)] + [(ANY, r) for r in first],
        [(ANY, (rows, DI), BF16)] * 4
        + [
            (VMEM, (16, DI), F32),
            (VMEM, (ITEMS, 48, 128), BF16),
            (VMEM, (8, DI), F32),
            (VMEM, (rows, 128), F32),
            (VMEM, (rows, 128), BF16),
        ],
        [
            pltpu.VMEM((ITEMS, 144, DI), BF16),
            pltpu.VMEM((ITEMS, 16, DI), BF16),
            pltpu.VMEM(tok.shape, BF16),
            pltpu.VMEM((rows, DI), BF16),
            pltpu.VMEM((rows, DI), BF16),
            pltpu.VMEM((rows, DI), BF16),
            pltpu.VMEM((rows, DI), BF16),
            pltpu.SemaphoreType.DMA((3,)),
            pltpu.SemaphoreType.DMA((4,)),
        ],
        flops=7_000_000_000,
        touched=10_000_000,
    )


def attend_kernel(lengths, vec, gv, normed_hbm, keys_hbm, values_hbm, norm_hbm, *rest):
    first, (mixed_hbm, z_value), scratch = rest[:9], rest[9:11], rest[11:]
    weights, normed, keys, values, norm_low, mixed, qf, kf, vf, mf, sems = scratch
    here = Place(lengths)
    owners = owner_table(here.dp)
    fetch(owners, first, 0, 48, weights, sems.at[0])
    early = [
        copy(src, dst, sems.at[1 + i])
        for i, (src, dst) in enumerate(
            ((normed_hbm, normed), (keys_hbm, keys), (values_hbm, values), (norm_hbm, norm_low))
        )
    ]
    drain(weights, sems.at[0])
    early[0].wait()
    early[1].wait()
    early[2].wait()

    def path(width, count):
        rows = count * 8
        span = 80 if count == 77 else count
        if span > count:
            for dst in (qf, kf, vf):
                dst[:, rows : span * 8, :] = jnp.zeros((6, span * 8 - rows, 128), F32)

        weight = weights[:, :, 0:width].reshape(DI, width)[0:width]
        prod = dot(normed[0:rows, 0:width], weight) + vec[2:3, 0:width]
        prod = prod.astype(BF16).astype(F32) * SCALE
        for pair in range(width // 128):
            lanes = pl.ds(pair * 128, 128)
            qf[pair, 0:rows, :] = prod[:, pair * 128 : pair * 128 + 128]
            kf[pair, 0:rows, :] = keys[0:rows, lanes].astype(F32)
            vf[pair, 0:rows, :] = values[0:rows, lanes].astype(F32)

        key_pos = lax.broadcasted_iota(jnp.int32, (span, 2 * span), 0)
        query_pos = lax.broadcasted_iota(jnp.int32, (span, 2 * span), 1) % span
        low_half = lax.broadcasted_iota(jnp.int32, (span, 128), 1) < HD

        @pl.loop(0, 8, unroll=2)
        def _(s):
            at = pl.ds(s, span, stride=8)
            allowed = key_pos < here.length(s)
            if width == DT:
                allowed = allowed & (key_pos <= query_pos)
            pairs = range(width // 128)
            raws = []
            for pair in pairs:
                query, key = qf.at[pair][at, :], kf.at[pair][at, :].astype(BF16)
                spread = [jnp.where(low_half, query, 0.0), jnp.where(low_half, 0.0, query)]
                spread = jnp.concatenate(spread, axis=0).astype(BF16)
                raws.append(dot(key, spread, 1, 1))
            probs = []
            for raw in raws:
                raw = jnp.where(allowed, raw, NEG_FILL)
                terms = jnp.exp(raw - jnp.max(raw, axis=0, keepdims=True))
                probs.append((terms / jnp.sum(terms, axis=0, keepdims=True)).astype(BF16))
            for pair in pairs:
                out = dot(probs[pair], vf.at[pair][at, :].astype(BF16), 0, 0)
                mf.at[pair][at, :] = jnp.where(low_half, out[0:span], out[span : 2 * span])

        stored = []
        for i in range(width // 128):
            lanes = pl.ds(128 * i, 128)
            mixed[0:rows, lanes] = mf[i, 0:rows, :].astype(BF16)
            stored.append(copy(mixed.at[0:rows, lanes], mixed_hbm.at[0:rows, lanes], sems.at[5 + i]))
        early[3].wait()
        z_value[...] = pltpu.roll(dot(norm_low[0:rows, :], gv[0:rows, :], 0, 0), 96, 1).astype(BF16)
        for item in stored:
            item.wait()

    here.either(path, 56)


def attend(lengths, vec, gv, normed, keys, values, norm_low, first):
    rows = keys.shape[0]
    high = rows + 24
    return call(
        attend_kernel,
        "attend",
        [(SMEM, lengths), (VMEM, vec), (VMEM, gv)]
        + [(ANY, r) for r in (normed, keys, values, norm_low, *first)],
        [(ANY, (rows, DI), BF16), (VMEM, (DI, 128), BF16)],
        [
            pltpu.VMEM((ITEMS, 48, DI), BF16),
            pltpu.VMEM((rows, DI), BF16),
            pltpu.VMEM((rows, DI), BF16),
            pltpu.VMEM((rows, DI), BF16),
            pltpu.VMEM((rows, DI), BF16),
            pltpu.VMEM((rows, DI), BF16),
            pltpu.VMEM((6, high, 128), F32),
            pltpu.VMEM((6, high, 128), F32),
            pltpu.VMEM((6, high, 128), F32),
            pltpu.VMEM((6, high, 128), F32),
            pltpu.SemaphoreType.DMA((11,)),
        ],
        flops=9_000_000_000,
        touched=10_000_000,
    )


def forward_kernel(lengths, vec, mixes, *rest):
    first, second, down = rest[:9], rest[9:18], rest[18:27]
    outs, scratch = rest[27:38], rest[38:]
    (e_out, proj_out, normf_out, invf_out, norm2_out, inv2_out, slope_out, n2_sl, mix_sl, head_sl,
     act_sl) = outs
    w_out, w_fc, w_down, w_emb, xs, mix, n2, act, head_all, sems = scratch
    here = Place(lengths)
    owners = owner_table(here.dp)
    fetch(owners, second, 0, 48, w_out, sems.at[1])
    fetch(owners, first, 144, 8, xs, sems.at[0])
    fetch(owners, second, 80, 192, w_fc, sems.at[2])
    keep, winv = here.keep, here.winv
    mix[...] = wide_rows(mixes[...]).astype(BF16)
    drain(w_out, sems.at[1])
    drain(xs, sems.at[0])
    fetch(owners, down, 0, 192, w_down, sems.at[3])
    fetch(owners, second, 48, 32, w_emb, sems.at[4])
    stream = xs[...].astype(F32).reshape(N, DI)
    middle = stream + dot(mix[...], w_out[...].reshape(DI, DI)) + vec[4:5, :]
    norm2, inv2 = normalize(middle, keep, winv)
    n2[...] = (norm2 * vec[5:6, :] + vec[6:7, :]).astype(BF16)
    norm2_out[...] = norm2
    inv2_out[...] = jnp.broadcast_to(inv2, (N, 128))
    drain(w_fc, sems.at[2])
    for block in range(4):
        lanes = pl.ds(block * DI, DI)
        weight = w_fc[:, block * 48 : block * 48 + 48, :].reshape(DI, DI)
        pre = dot(n2[...], weight) + vec[10 + block : 11 + block, :]
        gate = jax.nn.sigmoid(GELU_K * pre)
        act[:, lanes] = (pre * gate).astype(BF16)
        slope_out[:, lanes] = gate + GELU_K * pre * gate * (1.0 - gate)

    drain(w_down, sems.at[3])
    last = middle + dot(act[...], w_down[...].reshape(4 * DI, DI)) + vec[7:8, :]
    normf, invf = normalize(last, keep, winv)
    normf_out[...] = normf
    invf_out[...] = jnp.broadcast_to(invf, (N, 128))
    head_all[...] = (normf * vec[8:9, :] + vec[9:10, :]).astype(BF16)
    drain(w_emb, sems.at[4])
    proj = dot(head_all[...], embed_matrix(w_emb[...]))
    proj_out[...] = proj
    scale = lax.rsqrt(jnp.sum(proj * proj, axis=-1, keepdims=True) + NORM_EPS)
    e_out[...] = (proj * scale).astype(BF16)

    def mine(owner):
        lanes = slice(owner * 48, owner * 48 + 48)
        n2_sl[...] = n2[:, lanes]
        mix_sl[...] = mix[:, lanes]
        head_sl[...] = head_all[:, lanes]
        act_sl[...] = act[:, owner * 192 : owner * 192 + 192]

    here.mine(mine)


def pooled_forward(lengths, vec, mixes, first, second, down):
    return call(
        forward_kernel,
        "pooled_forward",
        [(SMEM, lengths), (VMEM, vec), (VMEM, mixes)] + [(ANY, r) for r in (*first, *second, *down)],
        [
            (VMEM, (N, EMB), BF16),
            (VMEM, (N, EMB), F32),
            (VMEM, (N, DI), F32),
            (VMEM, (N, 128), F32),
            (VMEM, (N, DI), F32),
            (VMEM, (N, 128), F32),
            (VMEM, (N, 4 * DI), F32),
            (VMEM, (N, 48), BF16),
            (VMEM, (N, 48), BF16),
            (VMEM, (N, 48), BF16),
            (VMEM, (N, 192), BF16),
        ],
        [
            pltpu.VMEM((ITEMS, 48, DI), BF16),
            pltpu.VMEM((ITEMS, 192, DI), BF16),
            pltpu.VMEM((ITEMS, 192, DI), BF16),
            pltpu.VMEM((ITEMS, 32, DI), BF16),
            pltpu.VMEM((ITEMS, 8, DI), BF16),
            pltpu.VMEM((N, DI), BF16),
            pltpu.VMEM((N, DI), BF16),
            pltpu.VMEM((N, 4 * DI), BF16),
            pltpu.VMEM((N, DI), BF16),
            pltpu.SemaphoreType.DMA((5,)),
        ],
        flops=11_000_000_000,
        touched=16_000_000,
        limit=50 * 1024 * 1024,
    )


def middle_kernel(lengths, tok_hbm, vec, mixed_hbm, *rest):
    second = rest[:9]
    (n2_hbm, middle_hbm), scratch = rest[9:11], rest[11:]
    w_out, middle, tok, mixed, n2, sems = scratch
    here = Place(lengths)
    owners = owner_table(here.dp)
    rows_in = copy(mixed_hbm, mixed, sems.at[1])
    fetch(owners, second, 0, 48, w_out, sems.at[0])
    tok_in = copy(tok_hbm, tok, sems.at[2])
    keep, winv = here.keep, here.winv
    rows_in.wait()
    drain(w_out, sems.at[0])

    def norm_chunk(position, row, count):
        at = pl.ds(row, count * 8)
        total = middle[at, :] + tok[pl.ds(position, count)].astype(F32).reshape(count * 8, DI)
        middle[at, :] = total
        norm, _ = normalize(total, keep, winv)
        n2[at, :] = (norm * vec[5:6, :] + vec[6:7, :]).astype(BF16)
        copy(middle.at[at, :], middle_hbm.at[at, :], sems.at[3])
        copy(n2.at[at, :], n2_hbm.at[at, :], sems.at[4])

    def path(width, count):
        rows = count * 8

        weight = w_out[:, :, 0:width].reshape(DI, width)[0:width]
        middle[0:rows, 0:width] = dot(mixed[0:rows, 0:width], weight) + vec[4:5, 0:width]
        if width < DI:
            middle[0:rows, width:DI] = jnp.zeros((rows, DI - width), F32)
        tok_in.wait()
        chunks(count, norm_chunk)
        drain(middle.at[pl.ds(0, rows), :], sems.at[3])
        drain(n2.at[pl.ds(0, rows), :], sems.at[4])

    here.either(path, 56)


def middle_part(lengths, tok, vec, mixed, second):
    rows = mixed.shape[0]
    return call(
        middle_kernel,
        "middle_part",
        [(SMEM, lengths), (ANY, tok), (VMEM, vec), (ANY, mixed)] + [(ANY, r) for r in second],
        [(ANY, (rows, DI), BF16), (ANY, (rows, DI), F32)],
        [
            pltpu.VMEM((ITEMS, 48, DI), BF16),
            pltpu.VMEM((rows, DI), F32),
            pltpu.VMEM(tok.shape, BF16),
            pltpu.VMEM((rows, DI), BF16),
            pltpu.VMEM((rows, DI), BF16),
            pltpu.SemaphoreType.DMA((5,)),
        ],
        flops=5_000_000_000,
        touched=8_000_000,
        limit=50 * 1024 * 1024,
    )


def one_direction(left, right, mult):
    sims = dot(left, right, 1, 1)
    logits = mult * sims
    top = jnp.max(logits, axis=-1, keepdims=True)
    total = top + jnp.log(jnp.sum(jnp.exp(logits - top), axis=-1, keepdims=True))
    count = sims.shape[0]
    eye = lax.broadcasted_iota(jnp.int32, (count, count), 0) == lax.broadcasted_iota(
        jnp.int32, (count, count), 1
    )
    hot = eye.astype(F32)
    lost = jnp.sum(total - jnp.sum(hot * logits, axis=-1, keepdims=True), axis=0, keepdims=True)
    grad = (jnp.exp(logits - total) - hot) * 0.5
    scale = jnp.sum(jnp.sum(grad * sims, axis=-1, keepdims=True), axis=0, keepdims=True)
    return lost, scale, mult * grad


def pack_payload(payload, z_key, z_value, sum_key, sum_value, grad_q):
    lane = lax.broadcasted_iota(jnp.int32, (1, 128), 1)
    upper = jnp.where(lane < 96, z_key, z_value).astype(BF16)
    blocks = [grad_q[:, i * 128 : (i + 1) * 128] for i in range(6)]
    beside = jnp.concatenate(
        [half for block in blocks[:3] for half in (pltpu.roll(block, 64, 1), block)], axis=0
    )
    key_high = sum_key.astype(BF16).astype(F32)
    value_high = sum_value.astype(BF16).astype(F32)
    row_id = lax.broadcasted_iota(jnp.int32, (8, 128), 0)
    sums = jnp.zeros((8, 128), F32)
    for at, value in enumerate((key_high, sum_key - key_high, value_high, sum_value - value_high)):
        sums = jnp.where(row_id == at, jnp.broadcast_to(value, (8, 128)), sums)
    last = jnp.concatenate([*blocks[3:], sums], axis=0).astype(BF16)
    for owner in range(ITEMS):
        base, rows = owner * PAYLOAD, slice(owner * 48, owner * 48 + 48)
        payload[base : base + 48, :] = upper[rows]
        payload[base + 48 : base + 96, :] = jnp.where(lane < 64, z_value[rows], beside).astype(BF16)
        payload[base + 96 : base + 128, :] = last


def chain_kernel(lengths, log_mult, e_own_ref, e_oth_ref, vec, head_sl, act_sl, n2_sl, mix_sl, *rest):
    (proj_hbm, normf_hbm, invf_hbm, norm2_hbm, inv2_hbm, slope_hbm, keys_hbm, values_hbm, norm_hbm, probs_hbm,
     gv_hbm, z_hbm), rest = rest[:12], rest[12:]
    second, down = rest[:9], rest[9:18]
    outs, scratch = rest[18:37], rest[37:]
    (loss_out, scale_out, d_emb_hbm, d_down_hbm, d_fc_hbm, d_out_hbm, g_final, b_final, b_down, g_two, b_two, b_out, b_fc,
     mid_own, gm_out, gm_own, payload, gk_out, gq_out) = outs
    (w_out, w_fc, w_down, w_emb, gpre, mid_all, proj_v, normf_v, invf_v, norm2_v, inv2_v, slope, keys,
     values, norm_low, probs_v, gv_v, z_v, vec_grads, fcb_grads, d_emb, d_down, d_fc, d_out, sems, ins, ends) = scratch
    here = Place(lengths)
    owners = owner_table(here.dp)
    early = [
        copy(src, dst, ins.at[i])
        for i, (src, dst) in enumerate(
            ((proj_hbm, proj_v), (normf_hbm, normf_v), (invf_hbm, invf_v))
        )
    ]
    fetch(owners, second, 48, 32, w_emb, sems.at[0])
    fetch(owners, down, 0, 192, w_down, sems.at[1])
    slope_in = copy(slope_hbm, slope, ins.at[3])
    fetch(owners, second, 80, 192, w_fc, sems.at[2])
    later = [copy(norm2_hbm, norm2_v, ins.at[4]), copy(inv2_hbm, inv2_v, ins.at[5])]
    fetch(owners, second, 0, 48, w_out, sems.at[3])
    last = [
        copy(src, dst, ins.at[6 + i])
        for i, (src, dst) in enumerate(
            ((keys_hbm, keys), (values_hbm, values), (norm_hbm, norm_low), (probs_hbm, probs_v),
             (gv_hbm, gv_v), (z_hbm, z_v))
        )
    ]
    keep, winv = here.keep, here.winv
    text = here.text.astype(F32)
    mult = jnp.exp(jnp.full((1, 128), log_mult[0], F32))[:, 0:1]
    own, oth = e_own_ref[...].astype(F32), e_oth_ref[...].astype(F32)
    e_img = (own * (1.0 - text) + oth * text).astype(BF16)
    e_txt = (oth * (1.0 - text) + own * text).astype(BF16)
    lost_img, scale_img, grad_img = one_direction(e_img, e_txt, mult)
    lost_txt, scale_txt, grad_txt = one_direction(e_txt, e_img, mult)
    loss_out[...] = (lost_img + lost_txt) / (2.0 * N)
    scale_out[...] = mult * (scale_img + scale_txt)
    grad_own = (grad_img * (1.0 - text) + grad_txt * text).astype(BF16)
    grad_oth = (grad_txt * (1.0 - text) + grad_img * text).astype(BF16)
    oth_low = e_oth_ref[...]
    grad_e = dot(grad_own, oth_low) + dot(grad_oth, oth_low, 0, 0)
    for item in early:
        item.wait()
    drain(w_emb, sems.at[0])
    proj = proj_v[...]
    r = lax.rsqrt(jnp.sum(proj * proj, axis=-1, keepdims=True) + NORM_EPS)
    cross = jnp.sum(grad_e * proj, axis=-1, keepdims=True)
    grad_proj = (r * grad_e - proj * (r * r * r) * cross).astype(BF16)
    grad_head = dot(grad_proj, embed_matrix(w_emb[...]), 1, 1)
    normf = normf_v[...]
    grad_y = normalize_back(grad_head, vec[8:9, :], normf, invf_v[:, 0:1], keep, winv)
    branch = grad_y.astype(BF16)
    d_emb[...] = dot(head_sl[...], grad_proj, 0, 0)
    stored = [copy(d_emb, d_emb_hbm, ends.at[0])]
    vec_grads[0:1, :] = row_sum(grad_head * normf)
    vec_grads[1:2, :] = row_sum(grad_head)
    vec_grads[2:3, :] = row_sum(branch.astype(F32))
    d_down[...] = dot(act_sl[...], branch, 0, 0)
    stored.append(copy(d_down, d_down_hbm, ends.at[1]))
    drain(w_down, sems.at[1])
    slope_in.wait()
    for block in range(4):
        lanes = pl.ds(block * DI, DI)
        back = dot(branch, w_down[block * 4 : block * 4 + 4].reshape(DI, DI), 1, 1)
        low = (back * slope[:, lanes]).astype(BF16)
        gpre[:, lanes] = low
        fcb_grads[:, lanes] = jnp.broadcast_to(row_sum(low.astype(F32)), (8, DI))

    drain(w_fc, sems.at[2])
    grad_n2 = jnp.zeros((N, DI), F32)
    for block in range(4):
        weight = w_fc[:, block * 48 : block * 48 + 48, :].reshape(DI, DI)
        grad_n2 = grad_n2 + dot(gpre[:, block * DI : block * DI + DI], weight, 1, 1)
    for item in later:
        item.wait()
    norm2 = norm2_v[...]
    vec_grads[3:4, :] = row_sum(grad_n2 * norm2)
    vec_grads[4:5, :] = row_sum(grad_n2)
    grad_mid = grad_y + normalize_back(grad_n2, vec[5:6, :], norm2, inv2_v[:, 0:1], keep, winv)
    mid_all[...] = grad_mid
    own_rows = pl.ds(aligned(here.dp * 8, 8), 8)
    mid_own[...] = mid_all[own_rows, :]
    attn = grad_mid.astype(BF16)
    vec_grads[5:6, :] = row_sum(attn.astype(F32))
    drain(w_out, sems.at[3])
    gm_out[...] = dot(attn, w_out[...].reshape(DI, DI), 1, 1).astype(BF16).astype(F32)
    gm_own[...] = gm_out[own_rows, :]

    @pl.loop(0, 6)
    def _(j):
        lanes = pl.ds(aligned(j * 512, 512), 512)
        d_fc[:, lanes] = dot(n2_sl[...], gpre[:, lanes], 0, 0)

    d_out[...] = dot(mix_sl[...], attn, 0, 0)
    stored += [copy(d_fc, d_fc_hbm, ends.at[2]), copy(d_out, d_out_hbm, ends.at[3])]

    def mine(owner):
        lanes = slice(owner * 48, owner * 48 + 48)
        for at, dst in enumerate((g_final, b_final, b_down, g_two, b_two, b_out)):
            dst[...] = vec_grads[at : at + 1, lanes]
        b_fc[...] = fcb_grads[0:1, owner * 192 : owner * 192 + 192]

    here.mine(mine)
    for item in last:
        item.wait()
    m_rows = head_rows(gm_own[...])

    def path(width, count):
        rows = count * 8
        probs = probs_v[0:rows, :]
        grad_probs = dot(values[0:rows, 0:width], m_rows[:, 0:width], 1, 1)
        gk = (probs * (grad_probs - row_sum(probs * grad_probs))).astype(BF16)
        gv = gv_v[0:rows, :]
        gk_out[0:rows, :] = gk
        gq_low = own_heads(dot(gk, keys[0:rows, 0:width], 0, 0) * SCALE, width).astype(BF16)
        gq_out[...] = gq_low
        z_key = dot(norm_low[0:rows, :], gk, 0, 0)
        pack_payload(
            payload,
            z_key,
            z_v[...].astype(F32),
            row_sum(gk.astype(F32)),
            pltpu.roll(jnp.broadcast_to(row_sum(gv.astype(F32)), (8, 128)), 96, 1)[0:1],
            gq_low.astype(F32),
        )

    here.either(path, 56)
    for item in stored:
        item.wait()


def chain(lengths, log_mult, e_own, e_oth, vec, slices, saved, second, down):
    rows = saved[-2].shape[0]
    return call(
        chain_kernel,
        "chain",
        [(SMEM, lengths), (SMEM, log_mult)]
        + [(VMEM, item) for item in (e_own, e_oth, vec, *slices)]
        + [(ANY, r) for r in (*saved, *second, *down)],
        [
            (VMEM, (1, 1), F32),
            (VMEM, (1, 1), F32),
            (ANY, (48, EMB), F32),
            (ANY, (192, DI), F32),
            (ANY, (48, 4 * DI), F32),
            (ANY, (48, DI), F32),
        ]
        + [(VMEM, (1, 48), F32)] * 6
        + [
            (VMEM, (1, 192), F32),
            (VMEM, (8, DI), F32),
            (VMEM, (N, DI), F32),
            (VMEM, (8, DI), F32),
            (VMEM, (ITEMS * PAYLOAD, 128), BF16),
            (VMEM, (rows, 128), BF16),
            (VMEM, (8, DI), BF16),
        ],
        [
            pltpu.VMEM((ITEMS, 48, DI), BF16),
            pltpu.VMEM((ITEMS, 192, DI), BF16),
            pltpu.VMEM((ITEMS, 192, DI), BF16),
            pltpu.VMEM((ITEMS, 32, DI), BF16),
            pltpu.VMEM((N, 4 * DI), BF16),
            pltpu.VMEM((N, DI), F32),
            pltpu.VMEM((N, EMB), F32),
            pltpu.VMEM((N, DI), F32),
            pltpu.VMEM((N, 128), F32),
            pltpu.VMEM((N, DI), F32),
            pltpu.VMEM((N, 128), F32),
            pltpu.VMEM((N, 4 * DI), F32),
            pltpu.VMEM((rows, DI), BF16),
            pltpu.VMEM((rows, DI), BF16),
            pltpu.VMEM((rows, DI), BF16),
            pltpu.VMEM((rows, 128), F32),
            pltpu.VMEM((rows, 128), BF16),
            pltpu.VMEM((DI, 128), BF16),
            pltpu.VMEM((8, DI), F32),
            pltpu.VMEM((8, 4 * DI), F32),
            pltpu.VMEM((48, EMB), F32),
            pltpu.VMEM((192, DI), F32),
            pltpu.VMEM((48, 4 * DI), F32),
            pltpu.VMEM((48, DI), F32),
            pltpu.SemaphoreType.DMA((4,)),
            pltpu.SemaphoreType.DMA((12,)),
            pltpu.SemaphoreType.DMA((4,)),
        ],
        flops=15_000_000_000,
        touched=20_000_000,
        limit=50 * 1024 * 1024,
    )


def close_kernel(lengths, tok, vec, gk, gv, q_own, gm_own, gq, mid_own, n2_hbm, middle_hbm, *rest):
    first, second, down = rest[:9], rest[9:18], rest[18:27]
    (block_out, out_hbm, q_out, norm_sl), scratch = rest[27:31], rest[31:]
    weights, w_fc, w_down, n2, act, middle, acc, xs, norm1_all, out, sems = scratch
    here = Place(lengths)
    owners = owner_table(here.dp)
    fetch(owners, first, 0, 144, weights, sems.at[0])
    fetch(owners, first, 144, 8, xs, sems.at[5])
    ready = copy(n2_hbm, n2, sems.at[1])
    fetch(owners, second, 80, 192, w_fc, sems.at[4])
    fetch(owners, down, 0, 192, w_down, sems.at[3])
    early = [copy(middle_hbm, middle, sems.at[2])]
    keep, winv = here.keep, here.winv
    q_rows = head_rows(q_own[...])
    m_rows = head_rows(gm_own[...])
    pool = here.column(here.pool)
    length = here.column(here.length)
    all_rows = out.shape[0]
    drain(weights, sems.at[0])
    u_key = (dot(q_rows, weights[:, 48:96, :].reshape(DI, DI), 1, 1) * SCALE).astype(BF16)
    u_value = dot(m_rows, weights[:, 96:144, :].reshape(DI, DI), 1, 1).astype(BF16)
    u_query = dot(gq[...], weights[:, 0:48, :].reshape(DI, DI), 1, 1)

    def path(width, count):
        rows = count * 8
        acc[0:rows, :] = dot(gk[0:rows, :], u_key) + dot(gv[0:rows, :], u_value)

        def back_chunk(position, row, count):
            at = pl.ds(row, count * 8)
            hit = lax.broadcasted_iota(jnp.int32, (count, 8, DI), 0) + position == pool
            norm, inv = normalize(tok[pl.ds(position, count)].astype(F32).reshape(count * 8, DI), keep, winv)
            total = acc[at, :] + jnp.where(hit, u_query[None], 0.0).reshape(count * 8, DI)
            back = normalize_back(total, vec[0:1, :], norm, inv, keep, winv)
            out[at, :] = back + jnp.where(hit, mid_own[...][None], 0.0).reshape(count * 8, DI)

        if rows < all_rows:
            out[rows:all_rows, :] = jnp.zeros((all_rows - rows, DI), F32)
        chunks(count, back_chunk)
        stored = copy(out, out_hbm, sems.at[6])
        short = count if width == DT else IMG_ROWS
        rows = short * 8
        ready.wait()
        drain(w_fc, sems.at[4])
        for block in range(4):
            size = min(DI, 4 * width - block * DI)
            if size > 0:
                weight = w_fc[:, block * 48 : block * 48 + 48, 0:size].reshape(DI, size)[0:width]
                pre = dot(n2[0:rows, 0:width], weight) + vec[10 + block : 11 + block, 0:size]
                low = (pre * jax.nn.sigmoid(GELU_K * pre)).astype(BF16)
                act[0:rows, block * DI : block * DI + size] = low

        for item in early:
            item.wait()
        drain(w_down, sems.at[3])

        weight = w_down[:, :, 0:width].reshape(4 * DI, width)[0 : 4 * width]
        total = dot(act[0:rows, 0 : 4 * width], weight)
        total = (total + vec[7:8, 0:width] + middle[0:rows, 0:width]).reshape(short, 8, width)
        where = lax.broadcasted_iota(jnp.int32, (short, 8, width), 0)
        block_out[0:rows, 0:width] = jnp.where(where < length, total, 0.0).reshape(rows, width).astype(BF16)

        if width < DI:
            block_out[:, width:DI] = jnp.zeros((all_rows, DI - width), BF16)
        if rows < all_rows:
            block_out[rows:all_rows, :] = jnp.zeros((all_rows - rows, DI), BF16)
        stored.wait()

    here.either(path, 56)
    drain(xs, sems.at[5])
    stream = xs[...].astype(F32).reshape(N, DI)
    norm1, _ = normalize(stream, keep, winv)
    norm1_all[...] = norm1.astype(BF16)
    n1 = (norm1 * vec[0:1, :] + vec[1:2, :]).astype(BF16)
    q_out[...] = (dot(n1, weights[:, 0:48, :].reshape(DI, DI)) + vec[2:3, :]).astype(BF16).astype(F32)

    def mine(owner):
        norm_sl[...] = norm1_all[:, owner * 48 : owner * 48 + 48]

    here.mine(mine)


def close(lengths, tok, vec, gk, gv, q_own, gm_own, gq, mid_own, n2, middle, first, second, down):
    rows = tok.shape[0] * tok.shape[1]
    return call(
        close_kernel,
        "close",
        [(SMEM, lengths)]
        + [(VMEM, item) for item in (tok, vec, gk, gv, q_own, gm_own, gq, mid_own)]
        + [(ANY, r) for r in (n2, middle, *first, *second, *down)],
        [(VMEM, (rows, DI), BF16), (ANY, (rows, DI), F32), (VMEM, (N, DI), F32), (VMEM, (N, 48), BF16)],
        [
            pltpu.VMEM((ITEMS, 144, DI), BF16),
            pltpu.VMEM((ITEMS, 192, DI), BF16),
            pltpu.VMEM((ITEMS, 192, DI), BF16),
            pltpu.VMEM((rows, DI), BF16),
            pltpu.VMEM((rows, 4 * DI), BF16),
            pltpu.VMEM((rows, DI), F32),
            pltpu.VMEM((rows, DI), F32),
            pltpu.VMEM((ITEMS, 8, DI), BF16),
            pltpu.VMEM((N, DI), BF16),
            pltpu.VMEM((rows, DI), F32),
            pltpu.SemaphoreType.DMA((7,)),
        ],
        flops=17_000_000_000,
        touched=18_000_000,
        limit=50 * 1024 * 1024,
    )


def shard_kernel(got, q_all, gm_all, norm_sl, w_own, gain, bias, d_qkv, g_one, b_one, qv_out, by_keys, by_values, product):
    dp = lax.axis_index("dp")

    low_half = lax.broadcasted_iota(jnp.int32, (N, 128), 1) < HD

    for j in range(ITEMS):
        found = got[j].astype(F32)
        upper = jnp.concatenate([found[0:48], found[120:128]], axis=0).T
        lower = jnp.concatenate([found[48:96], found[120:128]], axis=0).T
        by_keys[j] = upper[0:96]
        by_values[j, 0:32, :] = upper[96:128]
        by_values[j, 32:96, :] = lower[0:64]

    def moments(turned, source):
        for pair in range(DI // 128):
            lanes = slice(pair * 128, pair * 128 + 128)
            rows = source[:, lanes]
            both = [jnp.where(low_half, rows, 0.0), jnp.where(low_half, 0.0, rows)]
            both = [half.reshape(ITEMS, 8, 128) for half in both]
            both = jnp.concatenate(both, axis=1).reshape(2 * N, 128).astype(BF16)
            part = turned[:, pair * 16 : pair * 16 + 16, :].reshape(2 * N, 56).astype(BF16)
            product[:, lanes] = dot(part, both, 0, 0)
        return product[...]

    def column(row):
        square = (48, 48)
        same = lax.broadcasted_iota(jnp.int32, square, 0) == lax.broadcasted_iota(jnp.int32, square, 1)
        return jnp.sum(jnp.where(same, row[...].astype(F32), 0.0), axis=1, keepdims=True)

    by_key = moments(by_keys, q_all) * SCALE
    m_key, s_key = by_key[0:48], by_key[48:49] + by_key[49:50]
    by_value = moments(by_values, gm_all)
    m_value, s_value = by_value[0:48], by_value[50:51] + by_value[51:52]
    beside = got[:, 48:96, :].astype(F32)
    last = got[:, 96:128, :].astype(F32)
    lane = lax.broadcasted_iota(jnp.int32, (1, 1, 128), 2)
    blocks = []
    for i in range(3):
        low = pltpu.roll(beside[:, 16 * i : 16 * i + 8, :], 64, 2)
        blocks.append(jnp.where(lane < 64, low, beside[:, 16 * i + 8 : 16 * i + 16, :]).reshape(N, 128))
    blocks += [last[:, 8 * i : 8 * i + 8, :].reshape(N, 128) for i in range(3)]
    grad_q = jnp.concatenate(blocks, axis=1)
    s_query = row_sum(grad_q)
    m_query = dot(norm_sl[...], grad_q.astype(BF16), 0, 0)
    gain_col, bias_col = column(gain), column(bias)
    by_gain = jnp.zeros((48, DI), F32)
    by_bias = jnp.zeros((48, DI), F32)
    for third, (moment, total) in enumerate(((m_query, s_query), (m_key, s_key), (m_value, s_value))):
        d_qkv[third] = gain_col * moment + bias_col * total
        weight = w_own[third].astype(F32)
        by_gain = by_gain + weight * moment
        by_bias = by_bias + weight * total
    ones = jnp.ones((8, DI), F32)
    line = (((1,), (1,)), ((), ()))
    for dst, item in ((g_one, by_gain), (b_one, by_bias)):
        dst[...] = lax.dot_general(
            ones, item, line, precision=lax.Precision.HIGHEST, preferred_element_type=F32
        )[0:1]
    for owner in range(ITEMS):

        @pl.when(dp == owner)
        def _(owner=owner):
            lanes = slice(owner * 48, owner * 48 + 48)
            qv_out[0:1, :] = s_query[:, lanes]
            qv_out[1:2, :] = s_value[:, lanes]


def shard_grads(got, q_all, gm_all, norm_sl, w_own, gain, bias):
    plain = (got, q_all, gm_all, norm_sl, w_own, gain, bias)
    return call(
        shard_kernel,
        "shard_grads",
        [(VMEM, item) for item in plain],
        [
            (VMEM, (3, 48, DI), F32),
            (VMEM, (1, 48), F32),
            (VMEM, (1, 48), F32),
            (VMEM, (2, 48), F32),
        ],
        [
            pltpu.VMEM((ITEMS, 96, 56), F32),
            pltpu.VMEM((ITEMS, 96, 56), F32),
            pltpu.VMEM((56, DI), F32),
        ],
        flops=5_000_000_000,
        touched=2_000_000,
        limit=50 * 1024 * 1024,
    )


BOTH = ("tower", "dp")


def device(tower, place, core):
    return tower * 16 + (RING_Z[place] * 2 + RING_Y[place]) * 2 + core


def routes(towers):
    swap, turn = [], []
    for tower in range(towers):
        for place in range(8):
            for core, step in ((0, 1), (1, -1)):
                here = device(tower, place, core)
                swap.append((here, device(tower, place, 1 - core)))
                turn.append((here, device(tower, (place + step) % 8, core)))
    return swap, turn


def after(item, *earlier):
    return lax.optimization_barrier((item, *earlier))[0] if earlier else item


class Ring:
    def __init__(self, shard, swap, turn, first_core):
        self.swap, self.turn, self.first_core = swap, turn, first_core
        self.shard, self.other = shard, lax.ppermute(shard, BOTH, swap)
        self.last = self.joined(shard, self.other)
        self.items = [self.last]
        self.hops = 0

    def joined(self, own, other):
        return jnp.stack([jnp.where(self.first_core, own, other), jnp.where(self.first_core, other, own)])

    def first_step(self):
        held = self.joined(*(lax.ppermute(item, BOTH, self.turn) for item in (self.shard, self.other)))
        self.items += [held, lax.ppermute(held, BOTH, self.swap)]
        self.last = held
        self.hops += 1
        return held

    def step(self, *earlier, swap_after=(), later=False):
        held = self.last
        if self.hops == 3:
            held = jnp.where(self.first_core, held[0], held[1])
        held = lax.ppermute(after(held, *earlier), BOTH, self.turn)
        self.items += [held, None if later else lax.ppermute(after(held, *swap_after), BOTH, self.swap)]
        self.last = held
        self.hops += 1
        return held

    def finish(self, *earlier):
        for i, item in enumerate(self.items):
            if item is None:
                self.items[i] = lax.ppermute(after(self.items[i - 1], *earlier), BOTH, self.swap)
        return self.items


def ring_body(
    tokens,
    lengths,
    ln1_gain,
    ln1_bias,
    qkv_weight,
    qv_bias,
    out_weight,
    out_bias,
    ln2_gain,
    ln2_bias,
    fc_weight,
    fc_bias,
    down_weight,
    down_bias,
    final_gain,
    final_bias,
    embed_weight,
    logit_scale,
):
    towers = lax.axis_size("tower")
    dp_index = lax.axis_index("dp")
    swap, turn = routes(towers)
    tok = tokens[0].transpose(1, 0, 2)
    w_own = qkv_weight[0].transpose(1, 0, 2)
    vectors = (ln1_gain, ln1_bias, out_bias, ln2_gain, ln2_bias, down_bias, final_gain, final_bias)
    first_own = pack_first(lengths, w_own.reshape(144, DI), tok, vectors, qv_bias[0], fc_bias)
    second_own = pack_rest(out_weight[0], fc_weight[0], embed_weight[0])
    first_core = dp_index % 2 == 0

    qkv_ring = Ring(first_own, swap, turn, first_core)
    wide_ring = Ring(second_own, swap, turn, first_core)
    down_ring = Ring(down_weight[0], swap, turn, first_core)
    qkv_ring.first_step()
    d1 = down_ring.step()
    qkv_ring.step()
    q3 = qkv_ring.step(d1)
    wide_ring.step()
    qkv_ring.step()
    first = qkv_ring.items
    keys, values, norm_low, normed, vec, pooled, q_own, probs, gv = attend_pooled(lengths, tok, first)
    w2 = wide_ring.step(q3, swap_after=(q_own,))
    d2 = down_ring.step(q3, swap_after=(q_own,))
    mixes = lax.all_to_all(pooled, "dp", 0, 0, tiled=True)
    w3 = wide_ring.step(q_own)
    mixed, z_value = attend(lengths, vec, gv, after(normed, w2), keys, values, norm_low, first)
    wide_ring.step(z_value)
    d3 = down_ring.step(z_value, mixes)
    second = wide_ring.items
    down_ring.step()
    down = down_ring.items
    e_own, proj, normf, invf, norm2, inv2, slope, n2_sl, mix_sl, head_sl, act_sl = pooled_forward(
        lengths, vec, mixes, first, second, down
    )
    across = [(t * 16 + d, (1 - t) * 16 + d) for t in range(2) for d in range(16)]
    e_oth = lax.ppermute(e_own, BOTH, across)
    n2, middle = middle_part(lengths, tok, vec, after(mixed, e_own), second)
    (loss, scale, d_emb, d_down, d_fc, d_out, g_final, b_final, b_down, g_two, b_two, b_out, b_fc,
     mid_own, gm_all, gm_own, payload, gk, gq) = chain(
        lengths, logit_scale, after(e_own, n2), e_oth, vec, (head_sl, act_sl, n2_sl, mix_sl),
        (proj, normf, invf, norm2, inv2, slope, keys, values, norm_low, probs, gv, z_value), second, down,
    )
    got = lax.all_to_all(payload, "dp", 0, 0, tiled=True).reshape(ITEMS, PAYLOAD, 128)
    block_out, tokens_grad, q_all, norm_sl = close(
        lengths, tok, vec, gk, gv, q_own, gm_own, gq, mid_own, n2, middle, first, second, down
    )
    d_qkv, g_one, b_one, qv_sums = shard_grads(got, q_all, gm_all, norm_sl, w_own, ln1_gain, ln1_bias)
    seq = tok.shape[0]
    return (
        block_out.reshape(seq, 8, DI).transpose(1, 0, 2)[None],
        tokens_grad.reshape(seq, 8, DI).transpose(1, 0, 2)[None],
        loss.reshape(1),
        g_one,
        b_one,
        d_qkv.transpose(1, 0, 2)[None],
        qv_sums[None],
        d_out[None],
        b_out,
        g_two,
        b_two,
        d_fc[None],
        b_fc,
        d_down[None],
        b_down,
        g_final,
        b_final,
        d_emb[None],
        scale.reshape(1),
    )


def solution(mesh):
    fits = mesh.shape["dp"] == ITEMS and mesh.shape["tower"] == 2
    return jax.shard_map(
        ring_body if fits else body,
        mesh=mesh,
        in_specs=(
            P("tower", "dp", None, None),
            P("dp"),
            P("tower", "dp"),
            P("tower", "dp"),
            P("tower", "dp", None, None),
            P("tower", None, "dp"),
            P("tower", "dp", None),
            P("tower", "dp"),
            P("tower", "dp"),
            P("tower", "dp"),
            P("tower", "dp", None),
            P("tower", "dp"),
            P("tower", "dp", None),
            P("tower", "dp"),
            P("tower", "dp"),
            P("tower", "dp"),
            P("tower", "dp", None),
            P(),
        ),
        out_specs=(
            P("tower", "dp", None, None),
            P("tower", "dp", None, None),
            P(),
            P("tower", "dp"),
            P("tower", "dp"),
            P("tower", "dp", None, None),
            P("tower", None, "dp"),
            P("tower", "dp", None),
            P("tower", "dp"),
            P("tower", "dp"),
            P("tower", "dp"),
            P("tower", "dp", None),
            P("tower", "dp"),
            P("tower", "dp", None),
            P("tower", "dp"),
            P("tower", "dp"),
            P("tower", "dp"),
            P("tower", "dp", None),
            P(),
        ),
        check_vma=False,
    )
```
